32 devices in a mesh: fsdp: 4 (over x, core), ctx: 2 (over y), tp: 4 (over z).
Axes of the slice: x: 2, y: 2, z: 4, core: 2. Of those that a mesh axis runs over, the one named last changes fastest.
Arguments:
- inputs: bfloat16 [2048, 8, 768], P('ctx', 'fsdp'), may hold values from -6 to 6
- thoughts: bfloat16 [6, 8, 768], P(None, 'fsdp'), may hold values from -6 to 6
- positions: int32 [6, 8], P(None, 'fsdp'), may hold values from 0 to 2047, as said below
- lengths: int32 [8, 3], P('fsdp'), may hold values from 1 to 1024, 2048 in all within a row
- w_qkv: bfloat16 [3, 768, 768], P(None, 'fsdp', 'tp'), may hold values from -0.21875 to 0.21875
- w_out: bfloat16 [768, 768], P('tp', 'fsdp'), may hold values from -3.5 to 3.5
- w_fc: bfloat16 [768, 3072], P('fsdp', 'tp'), may hold values from -0.21875 to 0.21875
- w_proj: bfloat16 [3072, 768], P('tp', 'fsdp'), may hold values from -0.109375 to 0.109375
- norm_gains: bfloat16 [2, 768], P(None, 'fsdp'), may hold values from 0.099609375 to 1.8984375
- norm_biases: bfloat16 [2, 768], P(None, 'fsdp'), may hold values from -0.14941406 to 0.14941406
- out_grad: bfloat16 [2048, 8, 768], P('ctx', 'fsdp'), may hold values from -6 to 6
Outputs:
- output: bfloat16 [2048, 8, 768], P('ctx', 'fsdp')
- d_inputs: float32 [2048, 8, 768], P('ctx', 'fsdp')
- d_thoughts: float32 [6, 8, 768], P(None, 'fsdp')
- d_w_qkv: float32 [3, 768, 768], P(None, 'fsdp', 'tp')
- d_w_out: float32 [768, 768], P('tp', 'fsdp')
- d_w_fc: float32 [768, 3072], P('fsdp', 'tp')
- d_w_proj: float32 [3072, 768], P('tp', 'fsdp')
- d_norm_gains: float32 [2, 768], P(None, 'fsdp')
- d_bias_first: float32 [768], P('fsdp')
- d_bias_second: float32 [768], P('fsdp')
The draws below stay inside these ranges and needn't reach their ends.
Inputs may be any that keep to these rules, and one draw needn't show every extreme that they name: Each entry is a position of its sequence; the 6 positions of one sequence are distinct.
All inputs are finite; a program needn't handle non-finite values.
Results may differ from the reference program's by a relative error of at most 0.017.
Values may be sent and summed in bfloat16 or wider, within the bound.
A program may use at most 192 MiB of HBM per device.

```python
import math
import jax
import jax.numpy as jnp
import numpy as np
from jax import lax

D = 768
HEADS = 12
HEAD_DIM = 64
FF = 3072
THOUGHTS = 6
SEQ_LEN = 2048
SEQS = 8
NDOCS = 3
DOC_MOST = 1024


def draw_positions(key, part):
    seq_keys = jax.random.split(key, SEQS)
    chosen = jax.vmap(lambda one_key: jax.random.permutation(one_key, SEQ_LEN)[:THOUGHTS])(seq_keys)
    inner = jax.random.permutation(jax.random.fold_in(key, 7), SEQ_LEN - 2)[:THOUGHTS - 2] + 1
    ends = jnp.array([0, SEQ_LEN - 1], dtype=jnp.int32)
    first = jnp.concatenate([ends, inner.astype(jnp.int32)])
    chosen = chosen.astype(jnp.int32).at[0].set(first)
    return chosen.T


def block_levels(own_key, extent, pieces, smallest, top_value):
    factor_of = 1.0
    for dim, parts in pieces:
        draws = jax.random.uniform(jax.random.fold_in(jax.random.fold_in(own_key, 6), dim), (parts,), jnp.float32, smallest / len(pieces), top_value / len(pieces))
        factor_of = factor_of * jnp.repeat(jnp.exp(draws), extent[dim] // parts).reshape((-1,) + (1,) * (len(extent) - 1 - dim))
    return factor_of


def split_up(amount, total, most, lean):
    portions = [(1 << 20) // math.isqrt(grade ** lean) + 1 for grade in range(2, amount + 1)]
    spare, holding = total - most - (amount - 1), [1] * (amount - 1)
    while spare > 0:
        movable = [i for i in range(amount - 1) if holding[i] < most]
        whole, left = sum([portions[i] for i in movable]), spare
        for i in movable:
            more = min(most - holding[i], max(1, left * portions[i] // whole), spare)
            holding[i] = holding[i] + more
            spare = spare - more
    return np.array([most] + holding)


def ragged(rng, number_of, total, limit, lean):
    if number_of == 2:
        one = jax.random.randint(rng, (), max(1, total - limit), min(limit, total - 1) + 1)
        return jnp.stack([one, total - one])
    sizes = jnp.asarray(split_up(number_of, total, limit, lean), jnp.int32)
    twos = (number_of - 1) // 2
    donor, receiver = sizes[1:1 + 2 * twos:2], sizes[2:2 + 2 * twos:2]
    slack = jnp.minimum(donor - 1, limit - receiver)
    passed = jax.random.randint(jax.random.fold_in(rng, 1), (twos,), 0, 1 << 20) % (slack + 1)
    sizes = sizes.at[1:1 + 2 * twos:2].set(donor - passed).at[2:2 + 2 * twos:2].set(receiver + passed)
    return sizes[jax.random.permutation(jax.random.fold_in(rng, 2), number_of)]


def bell_draw(key, shape, width, most, cuts=(), held_as=jnp.bfloat16):
    factor_of = block_levels(key, shape, cuts, -0.22, 0.18) if cuts else 1.0
    values = jax.random.normal(key, shape, jnp.float32) * width * factor_of
    return jnp.minimum(jnp.maximum(values, -most), most).astype(held_as)


def setup_inputs(seed: int = 0) -> dict:
    keys = jax.random.split(jax.random.key(seed), 12)
    return {
        "inputs": bell_draw(keys[0], (SEQ_LEN, SEQS, D), 1.0, 6.0, ((0, 2), (1, 4))),
        "thoughts": bell_draw(keys[1], (THOUGHTS, SEQS, D), 1.0, 6.0, ((1, 4),)),
        "positions": draw_positions(jax.random.fold_in(keys[11], 71), 0),
        "lengths": jax.vmap(lambda own: ragged(own, NDOCS, SEQ_LEN, DOC_MOST, 1))(jax.random.split(keys[3], SEQS)).reshape((SEQS, NDOCS)).astype(jnp.int32),
        "w_qkv": bell_draw(keys[4], (3, D, D), D ** -0.5, 0.21875, ((1, 4), (2, 4))),
        "w_out": bell_draw(keys[5], (D, D), (max(1, D // 256)) ** -0.5, 3.5, ((0, 4), (1, 4))),
        "w_fc": bell_draw(keys[6], (D, FF), D ** -0.5, 0.21875, ((0, 4), (1, 4))),
        "w_proj": bell_draw(keys[7], (FF, D), FF ** -0.5, 0.109375, ((0, 4), (1, 4))),
        "norm_gains": jnp.clip(1.0 + 0.18 * jax.random.normal(keys[8], (2, D), jnp.float32), 0.099609375, 1.8984375).astype(jnp.bfloat16),
        "norm_biases": bell_draw(keys[9], (2, D), 0.05, 0.14941406, ((1, 4),)),
        "out_grad": bell_draw(keys[10], (SEQ_LEN, SEQS, D), 1.0, 6.0, ((0, 2), (1, 4))),
    }


EPSILON = 1e-05
NEGATIVE = -1000000000.0
PRECISE = lax.Precision.HIGHEST

@jax.custom_vjp
def low(v):
    return lax.optimization_barrier(v.astype(jnp.bfloat16)).astype(jnp.float32)

@jax.custom_vjp
def low_back(v):
    return v

def low_keep(v):
    return (low(v), None)

def low_pass(kept, grad):
    return (grad,)

def back_keep(v):
    return (v, None)

def back_low(kept, grad):
    return (low(grad),)
low.defvjp(low_keep, low_pass)
low_back.defvjp(back_keep, back_low)

def rounded(values):
    return low_back(low(values))

def layer_norm(values, gain_row, offset):
    centre = lax.optimization_barrier(jnp.mean(values, axis=-1, keepdims=True))
    shifted = values - centre
    spread = lax.optimization_barrier(jnp.mean(shifted * shifted, axis=-1, keepdims=True))
    return shifted * lax.rsqrt(spread + EPSILON) * gain_row + offset

def segment_ids(lengths, length):
    doc_ends = jnp.cumsum(lengths, dtype=jnp.int32)
    places = jnp.arange(length, dtype=jnp.int32)
    return lax.optimization_barrier(jnp.sum((places[:, None] >= doc_ends[None, :]).astype(jnp.int32), axis=1))

def sequence_forward(inputs_f, thoughts_f, weights_f, positions_col, segments):
    w_qkv, w_out, w_fc, w_proj, gains, offsets = weights_f
    length = inputs_f.shape[0]
    places = jnp.arange(length, dtype=jnp.int32)
    select = (places[:, None] == positions_col[None, :]).astype(jnp.float32)
    keep_rows = 1.0 - lax.optimization_barrier(jnp.sum(select, axis=1, keepdims=True))
    start = inputs_f * keep_rows + jnp.dot(select, thoughts_f, precision=PRECISE)
    normed = low(layer_norm(start, gains[0], offsets[0]))
    queries = rounded(jnp.dot(normed, w_qkv[0], precision=PRECISE)).reshape(length, HEADS, HEAD_DIM)
    key_rows = rounded(jnp.dot(normed, w_qkv[1], precision=PRECISE)).reshape(length, HEADS, HEAD_DIM)
    value_rows = rounded(jnp.dot(normed, w_qkv[2], precision=PRECISE)).reshape(length, HEADS, HEAD_DIM)
    score_scale = HEAD_DIM ** (-0.5)

    def attend(block_pair):
        query_block, block_start = block_pair
        scores = jnp.einsum('qhd,khd->hqk', query_block, key_rows, precision=PRECISE) * score_scale
        scores = low_back(scores)
        query_pos = block_start + jnp.arange(512, dtype=jnp.int32)
        query_seg = lax.dynamic_slice_in_dim(segments, block_start, 512, 0)
        allowed = (query_pos[:, None] >= places[None, :]) & (query_seg[:, None] == segments[None, :])
        scores = jnp.where(allowed[None], scores, NEGATIVE)
        attn_probs = low(jax.nn.softmax(scores, axis=-1))
        return jnp.einsum('hqk,khd->qhd', attn_probs, value_rows, precision=PRECISE)
    block_starts = jnp.arange(length // 512, dtype=jnp.int32) * 512
    attended = lax.map(jax.checkpoint(attend), (queries.reshape(length // 512, 512, HEADS, HEAD_DIM), block_starts))
    attended = rounded(attended.reshape(length, HEADS * HEAD_DIM))
    middle = start + low_back(jnp.dot(attended, w_out, precision=PRECISE))
    normed_mid = low(layer_norm(middle, gains[1], offsets[1]))
    expanded = low_back(jnp.dot(normed_mid, w_fc, precision=PRECISE))
    activated = low(jax.nn.gelu(expanded, approximate=True))
    return middle + low_back(jnp.dot(activated, w_proj, precision=PRECISE))

def reference(inputs, thoughts, positions, lengths, w_qkv, w_out, w_fc, w_proj, norm_gains, norm_biases, out_grad):
    weights_f = tuple((weight.astype(jnp.float32) for weight in (w_qkv, w_out, w_fc, w_proj, norm_gains, norm_biases)))

    def one_sequence(totals, column):
        inputs_col, thoughts_col, positions_col, lengths_col, grad_col = column
        segments = segment_ids(lengths_col, SEQ_LEN)

        def forward(inputs_f, thoughts_f, weights_in):
            return sequence_forward(inputs_f, thoughts_f, weights_in, positions_col, segments)
        result, pullback = jax.vjp(forward, inputs_col.astype(jnp.float32), thoughts_col.astype(jnp.float32), weights_f)
        d_in, d_thought, d_weights = pullback(grad_col.astype(jnp.float32))
        totals = jax.tree.map(lambda running, addition: running + addition, totals, d_weights)
        return (totals, (result.astype(jnp.bfloat16), d_in, d_thought))
    zeros = jax.tree.map(jnp.zeros_like, weights_f)
    columns = (jnp.moveaxis(inputs, 1, 0), jnp.moveaxis(thoughts, 1, 0), positions.T, lengths, jnp.moveaxis(out_grad, 1, 0))
    totals, (outputs, d_inputs, d_thoughts) = lax.scan(one_sequence, zeros, columns)
    return (jnp.moveaxis(outputs, 0, 1), jnp.moveaxis(d_inputs, 0, 1), jnp.moveaxis(d_thoughts, 0, 1), totals[0], totals[1], totals[2], totals[3], totals[4], totals[5][0], totals[5][1])
```

```python
import functools

import jax
import jax.numpy as jnp
from jax import lax
from jax.experimental import pallas as pl
from jax.experimental.pallas import tpu as pltpu
from jax.sharding import PartitionSpec as P

HEAD_DIM = 64
DOC_MOST = 1024
EPSILON = 1e-05
MASKED = -1e30


def dot(a, b, dims=((1,), (0,))):
    return lax.dot_general(a, b, (dims, ((), ())), preferred_element_type=jnp.float32)


def hat_rows(values):
    centre = jnp.mean(values, axis=-1, keepdims=True)
    shifted = values - centre
    spread = jnp.mean(shifted * shifted, axis=-1, keepdims=True)
    inv = lax.rsqrt(spread + EPSILON)
    return shifted * inv, inv


def norm_back(hat, inv, gain, grad):
    eg = grad * gain
    return inv * (
        eg
        - jnp.mean(eg, axis=-1, keepdims=True)
        - hat * jnp.mean(eg * hat, axis=-1, keepdims=True)
    )


def attend_kernel(heads, far, block, first_ref, qkv_ref, prev_ref, low_ref, out_ref, out_t_ref, log_ref, k_s, vt_s, qt_s):
    s = pl.program_id(0)
    rows = qkv_ref.shape[0]
    width = heads * HEAD_DIM
    for h in range(heads):
        cols = slice(h * HEAD_DIM, (h + 1) * HEAD_DIM)
        kcols = slice(width + h * HEAD_DIM, width + (h + 1) * HEAD_DIM)
        vcols = slice(2 * width + h * HEAD_DIM, 2 * width + (h + 1) * HEAD_DIM)
        qt_s[h] = (qkv_ref[:, cols].astype(jnp.float32) * 0.125).T.astype(jnp.bfloat16)
        if far:
            k_s[h, : far * rows] = prev_ref[:, cols]
            vt_s[h, :, : far * rows] = prev_ref[:, kcols].astype(jnp.float32).T.astype(jnp.bfloat16)
        k_s[h, far * rows :] = qkv_ref[:, kcols]
        vt_s[h, :, far * rows :] = qkv_ref[:, vcols].astype(jnp.float32).T.astype(jnp.bfloat16)
    for i in range(rows // block):
        span = slice(i * block, (i + 1) * block)
        low = low_ref[:, span]
        top = far * rows + i * block + lax.broadcasted_iota(jnp.int32, (1, block), 1)
        last = far * (rows // block) + i + 1
        for h in range(heads):
            q_t = qt_s[h, :, span]

            def step(kb, carry):
                m, l, acc = carry
                base = pl.multiple_of(kb * block, block)
                scores = dot(k_s[h, pl.ds(base, block), :], q_t)
                place = base + lax.broadcasted_iota(jnp.int32, (block, 1), 0)
                scores = jnp.where((place >= low) & (place <= top), scores, MASKED)
                m_new = jnp.maximum(m, jnp.max(scores, axis=0, keepdims=True))
                p = jnp.exp(scores - m_new)
                alpha = jnp.exp(m - m_new)
                l = alpha * l + jnp.sum(p, axis=0, keepdims=True)
                acc = alpha * acc + dot(vt_s[h, :, pl.ds(base, block)], p.astype(jnp.bfloat16))
                return m_new, l, acc

            m, l, acc = lax.fori_loop(
                first_ref[s, i],
                last,
                step,
                (
                    jnp.full((1, block), MASKED, jnp.float32),
                    jnp.zeros((1, block), jnp.float32),
                    jnp.zeros((HEAD_DIM, block), jnp.float32),
                ),
            )
            mixed = acc / l
            out_t_ref[h * HEAD_DIM : (h + 1) * HEAD_DIM, span] = mixed
            log_ref[h : h + 1, span] = m + jnp.log(l)
        out_ref[span, :] = out_t_ref[:, span].T.astype(jnp.bfloat16)


def attend(qkv, prev, low, first, block):
    seqs, rows, width3 = qkv.shape
    width = width3 // 3
    heads = width // HEAD_DIM
    far = 0 if prev is None else prev.shape[1] // rows
    if prev is None:
        prev = jnp.zeros((seqs, 16, 2 * width), qkv.dtype)
    spec = lambda *shape: pl.BlockSpec((None,) + shape, lambda s, *_: (s, 0, 0))
    return pl.pallas_call(
        functools.partial(attend_kernel, heads, far, block),
        grid_spec=pltpu.PrefetchScalarGridSpec(
            num_scalar_prefetch=1,
            grid=(seqs,),
            in_specs=[spec(rows, width3), spec(prev.shape[1], 2 * width), spec(1, rows)],
            out_specs=[spec(rows, width), spec(width, rows), spec(8, rows)],
            scratch_shapes=[
                pltpu.VMEM((heads, (far + 1) * rows, HEAD_DIM), jnp.bfloat16),
                pltpu.VMEM((heads, HEAD_DIM, (far + 1) * rows), jnp.bfloat16),
                pltpu.VMEM((heads, HEAD_DIM, rows), jnp.bfloat16),
            ],
        ),
        out_shape=[
            jax.ShapeDtypeStruct((seqs, rows, width), jnp.bfloat16),
            jax.ShapeDtypeStruct((seqs, width, rows), jnp.float32),
            jax.ShapeDtypeStruct((seqs, 8, rows), jnp.float32),
        ],
        compiler_params=pltpu.CompilerParams(vmem_limit_bytes=48 << 20),
        cost_estimate=pl.CostEstimate(flops=8 * 10**9, bytes_accessed=8 << 20, transcendentals=8 << 20),
    )(first, qkv, prev, low)


def attend_back_kernel(
    heads, far, block, first_ref, qkv_ref, prev_ref, low_ref, grad_ref, out_t_ref, log_ref,
    dq_ref, dkv_ref, dprev_ref, k_s, kt_s, v_s, q_s, qt_s, g_s, gt_s, dqt_s, dk_s, dv_s,
):
    s = pl.program_id(0)
    rows = qkv_ref.shape[0]
    width = heads * HEAD_DIM
    for h in range(heads):
        cols = slice(h * HEAD_DIM, (h + 1) * HEAD_DIM)
        kcols = slice(width + h * HEAD_DIM, width + (h + 1) * HEAD_DIM)
        vcols = slice(2 * width + h * HEAD_DIM, 2 * width + (h + 1) * HEAD_DIM)
        q = qkv_ref[:, cols].astype(jnp.float32) * 0.125
        q_s[h] = q.astype(jnp.bfloat16)
        qt_s[h] = q.T.astype(jnp.bfloat16)
        g = grad_ref[:, cols]
        g_s[h] = g
        gt_s[h] = g.astype(jnp.float32).T.astype(jnp.bfloat16)
        if far:
            k = prev_ref[:, cols]
            k_s[h, : far * rows] = k
            kt_s[h, :, : far * rows] = k.astype(jnp.float32).T.astype(jnp.bfloat16)
            v_s[h, : far * rows] = prev_ref[:, kcols]
        k = qkv_ref[:, kcols]
        k_s[h, far * rows :] = k
        kt_s[h, :, far * rows :] = k.astype(jnp.float32).T.astype(jnp.bfloat16)
        v_s[h, far * rows :] = qkv_ref[:, vcols]
    dk_s[...] = jnp.zeros_like(dk_s)
    dv_s[...] = jnp.zeros_like(dv_s)
    for i in range(rows // block):
        span = slice(i * block, (i + 1) * block)
        low = low_ref[:, span]
        top = far * rows + i * block + lax.broadcasted_iota(jnp.int32, (1, block), 1)
        last = far * (rows // block) + i + 1
        for h in range(heads):
            cols = slice(h * HEAD_DIM, (h + 1) * HEAD_DIM)
            q_t = qt_s[h, :, span]
            q = q_s[h, span, :]
            g = g_s[h, span, :]
            g_t = gt_s[h, :, span]
            log = log_ref[h : h + 1, span]
            delta = jnp.sum(g_t.astype(jnp.float32) * out_t_ref[cols, span], axis=0, keepdims=True)

            def step(kb, dq_t):
                base = pl.multiple_of(kb * block, block)
                here = pl.ds(base, block)
                scores = dot(k_s[h, here, :], q_t)
                place = base + lax.broadcasted_iota(jnp.int32, (block, 1), 0)
                p = jnp.exp(jnp.where((place >= low) & (place <= top), scores - log, MASKED))
                dp = dot(v_s[h, here, :], g_t)
                ds = (p * (dp - delta)).astype(jnp.bfloat16)
                dv_s[h, here, :] += dot(p.astype(jnp.bfloat16), g)
                dk_s[h, here, :] += dot(ds, q)
                return dq_t + dot(kt_s[h, :, here], ds)

            dqt_s[cols, span] = 0.125 * lax.fori_loop(
                first_ref[s, i], last, step, jnp.zeros((HEAD_DIM, block), jnp.float32)
            )
        dq_ref[span, :] = dqt_s[:, span].T.astype(jnp.bfloat16)
    own = slice(far * rows, (far + 1) * rows)
    dkv_ref[...] = jnp.concatenate(
        [dk_s[h, own] for h in range(heads)] + [dv_s[h, own] for h in range(heads)], axis=1
    )
    if far:
        past = slice(0, far * rows)
        dprev_ref[...] = jnp.concatenate(
            [dk_s[h, past] for h in range(heads)] + [dv_s[h, past] for h in range(heads)], axis=1
        ).astype(jnp.bfloat16)


def attend_back(qkv, prev, low, first, grad, out_t, logs, block):
    seqs, rows, width3 = qkv.shape
    width = width3 // 3
    heads = width // HEAD_DIM
    far = 0 if prev is None else prev.shape[1] // rows
    if prev is None:
        prev = jnp.zeros((seqs, 16, 2 * width), qkv.dtype)
    spec = lambda *shape: pl.BlockSpec((None,) + shape, lambda s, *_: (s, 0, 0))
    span = (far + 1) * rows
    bf, f32 = jnp.bfloat16, jnp.float32
    return pl.pallas_call(
        functools.partial(attend_back_kernel, heads, far, block),
        grid_spec=pltpu.PrefetchScalarGridSpec(
            num_scalar_prefetch=1,
            grid=(seqs,),
            in_specs=[
                spec(rows, width3), spec(prev.shape[1], 2 * width), spec(1, rows),
                spec(rows, width), spec(width, rows), spec(8, rows),
            ],
            out_specs=[spec(rows, width), spec(rows, 2 * width), spec(prev.shape[1], 2 * width)],
            scratch_shapes=[
                pltpu.VMEM((heads, span, HEAD_DIM), bf),
                pltpu.VMEM((heads, HEAD_DIM, span), bf),
                pltpu.VMEM((heads, span, HEAD_DIM), bf),
                pltpu.VMEM((heads, rows, HEAD_DIM), bf),
                pltpu.VMEM((heads, HEAD_DIM, rows), bf),
                pltpu.VMEM((heads, rows, HEAD_DIM), bf),
                pltpu.VMEM((heads, HEAD_DIM, rows), bf),
                pltpu.VMEM((width, rows), f32),
                pltpu.VMEM((heads, span, HEAD_DIM), f32),
                pltpu.VMEM((heads, span, HEAD_DIM), f32),
            ],
        ),
        out_shape=[
            jax.ShapeDtypeStruct((seqs, rows, width), bf),
            jax.ShapeDtypeStruct((seqs, rows, 2 * width), f32),
            jax.ShapeDtypeStruct((seqs, prev.shape[1], 2 * width), bf),
        ],
        compiler_params=pltpu.CompilerParams(vmem_limit_bytes=56 << 20),
        cost_estimate=pl.CostEstimate(flops=16 * 10**9, bytes_accessed=16 << 20, transcendentals=8 << 20),
    )(first, qkv, prev, low, grad, out_t, logs)


def local(
    inputs, thoughts, positions, lengths, w_qkv, w_out, w_fc, w_proj, norm_gains, norm_biases, out_grad,
):
    rows, seqs, width = inputs.shape
    ctx_count = lax.axis_size("ctx")
    tp_count = lax.axis_size("tp")
    ctx, tp = lax.axis_index("ctx"), lax.axis_index("tp")
    first_row = ctx * rows
    own_rows = rows // tp_count
    own_tokens = own_rows * seqs
    far = min(ctx_count - 1, -(-(DOC_MOST - 1) // rows))
    block = min(256, rows)
    bf, f32 = jnp.bfloat16, jnp.float32

    qkv_full = lax.all_gather(w_qkv, "fsdp", axis=1, tiled=True)
    params = lax.all_gather(jnp.concatenate([norm_gains, norm_biases]), "fsdp", axis=1, tiled=True).astype(f32)
    gains, biases = params[:2], params[2:]
    everywhere = lambda w, axes: functools.reduce(
        lambda v, pair: lax.all_gather(v, pair[0], axis=pair[1], tiled=True), axes, w
    )
    out_full = everywhere(w_out, (("tp", 0), ("fsdp", 1)))
    fc_full = everywhere(w_fc, (("tp", 1), ("fsdp", 0)))
    proj_full = everywhere(w_proj, (("tp", 0), ("fsdp", 1)))
    qkv_all = everywhere(w_qkv, (("tp", 2), ("fsdp", 1)))

    local_width = qkv_full.shape[2]
    qkv_matrix = jnp.transpose(qkv_full, (1, 0, 2)).reshape(width, 3 * local_width)
    places = first_row + jnp.arange(rows, dtype=jnp.int32)
    is_thought = places[None, None, :] == positions[:, :, None]
    keep = jnp.logical_not(jnp.any(is_thought, axis=0))
    start = jnp.transpose(inputs, (1, 0, 2))
    for t in range(thoughts.shape[0]):
        start = jnp.where(is_thought[t][:, :, None], thoughts[t][:, None, :], start)
    hat, inv = hat_rows(start.astype(f32))
    normed = (hat * gains[0] + biases[0]).astype(bf)
    normed_flat = normed.reshape(seqs * rows, width)
    qkv = dot(normed_flat, qkv_matrix).astype(bf).reshape(seqs, rows, 3 * local_width)

    ends = jnp.cumsum(lengths, axis=1, dtype=jnp.int32)
    low = jnp.max(jnp.where(ends[:, :, None] <= places[None, None, :], ends[:, :, None], 0), axis=1)
    low = low - (first_row - far * rows)
    first = low[:, ::block] // block

    kv = qkv[:, :, local_width:]
    prev = None
    if far:
        prev = jnp.concatenate(
            [
                lax.ppermute(kv, "ctx", [(i, i + d) for i in range(ctx_count - d)])
                for d in range(far, 0, -1)
            ],
            axis=1,
        )
    low3 = low[:, None, :]
    attended, out_t, logs = attend(qkv, prev, low3, first, block)

    own = lambda a: lax.dynamic_slice_in_dim(a, tp * own_rows, own_rows, 1).reshape(own_tokens, width)
    spread = lambda a: lax.all_to_all(a, "tp", split_axis=1, concat_axis=2, tiled=True).reshape(own_tokens, -1)
    attended_own = spread(attended)
    start_own = own(start).astype(f32)
    grad_own = jnp.transpose(
        lax.dynamic_slice_in_dim(out_grad, tp * own_rows, own_rows, 0), (1, 0, 2)
    ).reshape(own_tokens, width)
    middle = start_own + dot(attended_own, out_full)
    mid_hat, mid_inv = hat_rows(middle)
    normed_mid = (mid_hat * gains[1] + biases[1]).astype(bf)
    expanded = dot(normed_mid, fc_full)
    act, gelu_back = jax.vjp(lambda v: jax.nn.gelu(v, approximate=True), expanded)
    activated = act.astype(bf)
    output_own = (middle + dot(activated, proj_full)).astype(bf)
    d_activated = dot(grad_own, proj_full, ((1,), (1,)))
    d_expanded = gelu_back(d_activated)[0].astype(bf)
    d_normed_mid = dot(d_expanded, fc_full, ((1,), (1,)))
    d_middle = grad_own.astype(f32) + norm_back(mid_hat, mid_inv, gains[1], d_normed_mid)
    d_middle_b = d_middle.astype(bf)
    d_attended_own = dot(d_middle_b, out_full, ((1,), (1,))).astype(bf)
    d_attended = lax.all_to_all(
        d_attended_own.reshape(seqs, own_rows, width), "tp", split_axis=2, concat_axis=1, tiled=True
    )
    output = lax.all_gather(output_own.reshape(seqs, own_rows, width), "tp", axis=1, tiled=True)
    output = jnp.transpose(output, (1, 0, 2))
    d_proj = dot(activated, grad_own, ((0,), (0,)))
    d_fc = dot(normed_mid, d_expanded, ((0,), (0,)))
    d_out = dot(attended_own, d_middle_b, ((0,), (0,)))

    d_q, d_kv, d_prev = attend_back(qkv, prev, low3, first, d_attended, out_t, logs, block)
    for index, d in enumerate(range(far, 0, -1)):
        piece = d_prev[:, index * rows : (index + 1) * rows]
        d_kv = d_kv + lax.ppermute(piece, "ctx", [(i + d, i) for i in range(ctx_count - d)]).astype(f32)
    d_qkv = jnp.concatenate([d_q, d_kv.astype(bf)], axis=2)
    d_w_qkv = dot(normed_flat, d_qkv.reshape(seqs * rows, -1), ((0,), (0,)))
    d_w_qkv = jnp.transpose(d_w_qkv.reshape(width, 3, local_width), (1, 0, 2))
    d_qkv_own = lax.all_to_all(d_qkv, "tp", split_axis=1, concat_axis=2, tiled=True)
    d_qkv_own = d_qkv_own.reshape(own_tokens, tp_count, 3, local_width)
    qkv_all = qkv_all.reshape(3, width, tp_count, local_width)
    d_normed = lax.dot_general(
        d_qkv_own, qkv_all, (((1, 2, 3), (2, 0, 3)), ((), ())), preferred_element_type=f32
    )
    hat_own, inv_own = hat_rows(start_own)
    d_start_own = d_middle + norm_back(hat_own, inv_own, gains[0], d_normed)
    d_start = lax.all_gather(d_start_own.astype(bf).reshape(seqs, own_rows, width), "tp", axis=1, tiled=True)
    d_inputs = jnp.transpose(jnp.where(keep[:, :, None], d_start.astype(f32), 0.0), (1, 0, 2))
    d_thoughts = jnp.einsum(
        "tsr,srd->tsd", is_thought.astype(bf), d_start, preferred_element_type=f32
    )
    small = jnp.stack(
        [
            jnp.sum(d_normed * hat_own, axis=0),
            jnp.sum(d_normed_mid * mid_hat, axis=0),
            jnp.sum(d_normed, axis=0),
            jnp.sum(d_normed_mid, axis=0),
        ]
    )
    reduce = lambda g, axes: lax.psum(
        functools.reduce(
            lambda v, pair: lax.psum_scatter(v, pair[0], scatter_dimension=pair[1], tiled=True),
            axes,
            g.astype(bf),
        ),
        "ctx",
    ).astype(f32)
    small = lax.psum(lax.psum_scatter(small, "fsdp", scatter_dimension=1, tiled=True), ("ctx", "tp"))
    return (
        output,
        d_inputs,
        lax.psum(d_thoughts.astype(bf), "ctx").astype(f32),
        reduce(d_w_qkv, (("fsdp", 1),)),
        reduce(d_out, (("fsdp", 1), ("tp", 0))),
        reduce(d_fc, (("fsdp", 0), ("tp", 1))),
        reduce(d_proj, (("fsdp", 1), ("tp", 0))),
        small[:2],
        small[2],
        small[3],
    )


def solution(mesh):
    in_specs = (
        P("ctx", "fsdp", None),
        P(None, "fsdp", None),
        P(None, "fsdp"),
        P("fsdp", None),
        P(None, "fsdp", "tp"),
        P("tp", "fsdp"),
        P("fsdp", "tp"),
        P("tp", "fsdp"),
        P(None, "fsdp"),
        P(None, "fsdp"),
        P("ctx", "fsdp", None),
    )
    out_specs = (
        P("ctx", "fsdp", None),
        P("ctx", "fsdp", None),
        P(None, "fsdp", None),
        P(None, "fsdp", "tp"),
        P("tp", "fsdp"),
        P("fsdp", "tp"),
        P("tp", "fsdp"),
        P(None, "fsdp"),
        P("fsdp"),
        P("fsdp"),
    )
    return jax.shard_map(local, mesh=mesh, in_specs=in_specs, out_specs=out_specs, check_vma=False)
```

```python
import functools

import jax
import jax.numpy as jnp
from jax import lax
from jax.experimental import pallas as pl
from jax.experimental.pallas import tpu as pltpu
from jax.sharding import PartitionSpec as P

HEAD_DIM = 64
DOC_MOST = 1024
EPSILON = 1e-05
MASKED = -1e30


def dot(a, b, dims=((1,), (0,))):
    return lax.dot_general(a, b, (dims, ((), ())), preferred_element_type=jnp.float32)


def hat_rows(values):
    centre = jnp.mean(values, axis=-1, keepdims=True)
    shifted = values - centre
    spread = jnp.mean(shifted * shifted, axis=-1, keepdims=True)
    inv = lax.rsqrt(spread + EPSILON)
    return shifted * inv, inv


def norm_back(hat, inv, gain, grad):
    eg = grad * gain
    return inv * (
        eg
        - jnp.mean(eg, axis=-1, keepdims=True)
        - hat * jnp.mean(eg * hat, axis=-1, keepdims=True)
    )


MESH = pl.DeviceIdType.MESH
VMEM_LIMIT = 60 << 20


def column(index, size=HEAD_DIM):
    return slice(index * size, (index + 1) * size)


def turn(value):
    return value.astype(jnp.float32).T.astype(jnp.bfloat16)


def attend_kernel(heads, far, block, first_ref, qkv_ref, prev_ref, low_ref, out_ref, out_t_ref, log_ref, k_s, vt_s, qt_s):
    s = pl.program_id(0)
    rows = qkv_ref.shape[0]
    parts, own_rows = out_ref.shape[0], out_ref.shape[1]
    for h in range(heads):
        qt_s[h] = turn(qkv_ref[:, column(h)].astype(jnp.float32) * 0.125)
        if far:
            k_s[h, : far * rows] = prev_ref[:, column(h)]
            vt_s[h, :, : far * rows] = turn(prev_ref[:, column(heads + h)])
        k_s[h, far * rows :] = qkv_ref[:, column(heads + h)]
        vt_s[h, :, far * rows :] = turn(qkv_ref[:, column(2 * heads + h)])
    for i in range(rows // block):
        span = column(i, block)
        low = low_ref[:, span]
        top = far * rows + i * block + lax.broadcasted_iota(jnp.int32, (1, block), 1)
        last = far * (rows // block) + i + 1

        def step(kb, carry):
            base = pl.multiple_of(kb * block, block)
            here = pl.ds(base, block)
            place = base + lax.broadcasted_iota(jnp.int32, (block, 1), 0)
            allowed = (place >= low) & (place <= top)
            after = []
            for h in range(heads):
                m, l, acc = carry[h]
                scores = dot(k_s[h, here, :], qt_s[h, :, span])
                scores = jnp.where(allowed, scores, MASKED)
                m_new = jnp.maximum(m, jnp.max(scores, axis=0, keepdims=True))
                p = jnp.exp(scores - m_new)
                alpha = jnp.exp(m - m_new)
                l = alpha * l + jnp.sum(p, axis=0, keepdims=True)
                acc = alpha * acc + dot(vt_s[h, :, here], p.astype(jnp.bfloat16))
                after.append((m_new, l, acc))
            return tuple(after)

        ends = lax.fori_loop(
            first_ref[s, i],
            last,
            step,
            tuple(
                (
                    jnp.full((1, block), MASKED, jnp.float32),
                    jnp.zeros((1, block), jnp.float32),
                    jnp.zeros((HEAD_DIM, block), jnp.float32),
                )
                for _ in range(heads)
            ),
        )
        for h, (m, l, acc) in enumerate(ends):
            out_t_ref[column(h), span] = acc / l
            log_ref[h : h + 1, span] = m + jnp.log(l)
    for t in range(parts):
        out_ref[t] = turn_back(out_t_ref[:, column(t, own_rows)])


def turn_back(value):
    return value.T.astype(jnp.bfloat16)


def attend(qkv, prev, low, first, block, parts):
    seqs, rows, width3 = qkv.shape
    width = width3 // 3
    heads = width // HEAD_DIM
    far = 0 if prev is None else prev.shape[1] // rows
    if prev is None:
        prev = jnp.zeros((seqs, 16, 2 * width), qkv.dtype)
    spec = lambda *shape: pl.BlockSpec((None,) + shape, lambda s, *_: (s, 0, 0))
    return pl.pallas_call(
        functools.partial(attend_kernel, heads, far, block),
        grid_spec=pltpu.PrefetchScalarGridSpec(
            num_scalar_prefetch=1,
            grid=(seqs,),
            in_specs=[spec(rows, width3), spec(prev.shape[1], 2 * width), spec(1, rows)],
            out_specs=[
                pl.BlockSpec((parts, None, rows // parts, width), lambda s, *_: (0, s, 0, 0)),
                spec(width, rows),
                spec(8, rows),
            ],
            scratch_shapes=[
                pltpu.VMEM((heads, (far + 1) * rows, HEAD_DIM), jnp.bfloat16),
                pltpu.VMEM((heads, HEAD_DIM, (far + 1) * rows), jnp.bfloat16),
                pltpu.VMEM((heads, HEAD_DIM, rows), jnp.bfloat16),
            ],
        ),
        out_shape=[
            jax.ShapeDtypeStruct((parts, seqs, rows // parts, width), jnp.bfloat16),
            jax.ShapeDtypeStruct((seqs, width, rows), jnp.float32),
            jax.ShapeDtypeStruct((seqs, 8, rows), jnp.float32),
        ],
        compiler_params=pltpu.CompilerParams(vmem_limit_bytes=48 << 20),
        cost_estimate=pl.CostEstimate(flops=8 * 10**9, bytes_accessed=8 << 20, transcendentals=8 << 20),
    )(first, qkv, prev, low)


def attend_back_kernel(
    heads, far, block, first_ref, qkv_ref, prev_ref, low_ref, grad_ref, out_t_ref, log_ref,
    dq_ref, dkv_ref, dprev_ref, k_s, kt_s, v_s, q_s, qt_s, g_s, gt_s, dqt_s, dk_s, dv_s,
):
    s = pl.program_id(0)
    rows = qkv_ref.shape[0]
    parts, own_rows = grad_ref.shape[0], grad_ref.shape[1]
    for h in range(heads):
        q = qkv_ref[:, column(h)].astype(jnp.float32) * 0.125
        q_s[h] = q.astype(jnp.bfloat16)
        qt_s[h] = turn_back(q)
        for t in range(parts):
            g_s[h, column(t, own_rows), :] = grad_ref[t, :, column(h)]
        gt_s[h] = turn(g_s[h])
        if far:
            k = prev_ref[:, column(h)]
            k_s[h, : far * rows] = k
            kt_s[h, :, : far * rows] = turn(k)
            v_s[h, : far * rows] = prev_ref[:, column(heads + h)]
        k = qkv_ref[:, column(heads + h)]
        k_s[h, far * rows :] = k
        kt_s[h, :, far * rows :] = turn(k)
        v_s[h, far * rows :] = qkv_ref[:, column(2 * heads + h)]
    dk_s[...] = jnp.zeros_like(dk_s)
    dv_s[...] = jnp.zeros_like(dv_s)
    for i in range(rows // block):
        span = column(i, block)
        low = low_ref[:, span]
        top = far * rows + i * block + lax.broadcasted_iota(jnp.int32, (1, block), 1)
        last = far * (rows // block) + i + 1
        deltas = [
            jnp.sum(gt_s[h, :, span].astype(jnp.float32) * out_t_ref[column(h), span], axis=0, keepdims=True)
            for h in range(heads)
        ]

        def step(kb, carry):
            base = pl.multiple_of(kb * block, block)
            here = pl.ds(base, block)
            place = base + lax.broadcasted_iota(jnp.int32, (block, 1), 0)
            allowed = (place >= low) & (place <= top)
            after = []
            for h in range(heads):
                scores = dot(k_s[h, here, :], qt_s[h, :, span])
                p = jnp.exp(jnp.where(allowed, scores - log_ref[h : h + 1, span], MASKED))
                dp = dot(v_s[h, here, :], gt_s[h, :, span])
                ds = (p * (dp - deltas[h])).astype(jnp.bfloat16)
                dv_s[h, here, :] += dot(p.astype(jnp.bfloat16), g_s[h, span, :])
                dk_s[h, here, :] += dot(ds, q_s[h, span, :])
                after.append(carry[h] + dot(kt_s[h, :, here], ds))
            return tuple(after)

        ends = lax.fori_loop(
            first_ref[s, i], last, step, tuple(jnp.zeros((HEAD_DIM, block), jnp.float32) for _ in range(heads))
        )
        for h in range(heads):
            dqt_s[column(h), span] = 0.125 * ends[h]
    for t in range(parts):
        dq_ref[t] = dqt_s[:, column(t, own_rows)].astype(jnp.bfloat16)
    for h in range(heads):
        for source, at in ((dk_s, h), (dv_s, heads + h)):
            whole = source[h].T
            for d in range(far):
                for t in range(parts):
                    dprev_ref[d, t, column(at), :] = whole[:, column(d * parts + t, own_rows)].astype(jnp.bfloat16)
            for t in range(parts):
                dkv_ref[t, column(at), :] = whole[:, column(far * parts + t, own_rows)]


def attend_back(qkv, prev, low, first, grad, out_t, logs, block):
    seqs, rows, width3 = qkv.shape
    parts = grad.shape[0]
    own_rows = rows // parts
    width = width3 // 3
    heads = width // HEAD_DIM
    far = 0 if prev is None else prev.shape[1] // rows
    if prev is None:
        prev = jnp.zeros((seqs, 16, 2 * width), qkv.dtype)
    spec = lambda *shape: pl.BlockSpec((None,) + shape, lambda s, *_: (s, 0, 0))
    chunked = lambda *shape: pl.BlockSpec((parts, None) + shape, lambda s, *_: (0, s, 0, 0))
    span = (far + 1) * rows
    dists = max(far, 1)
    bf, f32 = jnp.bfloat16, jnp.float32
    return pl.pallas_call(
        functools.partial(attend_back_kernel, heads, far, block),
        grid_spec=pltpu.PrefetchScalarGridSpec(
            num_scalar_prefetch=1,
            grid=(seqs,),
            in_specs=[
                spec(rows, width3), spec(prev.shape[1], 2 * width), spec(1, rows),
                chunked(own_rows, width), spec(width, rows), spec(8, rows),
            ],
            out_specs=[
                chunked(width, own_rows), chunked(2 * width, own_rows),
                pl.BlockSpec((dists, parts, None, 2 * width, own_rows), lambda s, *_: (0, 0, s, 0, 0)),
            ],
            scratch_shapes=[
                pltpu.VMEM((heads, span, HEAD_DIM), bf),
                pltpu.VMEM((heads, HEAD_DIM, span), bf),
                pltpu.VMEM((heads, span, HEAD_DIM), bf),
                pltpu.VMEM((heads, rows, HEAD_DIM), bf),
                pltpu.VMEM((heads, HEAD_DIM, rows), bf),
                pltpu.VMEM((heads, rows, HEAD_DIM), bf),
                pltpu.VMEM((heads, HEAD_DIM, rows), bf),
                pltpu.VMEM((width, rows), f32),
                pltpu.VMEM((heads, span, HEAD_DIM), f32),
                pltpu.VMEM((heads, span, HEAD_DIM), f32),
            ],
        ),
        out_shape=[
            jax.ShapeDtypeStruct((parts, seqs, width, own_rows), bf),
            jax.ShapeDtypeStruct((parts, seqs, 2 * width, own_rows), f32),
            jax.ShapeDtypeStruct((dists, parts, seqs, 2 * width, own_rows), bf),
        ],
        compiler_params=pltpu.CompilerParams(vmem_limit_bytes=VMEM_LIMIT),
        cost_estimate=pl.CostEstimate(flops=16 * 10**9, bytes_accessed=16 << 20, transcendentals=8 << 20),
    )(first, qkv, prev, low, grad, out_t, logs)


def feed_kernel(
    step_cols, att_ref, start_ref, grad_ref, out_w_ref, params_ref, fc_ref, proj_ref,
    out_ref, datt_ref, dmid_ref, g_ref, small_ref,
    mid_s, nm_s, nmt_s, gt_s, acc_s, dnm_s, stage_s, last_s, sems, last_sem,
):
    t = pl.program_id(0)
    parts = pl.num_programs(0)
    count = att_ref.shape[0]
    part_cols = att_ref.shape[2]
    shards = stage_s.shape[1]
    shard_rows = stage_s.shape[2]
    hidden = fc_ref.shape[1]
    bf, f32 = jnp.bfloat16, jnp.float32

    @pl.when(t == 0)
    def _():
        mid = start_ref[...].astype(f32)
        for c in range(count):
            mid = mid + dot(att_ref[c], out_w_ref[column(c, part_cols), :])
        mid_s[...] = mid
        hat, _ = hat_rows(mid)
        nm = hat * params_ref[1:2] + params_ref[3:4]
        nm_s[...] = nm.astype(bf)
        nmt_s[...] = turn_back(nm)
        gt_s[...] = turn(grad_ref[...])
        acc_s[...] = jnp.zeros_like(acc_s)
        dnm_s[...] = jnp.zeros_like(dnm_s)

    slot = lax.rem(t, 2)
    store = lambda at, where: pltpu.make_async_copy(
        stage_s.at[where], g_ref.at[:, at, :, pl.ds(0, 2 * hidden)], sems.at[where]
    )

    @pl.when(t >= 2)
    def _():
        store(t - 2, slot).wait()

    def one(j, _):
        here = pl.ds(pl.multiple_of(j * step_cols, step_cols), step_cols)
        there = pl.ds(pl.multiple_of(hidden + j * step_cols, step_cols), step_cols)
        fc = fc_ref[:, here]
        proj = proj_ref[:, here]
        x = dot(nm_s[...], fc)
        d_act = dot(grad_ref[...], proj)
        square = x * x
        th = jnp.tanh(0.7978845608028654 * (x + 0.044715 * (square * x)))
        half = 0.5 * (1.0 + th)
        act = (x * half).astype(bf)
        slope = half + (0.5 * x) * (1.0 - th * th) * (
            0.7978845608028654 * (1.0 + (3 * 0.044715) * square)
        )
        d_exp = (slope * d_act).astype(bf)
        acc_s[...] += dot(act, proj, ((1,), (1,)))
        dnm_s[...] += dot(d_exp, fc, ((1,), (1,)))
        d_fc = dot(nmt_s[...], d_exp).astype(bf)
        d_proj = dot(gt_s[...], act).astype(bf)
        for f in range(shards):
            stage_s[slot, f, :, here] = d_fc[column(f, shard_rows)]
            stage_s[slot, f, :, there] = d_proj[column(f, shard_rows)]
        return 0

    lax.fori_loop(0, hidden // step_cols, one, 0)
    store(t, slot).start()

    @pl.when(t == parts - 1)
    def _():
        mid = mid_s[...]
        out_ref[...] = (mid + acc_s[...]).astype(bf)
        hat, inv = hat_rows(mid)
        d_nm = dnm_s[...]
        d_mid = grad_ref[...].astype(f32) + norm_back(hat, inv, params_ref[1:2], d_nm)
        dmid_ref[...] = d_mid
        d_mid_b = d_mid.astype(bf)
        d_mid_t = turn_back(d_mid)
        small_ref[...] = jnp.concatenate(
            [
                jnp.zeros((1, mid.shape[1]), f32),
                jnp.sum(d_nm * hat, axis=0, keepdims=True),
                jnp.zeros((1, mid.shape[1]), f32),
                jnp.sum(d_nm, axis=0, keepdims=True),
                jnp.zeros((4, mid.shape[1]), f32),
            ],
            axis=0,
        )
        for c in range(count):
            datt_ref[c] = dot(d_mid_b, out_w_ref[column(c, part_cols), :], ((1,), (1,))).astype(bf)
            d_out = dot(d_mid_t, att_ref[c]).astype(bf)
            for f in range(shards):
                last_s[f, c, :, :part_cols] = d_out[column(f, shard_rows)]
        if last_s.shape[3] > part_cols:
            last_s[:, :, :, part_cols:] = jnp.zeros(last_s.shape[:3] + (last_s.shape[3] - part_cols,), bf)
        final = pltpu.make_async_copy(
            last_s, g_ref.at[:, :, :, pl.ds(2 * hidden, last_s.shape[3])], last_sem
        )
        final.start()
        if parts >= 2:
            store(parts - 2, (parts - 2) % 2).wait()
        store(parts - 1, (parts - 1) % 2).wait()
        final.wait()


def padded(size):
    return -(-size // 128) * 128


def feed(att, start, grad, out_w, params, fc, proj_t, shards):
    parts, tokens, part_cols = att.shape
    width, hidden_all = fc.shape
    hidden = hidden_all // parts
    shard_rows = width // shards
    step_cols = 256
    wide = 2 * hidden + padded(part_cols)
    bf, f32 = jnp.bfloat16, jnp.float32
    whole = lambda *shape: pl.BlockSpec(shape, lambda t: (0,) * len(shape))
    return pl.pallas_call(
        functools.partial(feed_kernel, step_cols),
        grid=(parts,),
        in_specs=[
            whole(parts, tokens, part_cols), whole(tokens, width), whole(tokens, width), whole(width, width),
            whole(4, width),
            pl.BlockSpec((width, hidden), lambda t: (0, t)),
            pl.BlockSpec((width, hidden), lambda t: (0, t)),
        ],
        out_specs=[
            whole(tokens, width), whole(parts, tokens, part_cols), whole(tokens, width),
            pl.BlockSpec(memory_space=pl.ANY), whole(8, width),
        ],
        out_shape=[
            jax.ShapeDtypeStruct((tokens, width), bf),
            jax.ShapeDtypeStruct((parts, tokens, part_cols), bf),
            jax.ShapeDtypeStruct((tokens, width), f32),
            jax.ShapeDtypeStruct((shards, parts, shard_rows, wide), bf),
            jax.ShapeDtypeStruct((8, width), f32),
        ],
        scratch_shapes=[
            pltpu.VMEM((tokens, width), f32),
            pltpu.VMEM((tokens, width), bf),
            pltpu.VMEM((width, tokens), bf),
            pltpu.VMEM((width, tokens), bf),
            pltpu.VMEM((tokens, width), f32),
            pltpu.VMEM((tokens, width), f32),
            pltpu.VMEM((2, shards, shard_rows, 2 * hidden), bf),
            pltpu.VMEM((shards, parts, shard_rows, padded(part_cols)), bf),
            pltpu.SemaphoreType.DMA((2,)),
            pltpu.SemaphoreType.DMA,
        ],
        compiler_params=pltpu.CompilerParams(vmem_limit_bytes=VMEM_LIMIT),
        cost_estimate=pl.CostEstimate(flops=17 * 10**9, bytes_accessed=40 << 20, transcendentals=2 << 20),
    )(att, start, grad, out_w, params, fc, proj_t)


def add_rows(target, sources, rows_at_once=16):
    def one(i, _):
        here = pl.ds(pl.multiple_of(i * rows_at_once, rows_at_once), rows_at_once)
        total = target[here, :].astype(jnp.float32)
        for source in sources:
            total = total + source[here, :].astype(jnp.float32)
        target[here, :] = total.astype(target.dtype)
        return 0

    lax.fori_loop(0, target.shape[0] // rows_at_once, one, 0)


def finish_kernel(
    sizes,
    dq_ref, dkv_ref, rec_ref, normed_ref, wall_ref, g_ref, start_ref, dmid_ref, gain_ref, small_in, pick_ref,
    dstart_ref, gw_ref, gq_ref, small_ref,
    kv_s, rq, rkv, normed_s, wall_s, own_g, rcore, rx, rc, rz, gq_acc, gq_s, rgq, rb, rgc,
    dst_s, sm_s, rst, rsc, rsf,
    core_sem, core_rec, x_sem, x_rec, c_sem, c_rec, z_sem, z_rec, b_sem, b_rec,
    aq_sem, aq_rec, ak_sem, ak_rec, ag_sem, ag_rec, gq_sem, gq_rec, gc_sem, gc_rec,
    st_sem, st_rec, sc_sem, sc_rec, sf_sem, sf_rec, loc_sem, own_sem,
):
    F, C, T = sizes
    f, c, t = lax.axis_index("fsdp"), lax.axis_index("ctx"), lax.axis_index("tp")
    S = dq_ref.shape[1]
    part = dq_ref.shape[2]
    own_rows = dq_ref.shape[3]
    bf, f32 = jnp.bfloat16, jnp.float32
    sib, across, opposite = f ^ 1, f ^ 2, f ^ 3

    def remote(src, dst, send, recv, **where):
        return pltpu.make_async_remote_copy(
            src_ref=src, dst_ref=dst, send_sem=send, recv_sem=recv, device_id=where, device_id_type=MESH
        )

    locals_ = []
    for tt in range(T):
        for ff in range(F):
            locals_.append(
                pltpu.make_async_copy(
                    wall_ref.at[tt, ff],
                    wall_s.at[tt, :, pl.ds(ff * part, part), :],
                    loc_sem.at[2 + tt * F + ff],
                )
            )
    normed_in = pltpu.make_async_copy(normed_ref, normed_s, loc_sem.at[0])
    g_in = [
        pltpu.make_async_copy(g_ref.at[f], own_g.at[0], own_sem.at[0]),
        pltpu.make_async_copy(g_ref.at[across], own_g.at[1], own_sem.at[1]),
    ]
    for copy in g_in:
        copy.start()
    normed_in.start()
    for copy in locals_:
        copy.start()

    barrier = pltpu.get_barrier_semaphore()
    peers = 0
    for d in range(1, F):
        pl.semaphore_signal(barrier, inc=1, device_id={"fsdp": f ^ d}, device_id_type=MESH)
        peers += 1
    for d in range(1, T):
        pl.semaphore_signal(barrier, inc=1, device_id={"tp": lax.rem(t + d, T)}, device_id_type=MESH)
        peers += 1
    for d in range(1, C):
        pl.semaphore_signal(barrier, inc=1, device_id={"ctx": lax.rem(c + d, C)}, device_id_type=MESH)
        peers += 1
    pl.semaphore_wait(barrier, peers)

    def tp_peer(d):
        return lax.rem(t + d, T)

    pending = []

    def go(copy):
        copy.start()
        pending.append(copy)
        return copy

    aq = [[None] * S for _ in range(T)]
    ak = [[None] * S for _ in range(T)]
    for s in range(S):
        for d in range(1, T):
            aq[d][s] = go(
                remote(dq_ref.at[tp_peer(d), s], rq.at[d, s], aq_sem.at[d, s], aq_rec.at[d, s], tp=tp_peer(d))
            )
    core = [[None, None] for _ in range(T)]
    for b in range(T):
        for k, target in enumerate((sib, opposite)):
            core[b][k] = go(
                remote(g_ref.at[target, b], rcore.at[b, k], core_sem.at[b, k], core_rec.at[b, k], fsdp=sib)
            )
    for s in range(S):
        for d in list(range(1, T)) + [0]:
            peer = tp_peer(d)
            kv_s[d, s] = (dkv_ref[peer, s] + rec_ref[peer, s].astype(f32)).astype(bf)
            if d:
                ak[d][s] = go(
                    remote(kv_s.at[d, s], rkv.at[d, s], ak_sem.at[d, s], ak_rec.at[d, s], tp=peer)
                )

    for copy in g_in:
        copy.wait()
    cross = [None] * T
    for b in range(T):
        core[b][1].wait_recv()
        add_rows(own_g.at[1, b], [rcore.at[b, 1]])
        cross[b] = go(remote(own_g.at[1, b], rx.at[b], x_sem.at[b], x_rec.at[b], fsdp=across))
        core[b][0].wait_recv()
        add_rows(own_g.at[0, b], [rcore.at[b, 0]])

    normed_in.wait()
    gq_acc[...] = jnp.zeros_like(gq_acc)
    for s in range(S):
        for d in range(T):
            peer = tp_peer(d)
            rows = pl.ds(pl.multiple_of(peer * own_rows, own_rows), own_rows)
            gq_acc[:part, :] += dot(dq_ref[peer, s], normed_s[s, rows, :])
            gq_acc[part:, :] += dot(kv_s[d, s], normed_s[s, rows, :])
    for k in range(F):
        gq_s[k] = gq_acc[:, column(k, part)].astype(bf)
    gq = [None] * F
    for d in range(1, F):
        gq[d] = go(remote(gq_s.at[f ^ d], rgq.at[d], gq_sem.at[d], gq_rec.at[d], fsdp=f ^ d))

    held = [b // C for b in range(T)]

    def ctx_stage(b):
        owner = b % C
        cross[b].wait_recv()
        add_rows(own_g.at[0, b], [rx.at[b]])
        for d in range(1, C):
            @pl.when(lax.rem(c + d, C) == owner)
            def _():
                remote(
                    own_g.at[0, b], rc.at[held[b], d], c_sem.at[b], c_rec.at[b, d], ctx=owner
                ).start()

    def ctx_wait(b):
        owner = b % C

        @pl.when(c == owner)
        def _():
            for d in range(1, C):
                remote(own_g.at[0, b], rc.at[held[b], d], c_sem.at[b], c_rec.at[b, d], ctx=owner).wait_recv()
            add_rows(own_g.at[0, b], [rc.at[held[b], d] for d in range(1, C)])

    def z_stage(b):
        owner = b % C

        def hop(step, way):
            return remote(
                own_g.at[0, b], rz.at[held[b], way], z_sem.at[b], z_rec.at[b, way], tp=t + step
            )

        @pl.when(c == owner)
        def _():
            if b < T - 1:
                @pl.when((t >= b) & (t < T - 1))
                def _():
                    hop(-1, 0).wait_recv()
                    add_rows(own_g.at[0, b], [rz.at[held[b], 0]])

                @pl.when(t > b)
                def _():
                    hop(-1, 0).start()
            if b > 0:
                @pl.when((t <= b) & (t > 0))
                def _():
                    hop(1, 1).wait_recv()
                    add_rows(own_g.at[0, b], [rz.at[held[b], 1]])

                @pl.when(t < b)
                def _():
                    hop(1, 1).start()

    hat, inv = [None] * S, [None] * S
    gain = gain_ref[...]

    def norm_stage(s):
        total = jnp.zeros((wall_s.shape[2], own_rows), f32)
        for d in range(T):
            if d:
                aq[d][s].wait_recv()
                ak[d][s].wait_recv()
            source = lax.rem(t + T - d, T)
            for j in range(3):
                if d:
                    block = rq[d, s] if j == 0 else rkv[d, s, column(j - 1, part), :]
                else:
                    block = dq_ref[t, s] if j == 0 else kv_s[0, s, column(j - 1, part), :]
                total = total + dot(wall_s[source, j], block)
        d_normed = total.T
        hat, inv = hat_rows(start_ref[s].astype(f32))
        value = dmid_ref[s] + norm_back(hat, inv, gain, d_normed)
        dst_s[s] = value.astype(bf)
        return (
            jnp.sum(d_normed * hat, axis=0, keepdims=True),
            jnp.sum(d_normed, axis=0, keepdims=True),
        )

    def ag_copy(s, owner, step, way):
        rows = pl.ds(pl.multiple_of(owner * own_rows, own_rows), own_rows)
        src = dst_s.at[s] if step == 0 else dstart_ref.at[s, rows, :]
        return lambda to: remote(
            src, dstart_ref.at[s, rows, :], ag_sem.at[s, step, way], ag_rec.at[s, step, way], tp=to
        )

    def ag_start(s):
        @pl.when(t < T - 1)
        def _():
            ag_copy(s, t, 0, 0)(t + 1).start()

        @pl.when(t > 0)
        def _():
            ag_copy(s, t, 0, 1)(t - 1).start()

        rows = pl.ds(pl.multiple_of(t * own_rows, own_rows), own_rows)
        keep = pltpu.make_async_copy(dst_s.at[s], dstart_ref.at[s, rows, :], loc_sem.at[1])
        keep.start()
        keep.wait()

    def ag_step(s, step):
        @pl.when(t >= step)
        def _():
            ag_copy(s, t - step, step - 1, 0)(t).wait_recv()

        @pl.when((t >= step) & (t < T - 1))
        def _():
            ag_copy(s, t - step, step, 0)(t + 1).start()

        @pl.when(t + step <= T - 1)
        def _():
            ag_copy(s, t + step, step - 1, 1)(t).wait_recv()

        @pl.when((t + step <= T - 1) & (t > 0))
        def _():
            ag_copy(s, t + step, step, 1)(t - 1).start()

    def ag_drain(s):
        for step in range(T - 1):
            @pl.when((t >= step) & (t < T - 1))
            def _():
                ag_copy(s, t - step, step, 0)(t + 1).wait_send()

            @pl.when((t + step <= T - 1) & (t > 0))
            def _():
                ag_copy(s, t + step, step, 1)(t - 1).wait_send()

    for copy in locals_:
        copy.wait()
    sums = [None] * S
    for s in range(S):
        for b in range(s * T // S, (s + 1) * T // S):
            ctx_stage(b)
        sums[s] = norm_stage(s)
        ag_start(s)
    gain_sum = sum(pair[0] for pair in sums)
    bias_sum = sum(pair[1] for pair in sums)
    sm_s[0:8, :] = small_in[...] + jnp.concatenate(
        [gain_sum, jnp.zeros_like(gain_sum), bias_sum, jnp.zeros((5, gain_sum.shape[1]), f32)], axis=0
    )
    thoughts = jnp.zeros((pick_ref.shape[1], sm_s.shape[1]), f32)
    for s in range(S):
        thoughts = thoughts + dot(pick_ref[s], dst_s[s])
    sm_s[8:, :] = thoughts
    st = [None] * T
    for d in range(1, T):
        st[d] = go(remote(sm_s, rst.at[d], st_sem.at[d], st_rec.at[d], tp=tp_peer(d)))

    gq_sum = gq_s[f].astype(f32)
    for d in range(1, F):
        gq[d].wait_recv()
        gq_sum = gq_sum + rgq[d].astype(f32)
    rgc[c] = gq_sum.astype(bf)
    gc = [None] * C
    for d in range(1, C):
        gc[d] = go(remote(rgc.at[c], rgc.at[c], gc_sem.at[d], gc_rec.at[d], ctx=lax.rem(c + d, C)))

    for b in range(T):
        ctx_wait(b)
        z_stage(b)
    for step in range(1, T):
        for s in range(S):
            ag_step(s, step)

    for d in range(1, T):
        st[d].wait_recv()
    rst[0] = sm_s[...]
    total = jnp.zeros(sm_s.shape, f32)
    for k in range(T):
        total = total + rst[lax.rem(t + T - k, T)]
    rsc[c] = total
    sc = [None] * C
    for d in range(1, C):
        sc[d] = go(remote(rsc.at[c], rsc.at[c], sc_sem.at[d], sc_rec.at[d], ctx=lax.rem(c + d, C)))
    for d in range(1, C):
        sc[d].wait_recv()
    total = jnp.zeros(sm_s.shape, f32)
    for k in range(C):
        total = total + rsc[k]
    rsf[f] = total
    sf = [None] * F
    for d in range(1, F):
        sf[d] = go(remote(rsf.at[f], rsf.at[f], sf_sem.at[d], sf_rec.at[d], fsdp=f ^ d))
    for d in range(1, F):
        sf[d].wait_recv()
    norms = jnp.zeros((8, sm_s.shape[1]), f32)
    for k in range(F):
        norms = norms + rsf[k, 0:8, :]
    small_ref[0:8, :] = norms
    small_ref[8:, :] = total[8:]

    for d in range(1, C):
        gc[d].wait_recv()
    total = jnp.zeros(gq_ref.shape, f32)
    for k in range(C):
        total = total + rgc[k].astype(f32)
    gq_ref[...] = total

    for b in range(T):
        owner = b % C

        @pl.when((t == b) & (c == owner))
        def _():
            for d in range(1, C):
                remote(
                    own_g.at[0, b], rb, b_sem.at[d], b_rec, ctx=lax.rem(owner + d, C)
                ).start()
            gw_ref[...] = own_g[0, b]
            for d in range(1, C):
                remote(
                    own_g.at[0, b], rb, b_sem.at[d], b_rec, ctx=lax.rem(owner + d, C)
                ).wait_send()

        @pl.when((t == b) & (c != owner))
        def _():
            remote(own_g.at[0, b], rb, b_sem.at[1], b_rec, ctx=owner).wait_recv()
            gw_ref[...] = rb[...]

    for copy in pending:
        copy.wait_send()
    for b in range(T):
        owner = b % C

        @pl.when(c != owner)
        def _():
            remote(own_g.at[0, b], rc.at[held[b], 1], c_sem.at[b], c_rec.at[b, 1], ctx=owner).wait_send()

        @pl.when((c == owner) & (t != b))
        def _():
            remote(own_g.at[0, b], rz.at[held[b], 0], z_sem.at[b], z_rec.at[b, 0], tp=t).wait_send()
    for s in range(S):
        ag_drain(s)


def finish(dq, dkv, received, normed, wall, g, start, dmid, gain, small, pick, counts):
    F, C, T = counts
    _, S, part, own_rows = dq.shape
    width = normed.shape[2]
    _, _, shard_rows, wide = g.shape
    bf, f32 = jnp.bfloat16, jnp.float32
    rows = own_rows * T
    extra = 8 + pick.shape[1]
    mine = -(-T // C)
    vmem = pl.BlockSpec(memory_space=pltpu.VMEM)
    anywhere = pl.BlockSpec(memory_space=pl.ANY)
    dma = lambda *shape: pltpu.SemaphoreType.DMA(shape)
    return pl.pallas_call(
        functools.partial(finish_kernel, counts),
        in_specs=[vmem, vmem, vmem, anywhere, anywhere, anywhere, vmem, vmem, vmem, vmem, vmem],
        out_specs=[anywhere, vmem, vmem, vmem],
        out_shape=[
            jax.ShapeDtypeStruct((S, rows, width), bf),
            jax.ShapeDtypeStruct((shard_rows, wide), bf),
            jax.ShapeDtypeStruct((3 * part, shard_rows), f32),
            jax.ShapeDtypeStruct((extra, width), f32),
        ],
        scratch_shapes=[
            pltpu.VMEM((T, S, 2 * part, own_rows), bf),
            pltpu.VMEM((T, S, part, own_rows), bf),
            pltpu.VMEM((T, S, 2 * part, own_rows), bf),
            pltpu.VMEM((S, rows, width), bf),
            pltpu.VMEM((T, 3, width, part), bf),
            pltpu.VMEM((2, T, shard_rows, wide), bf),
            pltpu.VMEM((T, 2, shard_rows, wide), bf),
            pltpu.VMEM((T, shard_rows, wide), bf),
            pltpu.VMEM((mine, C, shard_rows, wide), bf),
            pltpu.VMEM((mine, 2, shard_rows, wide), bf),
            pltpu.VMEM((3 * part, width), f32),
            pltpu.VMEM((F, 3 * part, shard_rows), bf),
            pltpu.VMEM((F, 3 * part, shard_rows), bf),
            pltpu.VMEM((shard_rows, wide), bf),
            pltpu.VMEM((C, 3 * part, shard_rows), bf),
            pltpu.VMEM((S, own_rows, width), bf),
            pltpu.VMEM((extra, width), f32),
            pltpu.VMEM((T, extra, width), f32),
            pltpu.VMEM((C, extra, width), f32),
            pltpu.VMEM((F, extra, width), f32),
            dma(T, 2), dma(T, 2), dma(T), dma(T), dma(T), dma(T, C), dma(T), dma(T, 2), dma(C), pltpu.SemaphoreType.DMA,
            dma(T, S), dma(T, S), dma(T, S), dma(T, S), dma(S, T, 2), dma(S, T, 2), dma(F), dma(F), dma(C), dma(C),
            dma(T), dma(T), dma(C), dma(C), dma(F), dma(F), dma(2 + T * F), dma(2),
        ],
        compiler_params=pltpu.CompilerParams(
            vmem_limit_bytes=VMEM_LIMIT, collective_id=0, has_side_effects=True
        ),
        cost_estimate=pl.CostEstimate(flops=4 * 10**9, bytes_accessed=64 << 20, transcendentals=0),
    )(dq, dkv, received, normed, wall, g, start, dmid, gain, small, pick)


def local(
    inputs, thoughts, positions, lengths, w_qkv, w_out, w_fc, w_proj, norm_gains, norm_biases, out_grad,
):
    rows, seqs, width = inputs.shape
    ctx_count = lax.axis_size("ctx")
    tp_count = lax.axis_size("tp")
    fsdp_count = lax.axis_size("fsdp")
    ctx, tp, fsdp = lax.axis_index("ctx"), lax.axis_index("tp"), lax.axis_index("fsdp")
    first_row = ctx * rows
    own_rows = rows // tp_count
    own_tokens = own_rows * seqs
    far = min(ctx_count - 1, -(-(DOC_MOST - 1) // rows))
    block = min(256, rows)
    bf, f32 = jnp.bfloat16, jnp.float32

    qkv_full = lax.all_gather(w_qkv, "fsdp", axis=1, tiled=True)
    params = lax.all_gather(jnp.concatenate([norm_gains, norm_biases]), "fsdp", axis=1, tiled=True).astype(f32)
    gains, biases = params[:2], params[2:]
    everywhere = lambda w, axes: functools.reduce(
        lambda v, pair: lax.all_gather(v, pair[0], axis=pair[1], tiled=True), axes, w
    )
    out_full = everywhere(w_out, (("tp", 0), ("fsdp", 1)))
    fc_full = everywhere(w_fc, (("tp", 1), ("fsdp", 0)))
    proj_full_t = everywhere(w_proj.T, (("tp", 1), ("fsdp", 0)))
    qkv_all = lax.all_gather(w_qkv, ("tp", "fsdp"), axis=0, tiled=False)

    local_width = qkv_full.shape[2]
    qkv_matrix = jnp.transpose(qkv_full, (1, 0, 2)).reshape(width, 3 * local_width)
    places = first_row + jnp.arange(rows, dtype=jnp.int32)
    is_thought = places[None, None, :] == positions[:, :, None]
    keep = jnp.logical_not(jnp.any(is_thought, axis=0))
    start = jnp.transpose(inputs, (1, 0, 2))
    for t in range(thoughts.shape[0]):
        start = jnp.where(is_thought[t][:, :, None], thoughts[t][:, None, :], start)
    hat, inv = hat_rows(start.astype(f32))
    normed = (hat * gains[0] + biases[0]).astype(bf)
    normed_flat = normed.reshape(seqs * rows, width)
    qkv = dot(normed_flat, qkv_matrix).astype(bf).reshape(seqs, rows, 3 * local_width)

    ends = jnp.cumsum(lengths, axis=1, dtype=jnp.int32)
    low = jnp.max(jnp.where(ends[:, :, None] <= places[None, None, :], ends[:, :, None], 0), axis=1)
    low = low - (first_row - far * rows)
    first = low[:, ::block] // block

    kv = qkv[:, :, local_width:]
    prev = None
    if far:
        prev = jnp.concatenate(
            [
                lax.ppermute(kv, "ctx", [(i, i + d) for i in range(ctx_count - d)])
                for d in range(far, 0, -1)
            ],
            axis=1,
        )
    low3 = low[:, None, :]
    attended, out_t, logs = attend(qkv, prev, low3, first, block, tp_count)

    own = lambda a: lax.dynamic_slice_in_dim(a, tp * own_rows, own_rows, 1)
    exchange = lambda a: lax.all_to_all(a, "tp", split_axis=0, concat_axis=0, tiled=True)
    attended_own = exchange(attended).reshape(tp_count, own_tokens, local_width)
    start_own = own(start)
    grad_own = jnp.transpose(
        lax.dynamic_slice_in_dim(out_grad, tp * own_rows, own_rows, 0), (1, 0, 2)
    ).reshape(own_tokens, width)
    output_own, d_attended_own, d_middle, g, small = feed(
        attended_own, start_own.reshape(own_tokens, width), grad_own, out_full, params, fc_full, proj_full_t, fsdp_count
    )
    d_attended = exchange(d_attended_own.reshape(tp_count, seqs, own_rows, local_width))
    output = lax.all_gather(output_own.reshape(seqs, own_rows, width), "tp", axis=1, tiled=True)
    output = jnp.transpose(output, (1, 0, 2))

    d_q, d_kv, d_prev = attend_back(qkv, prev, low3, first, d_attended, out_t, logs, block)
    if far == 0:
        received = jnp.zeros(d_kv.shape, bf)
    else:
        pieces = [
            lax.ppermute(d_prev[index], "ctx", [(i + d, i) for i in range(ctx_count - d)])
            for index, d in enumerate(range(far, 0, -1))
        ]
        received = pieces[0] if far == 1 else sum(piece.astype(f32) for piece in pieces)

    own_places = lax.dynamic_slice_in_dim(places, tp * own_rows, own_rows, 0)
    count = thoughts.shape[0]
    pick = (own_places[None, None, :] == positions[:, :, None]).astype(bf)
    picks = []
    for s in range(seqs):
        picks.append(jnp.concatenate(
            [jnp.where(k == s, pick[:, s], jnp.zeros_like(pick[:, s])) for k in range(seqs)], axis=0
        ))
    pick = jnp.stack(picks)
    pick = jnp.pad(pick, ((0, 0), (0, -(-pick.shape[1] // 16) * 16 - pick.shape[1]), (0, 0)))
    wall = qkv_all.reshape((tp_count, fsdp_count) + w_qkv.shape)
    d_start, gw, gq, small = finish(
        d_q, d_kv, received, normed, wall, g, start_own, d_middle.reshape(seqs, own_rows, width),
        gains[0:1], small, pick, (fsdp_count, ctx_count, tp_count),
    )
    d_inputs = jnp.transpose(jnp.where(keep[:, :, None], d_start.astype(f32), 0.0), (1, 0, 2))
    d_thoughts = jnp.transpose(small[8 : 8 + count * seqs].reshape(seqs, count, width), (1, 0, 2))
    hidden = w_fc.shape[1]
    gw = gw.astype(f32)
    norms = lax.dynamic_slice_in_dim(small[:4], fsdp * w_fc.shape[0], w_fc.shape[0], 1)
    return (
        output,
        d_inputs,
        d_thoughts,
        jnp.transpose(gq.reshape(3, local_width, -1), (0, 2, 1)),
        gw[:, 2 * hidden : 2 * hidden + local_width].T,
        gw[:, :hidden],
        gw[:, hidden : 2 * hidden].T,
        norms[:2],
        norms[2],
        norms[3],
    )


def solution(mesh):
    in_specs = (
        P("ctx", "fsdp", None),
        P(None, "fsdp", None),
        P(None, "fsdp"),
        P("fsdp", None),
        P(None, "fsdp", "tp"),
        P("tp", "fsdp"),
        P("fsdp", "tp"),
        P("tp", "fsdp"),
        P(None, "fsdp"),
        P(None, "fsdp"),
        P("ctx", "fsdp", None),
    )
    out_specs = (
        P("ctx", "fsdp", None),
        P("ctx", "fsdp", None),
        P(None, "fsdp", None),
        P(None, "fsdp", "tp"),
        P("tp", "fsdp"),
        P("fsdp", "tp"),
        P("tp", "fsdp"),
        P(None, "fsdp"),
        P("fsdp"),
        P("fsdp"),
    )
    return jax.shard_map(local, mesh=mesh, in_specs=in_specs, out_specs=out_specs, check_vma=False)
```

```python
import functools

import jax
import jax.numpy as jnp
from jax import lax
from jax.experimental import pallas as pl
from jax.experimental.pallas import tpu as pltpu
from jax.sharding import PartitionSpec as P

HEAD_DIM = 64
DOC_MOST = 1024
EPSILON = 1e-05
MASKED = -1e30


def dot(a, b, dims=((1,), (0,))):
    return lax.dot_general(a, b, (dims, ((), ())), preferred_element_type=jnp.float32)


def hat_rows(values):
    centre = jnp.mean(values, axis=-1, keepdims=True)
    shifted = values - centre
    spread = jnp.mean(shifted * shifted, axis=-1, keepdims=True)
    inv = lax.rsqrt(spread + EPSILON)
    return shifted * inv, inv


def norm_back(hat, inv, gain, grad):
    eg = grad * gain
    return inv * (
        eg
        - jnp.mean(eg, axis=-1, keepdims=True)
        - hat * jnp.mean(eg * hat, axis=-1, keepdims=True)
    )


MESH = pl.DeviceIdType.MESH
VMEM_LIMIT = 60 << 20


def column(index, size=HEAD_DIM):
    return slice(index * size, (index + 1) * size)


def turn(value):
    return value.astype(jnp.float32).T.astype(jnp.bfloat16)


def turn_back(value):
    return value.T.astype(jnp.bfloat16)


def front_kernel(
    sizes, block,
    start_ref, low_ref, wq_ref, wo_ref, wf_ref, wp_ref, par_ref,
    att_ref, q_ref, kv_ref, prev_ref, out_t_ref, log_ref, normed_ref, ow_ref, fc_ref, pj_ref, params_ref,
    start_s, normed_s, wl_s, wo_s, par_s, q_s, kv_s, prev_s, qt_s, ko_s, vto_s, kp_s, vtp_s, m_s, l_s, att_s,
    in_sem, out_sem, w_loc, z_sem, z_rec, s_sem, s_rec, x_sem, x_rec, r_sem, r_rec,
    kv_sem, kv_rec, at_sem, at_rec, at_loc,
):
    F, C, T = sizes
    f, c, t = lax.axis_index("fsdp"), lax.axis_index("ctx"), lax.axis_index("tp")
    S, rows, width = start_ref.shape
    hw = q_ref.shape[2]
    heads = hw // HEAD_DIM
    own_rows = rows // T
    far = prev_ref.shape[1] // rows if C > 1 else 0
    shard = wq_ref.shape[1]
    hidden = wf_ref.shape[1]
    bf, f32 = jnp.bfloat16, jnp.float32
    sib, across = f ^ 1, f ^ 2

    def remote(src, dst, send, recv, **where):
        return pltpu.make_async_remote_copy(
            src_ref=src, dst_ref=dst, send_sem=send, recv_sem=recv, device_id=where, device_id_type=MESH
        )

    start_in = pltpu.make_async_copy(start_ref, start_s, in_sem.at[0])
    start_in.start()

    barrier = pltpu.get_barrier_semaphore()
    peers = 0
    for d in range(1, F):
        pl.semaphore_signal(barrier, inc=1, device_id={"fsdp": f ^ d}, device_id_type=MESH)
        peers += 1
    for d in range(1, T):
        pl.semaphore_signal(barrier, inc=1, device_id={"tp": lax.rem(t + d, T)}, device_id_type=MESH)
        peers += 1
    for d in range(1, C):
        pl.semaphore_signal(barrier, inc=1, device_id={"ctx": lax.rem(c + d, C)}, device_id_type=MESH)
        peers += 1
    pl.semaphore_wait(barrier, peers)

    pending = []

    def go(copy):
        copy.start()
        pending.append(copy)
        return copy

    def at_shard(ff):
        return pl.ds(pl.multiple_of(ff * shard, shard), shard)

    def at_hidden(tt):
        return pl.ds(pl.multiple_of(tt * hidden, hidden), hidden)

    def block_at(a, tt, ff):
        if a == 0:
            return par_s.at[ff]
        if a == 1:
            return wl_s.at[:, at_shard(ff), :]
        if a == 2:
            return wo_s.at[tt, ff]
        return (fc_ref if a == 3 else pj_ref).at[at_shard(ff), at_hidden(tt)]

    sources = (par_ref, wq_ref, wo_ref, wf_ref, wp_ref)
    slot = lambda d: lax.rem(t + T - d, T)

    def spread_chip(a, d):
        src = sources[a] if d == 0 else block_at(a, slot(d), f)
        dst = block_at(a, slot(d), f)
        go(remote(src, dst, x_sem.at[a, d], x_rec.at[a, d], fsdp=across))
        go(remote(src, dst, s_sem.at[a, d], s_rec.at[a, d], fsdp=sib))

    def take_z(a, d):
        here = block_at(a, slot(d), f)
        remote(here, here, z_sem.at[a, d], z_rec.at[a, d], tp=t).wait_recv()
        spread_chip(a, d)

    def relay(a, d):
        here = block_at(a, slot(d), across)
        remote(here, here, x_sem.at[a, d], x_rec.at[a, d], fsdp=f).wait_recv()
        go(remote(here, here, r_sem.at[a, d], r_rec.at[a, d], fsdp=sib))

    def take_chip(a, d):
        for ff, rec in ((sib, s_rec), (sib ^ 2, r_rec)):
            here = block_at(a, slot(d), ff)
            remote(here, here, s_sem.at[a, d], rec.at[a, d], fsdp=f).wait_recv()

    keeps = []
    for a in range(5):
        keep = pltpu.make_async_copy(sources[a], block_at(a, t, f), w_loc.at[a])
        keep.start()
        keeps.append(keep)
    spread_chip(0, 0)
    spread_chip(1, 0)
    for a in (2, 3, 4):
        for d in range(1, T):
            go(remote(sources[a], block_at(a, t, f), z_sem.at[a, d], z_rec.at[a, d], tp=lax.rem(t + d, T)))
        spread_chip(a, 0)

    relay(0, 0)
    take_chip(0, 0)
    keeps[0].wait()
    params = jnp.concatenate([par_s[ff] for ff in range(F)], axis=1)
    params_ref[...] = params
    start_in.wait()
    per_seq = rows // block

    def norm_one(index, _):
        s = index // per_seq
        here = pl.ds(pl.multiple_of(lax.rem(index, per_seq) * block, block), block)
        hat, _ = hat_rows(start_s[s, here, :].astype(f32))
        normed_s[s, here, :] = (hat * params_ref[0:1, :] + params_ref[2:3, :]).astype(bf)
        return 0

    lax.fori_loop(0, S * per_seq, norm_one, 0)
    normed_out = pltpu.make_async_copy(normed_s, normed_ref, out_sem.at[0])
    normed_out.start()

    relay(1, 0)
    take_chip(1, 0)
    keeps[1].wait()

    def kv_one(s, _):
        def one(index, _):
            here = pl.ds(pl.multiple_of(index * block, block), block)
            rows_in = normed_s[s, here, :]
            k = dot(rows_in, wl_s[1]).astype(bf)
            v = dot(rows_in, wl_s[2]).astype(bf)
            kv_s[s, here, :] = jnp.concatenate([k, v], axis=1)
            v_t = turn(v)
            for h in range(heads):
                ko_s[s, h, here, :] = k[:, column(h)]
                vto_s[s, h, :, here] = v_t[column(h)]
            return 0

        lax.fori_loop(0, per_seq, one, 0)
        return 0

    def kv_copy(s, d):
        return remote(
            kv_s.at[s], prev_s.at[s, pl.ds((far - d) * rows, rows), :],
            kv_sem.at[d, s], kv_rec.at[d, s], ctx=lax.rem(c + d, C),
        )

    for s in range(S):
        kv_one(s, 0)
        for d in range(1, far + 1):
            @pl.when(c + d < C)
            def _():
                kv_copy(s, d).start()

    def q_one(index, _):
        s = index // per_seq
        here = pl.ds(pl.multiple_of(lax.rem(index, per_seq) * block, block), block)
        q = dot(normed_s[s, here, :], wl_s[0]).astype(bf)
        q_s[s, here, :] = q
        q_t = turn(q.astype(f32) * 0.125)
        for h in range(heads):
            qt_s[s, h, :, here] = q_t[column(h)]
        return 0

    lax.fori_loop(0, S * per_seq, q_one, 0)
    outs = [
        pltpu.make_async_copy(q_s, q_ref, out_sem.at[1]),
        pltpu.make_async_copy(kv_s, kv_ref, out_sem.at[2]),
    ]
    for copy in outs:
        copy.start()

    def own_part(s):
        for i in range(per_seq):
            span = column(i, block)
            low = low_ref[s, :, span] - far * rows
            top = i * block + lax.broadcasted_iota(jnp.int32, (1, block), 1)
            first = max(0, i * block - (DOC_MOST - 1)) // block * block
            many = (i + 1) * block - first
            place = first + lax.broadcasted_iota(jnp.int32, (many, 1), 0)
            allowed = (place >= low) & (place <= top)
            for h in range(heads):
                scores = dot(ko_s[s, h, first : first + many, :], qt_s[s, h, :, span])
                scores = jnp.where(allowed, scores, MASKED)
                m = jnp.max(scores, axis=0, keepdims=True)
                p = jnp.exp(scores - m)
                m_s[s, h : h + 1, span] = m
                l_s[s, h : h + 1, span] = jnp.sum(p, axis=0, keepdims=True)
                out_t_ref[s, column(h), span] = dot(vto_s[s, h, :, first : first + many], p.astype(bf))

    def far_part(s):
        for h in range(heads):
            kp_s[h] = prev_s[s, :, column(h)]
            vtp_s[h] = turn(prev_s[s, :, column(heads + h)])
        for i in range(per_seq):
            span = column(i, block)
            low = low_ref[s, :, span]
            first = max(0, far * rows + i * block - (DOC_MOST - 1)) // block * block
            if first >= far * rows:
                continue
            many = far * rows - first
            place = first + lax.broadcasted_iota(jnp.int32, (many, 1), 0)
            allowed = place >= low
            for h in range(heads):
                scores = dot(kp_s[h, first : first + many, :], qt_s[s, h, :, span])
                scores = jnp.where(allowed, scores, MASKED)
                old = m_s[s, h : h + 1, span]
                m = jnp.maximum(old, jnp.max(scores, axis=0, keepdims=True))
                p = jnp.exp(scores - m)
                alpha = jnp.exp(old - m)
                m_s[s, h : h + 1, span] = m
                l_s[s, h : h + 1, span] = alpha * l_s[s, h : h + 1, span] + jnp.sum(p, axis=0, keepdims=True)
                out_t_ref[s, column(h), span] = alpha * out_t_ref[s, column(h), span] + dot(
                    vtp_s[h, :, first : first + many], p.astype(bf)
                )

    def finish_part(s):
        for h in range(heads):
            out_t_ref[s, column(h), :] = out_t_ref[s, column(h), :] / l_s[s, h : h + 1, :]
            log_ref[s, h : h + 1, :] = m_s[s, h : h + 1, :] + jnp.log(l_s[s, h : h + 1, :])
        for tt in range(T):
            att_s[tt, s] = turn_back(out_t_ref[s, :, column(tt, own_rows)])

    for d in range(1, T):
        take_z(2, d)

    def own_loop(s, _):
        own_part(s)
        return 0

    lax.fori_loop(0, S, own_loop, 0)
    for d in range(T):
        relay(2, d)
    take_z(3, 1)

    def wait_far(s):
        for d in range(1, far + 1):
            @pl.when(c >= d)
            def _():
                kv_copy(s, d).wait_recv()

            @pl.when(c < d)
            def _():
                prev_s[s, (far - d) * rows : (far - d + 1) * rows, :] = jnp.zeros((rows, 2 * hw), bf)

    at = [[None] * S for _ in range(T)]
    for s in range(S):
        if far:
            wait_far(s)

            @pl.when(c > 0)
            def _():
                far_part(s)
        finish_part(s)
        for d in range(1, T):
            peer = lax.rem(t + d, T)
            at[d][s] = go(
                remote(att_s.at[peer, s], att_ref.at[t, s], at_sem.at[d, s], at_rec.at[d, s], tp=peer)
            )
        own_at = pltpu.make_async_copy(att_s.at[t, s], att_ref.at[t, s], at_loc.at[s])
        own_at.start()
        at[0][s] = own_at
        if s == 0:
            take_z(3, 2)
            take_z(3, 3)
            for d in range(T):
                relay(3, d)
    prev_out = pltpu.make_async_copy(prev_s, prev_ref, out_sem.at[3])
    if far:
        prev_out.start()
    for d in range(1, T):
        take_z(4, d)
    for d in range(T):
        take_chip(2, d)
    keeps[2].wait()
    for tt in range(T):
        for ff in range(F):
            ow_ref[column(tt, hw), column(ff, shard)] = wo_s[tt, ff]
    for d in range(T):
        relay(4, d)
    for a in (3, 4):
        for d in range(T):
            take_chip(a, d)
        keeps[a].wait()
    for s in range(S):
        at[0][s].wait()
        for d in range(1, T):
            at[d][s].wait_recv()
    normed_out.wait()
    for copy in outs:
        copy.wait()
    if far:
        prev_out.wait()
    for copy in pending:
        copy.wait_send()
    for s in range(S):
        for d in range(1, far + 1):
            @pl.when(c + d < C)
            def _():
                kv_copy(s, d).wait_send()


def front(start, low, wq, wo, wf, wp, params, block, far, counts):
    F, C, T = counts
    S, rows, width = start.shape
    hw = wq.shape[2]
    shard = wq.shape[1]
    heads = hw // HEAD_DIM
    hidden = wf.shape[1]
    bf, f32 = jnp.bfloat16, jnp.float32
    vmem = pl.BlockSpec(memory_space=pltpu.VMEM)
    anywhere = pl.BlockSpec(memory_space=pl.ANY)
    dma = lambda *shape: pltpu.SemaphoreType.DMA(shape)
    past = max(far, 1) * rows
    shape = jax.ShapeDtypeStruct
    return pl.pallas_call(
        functools.partial(front_kernel, counts, block),
        in_specs=[anywhere, vmem, anywhere, anywhere, anywhere, anywhere, anywhere],
        out_specs=[anywhere, anywhere, anywhere, anywhere, vmem, vmem, anywhere, vmem, anywhere, anywhere, vmem],
        out_shape=[
            shape((T, S, rows // T, hw), bf),
            shape((S, rows, hw), bf),
            shape((S, rows, 2 * hw), bf),
            shape((S, past, 2 * hw), bf),
            shape((S, hw, rows), f32),
            shape((S, 8, rows), f32),
            shape((S, rows, width), bf),
            shape((T * hw, F * shard), bf),
            shape((F * shard, T * hidden), bf),
            shape((F * shard, T * hidden), bf),
            shape((8, F * shard), f32),
        ],
        scratch_shapes=[
            pltpu.VMEM((S, rows, width), bf),
            pltpu.VMEM((S, rows, width), bf),
            pltpu.VMEM((3, F * shard, hw), bf),
            pltpu.VMEM((T, F, hw, shard), bf),
            pltpu.VMEM((F, 8, shard), f32),
            pltpu.VMEM((S, rows, hw), bf),
            pltpu.VMEM((S, rows, 2 * hw), bf),
            pltpu.VMEM((S, past, 2 * hw), bf),
            pltpu.VMEM((S, heads, HEAD_DIM, rows), bf),
            pltpu.VMEM((S, heads, rows, HEAD_DIM), bf),
            pltpu.VMEM((S, heads, HEAD_DIM, rows), bf),
            pltpu.VMEM((heads, past, HEAD_DIM), bf),
            pltpu.VMEM((heads, HEAD_DIM, past), bf),
            pltpu.VMEM((S, 8, rows), f32),
            pltpu.VMEM((S, 8, rows), f32),
            pltpu.VMEM((T, S, rows // T, hw), bf),
            dma(1), dma(4), dma(5),
            dma(5, T), dma(5, T), dma(5, T), dma(5, T), dma(5, T), dma(5, T), dma(5, T), dma(5, T),
            dma(far + 1, S), dma(far + 1, S), dma(T, S), dma(T, S), dma(S),
        ],
        compiler_params=pltpu.CompilerParams(
            vmem_limit_bytes=VMEM_LIMIT, collective_id=1, has_side_effects=True
        ),
        cost_estimate=pl.CostEstimate(flops=8 * 10**9, bytes_accessed=64 << 20, transcendentals=8 << 20),
    )(start, low, wq, wo, wf, wp, params)


def attend_back_kernel(
    heads, far, block, first_ref, q_ref, kv_ref, prev_ref, low_ref, grad_ref, out_t_ref, log_ref,
    dq_ref, dkv_ref, dprev_ref, k_s, kt_s, v_s, q_s, qt_s, g_s, gt_s, dqt_s, dk_s, dv_s,
):
    s = pl.program_id(0)
    rows = q_ref.shape[0]
    parts, own_rows = grad_ref.shape[0], grad_ref.shape[1]
    for h in range(heads):
        q = q_ref[:, column(h)].astype(jnp.float32) * 0.125
        q_s[h] = q.astype(jnp.bfloat16)
        qt_s[h] = turn_back(q)
        for t in range(parts):
            g_s[h, column(t, own_rows), :] = grad_ref[t, :, column(h)]
        gt_s[h] = turn(g_s[h])
        if far:
            k = prev_ref[:, column(h)]
            k_s[h, : far * rows] = k
            kt_s[h, :, : far * rows] = turn(k)
            v_s[h, : far * rows] = prev_ref[:, column(heads + h)]
        k = kv_ref[:, column(h)]
        k_s[h, far * rows :] = k
        kt_s[h, :, far * rows :] = turn(k)
        v_s[h, far * rows :] = kv_ref[:, column(heads + h)]
    dk_s[...] = jnp.zeros_like(dk_s)
    dv_s[...] = jnp.zeros_like(dv_s)
    for i in range(rows // block):
        span = column(i, block)
        low = low_ref[:, span]
        top = far * rows + i * block + lax.broadcasted_iota(jnp.int32, (1, block), 1)
        last = far * (rows // block) + i + 1
        deltas = [
            jnp.sum(gt_s[h, :, span].astype(jnp.float32) * out_t_ref[column(h), span], axis=0, keepdims=True)
            for h in range(heads)
        ]

        def step(kb, carry):
            base = pl.multiple_of(kb * block, block)
            here = pl.ds(base, block)
            place = base + lax.broadcasted_iota(jnp.int32, (block, 1), 0)
            allowed = (place >= low) & (place <= top)
            after = []
            for h in range(heads):
                scores = dot(k_s[h, here, :], qt_s[h, :, span])
                p = jnp.exp(jnp.where(allowed, scores - log_ref[h : h + 1, span], MASKED))
                dp = dot(v_s[h, here, :], gt_s[h, :, span])
                ds = (p * (dp - deltas[h])).astype(jnp.bfloat16)
                dv_s[h, here, :] += dot(p.astype(jnp.bfloat16), g_s[h, span, :])
                dk_s[h, here, :] += dot(ds, q_s[h, span, :])
                after.append(carry[h] + dot(kt_s[h, :, here], ds))
            return tuple(after)

        ends = lax.fori_loop(
            first_ref[s, i], last, step, tuple(jnp.zeros((HEAD_DIM, block), jnp.float32) for _ in range(heads))
        )
        for h in range(heads):
            dqt_s[column(h), span] = 0.125 * ends[h]
    for t in range(parts):
        dq_ref[t] = dqt_s[:, column(t, own_rows)].astype(jnp.bfloat16)
    for h in range(heads):
        for source, at in ((dk_s, h), (dv_s, heads + h)):
            whole = source[h].T
            for d in range(far):
                for t in range(parts):
                    dprev_ref[d, t, column(at), :] = whole[:, column(d * parts + t, own_rows)].astype(jnp.bfloat16)
            for t in range(parts):
                dkv_ref[t, column(at), :] = whole[:, column(far * parts + t, own_rows)]


def attend_back(q, kv, prev, low, first, grad, out_t, logs, block, far):
    seqs, rows, width = q.shape
    parts = grad.shape[0]
    own_rows = rows // parts
    heads = width // HEAD_DIM
    spec = lambda *shape: pl.BlockSpec((None,) + shape, lambda s, *_: (s, 0, 0))
    chunked = lambda *shape: pl.BlockSpec((parts, None) + shape, lambda s, *_: (0, s, 0, 0))
    span = (far + 1) * rows
    dists = max(far, 1)
    bf, f32 = jnp.bfloat16, jnp.float32
    return pl.pallas_call(
        functools.partial(attend_back_kernel, heads, far, block),
        grid_spec=pltpu.PrefetchScalarGridSpec(
            num_scalar_prefetch=1,
            grid=(seqs,),
            in_specs=[
                spec(rows, width), spec(rows, 2 * width), spec(prev.shape[1], 2 * width), spec(1, rows),
                chunked(own_rows, width), spec(width, rows), spec(8, rows),
            ],
            out_specs=[
                chunked(width, own_rows), chunked(2 * width, own_rows),
                pl.BlockSpec((dists, parts, None, 2 * width, own_rows), lambda s, *_: (0, 0, s, 0, 0)),
            ],
            scratch_shapes=[
                pltpu.VMEM((heads, span, HEAD_DIM), bf),
                pltpu.VMEM((heads, HEAD_DIM, span), bf),
                pltpu.VMEM((heads, span, HEAD_DIM), bf),
                pltpu.VMEM((heads, rows, HEAD_DIM), bf),
                pltpu.VMEM((heads, HEAD_DIM, rows), bf),
                pltpu.VMEM((heads, rows, HEAD_DIM), bf),
                pltpu.VMEM((heads, HEAD_DIM, rows), bf),
                pltpu.VMEM((width, rows), f32),
                pltpu.VMEM((heads, span, HEAD_DIM), f32),
                pltpu.VMEM((heads, span, HEAD_DIM), f32),
            ],
        ),
        out_shape=[
            jax.ShapeDtypeStruct((parts, seqs, width, own_rows), bf),
            jax.ShapeDtypeStruct((parts, seqs, 2 * width, own_rows), f32),
            jax.ShapeDtypeStruct((dists, parts, seqs, 2 * width, own_rows), bf),
        ],
        compiler_params=pltpu.CompilerParams(vmem_limit_bytes=VMEM_LIMIT),
        cost_estimate=pl.CostEstimate(flops=16 * 10**9, bytes_accessed=16 << 20, transcendentals=8 << 20),
    )(first, q, kv, prev, low, grad, out_t, logs)


def feed_kernel(
    step_cols, att_ref, start_ref, grad_ref, out_w_ref, params_ref, fc_ref, proj_ref,
    out_ref, datt_ref, dmid_ref, g_ref, small_ref,
    mid_s, nm_s, nmt_s, gt_s, acc_s, dnm_s, stage_s, last_s, sems, last_sem,
):
    t = pl.program_id(0)
    parts = pl.num_programs(0)
    count = att_ref.shape[0]
    part_cols = att_ref.shape[2]
    shards = stage_s.shape[1]
    shard_rows = stage_s.shape[2]
    hidden = fc_ref.shape[1]
    bf, f32 = jnp.bfloat16, jnp.float32

    @pl.when(t == 0)
    def _():
        mid = start_ref[...].astype(f32)
        for c in range(count):
            mid = mid + dot(att_ref[c], out_w_ref[column(c, part_cols), :])
        mid_s[...] = mid
        hat, _ = hat_rows(mid)
        nm = hat * params_ref[1:2] + params_ref[3:4]
        nm_s[...] = nm.astype(bf)
        nmt_s[...] = turn_back(nm)
        gt_s[...] = turn(grad_ref[...])
        acc_s[...] = jnp.zeros_like(acc_s)
        dnm_s[...] = jnp.zeros_like(dnm_s)

    slot = lax.rem(t, 2)
    store = lambda at, where: pltpu.make_async_copy(
        stage_s.at[where], g_ref.at[:, at, :, pl.ds(0, 2 * hidden)], sems.at[where]
    )

    @pl.when(t >= 2)
    def _():
        store(t - 2, slot).wait()

    def one(j, _):
        here = pl.ds(pl.multiple_of(j * step_cols, step_cols), step_cols)
        there = pl.ds(pl.multiple_of(hidden + j * step_cols, step_cols), step_cols)
        fc = fc_ref[:, here]
        proj = proj_ref[:, here]
        x = dot(nm_s[...], fc)
        d_act = dot(grad_ref[...], proj)
        square = x * x
        th = jnp.tanh(0.7978845608028654 * (x + 0.044715 * (square * x)))
        half = 0.5 * (1.0 + th)
        act = (x * half).astype(bf)
        slope = half + (0.5 * x) * (1.0 - th * th) * (
            0.7978845608028654 * (1.0 + (3 * 0.044715) * square)
        )
        d_exp = (slope * d_act).astype(bf)
        acc_s[...] += dot(act, proj, ((1,), (1,)))
        dnm_s[...] += dot(d_exp, fc, ((1,), (1,)))
        d_fc = dot(nmt_s[...], d_exp).astype(bf)
        d_proj = dot(gt_s[...], act).astype(bf)
        for f in range(shards):
            stage_s[slot, f, :, here] = d_fc[column(f, shard_rows)]
            stage_s[slot, f, :, there] = d_proj[column(f, shard_rows)]
        return 0

    lax.fori_loop(0, hidden // step_cols, one, 0)
    store(t, slot).start()

    @pl.when(t == parts - 1)
    def _():
        mid = mid_s[...]
        out_ref[...] = (mid + acc_s[...]).astype(bf)
        hat, inv = hat_rows(mid)
        d_nm = dnm_s[...]
        d_mid = grad_ref[...].astype(f32) + norm_back(hat, inv, params_ref[1:2], d_nm)
        dmid_ref[...] = d_mid
        d_mid_b = d_mid.astype(bf)
        d_mid_t = turn_back(d_mid)
        small_ref[...] = jnp.concatenate(
            [
                jnp.zeros((1, mid.shape[1]), f32),
                jnp.sum(d_nm * hat, axis=0, keepdims=True),
                jnp.zeros((1, mid.shape[1]), f32),
                jnp.sum(d_nm, axis=0, keepdims=True),
                jnp.zeros((4, mid.shape[1]), f32),
            ],
            axis=0,
        )
        for c in range(count):
            datt_ref[c] = dot(d_mid_b, out_w_ref[column(c, part_cols), :], ((1,), (1,))).astype(bf)
            d_out = dot(d_mid_t, att_ref[c]).astype(bf)
            for f in range(shards):
                last_s[f, c, :, :part_cols] = d_out[column(f, shard_rows)]
        if last_s.shape[3] > part_cols:
            last_s[:, :, :, part_cols:] = jnp.zeros(last_s.shape[:3] + (last_s.shape[3] - part_cols,), bf)
        final = pltpu.make_async_copy(
            last_s, g_ref.at[:, :, :, pl.ds(2 * hidden, last_s.shape[3])], last_sem
        )
        final.start()
        if parts >= 2:
            store(parts - 2, (parts - 2) % 2).wait()
        store(parts - 1, (parts - 1) % 2).wait()
        final.wait()


def padded(size):
    return -(-size // 128) * 128


def feed(att, start, grad, out_w, params, fc, proj_t, shards):
    parts, tokens, part_cols = att.shape
    width, hidden_all = fc.shape
    hidden = hidden_all // parts
    shard_rows = width // shards
    step_cols = 256
    wide = 2 * hidden + padded(part_cols)
    bf, f32 = jnp.bfloat16, jnp.float32
    whole = lambda *shape: pl.BlockSpec(shape, lambda t: (0,) * len(shape))
    return pl.pallas_call(
        functools.partial(feed_kernel, step_cols),
        grid=(parts,),
        in_specs=[
            whole(parts, tokens, part_cols), whole(tokens, width), whole(tokens, width), whole(width, width),
            whole(8, width),
            pl.BlockSpec((width, hidden), lambda t: (0, t)),
            pl.BlockSpec((width, hidden), lambda t: (0, t)),
        ],
        out_specs=[
            whole(tokens, width), whole(parts, tokens, part_cols), whole(tokens, width),
            pl.BlockSpec(memory_space=pl.ANY), whole(8, width),
        ],
        out_shape=[
            jax.ShapeDtypeStruct((tokens, width), bf),
            jax.ShapeDtypeStruct((parts, tokens, part_cols), bf),
            jax.ShapeDtypeStruct((tokens, width), f32),
            jax.ShapeDtypeStruct((shards, parts, shard_rows, wide), bf),
            jax.ShapeDtypeStruct((8, width), f32),
        ],
        scratch_shapes=[
            pltpu.VMEM((tokens, width), f32),
            pltpu.VMEM((tokens, width), bf),
            pltpu.VMEM((width, tokens), bf),
            pltpu.VMEM((width, tokens), bf),
            pltpu.VMEM((tokens, width), f32),
            pltpu.VMEM((tokens, width), f32),
            pltpu.VMEM((2, shards, shard_rows, 2 * hidden), bf),
            pltpu.VMEM((shards, parts, shard_rows, padded(part_cols)), bf),
            pltpu.SemaphoreType.DMA((2,)),
            pltpu.SemaphoreType.DMA,
        ],
        compiler_params=pltpu.CompilerParams(vmem_limit_bytes=VMEM_LIMIT),
        cost_estimate=pl.CostEstimate(flops=17 * 10**9, bytes_accessed=40 << 20, transcendentals=2 << 20),
    )(att, start, grad, out_w, params, fc, proj_t)


def add_rows(target, sources, rows_at_once=16):
    def one(i, _):
        here = pl.ds(pl.multiple_of(i * rows_at_once, rows_at_once), rows_at_once)
        total = target[here, :].astype(jnp.float32)
        for source in sources:
            total = total + source[here, :].astype(jnp.float32)
        target[here, :] = total.astype(target.dtype)
        return 0

    lax.fori_loop(0, target.shape[0] // rows_at_once, one, 0)


def finish_kernel(
    sizes,
    dq_ref, dkv_ref, rec_ref, normed_ref, wall_ref, g_ref, start_ref, dmid_ref, gain_ref, small_in, pick_ref,
    dstart_ref, gw_ref, gq_ref, small_ref,
    kv_s, rq, rkv, normed_s, wall_s, own_g, rcore, rx, rc, rz, gq_acc, gq_s, rgq, rb, rgc,
    dst_s, sm_s, rst, rsc, rsf,
    core_sem, core_rec, x_sem, x_rec, c_sem, c_rec, z_sem, z_rec, b_sem, b_rec,
    aq_sem, aq_rec, ak_sem, ak_rec, ag_sem, ag_rec, gq_sem, gq_rec, gc_sem, gc_rec,
    st_sem, st_rec, sc_sem, sc_rec, sf_sem, sf_rec, loc_sem, own_sem,
):
    F, C, T = sizes
    f, c, t = lax.axis_index("fsdp"), lax.axis_index("ctx"), lax.axis_index("tp")
    S = dq_ref.shape[1]
    part = dq_ref.shape[2]
    own_rows = dq_ref.shape[3]
    bf, f32 = jnp.bfloat16, jnp.float32
    sib, across, opposite = f ^ 1, f ^ 2, f ^ 3

    def remote(src, dst, send, recv, **where):
        return pltpu.make_async_remote_copy(
            src_ref=src, dst_ref=dst, send_sem=send, recv_sem=recv, device_id=where, device_id_type=MESH
        )

    locals_ = []
    for tt in range(T):
        for ff in range(F):
            locals_.append(
                pltpu.make_async_copy(
                    wall_ref.at[tt, ff],
                    wall_s.at[tt, :, pl.ds(ff * part, part), :],
                    loc_sem.at[2 + tt * F + ff],
                )
            )
    normed_in = pltpu.make_async_copy(normed_ref, normed_s, loc_sem.at[0])
    g_in = [
        pltpu.make_async_copy(g_ref.at[f], own_g.at[0], own_sem.at[0]),
        pltpu.make_async_copy(g_ref.at[across], own_g.at[1], own_sem.at[1]),
    ]
    for copy in g_in:
        copy.start()
    normed_in.start()
    for copy in locals_:
        copy.start()

    barrier = pltpu.get_barrier_semaphore()
    peers = 0
    for d in range(1, F):
        pl.semaphore_signal(barrier, inc=1, device_id={"fsdp": f ^ d}, device_id_type=MESH)
        peers += 1
    for d in range(1, T):
        pl.semaphore_signal(barrier, inc=1, device_id={"tp": lax.rem(t + d, T)}, device_id_type=MESH)
        peers += 1
    for d in range(1, C):
        pl.semaphore_signal(barrier, inc=1, device_id={"ctx": lax.rem(c + d, C)}, device_id_type=MESH)
        peers += 1
    pl.semaphore_wait(barrier, peers)

    def tp_peer(d):
        return lax.rem(t + d, T)

    pending = []

    def go(copy):
        copy.start()
        pending.append(copy)
        return copy

    aq = [[None] * S for _ in range(T)]
    ak = [[None] * S for _ in range(T)]
    for s in range(S):
        for d in range(1, T):
            aq[d][s] = go(
                remote(dq_ref.at[tp_peer(d), s], rq.at[d, s], aq_sem.at[d, s], aq_rec.at[d, s], tp=tp_peer(d))
            )
    core = [[None, None] for _ in range(T)]
    for b in range(T):
        for k, target in enumerate((sib, opposite)):
            core[b][k] = go(
                remote(g_ref.at[target, b], rcore.at[b, k], core_sem.at[b, k], core_rec.at[b, k], fsdp=sib)
            )
    for s in range(S):
        for d in list(range(1, T)) + [0]:
            peer = tp_peer(d)
            kv_s[d, s] = (dkv_ref[peer, s] + rec_ref[peer, s].astype(f32)).astype(bf)
            if d:
                ak[d][s] = go(
                    remote(kv_s.at[d, s], rkv.at[d, s], ak_sem.at[d, s], ak_rec.at[d, s], tp=peer)
                )

    for copy in g_in:
        copy.wait()
    cross = [None] * T
    for b in range(T):
        core[b][1].wait_recv()
        add_rows(own_g.at[1, b], [rcore.at[b, 1]])
        cross[b] = go(remote(own_g.at[1, b], rx.at[b], x_sem.at[b], x_rec.at[b], fsdp=across))
        core[b][0].wait_recv()
        add_rows(own_g.at[0, b], [rcore.at[b, 0]])

    normed_in.wait()
    gq_acc[...] = jnp.zeros_like(gq_acc)
    for s in range(S):
        for d in range(T):
            peer = tp_peer(d)
            rows = pl.ds(pl.multiple_of(peer * own_rows, own_rows), own_rows)
            gq_acc[:part, :] += dot(dq_ref[peer, s], normed_s[s, rows, :])
            gq_acc[part:, :] += dot(kv_s[d, s], normed_s[s, rows, :])
    for k in range(F):
        gq_s[k] = gq_acc[:, column(k, part)].astype(bf)
    gq = [None] * F
    for d in range(1, F):
        gq[d] = go(remote(gq_s.at[f ^ d], rgq.at[d], gq_sem.at[d], gq_rec.at[d], fsdp=f ^ d))

    held = [b // C for b in range(T)]

    def ctx_stage(b):
        owner = b % C
        cross[b].wait_recv()
        add_rows(own_g.at[0, b], [rx.at[b]])
        for d in range(1, C):
            @pl.when(lax.rem(c + d, C) == owner)
            def _():
                remote(
                    own_g.at[0, b], rc.at[held[b], d], c_sem.at[b], c_rec.at[b, d], ctx=owner
                ).start()

    def ctx_wait(b):
        owner = b % C

        @pl.when(c == owner)
        def _():
            for d in range(1, C):
                remote(own_g.at[0, b], rc.at[held[b], d], c_sem.at[b], c_rec.at[b, d], ctx=owner).wait_recv()
            add_rows(own_g.at[0, b], [rc.at[held[b], d] for d in range(1, C)])

    def z_round(b, step):
        def hop(to, way):
            return remote(own_g.at[0, b], rz.at[held[b], way], z_sem.at[b], z_rec.at[b, way], tp=to)

        def visit(from_end, way, before, here):
            @pl.when((c == b % C) & here)
            def _():
                if step:
                    hop(t, way).wait_recv()
                    add_rows(own_g.at[0, b], [rz.at[held[b], way]])

                @pl.when(before)
                def _():
                    hop(t - 1 if way == 0 else t + 1, way).start()

        if T - 1 - step >= b and b < T - 1:
            visit(step, 0, t > b, t == T - 1 - step)
        if step <= b and b > 0:
            visit(step, 1, t < b, t == step)

    hat, inv = [None] * S, [None] * S
    gain = gain_ref[...]

    def norm_stage(s):
        total = jnp.zeros((wall_s.shape[2], own_rows), f32)
        for d in range(T):
            if d:
                aq[d][s].wait_recv()
                ak[d][s].wait_recv()
            source = lax.rem(t + T - d, T)
            for j in range(3):
                if d:
                    block = rq[d, s] if j == 0 else rkv[d, s, column(j - 1, part), :]
                else:
                    block = dq_ref[t, s] if j == 0 else kv_s[0, s, column(j - 1, part), :]
                total = total + dot(wall_s[source, j], block)
        d_normed = total.T
        hat, inv = hat_rows(start_ref[s].astype(f32))
        value = dmid_ref[s] + norm_back(hat, inv, gain, d_normed)
        dst_s[s] = value.astype(bf)
        return (
            jnp.sum(d_normed * hat, axis=0, keepdims=True),
            jnp.sum(d_normed, axis=0, keepdims=True),
        )

    def ag_copy(s, owner, step, way):
        rows = pl.ds(pl.multiple_of(owner * own_rows, own_rows), own_rows)
        src = dst_s.at[s] if step == 0 else dstart_ref.at[s, rows, :]
        return lambda to: remote(
            src, dstart_ref.at[s, rows, :], ag_sem.at[s, step, way], ag_rec.at[s, step, way], tp=to
        )

    def ag_start(s):
        @pl.when(t < T - 1)
        def _():
            ag_copy(s, t, 0, 0)(t + 1).start()

        @pl.when(t > 0)
        def _():
            ag_copy(s, t, 0, 1)(t - 1).start()

        rows = pl.ds(pl.multiple_of(t * own_rows, own_rows), own_rows)
        keep = pltpu.make_async_copy(dst_s.at[s], dstart_ref.at[s, rows, :], loc_sem.at[1])
        keep.start()
        keep.wait()

    def ag_step(s, step):
        @pl.when(t >= step)
        def _():
            ag_copy(s, t - step, step - 1, 0)(t).wait_recv()

        @pl.when((t >= step) & (t < T - 1))
        def _():
            ag_copy(s, t - step, step, 0)(t + 1).start()

        @pl.when(t + step <= T - 1)
        def _():
            ag_copy(s, t + step, step - 1, 1)(t).wait_recv()

        @pl.when((t + step <= T - 1) & (t > 0))
        def _():
            ag_copy(s, t + step, step, 1)(t - 1).start()

    def ag_drain(s):
        for step in range(T - 1):
            @pl.when((t >= step) & (t < T - 1))
            def _():
                ag_copy(s, t - step, step, 0)(t + 1).wait_send()

            @pl.when((t + step <= T - 1) & (t > 0))
            def _():
                ag_copy(s, t + step, step, 1)(t - 1).wait_send()

    for copy in locals_:
        copy.wait()
    sums = [None] * S
    for s in range(S):
        for b in range(s * T // S, (s + 1) * T // S):
            ctx_stage(b)
        sums[s] = norm_stage(s)
        ag_start(s)
    gain_sum = sum(pair[0] for pair in sums)
    bias_sum = sum(pair[1] for pair in sums)
    sm_s[0:8, :] = small_in[...] + jnp.concatenate(
        [gain_sum, jnp.zeros_like(gain_sum), bias_sum, jnp.zeros((5, gain_sum.shape[1]), f32)], axis=0
    )
    thoughts = jnp.zeros((pick_ref.shape[1], sm_s.shape[1]), f32)
    for s in range(S):
        thoughts = thoughts + dot(pick_ref[s], dst_s[s])
    sm_s[8:, :] = thoughts
    st = [None] * T
    for d in range(1, T):
        st[d] = go(remote(sm_s, rst.at[d], st_sem.at[d], st_rec.at[d], tp=tp_peer(d)))

    gq_sum = gq_s[f].astype(f32)
    for d in range(1, F):
        gq[d].wait_recv()
        gq_sum = gq_sum + rgq[d].astype(f32)
    rgc[c] = gq_sum.astype(bf)
    gc = [None] * C
    for d in range(1, C):
        gc[d] = go(remote(rgc.at[c], rgc.at[c], gc_sem.at[d], gc_rec.at[d], ctx=lax.rem(c + d, C)))

    for step in range(T):
        if step:
            for s in range(S):
                ag_step(s, step)
        for b in range(T):
            if step == 0:
                ctx_wait(b)
            z_round(b, step)

    for d in range(1, T):
        st[d].wait_recv()
    rst[0] = sm_s[...]
    total = jnp.zeros(sm_s.shape, f32)
    for k in range(T):
        total = total + rst[lax.rem(t + T - k, T)]
    rsc[c] = total
    sc = [None] * C
    for d in range(1, C):
        sc[d] = go(remote(rsc.at[c], rsc.at[c], sc_sem.at[d], sc_rec.at[d], ctx=lax.rem(c + d, C)))
    for d in range(1, C):
        sc[d].wait_recv()
    total = jnp.zeros(sm_s.shape, f32)
    for k in range(C):
        total = total + rsc[k]
    rsf[f] = total
    sf = [None] * F
    for d in range(1, F):
        sf[d] = go(remote(rsf.at[f], rsf.at[f], sf_sem.at[d], sf_rec.at[d], fsdp=f ^ d))
    for d in range(1, F):
        sf[d].wait_recv()
    norms = jnp.zeros((8, sm_s.shape[1]), f32)
    for k in range(F):
        norms = norms + rsf[k, 0:8, :]
    small_ref[0:8, :] = norms
    small_ref[8:, :] = total[8:]

    for d in range(1, C):
        gc[d].wait_recv()
    total = jnp.zeros(gq_ref.shape, f32)
    for k in range(C):
        total = total + rgc[k].astype(f32)
    gq_ref[...] = total

    for b in range(T):
        owner = b % C

        @pl.when((t == b) & (c == owner))
        def _():
            for d in range(1, C):
                remote(
                    own_g.at[0, b], rb, b_sem.at[d], b_rec, ctx=lax.rem(owner + d, C)
                ).start()
            gw_ref[...] = own_g[0, b]
            for d in range(1, C):
                remote(
                    own_g.at[0, b], rb, b_sem.at[d], b_rec, ctx=lax.rem(owner + d, C)
                ).wait_send()

        @pl.when((t == b) & (c != owner))
        def _():
            remote(own_g.at[0, b], rb, b_sem.at[1], b_rec, ctx=owner).wait_recv()
            gw_ref[...] = rb[...]

    for copy in pending:
        copy.wait_send()
    for b in range(T):
        owner = b % C

        @pl.when(c != owner)
        def _():
            remote(own_g.at[0, b], rc.at[held[b], 1], c_sem.at[b], c_rec.at[b, 1], ctx=owner).wait_send()

        @pl.when((c == owner) & (t != b))
        def _():
            remote(own_g.at[0, b], rz.at[held[b], 0], z_sem.at[b], z_rec.at[b, 0], tp=t).wait_send()
    for s in range(S):
        ag_drain(s)


def finish(dq, dkv, received, normed, wall, g, start, dmid, gain, small, pick, counts):
    F, C, T = counts
    _, S, part, own_rows = dq.shape
    width = normed.shape[2]
    _, _, shard_rows, wide = g.shape
    bf, f32 = jnp.bfloat16, jnp.float32
    rows = own_rows * T
    extra = 8 + pick.shape[1]
    mine = -(-T // C)
    vmem = pl.BlockSpec(memory_space=pltpu.VMEM)
    anywhere = pl.BlockSpec(memory_space=pl.ANY)
    dma = lambda *shape: pltpu.SemaphoreType.DMA(shape)
    return pl.pallas_call(
        functools.partial(finish_kernel, counts),
        in_specs=[vmem, vmem, vmem, anywhere, anywhere, anywhere, vmem, vmem, vmem, vmem, vmem],
        out_specs=[anywhere, vmem, vmem, vmem],
        out_shape=[
            jax.ShapeDtypeStruct((S, rows, width), bf),
            jax.ShapeDtypeStruct((shard_rows, wide), bf),
            jax.ShapeDtypeStruct((3 * part, shard_rows), f32),
            jax.ShapeDtypeStruct((extra, width), f32),
        ],
        scratch_shapes=[
            pltpu.VMEM((T, S, 2 * part, own_rows), bf),
            pltpu.VMEM((T, S, part, own_rows), bf),
            pltpu.VMEM((T, S, 2 * part, own_rows), bf),
            pltpu.VMEM((S, rows, width), bf),
            pltpu.VMEM((T, 3, width, part), bf),
            pltpu.VMEM((2, T, shard_rows, wide), bf),
            pltpu.VMEM((T, 2, shard_rows, wide), bf),
            pltpu.VMEM((T, shard_rows, wide), bf),
            pltpu.VMEM((mine, C, shard_rows, wide), bf),
            pltpu.VMEM((mine, 2, shard_rows, wide), bf),
            pltpu.VMEM((3 * part, width), f32),
            pltpu.VMEM((F, 3 * part, shard_rows), bf),
            pltpu.VMEM((F, 3 * part, shard_rows), bf),
            pltpu.VMEM((shard_rows, wide), bf),
            pltpu.VMEM((C, 3 * part, shard_rows), bf),
            pltpu.VMEM((S, own_rows, width), bf),
            pltpu.VMEM((extra, width), f32),
            pltpu.VMEM((T, extra, width), f32),
            pltpu.VMEM((C, extra, width), f32),
            pltpu.VMEM((F, extra, width), f32),
            dma(T, 2), dma(T, 2), dma(T), dma(T), dma(T), dma(T, C), dma(T), dma(T, 2), dma(C), pltpu.SemaphoreType.DMA,
            dma(T, S), dma(T, S), dma(T, S), dma(T, S), dma(S, T, 2), dma(S, T, 2), dma(F), dma(F), dma(C), dma(C),
            dma(T), dma(T), dma(C), dma(C), dma(F), dma(F), dma(2 + T * F), dma(2),
        ],
        compiler_params=pltpu.CompilerParams(
            vmem_limit_bytes=VMEM_LIMIT, collective_id=0, has_side_effects=True
        ),
        cost_estimate=pl.CostEstimate(flops=4 * 10**9, bytes_accessed=64 << 20, transcendentals=0),
    )(dq, dkv, received, normed, wall, g, start, dmid, gain, small, pick)


def local(
    inputs, thoughts, positions, lengths, w_qkv, w_out, w_fc, w_proj, norm_gains, norm_biases, out_grad,
):
    rows, seqs, width = inputs.shape
    ctx_count = lax.axis_size("ctx")
    tp_count = lax.axis_size("tp")
    fsdp_count = lax.axis_size("fsdp")
    ctx, tp, fsdp = lax.axis_index("ctx"), lax.axis_index("tp"), lax.axis_index("fsdp")
    first_row = ctx * rows
    own_rows = rows // tp_count
    own_tokens = own_rows * seqs
    far = min(ctx_count - 1, -(-(DOC_MOST - 1) // rows))
    block = min(256, rows)
    bf, f32 = jnp.bfloat16, jnp.float32

    counts = (fsdp_count, ctx_count, tp_count)
    local_width = w_qkv.shape[2]
    params = jnp.pad(jnp.concatenate([norm_gains, norm_biases]).astype(f32), ((0, 4), (0, 0)))
    places = first_row + jnp.arange(rows, dtype=jnp.int32)
    is_thought = places[None, None, :] == positions[:, :, None]
    keep = jnp.logical_not(jnp.any(is_thought, axis=0))
    start = jnp.transpose(inputs, (1, 0, 2))
    for t in range(thoughts.shape[0]):
        start = jnp.where(is_thought[t][:, :, None], thoughts[t][:, None, :], start)
    ends = jnp.cumsum(lengths, axis=1, dtype=jnp.int32)
    low = jnp.max(jnp.where(ends[:, :, None] <= places[None, None, :], ends[:, :, None], 0), axis=1)
    low = low - (first_row - far * rows)
    first = low[:, ::block] // block

    low3 = low[:, None, :]
    attended, q, kv, prev, out_t, logs, normed, out_full, fc_full, proj_full_t, params = front(
        start, low3, w_qkv, w_out, w_fc, w_proj.T, params, block, far, counts
    )
    gains = params[:2]
    w_qkv_late, attended = lax.optimization_barrier((w_qkv, attended))
    wall = lax.all_gather(w_qkv_late, ("tp", "fsdp"), axis=0, tiled=False)
    wall = wall.reshape((tp_count, fsdp_count) + w_qkv.shape)
    own = lambda a: lax.dynamic_slice_in_dim(a, tp * own_rows, own_rows, 1)
    exchange = lambda a: lax.all_to_all(a, "tp", split_axis=0, concat_axis=0, tiled=True)
    attended_own = attended.reshape(tp_count, own_tokens, local_width)
    start_own = own(start)
    grad_own = jnp.transpose(
        lax.dynamic_slice_in_dim(out_grad, tp * own_rows, own_rows, 0), (1, 0, 2)
    ).reshape(own_tokens, width)
    output_own, d_attended_own, d_middle, g, small = feed(
        attended_own, start_own.reshape(own_tokens, width), grad_own, out_full, params, fc_full, proj_full_t, fsdp_count
    )
    d_attended = exchange(d_attended_own.reshape(tp_count, seqs, own_rows, local_width))
    output = lax.all_gather(output_own.reshape(seqs, own_rows, width), "tp", axis=1, tiled=True)
    output = jnp.transpose(output, (1, 0, 2))

    d_q, d_kv, d_prev = attend_back(q, kv, prev, low3, first, d_attended, out_t, logs, block, far)
    if far == 0:
        received = jnp.zeros(d_kv.shape, bf)
    else:
        pieces = [
            lax.ppermute(d_prev[index], "ctx", [(i + d, i) for i in range(ctx_count - d)])
            for index, d in enumerate(range(far, 0, -1))
        ]
        received = pieces[0] if far == 1 else sum(piece.astype(f32) for piece in pieces)

    own_places = lax.dynamic_slice_in_dim(places, tp * own_rows, own_rows, 0)
    count = thoughts.shape[0]
    pick = (own_places[None, None, :] == positions[:, :, None]).astype(bf)
    picks = []
    for s in range(seqs):
        picks.append(jnp.concatenate(
            [jnp.where(k == s, pick[:, s], jnp.zeros_like(pick[:, s])) for k in range(seqs)], axis=0
        ))
    pick = jnp.stack(picks)
    pick = jnp.pad(pick, ((0, 0), (0, -(-pick.shape[1] // 16) * 16 - pick.shape[1]), (0, 0)))
    d_start, gw, gq, small = finish(
        d_q, d_kv, received, normed, wall, g, start_own, d_middle.reshape(seqs, own_rows, width),
        gains[0:1], small, pick, counts,
    )
    d_inputs = jnp.transpose(jnp.where(keep[:, :, None], d_start.astype(f32), 0.0), (1, 0, 2))
    d_thoughts = jnp.transpose(small[8 : 8 + count * seqs].reshape(seqs, count, width), (1, 0, 2))
    hidden = w_fc.shape[1]
    gw = gw.astype(f32)
    norms = lax.dynamic_slice_in_dim(small[:4], fsdp * w_fc.shape[0], w_fc.shape[0], 1)
    return (
        output,
        d_inputs,
        d_thoughts,
        jnp.transpose(gq.reshape(3, local_width, -1), (0, 2, 1)),
        gw[:, 2 * hidden : 2 * hidden + local_width].T,
        gw[:, :hidden],
        gw[:, hidden : 2 * hidden].T,
        norms[:2],
        norms[2],
        norms[3],
    )


def solution(mesh):
    in_specs = (
        P("ctx", "fsdp", None),
        P(None, "fsdp", None),
        P(None, "fsdp"),
        P("fsdp", None),
        P(None, "fsdp", "tp"),
        P("tp", "fsdp"),
        P("fsdp", "tp"),
        P("tp", "fsdp"),
        P(None, "fsdp"),
        P(None, "fsdp"),
        P("ctx", "fsdp", None),
    )
    out_specs = (
        P("ctx", "fsdp", None),
        P("ctx", "fsdp", None),
        P(None, "fsdp", None),
        P(None, "fsdp", "tp"),
        P("tp", "fsdp"),
        P("fsdp", "tp"),
        P("tp", "fsdp"),
        P(None, "fsdp"),
        P("fsdp"),
        P("fsdp"),
    )
    return jax.shard_map(local, mesh=mesh, in_specs=in_specs, out_specs=out_specs, check_vma=False)
```

```python
import functools

import jax
import jax.numpy as jnp
from jax import lax
from jax.experimental import pallas as pl
from jax.experimental.pallas import tpu as pltpu
from jax.sharding import PartitionSpec as P

HEAD_DIM = 64
DOC_MOST = 1024
EPSILON = 1e-05
MASKED = -1e30


def dot(a, b, dims=((1,), (0,))):
    return lax.dot_general(a, b, (dims, ((), ())), preferred_element_type=jnp.float32)


def hat_rows(values):
    centre = jnp.mean(values, axis=-1, keepdims=True)
    shifted = values - centre
    spread = jnp.mean(shifted * shifted, axis=-1, keepdims=True)
    inv = lax.rsqrt(spread + EPSILON)
    return shifted * inv, inv


def norm_back(hat, inv, gain, grad):
    eg = grad * gain
    return inv * (
        eg
        - jnp.mean(eg, axis=-1, keepdims=True)
        - hat * jnp.mean(eg * hat, axis=-1, keepdims=True)
    )


MESH = pl.DeviceIdType.MESH
VMEM_LIMIT = 60 << 20


def column(index, size=HEAD_DIM):
    return slice(index * size, (index + 1) * size)


def turn(value):
    return value.astype(jnp.float32).T.astype(jnp.bfloat16)


def turn_back(value):
    return value.T.astype(jnp.bfloat16)


def front_kernel(
    sizes, block,
    start_ref, low_ref, wq_ref, wo_ref, wf_ref, wp_ref, par_ref,
    att_ref, q_ref, kv_ref, prev_ref, out_t_ref, log_ref, normed_ref, ow_ref, fc_ref, pj_ref, params_ref,
    start_s, normed_s, wl_s, wo_s, par_s, q_s, kv_s, prev_s, qt_s, ko_s, vto_s, kp_s, vtp_s, m_s, l_s, att_s,
    in_sem, out_sem, w_loc, z_sem, z_rec, s_sem, s_rec, x_sem, x_rec, r_sem, r_rec,
    kv_sem, kv_rec, at_sem, at_rec, at_loc,
):
    F, C, T = sizes
    f, c, t = lax.axis_index("fsdp"), lax.axis_index("ctx"), lax.axis_index("tp")
    S, rows, width = start_ref.shape
    hw = q_ref.shape[2]
    heads = hw // HEAD_DIM
    own_rows = rows // T
    far = prev_ref.shape[1] // rows if C > 1 else 0
    shard = wq_ref.shape[1]
    hidden = wf_ref.shape[1]
    bf, f32 = jnp.bfloat16, jnp.float32
    sib, across = f ^ 1, f ^ 2

    def remote(src, dst, send, recv, **where):
        return pltpu.make_async_remote_copy(
            src_ref=src, dst_ref=dst, send_sem=send, recv_sem=recv, device_id=where, device_id_type=MESH
        )

    start_in = pltpu.make_async_copy(start_ref, start_s, in_sem.at[0])
    start_in.start()

    barrier = pltpu.get_barrier_semaphore()
    peers = 0
    for d in range(1, F):
        pl.semaphore_signal(barrier, inc=1, device_id={"fsdp": f ^ d}, device_id_type=MESH)
        peers += 1
    for d in range(1, T):
        pl.semaphore_signal(barrier, inc=1, device_id={"tp": lax.rem(t + d, T)}, device_id_type=MESH)
        peers += 1
    for d in range(1, C):
        pl.semaphore_signal(barrier, inc=1, device_id={"ctx": lax.rem(c + d, C)}, device_id_type=MESH)
        peers += 1
    pl.semaphore_wait(barrier, peers)

    pending = []

    def go(copy):
        copy.start()
        pending.append(copy)
        return copy

    def at_shard(ff):
        return pl.ds(pl.multiple_of(ff * shard, shard), shard)

    def at_hidden(tt):
        return pl.ds(pl.multiple_of(tt * hidden, hidden), hidden)

    def block_at(a, tt, ff):
        if a == 0:
            return par_s.at[ff]
        if a == 1:
            return wl_s.at[:, at_shard(ff), :]
        if a == 2:
            return wo_s.at[tt, ff]
        return (fc_ref if a == 3 else pj_ref).at[at_shard(ff), at_hidden(tt)]

    sources = (par_ref, wq_ref, wo_ref, wf_ref, wp_ref)
    slot = lambda d: lax.rem(t + T - d, T)

    def spread_chip(a, d):
        src = sources[a] if d == 0 else block_at(a, slot(d), f)
        dst = block_at(a, slot(d), f)
        go(remote(src, dst, x_sem.at[a, d], x_rec.at[a, d], fsdp=across))
        go(remote(src, dst, s_sem.at[a, d], s_rec.at[a, d], fsdp=sib))

    def take_z(a, d):
        here = block_at(a, slot(d), f)
        remote(here, here, z_sem.at[a, d], z_rec.at[a, d], tp=t).wait_recv()
        spread_chip(a, d)

    def relay(a, d):
        here = block_at(a, slot(d), across)
        remote(here, here, x_sem.at[a, d], x_rec.at[a, d], fsdp=f).wait_recv()
        go(remote(here, here, r_sem.at[a, d], r_rec.at[a, d], fsdp=sib))

    def take_chip(a, d):
        for ff, rec in ((sib, s_rec), (sib ^ 2, r_rec)):
            here = block_at(a, slot(d), ff)
            remote(here, here, s_sem.at[a, d], rec.at[a, d], fsdp=f).wait_recv()

    keeps = []
    for a in range(5):
        keep = pltpu.make_async_copy(sources[a], block_at(a, t, f), w_loc.at[a])
        keep.start()
        keeps.append(keep)
    spread_chip(0, 0)
    spread_chip(1, 0)
    for a in (2, 3, 4):
        for d in range(1, T):
            go(remote(sources[a], block_at(a, t, f), z_sem.at[a, d], z_rec.at[a, d], tp=lax.rem(t + d, T)))
        spread_chip(a, 0)

    relay(0, 0)
    take_chip(0, 0)
    keeps[0].wait()
    params = jnp.concatenate([par_s[ff] for ff in range(F)], axis=1)
    params_ref[...] = params
    start_in.wait()
    per_seq = rows // block

    def norm_one(index, _):
        s = index // per_seq
        here = pl.ds(pl.multiple_of(lax.rem(index, per_seq) * block, block), block)
        hat, _ = hat_rows(start_s[s, here, :].astype(f32))
        normed_s[s, here, :] = (hat * params_ref[0:1, :] + params_ref[2:3, :]).astype(bf)
        return 0

    lax.fori_loop(0, S * per_seq, norm_one, 0)
    normed_out = pltpu.make_async_copy(normed_s, normed_ref, out_sem.at[0])
    normed_out.start()

    relay(1, 0)
    take_chip(1, 0)
    keeps[1].wait()

    def kv_one(s, _):
        def one(index, _):
            here = pl.ds(pl.multiple_of(index * block, block), block)
            rows_in = normed_s[s, here, :]
            k = dot(rows_in, wl_s[1]).astype(bf)
            v = dot(rows_in, wl_s[2]).astype(bf)
            kv_s[s, here, :] = jnp.concatenate([k, v], axis=1)
            v_t = turn(v)
            for h in range(heads):
                ko_s[s, h, here, :] = k[:, column(h)]
                vto_s[s, h, :, here] = v_t[column(h)]
            return 0

        lax.fori_loop(0, per_seq, one, 0)
        return 0

    def kv_copy(s, d):
        return remote(
            kv_s.at[s], prev_s.at[s, pl.ds((far - d) * rows, rows), :],
            kv_sem.at[d, s], kv_rec.at[d, s], ctx=lax.rem(c + d, C),
        )

    for s in range(S):
        kv_one(s, 0)
        for d in range(1, far + 1):
            @pl.when(c + d < C)
            def _():
                kv_copy(s, d).start()

    def q_one(index, _):
        s = index // per_seq
        here = pl.ds(pl.multiple_of(lax.rem(index, per_seq) * block, block), block)
        q = dot(normed_s[s, here, :], wl_s[0]).astype(bf)
        q_s[s, here, :] = q
        q_t = turn(q.astype(f32) * 0.125)
        for h in range(heads):
            qt_s[s, h, :, here] = q_t[column(h)]
        return 0

    lax.fori_loop(0, S * per_seq, q_one, 0)
    outs = [
        pltpu.make_async_copy(q_s, q_ref, out_sem.at[1]),
        pltpu.make_async_copy(kv_s, kv_ref, out_sem.at[2]),
    ]
    for copy in outs:
        copy.start()

    def own_part(s):
        for i in range(per_seq):
            span = column(i, block)
            low = low_ref[s, :, span] - far * rows
            top = i * block + lax.broadcasted_iota(jnp.int32, (1, block), 1)
            first = max(0, i * block - (DOC_MOST - 1)) // block * block
            many = (i + 1) * block - first
            place = first + lax.broadcasted_iota(jnp.int32, (many, 1), 0)
            allowed = (place >= low) & (place <= top)
            for h in range(heads):
                scores = dot(ko_s[s, h, first : first + many, :], qt_s[s, h, :, span])
                scores = jnp.where(allowed, scores, MASKED)
                m = jnp.max(scores, axis=0, keepdims=True)
                p = jnp.exp(scores - m)
                m_s[s, h : h + 1, span] = m
                l_s[s, h : h + 1, span] = jnp.sum(p, axis=0, keepdims=True)
                out_t_ref[s, column(h), span] = dot(vto_s[s, h, :, first : first + many], p.astype(bf))

    def far_part(s):
        for h in range(heads):
            kp_s[h] = prev_s[s, :, column(h)]
            vtp_s[h] = turn(prev_s[s, :, column(heads + h)])
        for i in range(per_seq):
            span = column(i, block)
            low = low_ref[s, :, span]
            first = max(0, far * rows + i * block - (DOC_MOST - 1)) // block * block
            if first >= far * rows:
                continue
            many = far * rows - first
            place = first + lax.broadcasted_iota(jnp.int32, (many, 1), 0)
            allowed = place >= low
            for h in range(heads):
                scores = dot(kp_s[h, first : first + many, :], qt_s[s, h, :, span])
                scores = jnp.where(allowed, scores, MASKED)
                old = m_s[s, h : h + 1, span]
                m = jnp.maximum(old, jnp.max(scores, axis=0, keepdims=True))
                p = jnp.exp(scores - m)
                alpha = jnp.exp(old - m)
                m_s[s, h : h + 1, span] = m
                l_s[s, h : h + 1, span] = alpha * l_s[s, h : h + 1, span] + jnp.sum(p, axis=0, keepdims=True)
                out_t_ref[s, column(h), span] = alpha * out_t_ref[s, column(h), span] + dot(
                    vtp_s[h, :, first : first + many], p.astype(bf)
                )

    def finish_part(s):
        for h in range(heads):
            out_t_ref[s, column(h), :] = out_t_ref[s, column(h), :] / l_s[s, h : h + 1, :]
            log_ref[s, h : h + 1, :] = m_s[s, h : h + 1, :] + jnp.log(l_s[s, h : h + 1, :])
        for tt in range(T):
            att_s[tt, s] = turn_back(out_t_ref[s, :, column(tt, own_rows)])

    for d in range(1, T):
        take_z(2, d)

    def own_loop(s, _):
        own_part(s)
        return 0

    lax.fori_loop(0, S, own_loop, 0)
    for d in range(T):
        relay(2, d)
    take_z(3, 1)

    def wait_far(s):
        for d in range(1, far + 1):
            @pl.when(c >= d)
            def _():
                kv_copy(s, d).wait_recv()

            @pl.when(c < d)
            def _():
                prev_s[s, (far - d) * rows : (far - d + 1) * rows, :] = jnp.zeros((rows, 2 * hw), bf)

    at = [[None] * S for _ in range(T)]
    for s in range(S):
        if far:
            wait_far(s)

            @pl.when(c > 0)
            def _():
                far_part(s)
        finish_part(s)
        for d in range(1, T):
            peer = lax.rem(t + d, T)
            at[d][s] = go(
                remote(att_s.at[peer, s], att_ref.at[t, s], at_sem.at[d, s], at_rec.at[d, s], tp=peer)
            )
        own_at = pltpu.make_async_copy(att_s.at[t, s], att_ref.at[t, s], at_loc.at[s])
        own_at.start()
        at[0][s] = own_at
        if s == 0:
            take_z(3, 2)
            take_z(3, 3)
            for d in range(T):
                relay(3, d)
    prev_out = pltpu.make_async_copy(prev_s, prev_ref, out_sem.at[3])
    if far:
        prev_out.start()
    for d in range(1, T):
        take_z(4, d)
    for d in range(T):
        take_chip(2, d)
    keeps[2].wait()
    for tt in range(T):
        for ff in range(F):
            ow_ref[column(tt, hw), column(ff, shard)] = wo_s[tt, ff]
    for d in range(T):
        relay(4, d)
    for a in (3, 4):
        for d in range(T):
            take_chip(a, d)
        keeps[a].wait()
    for s in range(S):
        at[0][s].wait()
        for d in range(1, T):
            at[d][s].wait_recv()
    normed_out.wait()
    for copy in outs:
        copy.wait()
    if far:
        prev_out.wait()
    for copy in pending:
        copy.wait_send()
    for s in range(S):
        for d in range(1, far + 1):
            @pl.when(c + d < C)
            def _():
                kv_copy(s, d).wait_send()


def front(start, low, wq, wo, wf, wp, params, block, far, counts):
    F, C, T = counts
    S, rows, width = start.shape
    hw = wq.shape[2]
    shard = wq.shape[1]
    heads = hw // HEAD_DIM
    hidden = wf.shape[1]
    bf, f32 = jnp.bfloat16, jnp.float32
    vmem = pl.BlockSpec(memory_space=pltpu.VMEM)
    anywhere = pl.BlockSpec(memory_space=pl.ANY)
    dma = lambda *shape: pltpu.SemaphoreType.DMA(shape)
    past = max(far, 1) * rows
    shape = jax.ShapeDtypeStruct
    return pl.pallas_call(
        functools.partial(front_kernel, counts, block),
        in_specs=[anywhere, vmem, anywhere, anywhere, anywhere, anywhere, anywhere],
        out_specs=[anywhere, anywhere, anywhere, anywhere, vmem, vmem, anywhere, vmem, anywhere, anywhere, vmem],
        out_shape=[
            shape((T, S, rows // T, hw), bf),
            shape((S, rows, hw), bf),
            shape((S, rows, 2 * hw), bf),
            shape((S, past, 2 * hw), bf),
            shape((S, hw, rows), f32),
            shape((S, 8, rows), f32),
            shape((S, rows, width), bf),
            shape((T * hw, F * shard), bf),
            shape((F * shard, T * hidden), bf),
            shape((F * shard, T * hidden), bf),
            shape((8, F * shard), f32),
        ],
        scratch_shapes=[
            pltpu.VMEM((S, rows, width), bf),
            pltpu.VMEM((S, rows, width), bf),
            pltpu.VMEM((3, F * shard, hw), bf),
            pltpu.VMEM((T, F, hw, shard), bf),
            pltpu.VMEM((F, 8, shard), f32),
            pltpu.VMEM((S, rows, hw), bf),
            pltpu.VMEM((S, rows, 2 * hw), bf),
            pltpu.VMEM((S, past, 2 * hw), bf),
            pltpu.VMEM((S, heads, HEAD_DIM, rows), bf),
            pltpu.VMEM((S, heads, rows, HEAD_DIM), bf),
            pltpu.VMEM((S, heads, HEAD_DIM, rows), bf),
            pltpu.VMEM((heads, past, HEAD_DIM), bf),
            pltpu.VMEM((heads, HEAD_DIM, past), bf),
            pltpu.VMEM((S, 8, rows), f32),
            pltpu.VMEM((S, 8, rows), f32),
            pltpu.VMEM((T, S, rows // T, hw), bf),
            dma(1), dma(4), dma(5),
            dma(5, T), dma(5, T), dma(5, T), dma(5, T), dma(5, T), dma(5, T), dma(5, T), dma(5, T),
            dma(far + 1, S), dma(far + 1, S), dma(T, S), dma(T, S), dma(S),
        ],
        compiler_params=pltpu.CompilerParams(
            vmem_limit_bytes=VMEM_LIMIT, collective_id=1, has_side_effects=True
        ),
        cost_estimate=pl.CostEstimate(flops=8 * 10**9, bytes_accessed=64 << 20, transcendentals=8 << 20),
    )(start, low, wq, wo, wf, wp, params)


def padded(size):
    return -(-size // 128) * 128


def add_rows(target, sources, rows_at_once=16):
    def one(i, _):
        here = pl.ds(pl.multiple_of(i * rows_at_once, rows_at_once), rows_at_once)
        total = target[here, :].astype(jnp.float32)
        for source in sources:
            total = total + source[here, :].astype(jnp.float32)
        target[here, :] = total.astype(target.dtype)
        return 0

    lax.fori_loop(0, target.shape[0] // rows_at_once, one, 0)


def gelu_parts(x):
    square = x * x
    th = jnp.tanh(0.7978845608028654 * (x + 0.044715 * (square * x)))
    half = 0.5 * (1.0 + th)
    slope = half + (0.5 * x) * (1.0 - th * th) * (0.7978845608028654 * (1.0 + (3 * 0.044715) * square))
    return x * half, slope


def back_kernel(
    sizes, block, far, step_cols,
    att_ref, start_ref, grad_ref, outw_ref, fc_ref, pj_ref, params_ref,
    q_ref, kv_ref, prev_ref, low_ref, out_t_ref, log_ref, normed_ref, wq_ref, pick_ref,
    output_ref, dstart_ref, wall_ref, gw_ref, gq_ref, small_ref,
    start_s, mid_s, grad_s, ob_s, gbuf, rcore, rx, rc, rz, g2, r2c, r2x,
    da_s, da_r, dp_s, rec_s, kv_s, dq_s, rq, rkv, gq_s, rgq, rgc, sm_s, rst, rsc, rsf,
    in_sem, w_sem, core_sem, core_rec, x_sem, x_rec, c2_sem, c2_rec, x2_sem, x2_rec,
    c_sem, c_rec, z_sem, z_rec, b_sem, b_rec, da_sem, da_rec, dp_sem, dp_rec,
    aq_sem, aq_rec, ak_sem, ak_rec, ag_sem, ag_rec, gq_sem, gq_rec, gc_sem, gc_rec,
    st_sem, st_rec, sc_sem, sc_rec, sf_sem, sf_rec, loc_sem, wall_sem, wz_sem, wz_rec, ws_sem, ws_rec, wx_sem, wx_rec,
    wr_sem, wr_rec, wq_sem, credit,
):
    F, C, T = sizes
    f, c, t = lax.axis_index("fsdp"), lax.axis_index("ctx"), lax.axis_index("tp")
    S, rows, hw = q_ref.shape
    heads = hw // HEAD_DIM
    width = start_s.shape[2]
    own_rows = rows // T
    tokens = S * own_rows
    shard = gbuf.shape[1]
    hidden = fc_ref.shape[1] // T
    wide = 2 * hidden
    per_seq = rows // block
    bf, f32 = jnp.bfloat16, jnp.float32
    sib, across = f ^ 1, f ^ 2

    def remote(src, dst, send, recv, **where):
        return pltpu.make_async_remote_copy(
            src_ref=src, dst_ref=dst, send_sem=send, recv_sem=recv, device_id=where, device_id_type=MESH
        )

    pending = []

    def go(copy, like):
        copy.start()
        pending.append(like)

    def landed(ref, sem):
        remote(ref, ref, b_rec, sem, fsdp=f).wait_recv()

    def sent(ref, sem):
        remote(ref, ref, sem, b_rec, fsdp=f).wait_send()

    def tp_peer(d):
        return lax.rem(t + d, T)

    def tp_source(d):
        return lax.rem(t + T - d, T)

    def rows_of(owner):
        return pl.ds(pl.multiple_of(owner * own_rows, own_rows), own_rows)

    ag_own, ag_whole = (ob_s, ob_s), (output_ref, dstart_ref)

    def ag_copy(a, s, owner, step, way):
        whole = ag_whole[a].at[s, rows_of(owner), :]
        src = ag_own[a].at[s] if step == 0 else whole
        return lambda to: remote(src, whole, ag_sem.at[a, s, step, way], ag_rec.at[a, s, step, way], tp=to)

    def ag_keep(a, s):
        return pltpu.make_async_copy(ag_own[a].at[s], ag_whole[a].at[s, rows_of(t), :], loc_sem.at[a, s])

    def ag_start(a, s):
        @pl.when(t < T - 1)
        def _():
            ag_copy(a, s, t, 0, 0)(t + 1).start()

        @pl.when(t > 0)
        def _():
            ag_copy(a, s, t, 0, 1)(t - 1).start()

        ag_keep(a, s).start()

    def ag_step(a, s, step):
        @pl.when(t >= step)
        def _():
            ag_copy(a, s, t - step, step - 1, 0)(t).wait_recv()

        @pl.when((t >= step) & (t < T - 1))
        def _():
            ag_copy(a, s, t - step, step, 0)(t + 1).start()

        @pl.when(t + step <= T - 1)
        def _():
            ag_copy(a, s, t + step, step - 1, 1)(t).wait_recv()

        @pl.when((t + step <= T - 1) & (t > 0))
        def _():
            ag_copy(a, s, t + step, step, 1)(t - 1).start()

    def ag_drain(a, s, first):
        if not first:
            ag_keep(a, s).wait()
        for step in range(first, T - 1 if first or a else 1):
            @pl.when((t >= step) & (t < T - 1))
            def _():
                ag_copy(a, s, t - step, step, 0)(t + 1).wait_send()

            @pl.when((t + step <= T - 1) & (t > 0))
            def _():
                ag_copy(a, s, t + step, step, 1)(t - 1).wait_send()

    def wall_keep():
        return pltpu.make_async_copy(wq_ref, wall_ref.at[t, f], wq_sem)

    def wall_spread(d):
        src = wq_ref if d == 0 else wall_ref.at[tp_source(d), f]
        dst = wall_ref.at[tp_source(d), f]
        go(remote(src, dst, wx_sem.at[d], wx_rec.at[d], fsdp=across), lambda: (wq_ref, wx_sem.at[d]))
        go(remote(src, dst, ws_sem.at[d], ws_rec.at[d], fsdp=sib), lambda: (wq_ref, ws_sem.at[d]))

    def wall_start():
        wall_keep().start()
        for d in range(1, T):
            go(
                remote(wq_ref, wall_ref.at[t, f], wz_sem.at[d], wz_rec.at[d], tp=tp_peer(d)),
                lambda d=d: (wq_ref, wz_sem.at[d]),
            )
        wall_spread(0)

    def wall_take(d):
        landed(wall_ref.at[tp_source(d), f], wz_rec.at[d])
        wall_spread(d)

    def wall_relay(d):
        here = wall_ref.at[tp_source(d), across]
        landed(here, wx_rec.at[d])
        go(remote(here, here, wr_sem.at[d], wr_rec.at[d], fsdp=sib), lambda: (wq_ref, wr_sem.at[d]))

    def wall_finish():
        wall_keep().wait()
        for d in range(T):
            landed(wall_ref.at[tp_source(d), sib], ws_rec.at[d])
            landed(wall_ref.at[tp_source(d), sib ^ 2], wr_rec.at[d])

    across_at = lambda b: T + b
    main = pl.ds(0, wide)

    def core_send(b):
        slot = b % 2
        if b >= 2:
            pl.semaphore_wait(credit, 1)
        for k in range(2):
            remote(
                gbuf.at[2 * T + 2 * slot + k, :, main], rcore.at[slot, k],
                core_sem.at[b, k], core_rec.at[b, k], fsdp=sib,
            ).start()

    def core_add(b):
        slot = b % 2
        landed(rcore.at[slot, 1], core_rec.at[b, 1])
        add_rows(gbuf.at[across_at(b), :, main], [rcore.at[slot, 1]])
        out = gbuf.at[across_at(b), :, main]
        go(
            remote(out, rx.at[b, :, main], x_sem.at[b], x_rec.at[b], fsdp=across),
            lambda: (rx.at[b, :, main], x_sem.at[b]),
        )
        landed(rcore.at[slot, 0], core_rec.at[b, 0])
        add_rows(gbuf.at[b, :, main], [rcore.at[slot, 0]])
        if b < T - 2:
            pl.semaphore_signal(credit, inc=1, device_id={"fsdp": sib}, device_id_type=MESH)

    held = [b // C for b in range(T)]

    def ctx_copy(b, d, to):
        return remote(gbuf.at[b], rc.at[held[b], d - 1], c_sem.at[b], c_rec.at[b, d], ctx=to)

    def cross_add(b):
        landed(rx.at[b, :, main], x_rec.at[b])
        add_rows(gbuf.at[b, :, main], [rx.at[b, :, main]])

    def ctx_send(b):
        owner = b % C
        for d in range(1, C):
            @pl.when(lax.rem(c + d, C) == owner)
            def _():
                ctx_copy(b, d, owner).start()

    def ctx_wait(b):
        @pl.when(c == b % C)
        def _():
            for d in range(1, C):
                ctx_copy(b, d, c).wait_recv()
            if C > 1:
                add_rows(gbuf.at[b], [rc.at[held[b], d - 1] for d in range(1, C)])

    def z_round(b, step):
        def hop(to, way):
            return remote(gbuf.at[b], rz.at[held[b], way], z_sem.at[b], z_rec.at[b, way], tp=to)

        def visit(way, before, here):
            @pl.when((c == b % C) & here)
            def _():
                if step:
                    hop(t, way).wait_recv()
                    add_rows(gbuf.at[b], [rz.at[held[b], way]])

                @pl.when(before)
                def _():
                    hop(t - 1 if way == 0 else t + 1, way).start()

        if T - 1 - step >= b and b < T - 1:
            visit(0, t > b, t == T - 1 - step)
        if step <= b and b > 0:
            visit(1, t < b, t == step)

    def feed_phase(att_s, outw_s, w_s, x_s, nm_s, nmt_s, gt_s, acc_s):
        steps = hidden // step_cols
        ring = w_s.shape[0]
        total_steps = 2 * T * steps

        def stream(n):
            at = pl.ds(pl.multiple_of(lax.rem(n, T * steps) * step_cols, step_cols), step_cols)
            slot = lax.rem(n, ring)
            return [
                pltpu.make_async_copy(ref.at[:, at], w_s.at[slot, k], w_sem.at[slot, k])
                for k, ref in enumerate((fc_ref, pj_ref))
            ]

        def take(n):
            for copy in stream(n):
                copy.wait()

            @pl.when(n + ring - 1 < total_steps)
            def _():
                for copy in stream(n + ring - 1):
                    copy.start()

            return lax.rem(n, ring)

        loads = [
            pltpu.make_async_copy(att_ref, att_s, in_sem.at[0]),
            pltpu.make_async_copy(outw_ref, outw_s, in_sem.at[1]),
            pltpu.make_async_copy(start_ref, start_s, in_sem.at[2]),
            pltpu.make_async_copy(grad_ref, grad_s, in_sem.at[3]),
        ]
        for copy in loads:
            copy.start()
        for n in range(ring - 1):
            for copy in stream(n):
                copy.start()

        barrier = pltpu.get_barrier_semaphore()
        peers = 0
        for d in range(1, F):
            pl.semaphore_signal(barrier, inc=1, device_id={"fsdp": f ^ d}, device_id_type=MESH)
            peers += 1
        for d in range(1, T):
            pl.semaphore_signal(barrier, inc=1, device_id={"tp": tp_peer(d)}, device_id_type=MESH)
            peers += 1
        for d in range(1, C):
            pl.semaphore_signal(barrier, inc=1, device_id={"ctx": lax.rem(c + d, C)}, device_id_type=MESH)
            peers += 1
        pl.semaphore_wait(barrier, peers)
        wall_start()

        for copy in loads:
            copy.wait()
        mid = start_s[...].reshape(tokens, width).astype(f32)
        for g in range(T):
            mid = mid + dot(att_s[g].reshape(tokens, hw), outw_s[column(g, hw), :])
        mid_s[...] = mid
        hat, _ = hat_rows(mid)
        nm = hat * params_ref[1:2] + params_ref[3:4]
        nm_s[...] = nm.astype(bf)
        nmt_s[...] = turn_back(nm)
        gt_s[...] = turn(grad_s[...])
        acc_s[...] = jnp.zeros_like(acc_s)

        def forward(j, _):
            slot = take(j)
            x = dot(nm_s[...], w_s[slot, 0])
            x_s[j] = x
            act, _ = gelu_parts(x)
            acc_s[...] += dot(act.astype(bf), w_s[slot, 1], ((1,), (1,)))
            return 0

        lax.fori_loop(0, T * steps, forward, 0)
        ob_s[...] = (mid_s[...] + acc_s[...]).astype(bf).reshape(S, own_rows, width)
        for d in range(1, T):
            wall_take(d)
        for s in range(S):
            ag_start(0, s)
        acc_s[...] = jnp.zeros_like(acc_s)

        for n in range(T):
            if n >= 2:
                for k in range(2):
                    sent(rcore.at[0, 0], core_sem.at[n - 2, k])
            slot = n % 2

            def backward(j, _):
                here = pl.ds(pl.multiple_of(j * step_cols, step_cols), step_cols)
                there = pl.ds(pl.multiple_of(hidden + j * step_cols, step_cols), step_cols)
                at_w = take(T * steps + n * steps + j)
                fc, proj = w_s[at_w, 0], w_s[at_w, 1]
                act, slope = gelu_parts(x_s[n * steps + j])
                act = act.astype(bf)
                d_exp = (slope * dot(grad_s[...], proj)).astype(bf)
                acc_s[...] += dot(d_exp, fc, ((1,), (1,)))
                d_fc = dot(nmt_s[...], d_exp).astype(bf)
                d_proj = dot(gt_s[...], act).astype(bf)
                for ff in range(F):
                    r = f ^ ff
                    odd, half = lax.rem(r, 2), r // 2
                    at = (1 - odd) * (half * T + n) + odd * (2 * T + 2 * slot + half)
                    gbuf[at, :, here] = d_fc[column(ff, shard)]
                    gbuf[at, :, there] = d_proj[column(ff, shard)]
                return 0

            lax.fori_loop(0, steps, backward, 0)
            core_send(n)
            if n:
                core_add(n - 1)

        mid = mid_s[...]
        hat, inv = hat_rows(mid)
        d_nm = acc_s[...]
        d_mid = grad_s[...].astype(f32) + norm_back(hat, inv, params_ref[1:2], d_nm)
        d_mid_b = d_mid.astype(bf)
        for g in range(T):
            da_s[g] = dot(d_mid_b, outw_s[column(g, hw), :], ((1,), (1,))).astype(bf).reshape(S, own_rows, hw)
        for s in range(S):
            for d in range(1, T):
                go(
                    remote(da_s.at[tp_peer(d), s], da_r.at[d - 1, s], da_sem.at[d, s], da_rec.at[d, s], tp=tp_peer(d)),
                    lambda d=d, s=s: (da_s.at[0, s], da_sem.at[d, s]),
                )
        sm_s[...] = jnp.zeros_like(sm_s)
        sm_s[1:2, :] = jnp.sum(d_nm * hat, axis=0, keepdims=True)
        sm_s[3:4, :] = jnp.sum(d_nm, axis=0, keepdims=True)
        d_mid_t = turn_back(d_mid)
        mid_s[...] = d_mid
        if g2.shape[3] > hw:
            g2[:, :, :, hw:] = jnp.zeros(g2.shape[:3] + (g2.shape[3] - hw,), bf)
        for g in range(T):
            d_out = dot(d_mid_t, att_s[g].reshape(tokens, hw)).astype(bf)
            for ff in range(F):
                g2[f ^ ff, g, :, :hw] = d_out[column(ff, shard)]
        core_add(T - 1)

    bf_mem = lambda *shape: pltpu.VMEM(shape, bf)
    f32_mem = lambda *shape: pltpu.VMEM(shape, f32)
    pl.run_scoped(
        feed_phase,
        bf_mem(T, S, own_rows, hw), bf_mem(T * hw, width), bf_mem(4, 2, width, step_cols),
        f32_mem(T * hidden // step_cols, tokens, step_cols),
        bf_mem(tokens, width), bf_mem(width, tokens), bf_mem(width, tokens), f32_mem(tokens, width),
    )

    for k in range(2):
        out = g2.at[1 + 2 * k]
        go(
            remote(out, r2c.at[k], c2_sem.at[k], c2_rec.at[k], fsdp=sib),
            lambda k=k: (r2c.at[k], c2_sem.at[k]),
        )

    def dp_copy(d, s):
        return remote(
            dp_s.at[far - d, s], rec_s.at[d - 1, s], dp_sem.at[d, s], dp_rec.at[d, s], ctx=lax.rem(c + C - d, C)
        )

    def attention_phase(q_s, kvo_s, prv_s, ot_s, k_h, kt_h, v_h, q_h, qt_h, g_h, gt_h, dqt_s, dk_s, dv_s, del_s):
        loads = [
            pltpu.make_async_copy(ref, mem, in_sem.at[k])
            for k, (ref, mem) in enumerate(((q_ref, q_s), (kv_ref, kvo_s), (out_t_ref, ot_s), (prev_ref, prv_s)))
        ]
        for copy in loads:
            copy.start()
        for copy in loads:
            copy.wait()
        for s in range(S):
            ag_step(0, s, 1)
        for d in range(T):
            wall_relay(d)
        for k in (1, 0):
            landed(r2c.at[k], c2_rec.at[k])
            for b in range(T):
                add_rows(g2.at[2 * k, b], [r2c.at[k, b]])
            if k:
                go(remote(g2.at[2], r2x, x2_sem, x2_rec, fsdp=across), lambda: (r2x, x2_sem))

        def keys(s):
            for h in range(heads):
                q = q_s[s, :, column(h)].astype(f32) * 0.125
                q_h[h] = q.astype(bf)
                qt_h[h] = turn_back(q)
                if far:
                    k = prv_s[s, :, column(h)]
                    k_h[h, : far * rows] = k
                    kt_h[h, :, : far * rows] = turn(k)
                    v_h[h, : far * rows] = prv_s[s, :, column(heads + h)]
                k = kvo_s[s, :, column(h)]
                k_h[h, far * rows :] = k
                kt_h[h, :, far * rows :] = turn(k)
                v_h[h, far * rows :] = kvo_s[s, :, column(heads + h)]

        def grads(s):
            for d in range(T):
                if d:
                    landed(da_r.at[d - 1, s], da_rec.at[d, s])
                source = da_s[t, s] if d == 0 else da_r[d - 1, s]
                for h in range(heads):
                    g_h[h, rows_of(tp_source(d)), :] = source[:, column(h)]
            for h in range(heads):
                g_t = g_h[h].astype(f32).T
                gt_h[h] = g_t.astype(bf)
                del_s[h : h + 1, :] = jnp.sum(g_t * ot_s[s, column(h), :], axis=0, keepdims=True)
            dqt_s[...] = jnp.zeros_like(dqt_s)

        def part(s, h, base, count, own):
            spot = pl.ds(pl.multiple_of(h * HEAD_DIM, HEAD_DIM), HEAD_DIM)
            dk_s[:count] = jnp.zeros((count, HEAD_DIM), f32)
            dv_s[:count] = jnp.zeros((count, HEAD_DIM), f32)
            for i in range(per_seq):
                span = column(i, block)
                reach = far * rows + i * block
                first = max(0, reach - (DOC_MOST - 1) - base) // block * block
                last = min(count, reach + block - base)
                if first >= last:
                    continue
                low = low_ref[s, :, span] - base
                place = first + lax.broadcasted_iota(jnp.int32, (last - first, 1), 0)
                allowed = place >= low
                if own:
                    allowed = allowed & (place <= i * block + lax.broadcasted_iota(jnp.int32, (1, block), 1))
                here = slice(base + first, base + last)
                scores = dot(k_h[h, here, :], qt_h[h, :, span])
                p = jnp.exp(jnp.where(allowed, scores - log_ref[s, pl.ds(h, 1), span], MASKED))
                ds = (p * (dot(v_h[h, here, :], gt_h[h, :, span]) - del_s[pl.ds(h, 1), span])).astype(bf)
                dv_s[first:last] += dot(p.astype(bf), g_h[h, span, :])
                dk_s[first:last] += dot(ds, q_h[h, span, :])
                dqt_s[spot, span] += dot(kt_h[h, :, here], ds)
            return spot, pl.ds(pl.multiple_of(hw + h * HEAD_DIM, HEAD_DIM), HEAD_DIM)

        def far_part(s):
            def one(h, _):
                k_at, v_at = part(s, h, 0, far * rows, False)
                for at, source in ((k_at, dk_s), (v_at, dv_s)):
                    turned = source[: far * rows].T.astype(bf)
                    for j in range(far):
                        for g in range(T):
                            dp_s[j, s, g, at, :] = turned[:, column(j * T + g, own_rows)]
                return 0

            lax.fori_loop(0, heads, one, 0)

        def own_part(s):
            def one(h, _):
                k_at, v_at = part(s, h, far * rows, rows, True)
                for at, source in ((k_at, dk_s), (v_at, dv_s)):
                    turned = source[:rows].T.astype(bf)
                    for g in range(T):
                        kv_s[g, s, at, :] = turned[:, column(g, own_rows)]
                return 0

            lax.fori_loop(0, heads, one, 0)

        for s in range(S):
            keys(s)
            grads(s)
            if far:
                @pl.when(c > 0)
                def _():
                    far_part(s)

                for d in range(1, far + 1):
                    @pl.when(c >= d)
                    def _():
                        dp_copy(d, s).start()
            own_part(s)
            for g in range(T):
                dq_s[g, s] = (0.125 * dqt_s[:, column(g, own_rows)]).astype(bf)
            for d in range(1, T):
                go(
                    remote(dq_s.at[tp_peer(d), s], rq.at[d - 1, s], aq_sem.at[d, s], aq_rec.at[d, s], tp=tp_peer(d)),
                    lambda d=d, s=s: (dq_s.at[0, s], aq_sem.at[d, s]),
                )
            if s + 2 < T:
                for other in range(S):
                    ag_step(0, other, s + 2)
            for b in range(s * T // (2 * S), (s + 1) * T // (2 * S)):
                cross_add(b)

    pl.run_scoped(
        attention_phase,
        bf_mem(S, rows, hw), bf_mem(S, rows, 2 * hw), bf_mem(S, max(far, 1) * rows, 2 * hw), f32_mem(S, hw, rows),
        bf_mem(heads, (far + 1) * rows, HEAD_DIM), bf_mem(heads, HEAD_DIM, (far + 1) * rows),
        bf_mem(heads, (far + 1) * rows, HEAD_DIM),
        bf_mem(heads, rows, HEAD_DIM), bf_mem(heads, HEAD_DIM, rows),
        bf_mem(heads, rows, HEAD_DIM), bf_mem(heads, HEAD_DIM, rows),
        f32_mem(hw, rows), f32_mem(max(far, 1) * rows, HEAD_DIM), f32_mem(max(far, 1) * rows, HEAD_DIM), f32_mem(8, rows),
    )

    def last_phase(normed_s, wall_s, gq_acc):
        normed_in = pltpu.make_async_copy(normed_ref, normed_s, in_sem.at[0])
        normed_in.start()
        wall_finish()
        walls = []
        for tt in range(T):
            for ff in range(F):
                copy = pltpu.make_async_copy(
                    wall_ref.at[tt, ff], wall_s.at[tt, :, pl.ds(ff * shard, shard), :], wall_sem.at[tt, ff]
                )
                copy.start()
                walls.append(copy)

        for s in range(S):
            for d in range(1, far + 1):
                @pl.when(c + d < C)
                def _():
                    dp_copy(d, s).wait_recv()
                    for g in range(T):
                        kv_s[g, s] = (kv_s[g, s].astype(f32) + rec_s[d - 1, s, g].astype(f32)).astype(bf)
            for d in range(1, T):
                go(
                    remote(kv_s.at[tp_peer(d), s], rkv.at[d - 1, s], ak_sem.at[d, s], ak_rec.at[d, s], tp=tp_peer(d)),
                    lambda d=d, s=s: (kv_s.at[0, s], ak_sem.at[d, s]),
                )

        landed(r2x, x2_rec)
        side = pl.ds(wide, g2.shape[3])
        for b in range(T):
            gbuf[b, :, side] = (g2[0, b].astype(f32) + r2x[b].astype(f32)).astype(bf)
        for b in range(T):
            if b >= T // 2:
                cross_add(b)
            ctx_send(b)

        normed_in.wait()
        gq_acc[...] = jnp.zeros_like(gq_acc)
        for s in range(S):
            for d in range(T):
                near = normed_s[s, rows_of(tp_peer(d)), :]
                gq_acc[:hw, :] += dot(dq_s[tp_peer(d), s], near)
                gq_acc[hw:, :] += dot(kv_s[tp_peer(d), s], near)
        for k in range(F):
            gq_s[k] = gq_acc[:, column(k, shard)].astype(bf)
        for d in range(1, F):
            go(
                remote(gq_s.at[f ^ d], rgq.at[d - 1], gq_sem.at[d], gq_rec.at[d], fsdp=f ^ d),
                lambda d=d: (gq_s.at[0], gq_sem.at[d]),
            )

        for copy in walls:
            copy.wait()
        gain = params_ref[0:1]

        def norm_stage(s):
            total = jnp.zeros((width, own_rows), f32)
            for d in range(T):
                if d:
                    landed(rq.at[d - 1, s], aq_rec.at[d, s])
                    landed(rkv.at[d - 1, s], ak_rec.at[d, s])
                for j in range(3):
                    if d:
                        piece = rq[d - 1, s] if j == 0 else rkv[d - 1, s, column(j - 1, hw), :]
                    else:
                        piece = dq_s[t, s] if j == 0 else kv_s[t, s, column(j - 1, hw), :]
                    total = total + dot(wall_s[tp_source(d), j], piece)
            d_normed = total.T
            hat, inv = hat_rows(start_s[s].astype(f32))
            value = mid_s[column(s, own_rows), :] + norm_back(hat, inv, gain, d_normed)
            ob_s[s] = value.astype(bf)
            sm_s[0:1, :] += jnp.sum(d_normed * hat, axis=0, keepdims=True)
            sm_s[2:3, :] += jnp.sum(d_normed, axis=0, keepdims=True)

        for s in range(S):
            ag_drain(0, s, 0)
            norm_stage(s)
            ag_start(1, s)

        thoughts = jnp.zeros((pick_ref.shape[1], width), f32)
        for s in range(S):
            thoughts = thoughts + dot(pick_ref[s], ob_s[s])
        sm_s[8:, :] = thoughts
        for d in range(1, T):
            go(
                remote(sm_s, rst.at[d], st_sem.at[d], st_rec.at[d], tp=tp_peer(d)),
                lambda d=d: (sm_s, st_sem.at[d]),
            )

        gq_sum = gq_s[f].astype(f32)
        for d in range(1, F):
            landed(rgq.at[d - 1], gq_rec.at[d])
            gq_sum = gq_sum + rgq[d - 1].astype(f32)
        rgc[c] = gq_sum.astype(bf)
        for d in range(1, C):
            go(
                remote(rgc.at[c], rgc.at[c], gc_sem.at[d], gc_rec.at[d], ctx=lax.rem(c + d, C)),
                lambda d=d: (rgc.at[0], gc_sem.at[d]),
            )

        for step in range(T):
            if step:
                for s in range(S):
                    ag_step(1, s, step)
            for b in range(T):
                if step == 0:
                    ctx_wait(b)
                z_round(b, step)

        for d in range(1, T):
            landed(rst.at[d], st_rec.at[d])
        rst[0] = sm_s[...]
        total = jnp.zeros(sm_s.shape, f32)
        for k in range(T):
            total = total + rst[lax.rem(t + T - k, T)]
        rsc[c] = total
        for d in range(1, C):
            go(
                remote(rsc.at[c], rsc.at[c], sc_sem.at[d], sc_rec.at[d], ctx=lax.rem(c + d, C)),
                lambda d=d: (rsc.at[0], sc_sem.at[d]),
            )
        for d in range(1, C):
            landed(rsc.at[0], sc_rec.at[d])
        total = jnp.zeros(sm_s.shape, f32)
        for k in range(C):
            total = total + rsc[k]
        rsf[f] = total
        for d in range(1, F):
            go(
                remote(rsf.at[f], rsf.at[f], sf_sem.at[d], sf_rec.at[d], fsdp=f ^ d),
                lambda d=d: (rsf.at[0], sf_sem.at[d]),
            )
        for d in range(1, F):
            landed(rsf.at[0], sf_rec.at[d])
        norms = jnp.zeros((8, sm_s.shape[1]), f32)
        for k in range(F):
            norms = norms + rsf[k, 0:8, :]
        small_ref[0:8, :] = norms
        small_ref[8:, :] = total[8:]

        for d in range(1, C):
            landed(rgc.at[0], gc_rec.at[d])
        total = jnp.zeros(gq_ref.shape, f32)
        for k in range(C):
            total = total + rgc[k].astype(f32)
        gq_ref[...] = total

    pl.run_scoped(
        last_phase, bf_mem(S, rows, width), bf_mem(T, 3, width, hw), f32_mem(3 * hw, width)
    )

    for b in range(T):
        owner = b % C
        final = lambda d: remote(gbuf.at[b], rx.at[b], b_sem.at[d], b_rec, ctx=lax.rem(owner + d, C))

        @pl.when((t == b) & (c == owner))
        def _():
            for d in range(1, C):
                final(d).start()
            gw_ref[...] = gbuf[b]
            for d in range(1, C):
                final(d).wait_send()

        if C > 1:
            @pl.when((t == b) & (c != owner))
            def _():
                final(1).wait_recv()
                gw_ref[...] = rx[b]

    for like in pending:
        sent(*like())
    for n in range(max(T - 2, 0), T):
        for k in range(2):
            sent(rcore.at[0, 0], core_sem.at[n, k])
    for b in range(T):
        owner = b % C
        if C > 1:
            @pl.when(c != owner)
            def _():
                ctx_copy(b, 1, owner).wait_send()

        @pl.when((c == owner) & (t != b))
        def _():
            remote(gbuf.at[b], rz.at[held[b], 0], z_sem.at[b], z_rec.at[b, 0], tp=t).wait_send()
    for s in range(S):
        for d in range(1, far + 1):
            @pl.when(c >= d)
            def _():
                dp_copy(d, s).wait_send()
        ag_drain(0, s, 1)
        ag_drain(1, s, 0)


def back(att, start, grad, out_w, fc, proj_t, params, q, kv, prev, low, out_t, logs, normed, wq, pick, block, far, counts):
    F, C, T = counts
    S, rows, hw = q.shape
    width = normed.shape[2]
    own_rows = rows // T
    tokens = S * own_rows
    shard = width // F
    hidden = fc.shape[1] // T
    cols = padded(hw)
    wide = 2 * hidden + cols
    bf, f32 = jnp.bfloat16, jnp.float32
    extra = 8 + pick.shape[1]
    mine = -(-T // C)
    dists = max(far, 1)
    vmem = pl.BlockSpec(memory_space=pltpu.VMEM)
    anywhere = pl.BlockSpec(memory_space=pl.ANY)
    dma = lambda *shape: pltpu.SemaphoreType.DMA(shape)
    one = pltpu.SemaphoreType.DMA
    shape = jax.ShapeDtypeStruct
    b16 = lambda *size: pltpu.VMEM(size, bf)
    b32 = lambda *size: pltpu.VMEM(size, f32)
    return pl.pallas_call(
        functools.partial(back_kernel, counts, block, far, 256),
        in_specs=[anywhere] * 6 + [vmem] + [anywhere] * 3 + [vmem, anywhere, vmem, anywhere, anywhere, vmem],
        out_specs=[anywhere, anywhere, anywhere, vmem, vmem, vmem],
        out_shape=[
            shape((S, rows, width), bf),
            shape((S, rows, width), bf),
            shape((T, F) + wq.shape, bf),
            shape((shard, wide), bf),
            shape((3 * hw, shard), f32),
            shape((extra, width), f32),
        ],
        scratch_shapes=[
            b16(S, own_rows, width), b32(tokens, width), b16(tokens, width), b16(S, own_rows, width),
            b16(2 * T + 4, shard, wide), b16(2, 2, shard, 2 * hidden), b16(T, shard, wide),
            b16(mine, max(C - 1, 1), shard, wide), b16(mine, 2, shard, wide),
            b16(4, T, shard, cols), b16(2, T, shard, cols), b16(T, shard, cols),
            b16(T, S, own_rows, hw), b16(T - 1, S, own_rows, hw),
            b16(dists, S, T, 2 * hw, own_rows), b16(dists, S, T, 2 * hw, own_rows),
            b16(T, S, 2 * hw, own_rows), b16(T, S, hw, own_rows),
            b16(T - 1, S, hw, own_rows), b16(T - 1, S, 2 * hw, own_rows),
            b16(F, 3 * hw, shard), b16(F - 1, 3 * hw, shard), b16(C, 3 * hw, shard),
            b32(extra, width), b32(T, extra, width), b32(C, extra, width), b32(F, extra, width),
            dma(4), dma(4, 2), dma(T, 2), dma(T, 2), dma(T), dma(T), dma(2), dma(2), one, one,
            dma(T), dma(T, C), dma(T), dma(T, 2), dma(C), one, dma(T, S), dma(T, S), dma(far + 1, S), dma(far + 1, S),
            dma(T, S), dma(T, S), dma(T, S), dma(T, S), dma(2, S, T, 2), dma(2, S, T, 2), dma(F), dma(F), dma(C), dma(C),
            dma(T), dma(T), dma(C), dma(C), dma(F), dma(F), dma(2, S), dma(T, F),
            dma(T), dma(T), dma(T), dma(T), dma(T), dma(T), dma(T), dma(T), one, pltpu.SemaphoreType.REGULAR,
        ],
        compiler_params=pltpu.CompilerParams(
            vmem_limit_bytes=VMEM_LIMIT, collective_id=2, has_side_effects=True
        ),
        cost_estimate=pl.CostEstimate(flops=36 * 10**9, bytes_accessed=100 << 20, transcendentals=16 << 20),
    )(att, start, grad, out_w, fc, proj_t, params, q, kv, prev, low, out_t, logs, normed, wq, pick)


def local(
    inputs, thoughts, positions, lengths, w_qkv, w_out, w_fc, w_proj, norm_gains, norm_biases, out_grad,
):
    rows, seqs, width = inputs.shape
    ctx_count = lax.axis_size("ctx")
    tp_count = lax.axis_size("tp")
    fsdp_count = lax.axis_size("fsdp")
    ctx, tp, fsdp = lax.axis_index("ctx"), lax.axis_index("tp"), lax.axis_index("fsdp")
    first_row = ctx * rows
    own_rows = rows // tp_count
    own_tokens = own_rows * seqs
    far = min(ctx_count - 1, -(-(DOC_MOST - 1) // rows))
    block = min(256, rows)
    bf, f32 = jnp.bfloat16, jnp.float32

    counts = (fsdp_count, ctx_count, tp_count)
    local_width = w_qkv.shape[2]
    params = jnp.pad(jnp.concatenate([norm_gains, norm_biases]).astype(f32), ((0, 4), (0, 0)))
    places = first_row + jnp.arange(rows, dtype=jnp.int32)
    is_thought = places[None, None, :] == positions[:, :, None]
    keep = jnp.logical_not(jnp.any(is_thought, axis=0))
    start = jnp.transpose(inputs, (1, 0, 2))
    for t in range(thoughts.shape[0]):
        start = jnp.where(is_thought[t][:, :, None], thoughts[t][:, None, :], start)
    ends = jnp.cumsum(lengths, axis=1, dtype=jnp.int32)
    low = jnp.max(jnp.where(ends[:, :, None] <= places[None, None, :], ends[:, :, None], 0), axis=1)
    low = low - (first_row - far * rows)

    low3 = low[:, None, :]
    attended, q, kv, prev, out_t, logs, normed, out_full, fc_full, proj_full_t, params = front(
        start, low3, w_qkv, w_out, w_fc, w_proj.T, params, block, far, counts
    )
    start_own = lax.dynamic_slice_in_dim(start, tp * own_rows, own_rows, 1)
    grad_own = jnp.transpose(
        lax.dynamic_slice_in_dim(out_grad, tp * own_rows, own_rows, 0), (1, 0, 2)
    ).reshape(own_tokens, width)

    own_places = lax.dynamic_slice_in_dim(places, tp * own_rows, own_rows, 0)
    count = thoughts.shape[0]
    pick = (own_places[None, None, :] == positions[:, :, None]).astype(bf)
    picks = []
    for s in range(seqs):
        picks.append(jnp.concatenate(
            [jnp.where(k == s, pick[:, s], jnp.zeros_like(pick[:, s])) for k in range(seqs)], axis=0
        ))
    pick = jnp.stack(picks)
    pick = jnp.pad(pick, ((0, 0), (0, -(-pick.shape[1] // 16) * 16 - pick.shape[1]), (0, 0)))
    output, d_start, _, gw, gq, small = back(
        attended, start_own, grad_own, out_full, fc_full, proj_full_t, params, q, kv, prev, low3, out_t, logs, normed,
        w_qkv, pick, block, far, counts,
    )
    output = jnp.transpose(output, (1, 0, 2))
    d_inputs = jnp.transpose(jnp.where(keep[:, :, None], d_start.astype(f32), 0.0), (1, 0, 2))
    d_thoughts = jnp.transpose(small[8 : 8 + count * seqs].reshape(seqs, count, width), (1, 0, 2))
    hidden = w_fc.shape[1]
    gw = gw.astype(f32)
    norms = lax.dynamic_slice_in_dim(small[:4], fsdp * w_fc.shape[0], w_fc.shape[0], 1)
    return (
        output,
        d_inputs,
        d_thoughts,
        jnp.transpose(gq.reshape(3, local_width, -1), (0, 2, 1)),
        gw[:, 2 * hidden : 2 * hidden + local_width].T,
        gw[:, :hidden],
        gw[:, hidden : 2 * hidden].T,
        norms[:2],
        norms[2],
        norms[3],
    )


def solution(mesh):
    in_specs = (
        P("ctx", "fsdp", None),
        P(None, "fsdp", None),
        P(None, "fsdp"),
        P("fsdp", None),
        P(None, "fsdp", "tp"),
        P("tp", "fsdp"),
        P("fsdp", "tp"),
        P("tp", "fsdp"),
        P(None, "fsdp"),
        P(None, "fsdp"),
        P("ctx", "fsdp", None),
    )
    out_specs = (
        P("ctx", "fsdp", None),
        P("ctx", "fsdp", None),
        P(None, "fsdp", None),
        P(None, "fsdp", "tp"),
        P("tp", "fsdp"),
        P("fsdp", "tp"),
        P("tp", "fsdp"),
        P(None, "fsdp"),
        P("fsdp"),
        P("fsdp"),
    )
    return jax.shard_map(local, mesh=mesh, in_specs=in_specs, out_specs=out_specs, check_vma=False)
```

```python
import functools

import jax
import jax.numpy as jnp
from jax import lax
from jax.experimental import pallas as pl
from jax.experimental.pallas import tpu as pltpu
from jax.sharding import PartitionSpec as P

HEAD_DIM = 64
DOC_MOST = 1024
EPSILON = 1e-05
MASKED = -1e30


def dot(a, b, dims=((1,), (0,))):
    return lax.dot_general(a, b, (dims, ((), ())), preferred_element_type=jnp.float32)


def hat_rows(values):
    centre = jnp.mean(values, axis=-1, keepdims=True)
    shifted = values - centre
    spread = jnp.mean(shifted * shifted, axis=-1, keepdims=True)
    inv = lax.rsqrt(spread + EPSILON)
    return shifted * inv, inv


def norm_back(hat, inv, gain, grad):
    eg = grad * gain
    return inv * (
        eg
        - jnp.mean(eg, axis=-1, keepdims=True)
        - hat * jnp.mean(eg * hat, axis=-1, keepdims=True)
    )


MESH = pl.DeviceIdType.MESH
VMEM_LIMIT = 62 << 20


def column(index, size=HEAD_DIM):
    return slice(index * size, (index + 1) * size)


def turn(value):
    return value.astype(jnp.float32).T.astype(jnp.bfloat16)


def turn_back(value):
    return value.T.astype(jnp.bfloat16)


def front_kernel(
    sizes, block,
    start_ref, low_ref, wq_ref, wo_ref, wf_ref, wp_ref, par_ref,
    att_ref, q_ref, kv_ref, prev_ref, out_t_ref, log_ref, normed_ref, wl_ref, ow_ref, fc_ref, pj_ref, params_ref,
    start_s, normed_s, wl_s, wo_s, par_s, q_s, kv_s, prev_s, qt_s, ko_s, vto_s, kp_s, vtp_s, m_s, l_s, att_s,
    in_sem, out_sem, w_loc, z_sem, z_rec, s_sem, s_rec, x_sem, x_rec, r_sem, r_rec,
    kv_sem, kv_rec, at_sem, at_rec, at_loc,
):
    F, C, T = sizes
    f, c, t = lax.axis_index("fsdp"), lax.axis_index("ctx"), lax.axis_index("tp")
    S, rows, width = start_ref.shape
    hw = q_ref.shape[2]
    heads = hw // HEAD_DIM
    own_rows = rows // T
    far = prev_ref.shape[1] // rows if C > 1 else 0
    shard = wq_ref.shape[1]
    hidden = wf_ref.shape[1]
    bf, f32 = jnp.bfloat16, jnp.float32
    sib, across = f ^ 1, f ^ 2

    def remote(src, dst, send, recv, **where):
        return pltpu.make_async_remote_copy(
            src_ref=src, dst_ref=dst, send_sem=send, recv_sem=recv, device_id=where, device_id_type=MESH
        )

    start_in = pltpu.make_async_copy(start_ref, start_s, in_sem.at[0])
    start_in.start()

    barrier = pltpu.get_barrier_semaphore()
    peers = 0
    for d in range(1, F):
        pl.semaphore_signal(barrier, inc=1, device_id={"fsdp": f ^ d}, device_id_type=MESH)
        peers += 1
    for d in range(1, T):
        pl.semaphore_signal(barrier, inc=1, device_id={"tp": lax.rem(t + d, T)}, device_id_type=MESH)
        peers += 1
    for d in range(1, C):
        pl.semaphore_signal(barrier, inc=1, device_id={"ctx": lax.rem(c + d, C)}, device_id_type=MESH)
        peers += 1
    pl.semaphore_wait(barrier, peers)

    pending = []

    def go(copy):
        copy.start()
        pending.append(copy)
        return copy

    def at_shard(ff):
        return pl.ds(pl.multiple_of(ff * shard, shard), shard)

    def at_hidden(tt):
        return pl.ds(pl.multiple_of(tt * hidden, hidden), hidden)

    def block_at(a, tt, ff):
        if a == 0:
            return par_s.at[ff]
        if a == 1:
            return wl_s.at[:, at_shard(ff), :]
        if a == 2:
            return wo_s.at[tt, ff]
        return (fc_ref if a == 3 else pj_ref).at[at_shard(ff), at_hidden(tt)]

    sources = (par_ref, wq_ref, wo_ref, wf_ref, wp_ref)
    slot = lambda d: lax.rem(t + T - d, T)

    def spread_chip(a, d):
        src = sources[a] if d == 0 else block_at(a, slot(d), f)
        dst = block_at(a, slot(d), f)
        go(remote(src, dst, x_sem.at[a, d], x_rec.at[a, d], fsdp=across))
        go(remote(src, dst, s_sem.at[a, d], s_rec.at[a, d], fsdp=sib))

    def take_z(a, d):
        here = block_at(a, slot(d), f)
        remote(here, here, z_sem.at[a, d], z_rec.at[a, d], tp=t).wait_recv()
        spread_chip(a, d)

    def relay(a, d):
        here = block_at(a, slot(d), across)
        remote(here, here, x_sem.at[a, d], x_rec.at[a, d], fsdp=f).wait_recv()
        go(remote(here, here, r_sem.at[a, d], r_rec.at[a, d], fsdp=sib))

    def take_chip(a, d):
        for ff, rec in ((sib, s_rec), (sib ^ 2, r_rec)):
            here = block_at(a, slot(d), ff)
            remote(here, here, s_sem.at[a, d], rec.at[a, d], fsdp=f).wait_recv()

    keeps = []
    for a in range(5):
        keep = pltpu.make_async_copy(sources[a], block_at(a, t, f), w_loc.at[a])
        keep.start()
        keeps.append(keep)
    spread_chip(0, 0)
    spread_chip(1, 0)
    for a in (2, 3, 4):
        for d in range(1, T):
            go(remote(sources[a], block_at(a, t, f), z_sem.at[a, d], z_rec.at[a, d], tp=lax.rem(t + d, T)))
        spread_chip(a, 0)

    relay(0, 0)
    take_chip(0, 0)
    keeps[0].wait()
    params = jnp.concatenate([par_s[ff] for ff in range(F)], axis=1)
    params_ref[...] = params
    start_in.wait()
    per_seq = rows // block

    def norm_one(index, _):
        s = index // per_seq
        here = pl.ds(pl.multiple_of(lax.rem(index, per_seq) * block, block), block)
        hat, _ = hat_rows(start_s[s, here, :].astype(f32))
        normed_s[s, here, :] = (hat * params_ref[0:1, :] + params_ref[2:3, :]).astype(bf)
        return 0

    lax.fori_loop(0, S * per_seq, norm_one, 0)
    normed_out = pltpu.make_async_copy(normed_s, normed_ref, out_sem.at[0])
    normed_out.start()

    relay(1, 0)
    take_chip(1, 0)
    keeps[1].wait()

    def kv_one(s, _):
        def one(index, _):
            here = pl.ds(pl.multiple_of(index * block, block), block)
            rows_in = normed_s[s, here, :]
            k = dot(rows_in, wl_s[1]).astype(bf)
            v = dot(rows_in, wl_s[2]).astype(bf)
            kv_s[s, here, :] = jnp.concatenate([k, v], axis=1)
            v_t = turn(v)
            for h in range(heads):
                ko_s[s, h, here, :] = k[:, column(h)]
                vto_s[s, h, :, here] = v_t[column(h)]
            return 0

        lax.fori_loop(0, per_seq, one, 0)
        return 0

    def kv_copy(s, d):
        return remote(
            kv_s.at[s], prev_s.at[s, pl.ds((far - d) * rows, rows), :],
            kv_sem.at[d, s], kv_rec.at[d, s], ctx=lax.rem(c + d, C),
        )

    for s in range(S):
        kv_one(s, 0)
        for d in range(1, far + 1):
            @pl.when(c + d < C)
            def _():
                kv_copy(s, d).start()

    def q_one(index, _):
        s = index // per_seq
        here = pl.ds(pl.multiple_of(lax.rem(index, per_seq) * block, block), block)
        q = dot(normed_s[s, here, :], wl_s[0]).astype(bf)
        q_s[s, here, :] = q
        q_t = turn(q.astype(f32) * 0.125)
        for h in range(heads):
            qt_s[s, h, :, here] = q_t[column(h)]
        return 0

    lax.fori_loop(0, S * per_seq, q_one, 0)
    outs = [
        pltpu.make_async_copy(q_s, q_ref, out_sem.at[1]),
        pltpu.make_async_copy(kv_s, kv_ref, out_sem.at[2]),
        pltpu.make_async_copy(wl_s, wl_ref, out_sem.at[4]),
    ]
    for copy in outs:
        copy.start()

    def own_part(s):
        for i in range(per_seq):
            span = column(i, block)
            low = low_ref[s, :, span] - far * rows
            top = i * block + lax.broadcasted_iota(jnp.int32, (1, block), 1)
            first = max(0, i * block - (DOC_MOST - 1)) // block * block
            many = (i + 1) * block - first
            place = first + lax.broadcasted_iota(jnp.int32, (many, 1), 0)
            allowed = (place >= low) & (place <= top)
            for h in range(heads):
                scores = dot(ko_s[s, h, first : first + many, :], qt_s[s, h, :, span])
                scores = jnp.where(allowed, scores, MASKED)
                m = jnp.max(scores, axis=0, keepdims=True)
                p = jnp.exp(scores - m)
                m_s[s, h : h + 1, span] = m
                l_s[s, h : h + 1, span] = jnp.sum(p, axis=0, keepdims=True)
                out_t_ref[s, column(h), span] = dot(vto_s[s, h, :, first : first + many], p.astype(bf))

    def far_part(s):
        for h in range(heads):
            kp_s[h] = prev_s[s, :, column(h)]
            vtp_s[h] = turn(prev_s[s, :, column(heads + h)])
        for i in range(per_seq):
            span = column(i, block)
            low = low_ref[s, :, span]
            first = max(0, far * rows + i * block - (DOC_MOST - 1)) // block * block
            if first >= far * rows:
                continue
            many = far * rows - first
            place = first + lax.broadcasted_iota(jnp.int32, (many, 1), 0)
            allowed = place >= low
            for h in range(heads):
                scores = dot(kp_s[h, first : first + many, :], qt_s[s, h, :, span])
                scores = jnp.where(allowed, scores, MASKED)
                old = m_s[s, h : h + 1, span]
                m = jnp.maximum(old, jnp.max(scores, axis=0, keepdims=True))
                p = jnp.exp(scores - m)
                alpha = jnp.exp(old - m)
                m_s[s, h : h + 1, span] = m
                l_s[s, h : h + 1, span] = alpha * l_s[s, h : h + 1, span] + jnp.sum(p, axis=0, keepdims=True)
                out_t_ref[s, column(h), span] = alpha * out_t_ref[s, column(h), span] + dot(
                    vtp_s[h, :, first : first + many], p.astype(bf)
                )

    def finish_part(s):
        for h in range(heads):
            out_t_ref[s, column(h), :] = out_t_ref[s, column(h), :] / l_s[s, h : h + 1, :]
            log_ref[s, h : h + 1, :] = m_s[s, h : h + 1, :] + jnp.log(l_s[s, h : h + 1, :])
        for tt in range(T):
            att_s[tt, s] = out_t_ref[s, :, column(tt, own_rows)].astype(bf)

    for d in range(1, T):
        take_z(2, d)

    def own_loop(s, _):
        own_part(s)
        return 0

    lax.fori_loop(0, S, own_loop, 0)
    for d in range(T):
        relay(2, d)
    take_z(3, 1)

    def wait_far(s):
        for d in range(1, far + 1):
            @pl.when(c >= d)
            def _():
                kv_copy(s, d).wait_recv()

            @pl.when(c < d)
            def _():
                prev_s[s, (far - d) * rows : (far - d + 1) * rows, :] = jnp.zeros((rows, 2 * hw), bf)

    at = [[None] * S for _ in range(T)]
    for s in range(S):
        if far:
            wait_far(s)

            @pl.when(c > 0)
            def _():
                far_part(s)
        finish_part(s)
        for d in range(1, T):
            peer = lax.rem(t + d, T)
            at[d][s] = go(
                remote(att_s.at[peer, s], att_ref.at[t, s], at_sem.at[d, s], at_rec.at[d, s], tp=peer)
            )
        own_at = pltpu.make_async_copy(att_s.at[t, s], att_ref.at[t, s], at_loc.at[s])
        own_at.start()
        at[0][s] = own_at
        if s == 0:
            take_z(3, 2)
            take_z(3, 3)
            for d in range(T):
                relay(3, d)
    prev_out = pltpu.make_async_copy(prev_s, prev_ref, out_sem.at[3])
    if far:
        prev_out.start()
    for d in range(1, T):
        take_z(4, d)
    for d in range(T):
        take_chip(2, d)
    keeps[2].wait()
    for tt in range(T):
        for ff in range(F):
            ow_ref[column(tt, hw), column(ff, shard)] = wo_s[tt, ff]
    for d in range(T):
        relay(4, d)
    for a in (3, 4):
        for d in range(T):
            take_chip(a, d)
        keeps[a].wait()
    for s in range(S):
        at[0][s].wait()
        for d in range(1, T):
            at[d][s].wait_recv()
    normed_out.wait()
    for copy in outs:
        copy.wait()
    if far:
        prev_out.wait()
    for copy in pending:
        copy.wait_send()
    for s in range(S):
        for d in range(1, far + 1):
            @pl.when(c + d < C)
            def _():
                kv_copy(s, d).wait_send()


def front(start, low, wq, wo, wf, wp, params, block, far, counts):
    F, C, T = counts
    S, rows, width = start.shape
    hw = wq.shape[2]
    shard = wq.shape[1]
    heads = hw // HEAD_DIM
    hidden = wf.shape[1]
    bf, f32 = jnp.bfloat16, jnp.float32
    vmem = pl.BlockSpec(memory_space=pltpu.VMEM)
    anywhere = pl.BlockSpec(memory_space=pl.ANY)
    dma = lambda *shape: pltpu.SemaphoreType.DMA(shape)
    past = max(far, 1) * rows
    shape = jax.ShapeDtypeStruct
    return pl.pallas_call(
        functools.partial(front_kernel, counts, block),
        in_specs=[anywhere, vmem, anywhere, anywhere, anywhere, anywhere, anywhere],
        out_specs=[
            anywhere, anywhere, anywhere, anywhere, vmem, vmem, anywhere, anywhere, vmem, anywhere, anywhere, vmem
        ],
        out_shape=[
            shape((T, S, hw, rows // T), bf),
            shape((S, rows, hw), bf),
            shape((S, rows, 2 * hw), bf),
            shape((S, past, 2 * hw), bf),
            shape((S, hw, rows), f32),
            shape((S, 8, rows), f32),
            shape((S, rows, width), bf),
            shape((3, F * shard, hw), bf),
            shape((T * hw, F * shard), bf),
            shape((F * shard, T * hidden), bf),
            shape((F * shard, T * hidden), bf),
            shape((8, F * shard), f32),
        ],
        scratch_shapes=[
            pltpu.VMEM((S, rows, width), bf),
            pltpu.VMEM((S, rows, width), bf),
            pltpu.VMEM((3, F * shard, hw), bf),
            pltpu.VMEM((T, F, hw, shard), bf),
            pltpu.VMEM((F, 8, shard), f32),
            pltpu.VMEM((S, rows, hw), bf),
            pltpu.VMEM((S, rows, 2 * hw), bf),
            pltpu.VMEM((S, past, 2 * hw), bf),
            pltpu.VMEM((S, heads, HEAD_DIM, rows), bf),
            pltpu.VMEM((S, heads, rows, HEAD_DIM), bf),
            pltpu.VMEM((S, heads, HEAD_DIM, rows), bf),
            pltpu.VMEM((heads, past, HEAD_DIM), bf),
            pltpu.VMEM((heads, HEAD_DIM, past), bf),
            pltpu.VMEM((S, 8, rows), f32),
            pltpu.VMEM((S, 8, rows), f32),
            pltpu.VMEM((T, S, hw, rows // T), bf),
            dma(1), dma(5), dma(5),
            dma(5, T), dma(5, T), dma(5, T), dma(5, T), dma(5, T), dma(5, T), dma(5, T), dma(5, T),
            dma(far + 1, S), dma(far + 1, S), dma(T, S), dma(T, S), dma(S),
        ],
        compiler_params=pltpu.CompilerParams(
            vmem_limit_bytes=VMEM_LIMIT, collective_id=1, has_side_effects=True
        ),
        cost_estimate=pl.CostEstimate(flops=8 * 10**9, bytes_accessed=64 << 20, transcendentals=8 << 20),
    )(start, low, wq, wo, wf, wp, params)


def padded(size):
    return -(-size // 128) * 128


def add_rows(target, sources, rows_at_once=16):
    def one(i, _):
        here = pl.ds(pl.multiple_of(i * rows_at_once, rows_at_once), rows_at_once)
        total = target[here, :].astype(jnp.float32)
        for source in sources:
            total = total + source[here, :].astype(jnp.float32)
        target[here, :] = total.astype(target.dtype)
        return 0

    lax.fori_loop(0, target.shape[0] // rows_at_once, one, 0)


def gelu_parts(x):
    square = x * x
    th = jnp.tanh(0.7978845608028654 * (x + 0.044715 * (square * x)))
    half = 0.5 * (1.0 + th)
    slope = half + (0.5 * x) * (1.0 - th * th) * (0.7978845608028654 * (1.0 + (3 * 0.044715) * square))
    return x * half, slope


def back_kernel(
    sizes, block, far, step_cols,
    att_ref, start_ref, grad_ref, outw_ref, fc_ref, pj_ref, params_ref,
    q_ref, kv_ref, prev_ref, low_ref, out_t_ref, log_ref, normed_ref, wl_ref, pick_ref,
    output_ref, dstart_ref, gw_ref, gq_ref, small_ref,
    start_s, mid_s, grad_s, ob_s, gbuf, rcore, rx, rc, rz, g2, r2c, r2x,
    da_s, da_r, dp_s, rec_s, kv_s, dq_s, rs_r, gq_s, rgq, rgc, sm_s, rst, rsc, rsf,
    in_sem, w_sem, core_sem, core_rec, x_sem, x_rec, c2_sem, c2_rec, x2_sem, x2_rec,
    c_sem, c_rec, z_sem, z_rec, b_sem, b_rec, da_sem, da_rec, dp_sem, dp_rec,
    rs_sem, rs_rec, ag_sem, ag_rec, gq_sem, gq_rec, gc_sem, gc_rec,
    st_sem, st_rec, sc_sem, sc_rec, sf_sem, sf_rec, loc_sem, wl_sem, credit,
):
    F, C, T = sizes
    f, c, t = lax.axis_index("fsdp"), lax.axis_index("ctx"), lax.axis_index("tp")
    S, rows, hw = q_ref.shape
    heads = hw // HEAD_DIM
    width = start_s.shape[2]
    own_rows = rows // T
    tokens = S * own_rows
    shard = gbuf.shape[1]
    hidden = fc_ref.shape[1] // T
    wide = 2 * hidden
    per_seq = rows // block
    bf, f32 = jnp.bfloat16, jnp.float32
    sib, across = f ^ 1, f ^ 2

    def remote(src, dst, send, recv, **where):
        return pltpu.make_async_remote_copy(
            src_ref=src, dst_ref=dst, send_sem=send, recv_sem=recv, device_id=where, device_id_type=MESH
        )

    pending = []

    def go(copy, like):
        copy.start()
        pending.append(like)

    def landed(ref, sem):
        remote(ref, ref, b_rec, sem, fsdp=f).wait_recv()

    def sent(ref, sem):
        remote(ref, ref, sem, b_rec, fsdp=f).wait_send()

    def tp_peer(d):
        return lax.rem(t + d, T)

    def tp_source(d):
        return lax.rem(t + T - d, T)

    def rows_of(owner):
        return pl.ds(pl.multiple_of(owner * own_rows, own_rows), own_rows)

    ag_own, ag_whole = (ob_s, ob_s), (output_ref, dstart_ref)

    def ag_copy(a, s, owner, step, way):
        whole = ag_whole[a].at[s, rows_of(owner), :]
        src = ag_own[a].at[s] if step == 0 else whole
        return lambda to: remote(src, whole, ag_sem.at[a, s, step, way], ag_rec.at[a, s, step, way], tp=to)

    def ag_keep(a, s):
        return pltpu.make_async_copy(ag_own[a].at[s], ag_whole[a].at[s, rows_of(t), :], loc_sem.at[a, s])

    def ag_start(a, s):
        @pl.when(t < T - 1)
        def _():
            ag_copy(a, s, t, 0, 0)(t + 1).start()

        @pl.when(t > 0)
        def _():
            ag_copy(a, s, t, 0, 1)(t - 1).start()

        ag_keep(a, s).start()

    def ag_step(a, s, step):
        @pl.when(t >= step)
        def _():
            ag_copy(a, s, t - step, step - 1, 0)(t).wait_recv()

        @pl.when((t >= step) & (t < T - 1))
        def _():
            ag_copy(a, s, t - step, step, 0)(t + 1).start()

        @pl.when(t + step <= T - 1)
        def _():
            ag_copy(a, s, t + step, step - 1, 1)(t).wait_recv()

        @pl.when((t + step <= T - 1) & (t > 0))
        def _():
            ag_copy(a, s, t + step, step, 1)(t - 1).start()

    def ag_drain(a, s, first):
        if not first:
            ag_keep(a, s).wait()
        for step in range(first, T - 1 if first or a else 1):
            @pl.when((t >= step) & (t < T - 1))
            def _():
                ag_copy(a, s, t - step, step, 0)(t + 1).wait_send()

            @pl.when((t + step <= T - 1) & (t > 0))
            def _():
                ag_copy(a, s, t + step, step, 1)(t - 1).wait_send()

    across_at = lambda b: T + b
    main = pl.ds(0, wide)

    def core_send(b):
        slot = b % 2
        if b >= 2:
            pl.semaphore_wait(credit, 1)
        for k in range(2):
            remote(
                gbuf.at[2 * T + 2 * slot + k, :, main], rcore.at[slot, k],
                core_sem.at[b, k], core_rec.at[b, k], fsdp=sib,
            ).start()

    def core_add(b):
        slot = b % 2
        landed(rcore.at[slot, 1], core_rec.at[b, 1])
        add_rows(gbuf.at[across_at(b), :, main], [rcore.at[slot, 1]])
        out = gbuf.at[across_at(b), :, main]
        go(
            remote(out, rx.at[b, :, main], x_sem.at[b], x_rec.at[b], fsdp=across),
            lambda: (rx.at[b, :, main], x_sem.at[b]),
        )
        landed(rcore.at[slot, 0], core_rec.at[b, 0])
        add_rows(gbuf.at[b, :, main], [rcore.at[slot, 0]])
        if b < T - 2:
            pl.semaphore_signal(credit, inc=1, device_id={"fsdp": sib}, device_id_type=MESH)

    held = [b // C for b in range(T)]

    def ctx_copy(b, d, to):
        return remote(gbuf.at[b], rc.at[held[b], d - 1], c_sem.at[b], c_rec.at[b, d], ctx=to)

    def cross_add(b):
        landed(rx.at[b, :, main], x_rec.at[b])
        add_rows(gbuf.at[b, :, main], [rx.at[b, :, main]])

    def ctx_send(b):
        owner = b % C
        for d in range(1, C):
            @pl.when(lax.rem(c + d, C) == owner)
            def _():
                ctx_copy(b, d, owner).start()

    def ctx_wait(b):
        @pl.when(c == b % C)
        def _():
            for d in range(1, C):
                ctx_copy(b, d, c).wait_recv()
            if C > 1:
                add_rows(gbuf.at[b], [rc.at[held[b], d - 1] for d in range(1, C)])

    def z_round(b, step):
        def hop(to, way):
            return remote(gbuf.at[b], rz.at[held[b], way], z_sem.at[b], z_rec.at[b, way], tp=to)

        def visit(way, before, here):
            @pl.when((c == b % C) & here)
            def _():
                if step:
                    hop(t, way).wait_recv()
                    add_rows(gbuf.at[b], [rz.at[held[b], way]])

                @pl.when(before)
                def _():
                    hop(t - 1 if way == 0 else t + 1, way).start()

        if T - 1 - step >= b and b < T - 1:
            visit(0, t > b, t == T - 1 - step)
        if step <= b and b > 0:
            visit(1, t < b, t == step)

    def feed_phase(att_s, outw_s, w_s, x_s, nm_s, nmt_s, gt_s, acc_s):
        steps = hidden // step_cols
        ring = w_s.shape[0]
        total_steps = 2 * T * steps

        def stream(n):
            at = pl.ds(pl.multiple_of(lax.rem(n, T * steps) * step_cols, step_cols), step_cols)
            slot = lax.rem(n, ring)
            return [
                pltpu.make_async_copy(ref.at[:, at], w_s.at[slot, k], w_sem.at[slot, k])
                for k, ref in enumerate((fc_ref, pj_ref))
            ]

        def take(n):
            for copy in stream(n):
                copy.wait()

            @pl.when(n + ring - 1 < total_steps)
            def _():
                for copy in stream(n + ring - 1):
                    copy.start()

            return lax.rem(n, ring)

        loads = [
            pltpu.make_async_copy(att_ref, dq_s, in_sem.at[0]),
            pltpu.make_async_copy(outw_ref, outw_s, in_sem.at[1]),
            pltpu.make_async_copy(start_ref, start_s, in_sem.at[2]),
            pltpu.make_async_copy(grad_ref, grad_s, in_sem.at[3]),
        ]
        for copy in loads:
            copy.start()
        for n in range(ring - 1):
            for copy in stream(n):
                copy.start()

        barrier = pltpu.get_barrier_semaphore()
        peers = 0
        for d in range(1, F):
            pl.semaphore_signal(barrier, inc=1, device_id={"fsdp": f ^ d}, device_id_type=MESH)
            peers += 1
        for d in range(1, T):
            pl.semaphore_signal(barrier, inc=1, device_id={"tp": tp_peer(d)}, device_id_type=MESH)
            peers += 1
        for d in range(1, C):
            pl.semaphore_signal(barrier, inc=1, device_id={"ctx": lax.rem(c + d, C)}, device_id_type=MESH)
            peers += 1
        pl.semaphore_wait(barrier, peers)

        for copy in loads:
            copy.wait()
        mid = start_s[...].reshape(tokens, width).astype(f32)
        for g in range(T):
            for s in range(S):
                att_s[g, column(s, own_rows), :] = turn(dq_s[g, s])
            mid = mid + dot(att_s[g], outw_s[column(g, hw), :])
        mid_s[...] = mid
        hat, _ = hat_rows(mid)
        nm = hat * params_ref[1:2] + params_ref[3:4]
        nm_s[...] = nm.astype(bf)
        nmt_s[...] = turn_back(nm)
        gt_s[...] = turn(grad_s[...])
        acc_s[...] = jnp.zeros_like(acc_s)

        def forward(j, _):
            slot = take(j)
            x = dot(nm_s[...], w_s[slot, 0])
            x_s[j] = x
            act, _ = gelu_parts(x)
            acc_s[...] += dot(act.astype(bf), w_s[slot, 1], ((1,), (1,)))
            return 0

        lax.fori_loop(0, T * steps, forward, 0)
        ob_s[...] = (mid_s[...] + acc_s[...]).astype(bf).reshape(S, own_rows, width)
        for s in range(S):
            ag_start(0, s)
        acc_s[...] = jnp.zeros_like(acc_s)

        for n in range(T):
            if n >= 2:
                for k in range(2):
                    sent(rcore.at[0, 0], core_sem.at[n - 2, k])
            slot = n % 2

            def backward(j, _):
                here = pl.ds(pl.multiple_of(j * step_cols, step_cols), step_cols)
                there = pl.ds(pl.multiple_of(hidden + j * step_cols, step_cols), step_cols)
                at_w = take(T * steps + n * steps + j)
                fc, proj = w_s[at_w, 0], w_s[at_w, 1]
                act, slope = gelu_parts(x_s[n * steps + j])
                act = act.astype(bf)
                d_exp = (slope * dot(grad_s[...], proj)).astype(bf)
                acc_s[...] += dot(d_exp, fc, ((1,), (1,)))
                d_fc = dot(nmt_s[...], d_exp).astype(bf)
                d_proj = dot(gt_s[...], act).astype(bf)
                for ff in range(F):
                    r = f ^ ff
                    odd, half = lax.rem(r, 2), r // 2
                    at = (1 - odd) * (half * T + n) + odd * (2 * T + 2 * slot + half)
                    gbuf[at, :, here] = d_fc[column(ff, shard)]
                    gbuf[at, :, there] = d_proj[column(ff, shard)]
                return 0

            lax.fori_loop(0, steps, backward, 0)
            core_send(n)
            if n:
                core_add(n - 1)

        mid = mid_s[...]
        hat, inv = hat_rows(mid)
        d_nm = acc_s[...]
        d_mid = grad_s[...].astype(f32) + norm_back(hat, inv, params_ref[1:2], d_nm)
        d_mid_t = turn_back(d_mid)
        for g in range(T):
            d_att = dot(outw_s[column(g, hw), :], d_mid_t).astype(bf)
            for s in range(S):
                da_s[g, s] = d_att[:, column(s, own_rows)]
        for s in range(S):
            for d in range(1, T):
                go(
                    remote(da_s.at[tp_peer(d), s], da_r.at[t, s], da_sem.at[d, s], da_rec.at[d, s], tp=tp_peer(d)),
                    lambda d=d, s=s: (da_s.at[0, s], da_sem.at[d, s]),
                )
        sm_s[...] = jnp.zeros_like(sm_s)
        sm_s[1:2, :] = jnp.sum(d_nm * hat, axis=0, keepdims=True)
        sm_s[3:4, :] = jnp.sum(d_nm, axis=0, keepdims=True)
        mid_s[...] = d_mid
        if g2.shape[3] > hw:
            g2[:, :, :, hw:] = jnp.zeros(g2.shape[:3] + (g2.shape[3] - hw,), bf)
        for g in range(T):
            d_out = dot(d_mid_t, att_s[g]).astype(bf)
            for ff in range(F):
                g2[f ^ ff, g, :, :hw] = d_out[column(ff, shard)]
        core_add(T - 1)

    bf_mem = lambda *shape: pltpu.VMEM(shape, bf)
    f32_mem = lambda *shape: pltpu.VMEM(shape, f32)
    pl.run_scoped(
        feed_phase,
        bf_mem(T, tokens, hw), bf_mem(T * hw, width), bf_mem(3, 2, width, step_cols),
        f32_mem(T * hidden // step_cols, tokens, step_cols),
        bf_mem(tokens, width), bf_mem(width, tokens), bf_mem(width, tokens), f32_mem(tokens, width),
    )

    for k in range(2):
        out = g2.at[1 + 2 * k]
        go(
            remote(out, r2c.at[k], c2_sem.at[k], c2_rec.at[k], fsdp=sib),
            lambda k=k: (r2c.at[k], c2_sem.at[k]),
        )

    def dp_copy(d, s):
        return remote(
            dp_s.at[far - d, s], rec_s.at[d - 1, s], dp_sem.at[d, s], dp_rec.at[d, s], ctx=lax.rem(c + C - d, C)
        )

    def sums_along(snd, wl_s):
        def kv_sum(s):
            for d in range(1, far + 1):
                @pl.when(c + d < C)
                def _():
                    dp_copy(d, s).wait_recv()
                    for g in range(T):
                        kv_s[g, s] = (kv_s[g, s].astype(f32) + rec_s[d - 1, s, g].astype(f32)).astype(bf)

        def partials(s):
            if s == 0:
                pltpu.make_async_copy(wl_ref, wl_s, wl_sem).wait()

            def one(o, _):
                total = dot(wl_s[0], dq_s[o, s])
                for j in (1, 2):
                    total = total + dot(wl_s[j], kv_s[o, s, column(j - 1, hw), :])
                snd[s, o] = total.astype(bf)
                return 0

            lax.fori_loop(0, T, one, 0)

        def rs_copy(s, o, way, at):
            to = at - 1 if way == 0 else at + 1
            slot = T if (to == o and way == 1) else o
            return remote(
                snd.at[s, o], rs_r.at[s, slot], rs_sem.at[s, o], rs_rec.at[s, o, way], tp=t - 1 if way == 0 else t + 1
            )

        def rs_slot(s, k):
            for at in range(T):
                for way, o, begins in ((0, k - (T - 1 - at), at == T - 1), (1, T - 1 + at - k, at == 0)):
                    if not (0 <= o <= at if way == 0 else at <= o <= T - 1):
                        continue

                    @pl.when(t == at)
                    def _():
                        if not begins:
                            landed(rs_r.at[s, T if (o == at and way == 1) else o], rs_rec.at[s, o, way])
                        if o != at:
                            if not begins:
                                add_rows(snd.at[s, o], [rs_r.at[s, o]], 128)
                            rs_copy(s, o, way, at).start()

        return kv_sum, partials, rs_slot

    def attention_phase(
        snd, wl_s, q_s, kvo_s, prv_s, ot_s, k_h, kt_h, v_h, q_h, qt_h, g_h, gt_h, dqt_s, dk_s, dv_s, del_s
    ):
        kv_sum, partials, rs_slot = sums_along(snd, wl_s)

        def loads(s):
            return [
                pltpu.make_async_copy(ref.at[s], mem, in_sem.at[k])
                for k, (ref, mem) in enumerate(((q_ref, q_s), (kv_ref, kvo_s), (out_t_ref, ot_s), (prev_ref, prv_s)))
            ]

        for copy in loads(0):
            copy.start()
        for k in (1, 0):
            landed(r2c.at[k], c2_rec.at[k])
            for b in range(T):
                add_rows(g2.at[2 * k, b], [r2c.at[k, b]])
            if k:
                go(remote(g2.at[2], r2x, x2_sem, x2_rec, fsdp=across), lambda: (r2x, x2_sem))

        def keys(s):
            for h in range(heads):
                q = q_s[:, column(h)].astype(f32) * 0.125
                q_h[h] = q.astype(bf)
                qt_h[h] = turn_back(q)
                if far:
                    k = prv_s[:, column(h)]
                    k_h[h, : far * rows] = k
                    kt_h[h, :, : far * rows] = turn(k)
                    v_h[h, : far * rows] = prv_s[:, column(heads + h)]
                k = kvo_s[:, column(h)]
                k_h[h, far * rows :] = k
                kt_h[h, :, far * rows :] = turn(k)
                v_h[h, far * rows :] = kvo_s[:, column(heads + h)]

        def grads(s):
            da_r[t, s] = da_s[t, s]
            for d in range(1, T):
                landed(da_r.at[tp_source(d), s], da_rec.at[d, s])
            for h in range(heads):
                for g in range(T):
                    gt_h[h, :, column(g, own_rows)] = da_r[g, s, column(h), :]
                g_t = gt_h[h].astype(f32)
                g_h[h] = turn_back(g_t)
                del_s[h : h + 1, :] = jnp.sum(g_t * ot_s[column(h), :], axis=0, keepdims=True)
            dqt_s[...] = jnp.zeros_like(dqt_s)

        def part(s, h, base, count, own):
            spot = pl.ds(pl.multiple_of(h * HEAD_DIM, HEAD_DIM), HEAD_DIM)
            dk_s[:count] = jnp.zeros((count, HEAD_DIM), f32)
            dv_s[:count] = jnp.zeros((count, HEAD_DIM), f32)
            for i in range(per_seq):
                span = column(i, block)
                reach = far * rows + i * block
                first = max(0, reach - (DOC_MOST - 1) - base) // block * block
                last = min(count, reach + block - base)
                if first >= last:
                    continue
                low = low_ref[s, :, span] - base
                place = first + lax.broadcasted_iota(jnp.int32, (last - first, 1), 0)
                allowed = place >= low
                if own:
                    allowed = allowed & (place <= i * block + lax.broadcasted_iota(jnp.int32, (1, block), 1))
                here = slice(base + first, base + last)
                scores = dot(k_h[h, here, :], qt_h[h, :, span])
                p = jnp.exp(jnp.where(allowed, scores - log_ref[s, pl.ds(h, 1), span], MASKED))
                ds = (p * (dot(v_h[h, here, :], gt_h[h, :, span]) - del_s[pl.ds(h, 1), span])).astype(bf)
                dv_s[first:last] += dot(p.astype(bf), g_h[h, span, :])
                dk_s[first:last] += dot(ds, q_h[h, span, :])
                dqt_s[spot, span] += dot(kt_h[h, :, here], ds)
            return spot, pl.ds(pl.multiple_of(hw + h * HEAD_DIM, HEAD_DIM), HEAD_DIM)

        def far_part(s):
            def one(h, _):
                k_at, v_at = part(s, h, 0, far * rows, False)
                for at, source in ((k_at, dk_s), (v_at, dv_s)):
                    turned = source[: far * rows].T.astype(bf)
                    for j in range(far):
                        for g in range(T):
                            dp_s[j, s, g, at, :] = turned[:, column(j * T + g, own_rows)]
                return 0

            lax.fori_loop(0, heads, one, 0)

        def own_part(s):
            def one(h, _):
                k_at, v_at = part(s, h, far * rows, rows, True)
                for at, source in ((k_at, dk_s), (v_at, dv_s)):
                    turned = source[:rows].T.astype(bf)
                    for g in range(T):
                        kv_s[g, s, at, :] = turned[:, column(g, own_rows)]
                return 0

            lax.fori_loop(0, heads, one, 0)

        for s in range(S):
            for copy in loads(s):
                copy.wait()
            keys(s)
            grads(s)
            if s + 1 < S:
                for copy in loads(s + 1):
                    copy.start()
            if s == 0:
                for other in range(S):
                    ag_step(0, other, 1)
            if far:
                @pl.when(c > 0)
                def _():
                    far_part(s)

                for d in range(1, far + 1):
                    @pl.when(c >= d)
                    def _():
                        dp_copy(d, s).start()
            if s:
                rs_slot(s - 1, 1)
            else:
                cross_add(0)
            own_part(s)
            for g in range(T):
                dq_s[g, s] = (0.125 * dqt_s[:, column(g, own_rows)]).astype(bf)
            if s:
                rs_slot(s - 1, 2)
            if s < T - 2:
                for other in range(S):
                    ag_step(0, other, s + 2)
            if s + 1 < T:
                cross_add(s + 1)
            kv_sum(s)
            partials(s)
            rs_slot(s, 0)

    def last_phase(snd, wl_s, normed_s, gq_acc, tot_s):
        kv_sum, partials, rs_slot = sums_along(snd, wl_s)
        normed_in = pltpu.make_async_copy(normed_ref, normed_s, in_sem.at[0])
        normed_in.start()

        gain = params_ref[0:1]

        def norm_stage(s):
            tot_s[...] = snd[s, t].astype(f32)

            @pl.when(t < T - 1)
            def _():
                tot_s[...] += rs_r[s, t].astype(f32)

            @pl.when(t > 0)
            def _():
                tot_s[...] += rs_r[s, T].astype(f32)

            d_normed = tot_s[...].T
            hat, inv = hat_rows(start_s[s].astype(f32))
            value = mid_s[column(s, own_rows), :] + norm_back(hat, inv, gain, d_normed)
            ag_drain(0, s, 0)
            ob_s[s] = value.astype(bf)
            ag_start(1, s)
            sm_s[0:1, :] += jnp.sum(d_normed * hat, axis=0, keepdims=True)
            sm_s[2:3, :] += jnp.sum(d_normed, axis=0, keepdims=True)

        for k in range(3, T):
            rs_slot(0, k)
        norm_stage(0)
        landed(r2x, x2_rec)
        side = pl.ds(wide, g2.shape[3])
        for b in range(T):
            gbuf[b, :, side] = (g2[0, b].astype(f32) + r2x[b].astype(f32)).astype(bf)
        for b in range(min(S + 1, T)):
            ctx_send(b)

        normed_in.wait()
        gq_acc[...] = jnp.zeros_like(gq_acc)
        for s in range(S):

            def one(o, _):
                near = normed_s[s, rows_of(o), :]
                gq_acc[:hw, :] += dot(dq_s[o, s], near)
                gq_acc[hw:, :] += dot(kv_s[o, s], near)
                return 0

            lax.fori_loop(0, T, one, 0)
        for k in range(F):
            gq_s[k] = gq_acc[:, column(k, shard)].astype(bf)
        for d in range(1, F):
            go(
                remote(gq_s.at[f ^ d], rgq.at[d - 1], gq_sem.at[d], gq_rec.at[d], fsdp=f ^ d),
                lambda d=d: (gq_s.at[0], gq_sem.at[d]),
            )
        for b in range(min(S + 1, T), T):
            cross_add(b)
            ctx_send(b)
        for s in range(1, S):
            for k in range(1, T):
                rs_slot(s, k)
            norm_stage(s)
        ag_step(1, 0, 1)

        thoughts = jnp.zeros((pick_ref.shape[1], width), f32)
        for s in range(S):
            thoughts = thoughts + dot(pick_ref[s], ob_s[s])
        sm_s[8:, :] = thoughts
        for d in range(1, T):
            go(
                remote(sm_s, rst.at[d], st_sem.at[d], st_rec.at[d], tp=tp_peer(d)),
                lambda d=d: (sm_s, st_sem.at[d]),
            )
        for b in range(T):
            ctx_wait(b)
            z_round(b, 0)

        gq_sum = gq_s[f].astype(f32)
        for d in range(1, F):
            landed(rgq.at[d - 1], gq_rec.at[d])
            gq_sum = gq_sum + rgq[d - 1].astype(f32)
        rgc[c] = gq_sum.astype(bf)
        for d in range(1, C):
            go(
                remote(rgc.at[c], rgc.at[c], gc_sem.at[d], gc_rec.at[d], ctx=lax.rem(c + d, C)),
                lambda d=d: (rgc.at[0], gc_sem.at[d]),
            )

        for d in range(1, T):
            landed(rst.at[d], st_rec.at[d])
        rst[0] = sm_s[...]
        total = jnp.zeros(sm_s.shape, f32)
        for k in range(T):
            total = total + rst[lax.rem(t + T - k, T)]
        rsc[c] = total
        for d in range(1, C):
            go(
                remote(rsc.at[c], rsc.at[c], sc_sem.at[d], sc_rec.at[d], ctx=lax.rem(c + d, C)),
                lambda d=d: (rsc.at[0], sc_sem.at[d]),
            )
        for step in range(1, T):
            if step > 1:
                ag_step(1, 0, step)
            for s in range(1, S):
                ag_step(1, s, step)
            for b in range(T):
                z_round(b, step)
            if step == 1:
                for d in range(1, C):
                    landed(rsc.at[0], sc_rec.at[d])
                total = jnp.zeros(sm_s.shape, f32)
                for k in range(C):
                    total = total + rsc[k]
                small_ref[8:, :] = total[8:]
                rsf[f] = total
                for d in range(1, F):
                    go(
                        remote(rsf.at[f], rsf.at[f], sf_sem.at[d], sf_rec.at[d], fsdp=f ^ d),
                        lambda d=d: (rsf.at[0], sf_sem.at[d]),
                    )
        for d in range(1, F):
            landed(rsf.at[0], sf_rec.at[d])
        norms = jnp.zeros((8, sm_s.shape[1]), f32)
        for k in range(F):
            norms = norms + rsf[k, 0:8, :]
        small_ref[0:8, :] = norms

        for d in range(1, C):
            landed(rgc.at[0], gc_rec.at[d])
        total = jnp.zeros(gq_ref.shape, f32)
        for k in range(C):
            total = total + rgc[k].astype(f32)
        gq_ref[...] = total
        for o in range(T):
            @pl.when(t != o)
            def _():
                for s in range(S):
                    sent(snd.at[s, o], rs_sem.at[s, o])

    def after_feed(snd, wl_s):
        wl_in = pltpu.make_async_copy(wl_ref, wl_s, wl_sem)
        wl_in.start()
        pl.run_scoped(
            functools.partial(attention_phase, snd, wl_s),
            bf_mem(rows, hw), bf_mem(rows, 2 * hw), bf_mem(max(far, 1) * rows, 2 * hw), f32_mem(hw, rows),
            bf_mem(heads, (far + 1) * rows, HEAD_DIM), bf_mem(heads, HEAD_DIM, (far + 1) * rows),
            bf_mem(heads, (far + 1) * rows, HEAD_DIM),
            bf_mem(heads, rows, HEAD_DIM), bf_mem(heads, HEAD_DIM, rows),
            bf_mem(heads, rows, HEAD_DIM), bf_mem(heads, HEAD_DIM, rows),
            f32_mem(hw, rows), f32_mem(max(far, 1) * rows, HEAD_DIM), f32_mem(max(far, 1) * rows, HEAD_DIM),
            f32_mem(8, rows),
        )
        pl.run_scoped(
            functools.partial(last_phase, snd, wl_s),
            bf_mem(S, rows, width), f32_mem(3 * hw, width), f32_mem(width, own_rows),
        )

    pl.run_scoped(after_feed, bf_mem(S, T, width, own_rows), bf_mem(3, width, hw))

    for b in range(T):
        owner = b % C
        final = lambda d: remote(gbuf.at[b], rx.at[b], b_sem.at[d], b_rec, ctx=lax.rem(owner + d, C))

        @pl.when((t == b) & (c == owner))
        def _():
            for d in range(1, C):
                final(d).start()
            gw_ref[...] = gbuf[b]
            for d in range(1, C):
                final(d).wait_send()

        if C > 1:
            @pl.when((t == b) & (c != owner))
            def _():
                final(1).wait_recv()
                gw_ref[...] = rx[b]

    for like in pending:
        sent(*like())
    for n in range(max(T - 2, 0), T):
        for k in range(2):
            sent(rcore.at[0, 0], core_sem.at[n, k])
    for b in range(T):
        owner = b % C
        if C > 1:
            @pl.when(c != owner)
            def _():
                ctx_copy(b, 1, owner).wait_send()

        @pl.when((c == owner) & (t != b))
        def _():
            remote(gbuf.at[b], rz.at[held[b], 0], z_sem.at[b], z_rec.at[b, 0], tp=t).wait_send()
    for s in range(S):
        for d in range(1, far + 1):
            @pl.when(c >= d)
            def _():
                dp_copy(d, s).wait_send()
        ag_drain(0, s, 1)
        ag_drain(1, s, 0)


def back(att, start, grad, out_w, fc, proj_t, params, q, kv, prev, low, out_t, logs, normed, wl, pick, block, far, counts):
    F, C, T = counts
    S, rows, hw = q.shape
    width = normed.shape[2]
    own_rows = rows // T
    tokens = S * own_rows
    shard = width // F
    hidden = fc.shape[1] // T
    cols = padded(hw)
    wide = 2 * hidden + cols
    bf, f32 = jnp.bfloat16, jnp.float32
    extra = 8 + pick.shape[1]
    mine = -(-T // C)
    dists = max(far, 1)
    vmem = pl.BlockSpec(memory_space=pltpu.VMEM)
    anywhere = pl.BlockSpec(memory_space=pl.ANY)
    dma = lambda *shape: pltpu.SemaphoreType.DMA(shape)
    one = pltpu.SemaphoreType.DMA
    shape = jax.ShapeDtypeStruct
    b16 = lambda *size: pltpu.VMEM(size, bf)
    b32 = lambda *size: pltpu.VMEM(size, f32)
    return pl.pallas_call(
        functools.partial(back_kernel, counts, block, far, 256),
        in_specs=[anywhere] * 6 + [vmem] + [anywhere] * 3 + [vmem, anywhere, vmem, anywhere, anywhere, vmem],
        out_specs=[anywhere, anywhere, vmem, vmem, vmem],
        out_shape=[
            shape((S, rows, width), bf),
            shape((S, rows, width), bf),
            shape((shard, wide), bf),
            shape((3 * hw, shard), f32),
            shape((extra, width), f32),
        ],
        scratch_shapes=[
            b16(S, own_rows, width), b32(tokens, width), b16(tokens, width), b16(S, own_rows, width),
            b16(2 * T + 4, shard, wide), b16(2, 2, shard, 2 * hidden), b16(T, shard, wide),
            b16(mine, max(C - 1, 1), shard, wide), b16(mine, 2, shard, wide),
            b16(4, T, shard, cols), b16(2, T, shard, cols), b16(T, shard, cols),
            b16(T, S, hw, own_rows), b16(T, S, hw, own_rows),
            b16(dists, S, T, 2 * hw, own_rows), b16(dists, S, T, 2 * hw, own_rows),
            b16(T, S, 2 * hw, own_rows), b16(T, S, hw, own_rows),
            b16(S, T + 1, width, own_rows),
            b16(F, 3 * hw, shard), b16(F - 1, 3 * hw, shard), b16(C, 3 * hw, shard),
            b32(extra, width), b32(T, extra, width), b32(C, extra, width), b32(F, extra, width),
            dma(4), dma(3, 2), dma(T, 2), dma(T, 2), dma(T), dma(T), dma(2), dma(2), one, one,
            dma(T), dma(T, C), dma(T), dma(T, 2), dma(C), one, dma(T, S), dma(T, S), dma(far + 1, S), dma(far + 1, S),
            dma(S, T), dma(S, T, 2), dma(2, S, T, 2), dma(2, S, T, 2), dma(F), dma(F), dma(C), dma(C),
            dma(T), dma(T), dma(C), dma(C), dma(F), dma(F), dma(2, S), one, pltpu.SemaphoreType.REGULAR,
        ],
        compiler_params=pltpu.CompilerParams(
            vmem_limit_bytes=VMEM_LIMIT, collective_id=2, has_side_effects=True
        ),
        cost_estimate=pl.CostEstimate(flops=36 * 10**9, bytes_accessed=100 << 20, transcendentals=16 << 20),
    )(att, start, grad, out_w, fc, proj_t, params, q, kv, prev, low, out_t, logs, normed, wl, pick)


def local(
    inputs, thoughts, positions, lengths, w_qkv, w_out, w_fc, w_proj, norm_gains, norm_biases, out_grad,
):
    rows, seqs, width = inputs.shape
    ctx_count = lax.axis_size("ctx")
    tp_count = lax.axis_size("tp")
    fsdp_count = lax.axis_size("fsdp")
    ctx, tp, fsdp = lax.axis_index("ctx"), lax.axis_index("tp"), lax.axis_index("fsdp")
    first_row = ctx * rows
    own_rows = rows // tp_count
    own_tokens = own_rows * seqs
    far = min(ctx_count - 1, -(-(DOC_MOST - 1) // rows))
    block = min(256, rows)
    bf, f32 = jnp.bfloat16, jnp.float32

    counts = (fsdp_count, ctx_count, tp_count)
    local_width = w_qkv.shape[2]
    params = jnp.pad(jnp.concatenate([norm_gains, norm_biases]).astype(f32), ((0, 4), (0, 0)))
    places = first_row + jnp.arange(rows, dtype=jnp.int32)
    is_thought = places[None, None, :] == positions[:, :, None]
    keep = jnp.logical_not(jnp.any(is_thought, axis=0))
    start = jnp.transpose(inputs, (1, 0, 2))
    for t in range(thoughts.shape[0]):
        start = jnp.where(is_thought[t][:, :, None], thoughts[t][:, None, :], start)
    ends = jnp.cumsum(lengths, axis=1, dtype=jnp.int32)
    low = jnp.max(jnp.where(ends[:, :, None] <= places[None, None, :], ends[:, :, None], 0), axis=1)
    low = low - (first_row - far * rows)

    low3 = low[:, None, :]
    attended, q, kv, prev, out_t, logs, normed, w_local, out_full, fc_full, proj_full_t, params = front(
        start, low3, w_qkv, w_out, w_fc, w_proj.T, params, block, far, counts
    )
    start_own = lax.dynamic_slice_in_dim(start, tp * own_rows, own_rows, 1)
    grad_own = jnp.transpose(
        lax.dynamic_slice_in_dim(out_grad, tp * own_rows, own_rows, 0), (1, 0, 2)
    ).reshape(own_tokens, width)

    own_places = lax.dynamic_slice_in_dim(places, tp * own_rows, own_rows, 0)
    count = thoughts.shape[0]
    pick = (own_places[None, None, :] == positions[:, :, None]).astype(bf)
    picks = []
    for s in range(seqs):
        picks.append(jnp.concatenate(
            [jnp.where(k == s, pick[:, s], jnp.zeros_like(pick[:, s])) for k in range(seqs)], axis=0
        ))
    pick = jnp.stack(picks)
    pick = jnp.pad(pick, ((0, 0), (0, -(-pick.shape[1] // 16) * 16 - pick.shape[1]), (0, 0)))
    output, d_start, gw, gq, small = back(
        attended, start_own, grad_own, out_full, fc_full, proj_full_t, params, q, kv, prev, low3, out_t, logs, normed,
        w_local, pick, block, far, counts,
    )
    output = jnp.transpose(output, (1, 0, 2))
    d_inputs = jnp.transpose(jnp.where(keep[:, :, None], d_start.astype(f32), 0.0), (1, 0, 2))
    d_thoughts = jnp.transpose(small[8 : 8 + count * seqs].reshape(seqs, count, width), (1, 0, 2))
    hidden = w_fc.shape[1]
    gw = gw.astype(f32)
    norms = lax.dynamic_slice_in_dim(small[:4], fsdp * w_fc.shape[0], w_fc.shape[0], 1)
    return (
        output,
        d_inputs,
        d_thoughts,
        jnp.transpose(gq.reshape(3, local_width, -1), (0, 2, 1)),
        gw[:, 2 * hidden : 2 * hidden + local_width].T,
        gw[:, :hidden],
        gw[:, hidden : 2 * hidden].T,
        norms[:2],
        norms[2],
        norms[3],
    )


def solution(mesh):
    in_specs = (
        P("ctx", "fsdp", None),
        P(None, "fsdp", None),
        P(None, "fsdp"),
        P("fsdp", None),
        P(None, "fsdp", "tp"),
        P("tp", "fsdp"),
        P("fsdp", "tp"),
        P("tp", "fsdp"),
        P(None, "fsdp"),
        P(None, "fsdp"),
        P("ctx", "fsdp", None),
    )
    out_specs = (
        P("ctx", "fsdp", None),
        P("ctx", "fsdp", None),
        P(None, "fsdp", None),
        P(None, "fsdp", "tp"),
        P("tp", "fsdp"),
        P("fsdp", "tp"),
        P("tp", "fsdp"),
        P(None, "fsdp"),
        P("fsdp"),
        P("fsdp"),
    )
    return jax.shard_map(local, mesh=mesh, in_specs=in_specs, out_specs=out_specs, check_vma=False)
```

```python
import functools

import jax
import jax.numpy as jnp
from jax import lax
from jax.experimental import pallas as pl
from jax.experimental.pallas import tpu as pltpu
from jax.sharding import PartitionSpec as P

HEAD_DIM = 64
DOC_MOST = 1024
EPSILON = 1e-05
MASKED = -1e30


def dot(a, b, dims=((1,), (0,))):
    return lax.dot_general(a, b, (dims, ((), ())), preferred_element_type=jnp.float32)


def hat_rows(values):
    centre = jnp.mean(values, axis=-1, keepdims=True)
    shifted = values - centre
    spread = jnp.mean(shifted * shifted, axis=-1, keepdims=True)
    inv = lax.rsqrt(spread + EPSILON)
    return shifted * inv, inv


def norm_back(hat, inv, gain, grad):
    eg = grad * gain
    return inv * (
        eg
        - jnp.mean(eg, axis=-1, keepdims=True)
        - hat * jnp.mean(eg * hat, axis=-1, keepdims=True)
    )


MESH = pl.DeviceIdType.MESH
VMEM_LIMIT = 62 << 20


def column(index, size=HEAD_DIM):
    return slice(index * size, (index + 1) * size)


def turn(value):
    return value.astype(jnp.float32).T.astype(jnp.bfloat16)


def turn_back(value):
    return value.T.astype(jnp.bfloat16)


def front_kernel(
    sizes, block,
    start_ref, low_ref, wq_ref, wo_ref, wf_ref, wp_ref, par_ref,
    att_ref, q_ref, kv_ref, prev_ref, out_t_ref, log_ref, normed_ref, wl_ref, ow_ref, fc_ref, pj_ref, params_ref,
    start_s, normed_s, wl_s, wo_s, par_s, q_s, kv_s, prev_s, qt_s, ko_s, vto_s, kp_s, vtp_s, m_s, l_s, att_s,
    in_sem, out_sem, w_loc, z_sem, z_rec, s_sem, s_rec, x_sem, x_rec, r_sem, r_rec,
    kv_sem, kv_rec, at_sem, at_rec, at_loc,
):
    F, C, T = sizes
    f, c, t = lax.axis_index("fsdp"), lax.axis_index("ctx"), lax.axis_index("tp")
    S, rows, width = start_ref.shape
    hw = q_ref.shape[2]
    heads = hw // HEAD_DIM
    own_rows = rows // T
    far = prev_ref.shape[1] // rows if C > 1 else 0
    shard = wq_ref.shape[1]
    hidden = wf_ref.shape[1]
    bf, f32 = jnp.bfloat16, jnp.float32
    sib, across = f ^ 1, f ^ 2

    def remote(src, dst, send, recv, **where):
        return pltpu.make_async_remote_copy(
            src_ref=src, dst_ref=dst, send_sem=send, recv_sem=recv, device_id=where, device_id_type=MESH
        )

    start_in = pltpu.make_async_copy(start_ref, start_s, in_sem.at[0])
    start_in.start()

    barrier = pltpu.get_barrier_semaphore()
    peers = 0
    for d in range(1, F):
        pl.semaphore_signal(barrier, inc=1, device_id={"fsdp": f ^ d}, device_id_type=MESH)
        peers += 1
    for d in range(1, T):
        pl.semaphore_signal(barrier, inc=1, device_id={"tp": lax.rem(t + d, T)}, device_id_type=MESH)
        peers += 1
    for d in range(1, C):
        pl.semaphore_signal(barrier, inc=1, device_id={"ctx": lax.rem(c + d, C)}, device_id_type=MESH)
        peers += 1
    pl.semaphore_wait(barrier, peers)

    pending = []

    def go(copy):
        copy.start()
        pending.append(copy)
        return copy

    def at_shard(ff):
        return pl.ds(pl.multiple_of(ff * shard, shard), shard)

    def at_hidden(tt):
        return pl.ds(pl.multiple_of(tt * hidden, hidden), hidden)

    def block_at(a, tt, ff):
        if a == 0:
            return par_s.at[ff]
        if a == 1:
            return wl_s.at[:, at_shard(ff), :]
        if a == 2:
            return wo_s.at[tt, ff]
        return (fc_ref if a == 3 else pj_ref).at[at_shard(ff), at_hidden(tt)]

    sources = (par_ref, wq_ref, wo_ref, wf_ref, wp_ref)

    def origin(p):
        return t if p == 0 else (t - (p + 1) // 2 if p % 2 else t + p // 2)

    def has(p):
        return t >= (p + 1) // 2 if p % 2 else t + p // 2 <= T - 1

    def spread_chip(a, p):
        src = sources[a] if p == 0 else block_at(a, origin(p), f)
        dst = block_at(a, origin(p), f)
        remote(src, dst, x_sem.at[a, p], x_rec.at[a, p], fsdp=across).start()
        remote(src, dst, s_sem.at[a, p], s_rec.at[a, p], fsdp=sib).start()

    def along(a, p, way):
        src = sources[a] if p == 0 else block_at(a, origin(p), f)
        q = p + 2 if p else 1 + way
        return remote(
            src, block_at(a, origin(p), f), z_sem.at[a, p, way], z_rec.at[a, q], tp=t + 1 if way == 0 else t - 1
        )

    def line_start(a):
        @pl.when(t < T - 1)
        def _():
            along(a, 0, 0).start()

        @pl.when(t > 0)
        def _():
            along(a, 0, 1).start()

        spread_chip(a, 0)

    def line_step(a, k):
        for way, p in ((0, 2 * k - 1), (1, 2 * k)):
            on = t < T - 1 if way == 0 else t > 0

            @pl.when(has(p) & on)
            def _():
                here = block_at(a, origin(p), f)
                remote(here, here, z_sem.at[a, p, way], z_rec.at[a, p], tp=t).wait_recv()
                along(a, p, way).start()

            @pl.when(has(p) & jnp.logical_not(on))
            def _():
                here = block_at(a, origin(p), f)
                remote(here, here, z_sem.at[a, p, way], z_rec.at[a, p], tp=t).wait_recv()

            @pl.when(has(p))
            def _():
                spread_chip(a, p)

    def relay(a, p):
        here = block_at(a, origin(p), across)
        remote(here, here, x_sem.at[a, p], x_rec.at[a, p], fsdp=f).wait_recv()
        remote(here, here, r_sem.at[a, p], r_rec.at[a, p], fsdp=sib).start()

    def take_chip(a, p):
        for ff, rec in ((sib, s_rec), (sib ^ 2, r_rec)):
            here = block_at(a, origin(p), ff)
            remote(here, here, s_sem.at[a, p], rec.at[a, p], fsdp=f).wait_recv()

    def every(what, a, ps):
        for p in ps:
            if p == 0:
                what(a, 0)
            else:
                @pl.when(has(p))
                def _():
                    what(a, p)

    def drain(a):
        last = 1 if a < 2 else 2 * T - 1

        def chip(a, p):
            src = sources[a]
            for sem in (x_sem, s_sem, r_sem):
                remote(src, src, sem.at[a, p], x_rec.at[a, p], fsdp=f).wait_send()

        every(chip, a, range(last))
        if a >= 2:
            for p in range(2 * T - 1):
                for way in range(2):
                    if p and p % 2 != 1 - way:
                        continue
                    on = t < T - 1 if way == 0 else t > 0

                    @pl.when((on & has(p)) if p else on)
                    def _():
                        remote(sources[a], sources[a], z_sem.at[a, p, way], z_rec.at[a, p], tp=t).wait_send()

    keeps = []
    for a in range(5):
        keep = pltpu.make_async_copy(sources[a], block_at(a, t, f), w_loc.at[a])
        keep.start()
        keeps.append(keep)
    spread_chip(0, 0)
    spread_chip(1, 0)
    for a in (2, 3, 4):
        line_start(a)

    relay(0, 0)
    take_chip(0, 0)
    keeps[0].wait()
    params = jnp.concatenate([par_s[ff] for ff in range(F)], axis=1)
    params_ref[...] = params
    start_in.wait()
    per_seq = rows // block

    def norm_one(index, _):
        s = index // per_seq
        here = pl.ds(pl.multiple_of(lax.rem(index, per_seq) * block, block), block)
        hat, _ = hat_rows(start_s[s, here, :].astype(f32))
        normed_s[s, here, :] = (hat * params_ref[0:1, :] + params_ref[2:3, :]).astype(bf)
        return 0

    lax.fori_loop(0, S * per_seq, norm_one, 0)
    normed_out = pltpu.make_async_copy(normed_s, normed_ref, out_sem.at[0])
    normed_out.start()

    relay(1, 0)
    take_chip(1, 0)
    keeps[1].wait()

    def kv_one(s, _):
        def one(index, _):
            here = pl.ds(pl.multiple_of(index * block, block), block)
            rows_in = normed_s[s, here, :]
            k = dot(rows_in, wl_s[1]).astype(bf)
            v = dot(rows_in, wl_s[2]).astype(bf)
            kv_s[s, here, :] = jnp.concatenate([k, v], axis=1)
            v_t = turn(v)
            for h in range(heads):
                ko_s[s, h, here, :] = k[:, column(h)]
                vto_s[s, h, :, here] = v_t[column(h)]
            return 0

        lax.fori_loop(0, per_seq, one, 0)
        return 0

    def kv_copy(s, d):
        return remote(
            kv_s.at[s], prev_s.at[s, pl.ds((far - d) * rows, rows), :],
            kv_sem.at[d, s], kv_rec.at[d, s], ctx=lax.rem(c + d, C),
        )

    for s in range(S):
        kv_one(s, 0)
        for d in range(1, far + 1):
            @pl.when(c + d < C)
            def _():
                kv_copy(s, d).start()

    def q_one(index, _):
        s = index // per_seq
        here = pl.ds(pl.multiple_of(lax.rem(index, per_seq) * block, block), block)
        q = dot(normed_s[s, here, :], wl_s[0]).astype(bf)
        q_s[s, here, :] = q
        q_t = turn(q.astype(f32) * 0.125)
        for h in range(heads):
            qt_s[s, h, :, here] = q_t[column(h)]
        return 0

    lax.fori_loop(0, S * per_seq, q_one, 0)
    outs = [
        pltpu.make_async_copy(q_s, q_ref, out_sem.at[1]),
        pltpu.make_async_copy(kv_s, kv_ref, out_sem.at[2]),
        pltpu.make_async_copy(wl_s, wl_ref, out_sem.at[4]),
    ]
    for copy in outs:
        copy.start()

    def own_part(s):
        for i in range(per_seq):
            span = column(i, block)
            low = low_ref[s, :, span] - far * rows
            top = i * block + lax.broadcasted_iota(jnp.int32, (1, block), 1)
            first = max(0, i * block - (DOC_MOST - 1)) // block * block
            many = (i + 1) * block - first
            place = first + lax.broadcasted_iota(jnp.int32, (many, 1), 0)
            allowed = (place >= low) & (place <= top)
            for h in range(heads):
                scores = dot(ko_s[s, h, first : first + many, :], qt_s[s, h, :, span])
                scores = jnp.where(allowed, scores, MASKED)
                m = jnp.max(scores, axis=0, keepdims=True)
                p = jnp.exp(scores - m)
                m_s[s, h : h + 1, span] = m
                l_s[s, h : h + 1, span] = jnp.sum(p, axis=0, keepdims=True)
                out_t_ref[s, column(h), span] = dot(vto_s[s, h, :, first : first + many], p.astype(bf))

    def far_part(s):
        for h in range(heads):
            kp_s[h] = prev_s[s, :, column(h)]
            vtp_s[h] = turn(prev_s[s, :, column(heads + h)])
        for i in range(per_seq):
            span = column(i, block)
            low = low_ref[s, :, span]
            first = max(0, far * rows + i * block - (DOC_MOST - 1)) // block * block
            if first >= far * rows:
                continue
            many = far * rows - first
            place = first + lax.broadcasted_iota(jnp.int32, (many, 1), 0)
            allowed = place >= low
            for h in range(heads):
                scores = dot(kp_s[h, first : first + many, :], qt_s[s, h, :, span])
                scores = jnp.where(allowed, scores, MASKED)
                old = m_s[s, h : h + 1, span]
                m = jnp.maximum(old, jnp.max(scores, axis=0, keepdims=True))
                p = jnp.exp(scores - m)
                alpha = jnp.exp(old - m)
                m_s[s, h : h + 1, span] = m
                l_s[s, h : h + 1, span] = alpha * l_s[s, h : h + 1, span] + jnp.sum(p, axis=0, keepdims=True)
                out_t_ref[s, column(h), span] = alpha * out_t_ref[s, column(h), span] + dot(
                    vtp_s[h, :, first : first + many], p.astype(bf)
                )

    def finish_part(s):
        for h in range(heads):
            out_t_ref[s, column(h), :] = out_t_ref[s, column(h), :] / l_s[s, h : h + 1, :]
            log_ref[s, h : h + 1, :] = m_s[s, h : h + 1, :] + jnp.log(l_s[s, h : h + 1, :])
        for tt in range(T):
            att_s[tt, s] = out_t_ref[s, :, column(tt, own_rows)].astype(bf)

    every_p = range(2 * T - 1)
    for a in (2, 3):
        line_step(a, 1)

    def own_loop(s, _):
        own_part(s)
        return 0

    lax.fori_loop(0, 1, own_loop, 0)
    line_step(2, 2)
    line_step(4, 1)
    line_step(3, 2)
    lax.fori_loop(1, S, own_loop, 0)
    for k in range(3, T):
        line_step(2, k)
    every(relay, 2, every_p)

    def wait_far(s):
        for d in range(1, far + 1):
            @pl.when(c >= d)
            def _():
                kv_copy(s, d).wait_recv()

            @pl.when(c < d)
            def _():
                prev_s[s, (far - d) * rows : (far - d + 1) * rows, :] = jnp.zeros((rows, 2 * hw), bf)

    at = [[None] * S for _ in range(T)]
    for s in range(S):
        if far:
            wait_far(s)

            @pl.when(c > 0)
            def _():
                far_part(s)
        finish_part(s)
        for d in range(1, T):
            peer = lax.rem(t + d, T)
            at[d][s] = go(
                remote(att_s.at[peer, s], att_ref.at[t, s], at_sem.at[d, s], at_rec.at[d, s], tp=peer)
            )
        own_at = pltpu.make_async_copy(att_s.at[t, s], att_ref.at[t, s], at_loc.at[s])
        own_at.start()
        at[0][s] = own_at
        if s == 0:
            line_step(4, 2)
            for k in range(3, T):
                line_step(3, k)
            every(relay, 3, every_p)
    prev_out = pltpu.make_async_copy(prev_s, prev_ref, out_sem.at[3])
    if far:
        prev_out.start()
    for k in range(3, T):
        line_step(4, k)
    every(take_chip, 2, every_p)
    keeps[2].wait()
    for tt in range(T):
        for ff in range(F):
            ow_ref[column(tt, hw), column(ff, shard)] = wo_s[tt, ff]
    every(relay, 4, every_p)
    for a in (3, 4):
        every(take_chip, a, every_p)
        keeps[a].wait()
    for s in range(S):
        at[0][s].wait()
        for d in range(1, T):
            at[d][s].wait_recv()
    normed_out.wait()
    for copy in outs:
        copy.wait()
    if far:
        prev_out.wait()
    for copy in pending:
        copy.wait_send()
    for a in range(5):
        drain(a)
    for s in range(S):
        for d in range(1, far + 1):
            @pl.when(c + d < C)
            def _():
                kv_copy(s, d).wait_send()


def front(start, low, wq, wo, wf, wp, params, block, far, counts):
    F, C, T = counts
    S, rows, width = start.shape
    hw = wq.shape[2]
    shard = wq.shape[1]
    heads = hw // HEAD_DIM
    hidden = wf.shape[1]
    bf, f32 = jnp.bfloat16, jnp.float32
    vmem = pl.BlockSpec(memory_space=pltpu.VMEM)
    anywhere = pl.BlockSpec(memory_space=pl.ANY)
    dma = lambda *shape: pltpu.SemaphoreType.DMA(shape)
    past = max(far, 1) * rows
    shape = jax.ShapeDtypeStruct
    return pl.pallas_call(
        functools.partial(front_kernel, counts, block),
        in_specs=[anywhere, vmem, anywhere, anywhere, anywhere, anywhere, anywhere],
        out_specs=[
            anywhere, anywhere, anywhere, anywhere, vmem, vmem, anywhere, anywhere, vmem, anywhere, anywhere, vmem
        ],
        out_shape=[
            shape((T, S, hw, rows // T), bf),
            shape((S, rows, hw), bf),
            shape((S, rows, 2 * hw), bf),
            shape((S, past, 2 * hw), bf),
            shape((S, hw, rows), f32),
            shape((S, 8, rows), f32),
            shape((S, rows, width), bf),
            shape((3, F * shard, hw), bf),
            shape((T * hw, F * shard), bf),
            shape((F * shard, T * hidden), bf),
            shape((F * shard, T * hidden), bf),
            shape((8, F * shard), f32),
        ],
        scratch_shapes=[
            pltpu.VMEM((S, rows, width), bf),
            pltpu.VMEM((S, rows, width), bf),
            pltpu.VMEM((3, F * shard, hw), bf),
            pltpu.VMEM((T, F, hw, shard), bf),
            pltpu.VMEM((F, 8, shard), f32),
            pltpu.VMEM((S, rows, hw), bf),
            pltpu.VMEM((S, rows, 2 * hw), bf),
            pltpu.VMEM((S, past, 2 * hw), bf),
            pltpu.VMEM((S, heads, HEAD_DIM, rows), bf),
            pltpu.VMEM((S, heads, rows, HEAD_DIM), bf),
            pltpu.VMEM((S, heads, HEAD_DIM, rows), bf),
            pltpu.VMEM((heads, past, HEAD_DIM), bf),
            pltpu.VMEM((heads, HEAD_DIM, past), bf),
            pltpu.VMEM((S, 8, rows), f32),
            pltpu.VMEM((S, 8, rows), f32),
            pltpu.VMEM((T, S, hw, rows // T), bf),
            dma(1), dma(5), dma(5),
            dma(5, 2 * T, 2), dma(5, 2 * T), dma(5, 2 * T), dma(5, 2 * T), dma(5, 2 * T), dma(5, 2 * T), dma(5, 2 * T),
            dma(5, 2 * T),
            dma(far + 1, S), dma(far + 1, S), dma(T, S), dma(T, S), dma(S),
        ],
        compiler_params=pltpu.CompilerParams(
            vmem_limit_bytes=VMEM_LIMIT, collective_id=1, has_side_effects=True
        ),
        cost_estimate=pl.CostEstimate(flops=8 * 10**9, bytes_accessed=64 << 20, transcendentals=8 << 20),
    )(start, low, wq, wo, wf, wp, params)


def padded(size):
    return -(-size // 128) * 128


def add_rows(target, sources, rows_at_once=16):
    def one(i, _):
        here = pl.ds(pl.multiple_of(i * rows_at_once, rows_at_once), rows_at_once)
        total = target[here, :].astype(jnp.float32)
        for source in sources:
            total = total + source[here, :].astype(jnp.float32)
        target[here, :] = total.astype(target.dtype)
        return 0

    lax.fori_loop(0, target.shape[0] // rows_at_once, one, 0)


def gelu_parts(x):
    square = x * x
    th = jnp.tanh(0.7978845608028654 * (x + 0.044715 * (square * x)))
    half = 0.5 * (1.0 + th)
    slope = half + (0.5 * x) * (1.0 - th * th) * (0.7978845608028654 * (1.0 + (3 * 0.044715) * square))
    return x * half, slope


def back_kernel(
    sizes, block, far, step_cols,
    att_ref, start_ref, grad_ref, outw_ref, fc_ref, pj_ref, params_ref,
    q_ref, kv_ref, prev_ref, low_ref, out_t_ref, log_ref, normed_ref, wl_ref, pick_ref,
    output_ref, dstart_ref, gw_ref, gq_ref, small_ref,
    start_s, mid_s, grad_s, ob_s, gbuf, rcore, rx, rc, rz, g2, r2c, r2x,
    da_s, da_r, dp_s, rec_s, kv_s, dq_s, rs_r, gq_s, rgq, rgc, sm_s, rst, rsc, rsf,
    in_sem, w_sem, core_sem, core_rec, x_sem, x_rec, c2_sem, c2_rec, x2_sem, x2_rec,
    c_sem, c_rec, z_sem, z_rec, b_sem, b_rec, da_sem, da_rec, dp_sem, dp_rec,
    rs_sem, rs_rec, ag_sem, ag_rec, gq_sem, gq_rec, gc_sem, gc_rec,
    st_sem, st_rec, sc_sem, sc_rec, sf_sem, sf_rec, loc_sem, wl_sem, credit,
):
    F, C, T = sizes
    f, c, t = lax.axis_index("fsdp"), lax.axis_index("ctx"), lax.axis_index("tp")
    S, rows, hw = q_ref.shape
    heads = hw // HEAD_DIM
    width = start_s.shape[2]
    own_rows = rows // T
    tokens = S * own_rows
    shard = gbuf.shape[1]
    hidden = fc_ref.shape[1] // T
    wide = 2 * hidden
    per_seq = rows // block
    bf, f32 = jnp.bfloat16, jnp.float32
    sib, across = f ^ 1, f ^ 2

    def remote(src, dst, send, recv, **where):
        return pltpu.make_async_remote_copy(
            src_ref=src, dst_ref=dst, send_sem=send, recv_sem=recv, device_id=where, device_id_type=MESH
        )

    pending = []

    def go(copy, like):
        copy.start()
        pending.append(like)

    def landed(ref, sem):
        remote(ref, ref, b_rec, sem, fsdp=f).wait_recv()

    def sent(ref, sem):
        remote(ref, ref, sem, b_rec, fsdp=f).wait_send()

    def tp_peer(d):
        return lax.rem(t + d, T)

    def tp_source(d):
        return lax.rem(t + T - d, T)

    def rows_of(owner):
        return pl.ds(pl.multiple_of(owner * own_rows, own_rows), own_rows)

    ag_own, ag_whole = (ob_s, ob_s), (output_ref, dstart_ref)

    def ag_copy(a, s, owner, step, way):
        whole = ag_whole[a].at[s, rows_of(owner), :]
        src = ag_own[a].at[s] if step == 0 else whole
        return lambda to: remote(src, whole, ag_sem.at[a, s, step, way], ag_rec.at[a, s, step, way], tp=to)

    def ag_keep(a, s):
        return pltpu.make_async_copy(ag_own[a].at[s], ag_whole[a].at[s, rows_of(t), :], loc_sem.at[a, s])

    def ag_start(a, s):
        @pl.when(t < T - 1)
        def _():
            ag_copy(a, s, t, 0, 0)(t + 1).start()

        @pl.when(t > 0)
        def _():
            ag_copy(a, s, t, 0, 1)(t - 1).start()

        ag_keep(a, s).start()

    def ag_step(a, s, step):
        @pl.when(t >= step)
        def _():
            ag_copy(a, s, t - step, step - 1, 0)(t).wait_recv()

        @pl.when((t >= step) & (t < T - 1))
        def _():
            ag_copy(a, s, t - step, step, 0)(t + 1).start()

        @pl.when(t + step <= T - 1)
        def _():
            ag_copy(a, s, t + step, step - 1, 1)(t).wait_recv()

        @pl.when((t + step <= T - 1) & (t > 0))
        def _():
            ag_copy(a, s, t + step, step, 1)(t - 1).start()

    def ag_drain(a, s, first):
        if not first:
            ag_keep(a, s).wait()
        for step in range(first, T - 1 if first or a else 1):
            @pl.when((t >= step) & (t < T - 1))
            def _():
                ag_copy(a, s, t - step, step, 0)(t + 1).wait_send()

            @pl.when((t + step <= T - 1) & (t > 0))
            def _():
                ag_copy(a, s, t + step, step, 1)(t - 1).wait_send()

    across_at = lambda b: T + b
    main = pl.ds(0, wide)

    def core_send(b):
        slot = b % 2
        if b >= 2:
            pl.semaphore_wait(credit, 1)
        for k in range(2):
            remote(
                gbuf.at[2 * T + 2 * slot + k, :, main], rcore.at[slot, k],
                core_sem.at[b, k], core_rec.at[b, k], fsdp=sib,
            ).start()

    def core_add(b):
        slot = b % 2
        landed(rcore.at[slot, 1], core_rec.at[b, 1])
        add_rows(gbuf.at[across_at(b), :, main], [rcore.at[slot, 1]])
        out = gbuf.at[across_at(b), :, main]
        go(
            remote(out, rx.at[b, :, main], x_sem.at[b], x_rec.at[b], fsdp=across),
            lambda: (rx.at[b, :, main], x_sem.at[b]),
        )
        landed(rcore.at[slot, 0], core_rec.at[b, 0])
        add_rows(gbuf.at[b, :, main], [rcore.at[slot, 0]])
        if b < T - 2:
            pl.semaphore_signal(credit, inc=1, device_id={"fsdp": sib}, device_id_type=MESH)

    held = [b // C for b in range(T)]

    def ctx_copy(b, d, to):
        return remote(gbuf.at[b], rc.at[held[b], d - 1], c_sem.at[b], c_rec.at[b, d], ctx=to)

    def cross_add(b):
        landed(rx.at[b, :, main], x_rec.at[b])
        add_rows(gbuf.at[b, :, main], [rx.at[b, :, main]])

    def ctx_send(b):
        owner = b % C
        for d in range(1, C):
            @pl.when(lax.rem(c + d, C) == owner)
            def _():
                ctx_copy(b, d, owner).start()

    def ctx_wait(b):
        @pl.when(c == b % C)
        def _():
            for d in range(1, C):
                ctx_copy(b, d, c).wait_recv()
            if C > 1:
                add_rows(gbuf.at[b], [rc.at[held[b], d - 1] for d in range(1, C)])

    def z_round(b, step):
        def hop(to, way):
            return remote(gbuf.at[b], rz.at[held[b], way], z_sem.at[b], z_rec.at[b, way], tp=to)

        def visit(way, before, here):
            @pl.when((c == b % C) & here)
            def _():
                if step:
                    hop(t, way).wait_recv()
                    add_rows(gbuf.at[b], [rz.at[held[b], way]])

                @pl.when(before)
                def _():
                    hop(t - 1 if way == 0 else t + 1, way).start()

        if T - 1 - step >= b and b < T - 1:
            visit(0, t > b, t == T - 1 - step)
        if step <= b and b > 0:
            visit(1, t < b, t == step)

    def feed_phase(att_s, outw_s, w_s, x_s, nm_s, nmt_s, gt_s, acc_s):
        steps = hidden // step_cols
        ring = w_s.shape[0]
        total_steps = 2 * T * steps

        def stream(n):
            at = pl.ds(pl.multiple_of(lax.rem(n, T * steps) * step_cols, step_cols), step_cols)
            slot = lax.rem(n, ring)
            return [
                pltpu.make_async_copy(ref.at[:, at], w_s.at[slot, k], w_sem.at[slot, k])
                for k, ref in enumerate((fc_ref, pj_ref))
            ]

        def take(n):
            for copy in stream(n):
                copy.wait()

            @pl.when(n + ring - 1 < total_steps)
            def _():
                for copy in stream(n + ring - 1):
                    copy.start()

            return lax.rem(n, ring)

        loads = [
            pltpu.make_async_copy(att_ref, dq_s, in_sem.at[0]),
            pltpu.make_async_copy(outw_ref, outw_s, in_sem.at[1]),
            pltpu.make_async_copy(start_ref, start_s, in_sem.at[2]),
            pltpu.make_async_copy(grad_ref, grad_s, in_sem.at[3]),
        ]
        for copy in loads:
            copy.start()
        for n in range(ring - 1):
            for copy in stream(n):
                copy.start()

        barrier = pltpu.get_barrier_semaphore()
        peers = 0
        for d in range(1, F):
            pl.semaphore_signal(barrier, inc=1, device_id={"fsdp": f ^ d}, device_id_type=MESH)
            peers += 1
        for d in range(1, T):
            pl.semaphore_signal(barrier, inc=1, device_id={"tp": tp_peer(d)}, device_id_type=MESH)
            peers += 1
        for d in range(1, C):
            pl.semaphore_signal(barrier, inc=1, device_id={"ctx": lax.rem(c + d, C)}, device_id_type=MESH)
            peers += 1
        pl.semaphore_wait(barrier, peers)

        for copy in loads:
            copy.wait()
        mid = start_s[...].reshape(tokens, width).astype(f32)
        for g in range(T):
            for s in range(S):
                att_s[g, column(s, own_rows), :] = turn(dq_s[g, s])
            mid = mid + dot(att_s[g], outw_s[column(g, hw), :])
        mid_s[...] = mid
        hat, _ = hat_rows(mid)
        nm = hat * params_ref[1:2] + params_ref[3:4]
        nm_s[...] = nm.astype(bf)
        nmt_s[...] = turn_back(nm)
        gt_s[...] = turn(grad_s[...])
        acc_s[...] = jnp.zeros_like(acc_s)

        def forward(j, _):
            slot = take(j)
            x = dot(nm_s[...], w_s[slot, 0])
            x_s[j] = x
            act, _ = gelu_parts(x)
            acc_s[...] += dot(act.astype(bf), w_s[slot, 1], ((1,), (1,)))
            return 0

        lax.fori_loop(0, T * steps, forward, 0)
        ob_s[...] = (mid_s[...] + acc_s[...]).astype(bf).reshape(S, own_rows, width)
        for s in range(S):
            ag_start(0, s)
        acc_s[...] = jnp.zeros_like(acc_s)

        for n in range(T):
            if n >= 2:
                for k in range(2):
                    sent(rcore.at[0, 0], core_sem.at[n - 2, k])
            slot = n % 2

            def backward(j, _):
                here = pl.ds(pl.multiple_of(j * step_cols, step_cols), step_cols)
                there = pl.ds(pl.multiple_of(hidden + j * step_cols, step_cols), step_cols)
                at_w = take(T * steps + n * steps + j)
                fc, proj = w_s[at_w, 0], w_s[at_w, 1]
                act, slope = gelu_parts(x_s[n * steps + j])
                act = act.astype(bf)
                d_exp = (slope * dot(grad_s[...], proj)).astype(bf)
                acc_s[...] += dot(d_exp, fc, ((1,), (1,)))
                d_fc = dot(nmt_s[...], d_exp).astype(bf)
                d_proj = dot(gt_s[...], act).astype(bf)
                for ff in range(F):
                    r = f ^ ff
                    odd, half = lax.rem(r, 2), r // 2
                    at = (1 - odd) * (half * T + n) + odd * (2 * T + 2 * slot + half)
                    gbuf[at, :, here] = d_fc[column(ff, shard)]
                    gbuf[at, :, there] = d_proj[column(ff, shard)]
                return 0

            lax.fori_loop(0, steps, backward, 0)
            core_send(n)
            if n:
                core_add(n - 1)

        mid = mid_s[...]
        hat, inv = hat_rows(mid)
        d_nm = acc_s[...]
        d_mid = grad_s[...].astype(f32) + norm_back(hat, inv, params_ref[1:2], d_nm)
        d_mid_t = turn_back(d_mid)
        for g in range(T):
            d_att = dot(outw_s[column(g, hw), :], d_mid_t).astype(bf)
            for s in range(S):
                da_s[g, s] = d_att[:, column(s, own_rows)]
        for s in range(S):
            for d in range(1, T):
                go(
                    remote(da_s.at[tp_peer(d), s], da_r.at[t, s], da_sem.at[d, s], da_rec.at[d, s], tp=tp_peer(d)),
                    lambda d=d, s=s: (da_s.at[0, s], da_sem.at[d, s]),
                )
        sm_s[...] = jnp.zeros_like(sm_s)
        sm_s[1:2, :] = jnp.sum(d_nm * hat, axis=0, keepdims=True)
        sm_s[3:4, :] = jnp.sum(d_nm, axis=0, keepdims=True)
        mid_s[...] = d_mid
        if g2.shape[3] > hw:
            g2[:, :, :, hw:] = jnp.zeros(g2.shape[:3] + (g2.shape[3] - hw,), bf)
        for g in range(T):
            d_out = dot(d_mid_t, att_s[g]).astype(bf)
            for ff in range(F):
                g2[f ^ ff, g, :, :hw] = d_out[column(ff, shard)]
        core_add(T - 1)

    bf_mem = lambda *shape: pltpu.VMEM(shape, bf)
    f32_mem = lambda *shape: pltpu.VMEM(shape, f32)
    pl.run_scoped(
        feed_phase,
        bf_mem(T, tokens, hw), bf_mem(T * hw, width), bf_mem(3, 2, width, step_cols),
        f32_mem(T * hidden // step_cols, tokens, step_cols),
        bf_mem(tokens, width), bf_mem(width, tokens), bf_mem(width, tokens), f32_mem(tokens, width),
    )

    for k in range(2):
        out = g2.at[1 + 2 * k]
        go(
            remote(out, r2c.at[k], c2_sem.at[k], c2_rec.at[k], fsdp=sib),
            lambda k=k: (r2c.at[k], c2_sem.at[k]),
        )

    def dp_copy(d, s):
        return remote(
            dp_s.at[far - d, s], rec_s.at[d - 1, s], dp_sem.at[d, s], dp_rec.at[d, s], ctx=lax.rem(c + C - d, C)
        )

    def sums_along(snd, wl_s):
        def kv_sum(s):
            for d in range(1, far + 1):
                @pl.when(c + d < C)
                def _():
                    dp_copy(d, s).wait_recv()
                    for g in range(T):
                        kv_s[g, s] = (kv_s[g, s].astype(f32) + rec_s[d - 1, s, g].astype(f32)).astype(bf)

        def partials(s):
            if s == 0:
                pltpu.make_async_copy(wl_ref, wl_s, wl_sem).wait()

            def one(o, _):
                total = dot(wl_s[0], dq_s[o, s])
                for j in (1, 2):
                    total = total + dot(wl_s[j], kv_s[o, s, column(j - 1, hw), :])
                snd[s, o] = total.astype(bf)
                return 0

            lax.fori_loop(0, T, one, 0)

        def rs_copy(s, o, way, at):
            to = at - 1 if way == 0 else at + 1
            slot = T if (to == o and way == 1) else o
            return remote(
                snd.at[s, o], rs_r.at[s, slot], rs_sem.at[s, o], rs_rec.at[s, o, way], tp=t - 1 if way == 0 else t + 1
            )

        def rs_slot(s, k):
            for at in range(T):
                for way, o, begins in ((0, k - (T - 1 - at), at == T - 1), (1, T - 1 + at - k, at == 0)):
                    if not (0 <= o <= at if way == 0 else at <= o <= T - 1):
                        continue

                    @pl.when(t == at)
                    def _():
                        if not begins:
                            landed(rs_r.at[s, T if (o == at and way == 1) else o], rs_rec.at[s, o, way])
                        if o != at:
                            if not begins:
                                add_rows(snd.at[s, o], [rs_r.at[s, o]], 128)
                            before = o - 1 if way == 0 else o + 1
                            if 0 <= before < T:
                                sent(snd.at[s, before], rs_sem.at[s, before])
                            rs_copy(s, o, way, at).start()

        return kv_sum, partials, rs_slot

    def attention_phase(
        snd, wl_s, q_s, kvo_s, prv_s, ot_s, k_h, kt_h, v_h, q_h, qt_h, g_h, gt_h, dqt_s, dk_s, dv_s, del_s
    ):
        kv_sum, partials, rs_slot = sums_along(snd, wl_s)

        def loads(s):
            return [
                pltpu.make_async_copy(ref.at[s], mem, in_sem.at[k])
                for k, (ref, mem) in enumerate(((q_ref, q_s), (kv_ref, kvo_s), (out_t_ref, ot_s), (prev_ref, prv_s)))
            ]

        for copy in loads(0):
            copy.start()
        for k in (1, 0):
            landed(r2c.at[k], c2_rec.at[k])
            for b in range(T):
                add_rows(g2.at[2 * k, b], [r2c.at[k, b]])
            if k:
                go(remote(g2.at[2], r2x, x2_sem, x2_rec, fsdp=across), lambda: (r2x, x2_sem))

        def keys(s):
            for h in range(heads):
                q = q_s[:, column(h)].astype(f32) * 0.125
                q_h[h] = q.astype(bf)
                qt_h[h] = turn_back(q)
                if far:
                    k = prv_s[:, column(h)]
                    k_h[h, : far * rows] = k
                    kt_h[h, :, : far * rows] = turn(k)
                    v_h[h, : far * rows] = prv_s[:, column(heads + h)]
                k = kvo_s[:, column(h)]
                k_h[h, far * rows :] = k
                kt_h[h, :, far * rows :] = turn(k)
                v_h[h, far * rows :] = kvo_s[:, column(heads + h)]

        def grads(s):
            da_r[t, s] = da_s[t, s]
            for d in range(1, T):
                landed(da_r.at[tp_source(d), s], da_rec.at[d, s])
            for h in range(heads):
                for g in range(T):
                    gt_h[h, :, column(g, own_rows)] = da_r[g, s, column(h), :]
                g_t = gt_h[h].astype(f32)
                g_h[h] = turn_back(g_t)
                del_s[h : h + 1, :] = jnp.sum(g_t * ot_s[column(h), :], axis=0, keepdims=True)
            dqt_s[...] = jnp.zeros_like(dqt_s)

        def part(s, h, base, count, own):
            spot = pl.ds(pl.multiple_of(h * HEAD_DIM, HEAD_DIM), HEAD_DIM)
            dk_s[:count] = jnp.zeros((count, HEAD_DIM), f32)
            dv_s[:count] = jnp.zeros((count, HEAD_DIM), f32)
            for i in range(per_seq):
                span = column(i, block)
                reach = far * rows + i * block
                first = max(0, reach - (DOC_MOST - 1) - base) // block * block
                last = min(count, reach + block - base)
                if first >= last:
                    continue
                low = low_ref[s, :, span] - base
                place = first + lax.broadcasted_iota(jnp.int32, (last - first, 1), 0)
                allowed = place >= low
                if own:
                    allowed = allowed & (place <= i * block + lax.broadcasted_iota(jnp.int32, (1, block), 1))
                here = slice(base + first, base + last)
                scores = dot(k_h[h, here, :], qt_h[h, :, span])
                p = jnp.exp(jnp.where(allowed, scores - log_ref[s, pl.ds(h, 1), span], MASKED))
                ds = (p * (dot(v_h[h, here, :], gt_h[h, :, span]) - del_s[pl.ds(h, 1), span])).astype(bf)
                dv_s[first:last] += dot(p.astype(bf), g_h[h, span, :])
                dk_s[first:last] += dot(ds, q_h[h, span, :])
                dqt_s[spot, span] += dot(kt_h[h, :, here], ds)
            return spot, pl.ds(pl.multiple_of(hw + h * HEAD_DIM, HEAD_DIM), HEAD_DIM)

        def far_part(s):
            def one(h, _):
                k_at, v_at = part(s, h, 0, far * rows, False)
                for at, source in ((k_at, dk_s), (v_at, dv_s)):
                    turned = source[: far * rows].T.astype(bf)
                    for j in range(far):
                        for g in range(T):
                            dp_s[j, s, g, at, :] = turned[:, column(j * T + g, own_rows)]
                return 0

            lax.fori_loop(0, heads, one, 0)

        def own_part(s):
            def one(h, _):
                k_at, v_at = part(s, h, far * rows, rows, True)
                for at, source in ((k_at, dk_s), (v_at, dv_s)):
                    turned = source[:rows].T.astype(bf)
                    for g in range(T):
                        kv_s[g, s, at, :] = turned[:, column(g, own_rows)]
                return 0

            lax.fori_loop(0, heads, one, 0)

        for s in range(S):
            for copy in loads(s):
                copy.wait()
            keys(s)
            grads(s)
            if s + 1 < S:
                for copy in loads(s + 1):
                    copy.start()
            if s == 0:
                for other in range(S):
                    ag_step(0, other, 1)
            if far:
                @pl.when(c > 0)
                def _():
                    far_part(s)

                for d in range(1, far + 1):
                    @pl.when(c >= d)
                    def _():
                        dp_copy(d, s).start()
            if s:
                rs_slot(s - 1, 1)
            else:
                cross_add(0)
            own_part(s)
            for g in range(T):
                dq_s[g, s] = (0.125 * dqt_s[:, column(g, own_rows)]).astype(bf)
            if s:
                rs_slot(s - 1, 2)
            if s < T - 2:
                for other in range(S):
                    ag_step(0, other, s + 2)
            if s + 1 < T:
                cross_add(s + 1)
            kv_sum(s)
            partials(s)
            rs_slot(s, 0)

    def last_phase(snd, wl_s, normed_s, gq_acc, tot_s):
        kv_sum, partials, rs_slot = sums_along(snd, wl_s)
        normed_in = pltpu.make_async_copy(normed_ref, normed_s, in_sem.at[0])
        normed_in.start()

        gain = params_ref[0:1]

        def norm_stage(s):
            tot_s[...] = snd[s, t].astype(f32)

            @pl.when(t < T - 1)
            def _():
                tot_s[...] += rs_r[s, t].astype(f32)

            @pl.when(t > 0)
            def _():
                tot_s[...] += rs_r[s, T].astype(f32)

            d_normed = tot_s[...].T
            hat, inv = hat_rows(start_s[s].astype(f32))
            value = mid_s[column(s, own_rows), :] + norm_back(hat, inv, gain, d_normed)
            ag_drain(0, s, 0)
            ob_s[s] = value.astype(bf)
            ag_start(1, s)
            sm_s[0:1, :] += jnp.sum(d_normed * hat, axis=0, keepdims=True)
            sm_s[2:3, :] += jnp.sum(d_normed, axis=0, keepdims=True)

        for k in range(3, T):
            rs_slot(0, k)
        norm_stage(0)
        landed(r2x, x2_rec)
        side = pl.ds(wide, g2.shape[3])
        for b in range(T):
            gbuf[b, :, side] = (g2[0, b].astype(f32) + r2x[b].astype(f32)).astype(bf)
        for b in range(min(S + 1, T)):
            ctx_send(b)

        normed_in.wait()
        gq_acc[...] = jnp.zeros_like(gq_acc)
        for s in range(S):

            def one(o, _):
                near = normed_s[s, rows_of(o), :]
                gq_acc[:hw, :] += dot(dq_s[o, s], near)
                gq_acc[hw:, :] += dot(kv_s[o, s], near)
                return 0

            lax.fori_loop(0, T, one, 0)
        for k in range(F):
            gq_s[k] = gq_acc[:, column(k, shard)].astype(bf)
        for d in range(1, F):
            go(
                remote(gq_s.at[f ^ d], rgq.at[d - 1], gq_sem.at[d], gq_rec.at[d], fsdp=f ^ d),
                lambda d=d: (gq_s.at[0], gq_sem.at[d]),
            )
        for b in range(min(S + 1, T), T):
            cross_add(b)
            ctx_send(b)
        for s in range(1, S):
            for k in range(1, T):
                rs_slot(s, k)
                if k == T - 2:
                    ag_step(1, 0, 1)
            norm_stage(s)

        thoughts = jnp.zeros((pick_ref.shape[1], width), f32)
        for s in range(S):
            thoughts = thoughts + dot(pick_ref[s], ob_s[s])
        sm_s[8:, :] = thoughts
        for d in range(1, T):
            go(
                remote(sm_s, rst.at[d], st_sem.at[d], st_rec.at[d], tp=tp_peer(d)),
                lambda d=d: (sm_s, st_sem.at[d]),
            )
        for b in range(T):
            ctx_wait(b)
            z_round(b, 0)

        gq_sum = gq_s[f].astype(f32)
        for d in range(1, F):
            landed(rgq.at[d - 1], gq_rec.at[d])
            gq_sum = gq_sum + rgq[d - 1].astype(f32)
        rgc[c] = gq_sum.astype(bf)
        for d in range(1, C):
            go(
                remote(rgc.at[c], rgc.at[c], gc_sem.at[d], gc_rec.at[d], ctx=lax.rem(c + d, C)),
                lambda d=d: (rgc.at[0], gc_sem.at[d]),
            )

        for d in range(1, T):
            landed(rst.at[d], st_rec.at[d])
        rst[0] = sm_s[...]
        total = jnp.zeros(sm_s.shape, f32)
        for k in range(T):
            total = total + rst[lax.rem(t + T - k, T)]
        rsc[c] = total
        for d in range(1, C):
            go(
                remote(rsc.at[c], rsc.at[c], sc_sem.at[d], sc_rec.at[d], ctx=lax.rem(c + d, C)),
                lambda d=d: (rsc.at[0], sc_sem.at[d]),
            )
        for step in range(1, T):
            if step > 1:
                ag_step(1, 0, step)
            for s in range(1, S):
                ag_step(1, s, step)
            for b in range(T):
                z_round(b, step)
            if step == 1:
                for d in range(1, C):
                    landed(rsc.at[0], sc_rec.at[d])
                total = jnp.zeros(sm_s.shape, f32)
                for k in range(C):
                    total = total + rsc[k]
                small_ref[8:, :] = total[8:]
                rsf[f] = total
                for d in range(1, F):
                    go(
                        remote(rsf.at[f], rsf.at[f], sf_sem.at[d], sf_rec.at[d], fsdp=f ^ d),
                        lambda d=d: (rsf.at[0], sf_sem.at[d]),
                    )
        for d in range(1, F):
            landed(rsf.at[0], sf_rec.at[d])
        norms = jnp.zeros((8, sm_s.shape[1]), f32)
        for k in range(F):
            norms = norms + rsf[k, 0:8, :]
        small_ref[0:8, :] = norms

        for d in range(1, C):
            landed(rgc.at[0], gc_rec.at[d])
        total = jnp.zeros(gq_ref.shape, f32)
        for k in range(C):
            total = total + rgc[k].astype(f32)
        gq_ref[...] = total
        for o in range(T):
            @pl.when((t == o + 1) | (t == o - 1))
            def _():
                for s in range(S):
                    sent(snd.at[s, o], rs_sem.at[s, o])

    def after_feed(snd, wl_s):
        wl_in = pltpu.make_async_copy(wl_ref, wl_s, wl_sem)
        wl_in.start()
        pl.run_scoped(
            functools.partial(attention_phase, snd, wl_s),
            bf_mem(rows, hw), bf_mem(rows, 2 * hw), bf_mem(max(far, 1) * rows, 2 * hw), f32_mem(hw, rows),
            bf_mem(heads, (far + 1) * rows, HEAD_DIM), bf_mem(heads, HEAD_DIM, (far + 1) * rows),
            bf_mem(heads, (far + 1) * rows, HEAD_DIM),
            bf_mem(heads, rows, HEAD_DIM), bf_mem(heads, HEAD_DIM, rows),
            bf_mem(heads, rows, HEAD_DIM), bf_mem(heads, HEAD_DIM, rows),
            f32_mem(hw, rows), f32_mem(max(far, 1) * rows, HEAD_DIM), f32_mem(max(far, 1) * rows, HEAD_DIM),
            f32_mem(8, rows),
        )
        pl.run_scoped(
            functools.partial(last_phase, snd, wl_s),
            bf_mem(S, rows, width), f32_mem(3 * hw, width), f32_mem(width, own_rows),
        )

    pl.run_scoped(after_feed, bf_mem(S, T, width, own_rows), bf_mem(3, width, hw))

    for b in range(T):
        owner = b % C
        final = lambda d: remote(gbuf.at[b], rx.at[b], b_sem.at[d], b_rec, ctx=lax.rem(owner + d, C))

        @pl.when((t == b) & (c == owner))
        def _():
            for d in range(1, C):
                final(d).start()
            gw_ref[...] = gbuf[b]
            for d in range(1, C):
                final(d).wait_send()

        if C > 1:
            @pl.when((t == b) & (c != owner))
            def _():
                final(1).wait_recv()
                gw_ref[...] = rx[b]

    for like in pending:
        sent(*like())
    for n in range(max(T - 2, 0), T):
        for k in range(2):
            sent(rcore.at[0, 0], core_sem.at[n, k])
    for b in range(T):
        owner = b % C
        if C > 1:
            @pl.when(c != owner)
            def _():
                ctx_copy(b, 1, owner).wait_send()

        @pl.when((c == owner) & (t != b))
        def _():
            remote(gbuf.at[b], rz.at[held[b], 0], z_sem.at[b], z_rec.at[b, 0], tp=t).wait_send()
    for s in range(S):
        for d in range(1, far + 1):
            @pl.when(c >= d)
            def _():
                dp_copy(d, s).wait_send()
        ag_drain(0, s, 1)
        ag_drain(1, s, 0)


def back(att, start, grad, out_w, fc, proj_t, params, q, kv, prev, low, out_t, logs, normed, wl, pick, block, far, counts):
    F, C, T = counts
    S, rows, hw = q.shape
    width = normed.shape[2]
    own_rows = rows // T
    tokens = S * own_rows
    shard = width // F
    hidden = fc.shape[1] // T
    cols = padded(hw)
    wide = 2 * hidden + cols
    bf, f32 = jnp.bfloat16, jnp.float32
    extra = 8 + pick.shape[1]
    mine = -(-T // C)
    dists = max(far, 1)
    vmem = pl.BlockSpec(memory_space=pltpu.VMEM)
    anywhere = pl.BlockSpec(memory_space=pl.ANY)
    dma = lambda *shape: pltpu.SemaphoreType.DMA(shape)
    one = pltpu.SemaphoreType.DMA
    shape = jax.ShapeDtypeStruct
    b16 = lambda *size: pltpu.VMEM(size, bf)
    b32 = lambda *size: pltpu.VMEM(size, f32)
    return pl.pallas_call(
        functools.partial(back_kernel, counts, block, far, 256),
        in_specs=[anywhere] * 6 + [vmem] + [anywhere] * 3 + [vmem, anywhere, vmem, anywhere, anywhere, vmem],
        out_specs=[anywhere, anywhere, vmem, vmem, vmem],
        out_shape=[
            shape((S, rows, width), bf),
            shape((S, rows, width), bf),
            shape((shard, wide), bf),
            shape((3 * hw, shard), f32),
            shape((extra, width), f32),
        ],
        scratch_shapes=[
            b16(S, own_rows, width), b32(tokens, width), b16(tokens, width), b16(S, own_rows, width),
            b16(2 * T + 4, shard, wide), b16(2, 2, shard, 2 * hidden), b16(T, shard, wide),
            b16(mine, max(C - 1, 1), shard, wide), b16(mine, 2, shard, wide),
            b16(4, T, shard, cols), b16(2, T, shard, cols), b16(T, shard, cols),
            b16(T, S, hw, own_rows), b16(T, S, hw, own_rows),
            b16(dists, S, T, 2 * hw, own_rows), b16(dists, S, T, 2 * hw, own_rows),
            b16(T, S, 2 * hw, own_rows), b16(T, S, hw, own_rows),
            b16(S, T + 1, width, own_rows),
            b16(F, 3 * hw, shard), b16(F - 1, 3 * hw, shard), b16(C, 3 * hw, shard),
            b32(extra, width), b32(T, extra, width), b32(C, extra, width), b32(F, extra, width),
            dma(4), dma(3, 2), dma(T, 2), dma(T, 2), dma(T), dma(T), dma(2), dma(2), one, one,
            dma(T), dma(T, C), dma(T), dma(T, 2), dma(C), one, dma(T, S), dma(T, S), dma(far + 1, S), dma(far + 1, S),
            dma(S, T), dma(S, T, 2), dma(2, S, T, 2), dma(2, S, T, 2), dma(F), dma(F), dma(C), dma(C),
            dma(T), dma(T), dma(C), dma(C), dma(F), dma(F), dma(2, S), one, pltpu.SemaphoreType.REGULAR,
        ],
        compiler_params=pltpu.CompilerParams(
            vmem_limit_bytes=VMEM_LIMIT, collective_id=2, has_side_effects=True
        ),
        cost_estimate=pl.CostEstimate(flops=36 * 10**9, bytes_accessed=100 << 20, transcendentals=16 << 20),
    )(att, start, grad, out_w, fc, proj_t, params, q, kv, prev, low, out_t, logs, normed, wl, pick)


def local(
    inputs, thoughts, positions, lengths, w_qkv, w_out, w_fc, w_proj, norm_gains, norm_biases, out_grad,
):
    rows, seqs, width = inputs.shape
    ctx_count = lax.axis_size("ctx")
    tp_count = lax.axis_size("tp")
    fsdp_count = lax.axis_size("fsdp")
    ctx, tp, fsdp = lax.axis_index("ctx"), lax.axis_index("tp"), lax.axis_index("fsdp")
    first_row = ctx * rows
    own_rows = rows // tp_count
    own_tokens = own_rows * seqs
    far = min(ctx_count - 1, -(-(DOC_MOST - 1) // rows))
    block = min(256, rows)
    bf, f32 = jnp.bfloat16, jnp.float32

    counts = (fsdp_count, ctx_count, tp_count)
    local_width = w_qkv.shape[2]
    params = jnp.pad(jnp.concatenate([norm_gains, norm_biases]).astype(f32), ((0, 4), (0, 0)))
    places = first_row + jnp.arange(rows, dtype=jnp.int32)
    is_thought = places[None, None, :] == positions[:, :, None]
    keep = jnp.logical_not(jnp.any(is_thought, axis=0))
    start = jnp.transpose(inputs, (1, 0, 2))
    for t in range(thoughts.shape[0]):
        start = jnp.where(is_thought[t][:, :, None], thoughts[t][:, None, :], start)
    ends = jnp.cumsum(lengths, axis=1, dtype=jnp.int32)
    low = jnp.max(jnp.where(ends[:, :, None] <= places[None, None, :], ends[:, :, None], 0), axis=1)
    low = low - (first_row - far * rows)

    low3 = low[:, None, :]
    attended, q, kv, prev, out_t, logs, normed, w_local, out_full, fc_full, proj_full_t, params = front(
        start, low3, w_qkv, w_out, w_fc, w_proj.T, params, block, far, counts
    )
    start_own = lax.dynamic_slice_in_dim(start, tp * own_rows, own_rows, 1)
    grad_own = jnp.transpose(
        lax.dynamic_slice_in_dim(out_grad, tp * own_rows, own_rows, 0), (1, 0, 2)
    ).reshape(own_tokens, width)

    own_places = lax.dynamic_slice_in_dim(places, tp * own_rows, own_rows, 0)
    count = thoughts.shape[0]
    pick = (own_places[None, None, :] == positions[:, :, None]).astype(bf)
    picks = []
    for s in range(seqs):
        picks.append(jnp.concatenate(
            [jnp.where(k == s, pick[:, s], jnp.zeros_like(pick[:, s])) for k in range(seqs)], axis=0
        ))
    pick = jnp.stack(picks)
    pick = jnp.pad(pick, ((0, 0), (0, -(-pick.shape[1] // 16) * 16 - pick.shape[1]), (0, 0)))
    output, d_start, gw, gq, small = back(
        attended, start_own, grad_own, out_full, fc_full, proj_full_t, params, q, kv, prev, low3, out_t, logs, normed,
        w_local, pick, block, far, counts,
    )
    output = jnp.transpose(output, (1, 0, 2))
    d_start = lax.optimization_barrier(jnp.transpose(d_start, (1, 0, 2)))
    d_inputs = jnp.where(keep.T[:, :, None], d_start.astype(f32), 0.0)
    d_thoughts = jnp.transpose(small[8 : 8 + count * seqs].reshape(seqs, count, width), (1, 0, 2))
    hidden = w_fc.shape[1]
    gw = gw.astype(f32)
    norms = lax.dynamic_slice_in_dim(small[:4], fsdp * w_fc.shape[0], w_fc.shape[0], 1)
    return (
        output,
        d_inputs,
        d_thoughts,
        jnp.transpose(gq.reshape(3, local_width, -1), (0, 2, 1)),
        gw[:, 2 * hidden : 2 * hidden + local_width].T,
        gw[:, :hidden],
        gw[:, hidden : 2 * hidden].T,
        norms[:2],
        norms[2],
        norms[3],
    )


def solution(mesh):
    in_specs = (
        P("ctx", "fsdp", None),
        P(None, "fsdp", None),
        P(None, "fsdp"),
        P("fsdp", None),
        P(None, "fsdp", "tp"),
        P("tp", "fsdp"),
        P("fsdp", "tp"),
        P("tp", "fsdp"),
        P(None, "fsdp"),
        P(None, "fsdp"),
        P("ctx", "fsdp", None),
    )
    out_specs = (
        P("ctx", "fsdp", None),
        P("ctx", "fsdp", None),
        P(None, "fsdp", None),
        P(None, "fsdp", "tp"),
        P("tp", "fsdp"),
        P("fsdp", "tp"),
        P("tp", "fsdp"),
        P(None, "fsdp"),
        P("fsdp"),
        P("fsdp"),
    )
    return jax.shard_map(local, mesh=mesh, in_specs=in_specs, out_specs=out_specs, check_vma=False)
```

```python
import functools

import jax
import jax.numpy as jnp
from jax import lax
from jax.experimental import pallas as pl
from jax.experimental.pallas import tpu as pltpu
from jax.sharding import PartitionSpec as P

HEAD_DIM = 64
DOC_MOST = 1024
EPSILON = 1e-05
MASKED = -1e30


def dot(a, b, dims=((1,), (0,))):
    return lax.dot_general(a, b, (dims, ((), ())), preferred_element_type=jnp.float32)


def hat_rows(values):
    centre = jnp.mean(values, axis=-1, keepdims=True)
    shifted = values - centre
    spread = jnp.mean(shifted * shifted, axis=-1, keepdims=True)
    inv = lax.rsqrt(spread + EPSILON)
    return shifted * inv, inv


def norm_back(hat, inv, gain, grad):
    eg = grad * gain
    return inv * (
        eg
        - jnp.mean(eg, axis=-1, keepdims=True)
        - hat * jnp.mean(eg * hat, axis=-1, keepdims=True)
    )


MESH = pl.DeviceIdType.MESH
VMEM_LIMIT = 62 << 20


def column(index, size=HEAD_DIM):
    return slice(index * size, (index + 1) * size)


def turn(value):
    return value.astype(jnp.float32).T.astype(jnp.bfloat16)


def turn_back(value):
    return value.T.astype(jnp.bfloat16)


def front_kernel(
    sizes, block,
    start_ref, low_ref, wq_ref, wo_ref, wf_ref, wp_ref, par_ref,
    att_ref, q_ref, kv_ref, prev_ref, out_t_ref, log_ref, normed_ref, wl_ref, ow_ref, fc_ref, pj_ref, params_ref,
    start_s, normed_s, wl_s, wo_s, par_s, q_s, kv_s, prev_s, qt_s, ko_s, vto_s, kp_s, vtp_s, m_s, l_s, att_s,
    in_sem, out_sem, w_loc, z_sem, z_rec, s_sem, s_rec, x_sem, x_rec, r_sem, r_rec,
    kv_sem, kv_rec, at_sem, at_rec, at_loc,
):
    F, C, T = sizes
    f, c, t = lax.axis_index("fsdp"), lax.axis_index("ctx"), lax.axis_index("tp")
    S, rows, width = start_ref.shape
    hw = q_ref.shape[2]
    heads = hw // HEAD_DIM
    own_rows = rows // T
    far = prev_ref.shape[1] // rows if C > 1 else 0
    shard = wq_ref.shape[1]
    hidden = wf_ref.shape[1]
    bf, f32 = jnp.bfloat16, jnp.float32
    sib, across = f ^ 1, f ^ 2

    def remote(src, dst, send, recv, **where):
        return pltpu.make_async_remote_copy(
            src_ref=src, dst_ref=dst, send_sem=send, recv_sem=recv, device_id=where, device_id_type=MESH
        )

    start_in = pltpu.make_async_copy(start_ref, start_s, in_sem.at[0])
    start_in.start()

    barrier = pltpu.get_barrier_semaphore()
    peers = 0
    for d in range(1, F):
        pl.semaphore_signal(barrier, inc=1, device_id={"fsdp": f ^ d}, device_id_type=MESH)
        peers += 1
    for d in range(1, T):
        pl.semaphore_signal(barrier, inc=1, device_id={"tp": lax.rem(t + d, T)}, device_id_type=MESH)
        peers += 1
    for d in range(1, C):
        pl.semaphore_signal(barrier, inc=1, device_id={"ctx": lax.rem(c + d, C)}, device_id_type=MESH)
        peers += 1
    pl.semaphore_wait(barrier, peers)

    pending = []

    def go(copy):
        copy.start()
        pending.append(copy)
        return copy

    def at_shard(ff):
        return pl.ds(pl.multiple_of(ff * shard, shard), shard)

    def at_hidden(tt):
        return pl.ds(pl.multiple_of(tt * hidden, hidden), hidden)

    def block_at(a, tt, ff):
        if a == 0:
            return par_s.at[ff]
        if a == 1:
            return wl_s.at[:, at_shard(ff), :]
        if a == 2:
            return wo_s.at[tt, ff]
        return (fc_ref if a == 3 else pj_ref).at[at_shard(ff), at_hidden(tt)]

    sources = (par_ref, wq_ref, wo_ref, wf_ref, wp_ref)

    def origin(p):
        return t if p == 0 else (t - (p + 1) // 2 if p % 2 else t + p // 2)

    def has(p):
        return t >= (p + 1) // 2 if p % 2 else t + p // 2 <= T - 1

    def spread_chip(a, p):
        src = sources[a] if p == 0 else block_at(a, origin(p), f)
        dst = block_at(a, origin(p), f)
        remote(src, dst, x_sem.at[a, p], x_rec.at[a, p], fsdp=across).start()
        remote(src, dst, s_sem.at[a, p], s_rec.at[a, p], fsdp=sib).start()

    def along(a, p, way):
        src = sources[a] if p == 0 else block_at(a, origin(p), f)
        q = p + 2 if p else 1 + way
        return remote(
            src, block_at(a, origin(p), f), z_sem.at[a, p, way], z_rec.at[a, q], tp=t + 1 if way == 0 else t - 1
        )

    def line_start(a):
        @pl.when(t < T - 1)
        def _():
            along(a, 0, 0).start()

        @pl.when(t > 0)
        def _():
            along(a, 0, 1).start()

        spread_chip(a, 0)

    def line_step(a, k):
        for way, p in ((0, 2 * k - 1), (1, 2 * k)):
            on = t < T - 1 if way == 0 else t > 0

            @pl.when(has(p) & on)
            def _():
                here = block_at(a, origin(p), f)
                remote(here, here, z_sem.at[a, p, way], z_rec.at[a, p], tp=t).wait_recv()
                along(a, p, way).start()

            @pl.when(has(p) & jnp.logical_not(on))
            def _():
                here = block_at(a, origin(p), f)
                remote(here, here, z_sem.at[a, p, way], z_rec.at[a, p], tp=t).wait_recv()

            @pl.when(has(p))
            def _():
                spread_chip(a, p)

    def relay(a, p):
        here = block_at(a, origin(p), across)
        remote(here, here, x_sem.at[a, p], x_rec.at[a, p], fsdp=f).wait_recv()
        remote(here, here, r_sem.at[a, p], r_rec.at[a, p], fsdp=sib).start()

    def take_chip(a, p):
        for ff, rec in ((sib, s_rec), (sib ^ 2, r_rec)):
            here = block_at(a, origin(p), ff)
            remote(here, here, s_sem.at[a, p], rec.at[a, p], fsdp=f).wait_recv()

    def every(what, a, ps):
        for p in ps:
            if p == 0:
                what(a, 0)
            else:
                @pl.when(has(p))
                def _():
                    what(a, p)

    def drain(a):
        last = 1 if a < 2 else 2 * T - 1

        def chip(a, p):
            src = sources[a]
            for sem in (x_sem, s_sem, r_sem):
                remote(src, src, sem.at[a, p], x_rec.at[a, p], fsdp=f).wait_send()

        every(chip, a, range(last))
        if a >= 2:
            for p in range(2 * T - 1):
                for way in range(2):
                    if p and p % 2 != 1 - way:
                        continue
                    on = t < T - 1 if way == 0 else t > 0

                    @pl.when((on & has(p)) if p else on)
                    def _():
                        remote(sources[a], sources[a], z_sem.at[a, p, way], z_rec.at[a, p], tp=t).wait_send()

    keeps = []
    for a in range(5):
        keep = pltpu.make_async_copy(sources[a], block_at(a, t, f), w_loc.at[a])
        keep.start()
        keeps.append(keep)
    spread_chip(0, 0)
    spread_chip(1, 0)
    for a in (2, 3, 4):
        line_start(a)

    relay(0, 0)
    take_chip(0, 0)
    keeps[0].wait()
    params = jnp.concatenate([par_s[ff] for ff in range(F)], axis=1)
    params_ref[...] = params
    start_in.wait()
    per_seq = rows // block

    def norm_one(index, _):
        s = index // per_seq
        here = pl.ds(pl.multiple_of(lax.rem(index, per_seq) * block, block), block)
        hat, _ = hat_rows(start_s[s, here, :].astype(f32))
        normed_s[s, here, :] = (hat * params_ref[0:1, :] + params_ref[2:3, :]).astype(bf)
        return 0

    lax.fori_loop(0, S * per_seq, norm_one, 0)
    normed_out = pltpu.make_async_copy(normed_s, normed_ref, out_sem.at[0])
    normed_out.start()

    relay(1, 0)
    take_chip(1, 0)
    keeps[1].wait()

    def kv_one(s, _):
        def one(index, _):
            here = pl.ds(pl.multiple_of(index * block, block), block)
            rows_in = normed_s[s, here, :]
            k = dot(rows_in, wl_s[1]).astype(bf)
            v = dot(rows_in, wl_s[2]).astype(bf)
            kv_s[s, here, :] = jnp.concatenate([k, v], axis=1)
            v_t = turn(v)
            for h in range(heads):
                ko_s[s, h, here, :] = k[:, column(h)]
                vto_s[s, h, :, here] = v_t[column(h)]
            return 0

        lax.fori_loop(0, per_seq, one, 0)
        return 0

    def kv_copy(s, d):
        return remote(
            kv_s.at[s], prev_s.at[s, pl.ds((far - d) * rows, rows), :],
            kv_sem.at[d, s], kv_rec.at[d, s], ctx=lax.rem(c + d, C),
        )

    for s in range(S):
        kv_one(s, 0)
        for d in range(1, far + 1):
            @pl.when(c + d < C)
            def _():
                kv_copy(s, d).start()

    def q_one(index, _):
        s = index // per_seq
        here = pl.ds(pl.multiple_of(lax.rem(index, per_seq) * block, block), block)
        q = dot(normed_s[s, here, :], wl_s[0]).astype(bf)
        q_s[s, here, :] = q
        q_t = turn(q.astype(f32) * 0.125)
        for h in range(heads):
            qt_s[s, h, :, here] = q_t[column(h)]
        return 0

    lax.fori_loop(0, S * per_seq, q_one, 0)
    outs = [
        pltpu.make_async_copy(q_s, q_ref, out_sem.at[1]),
        pltpu.make_async_copy(kv_s, kv_ref, out_sem.at[2]),
        pltpu.make_async_copy(wl_s, wl_ref, out_sem.at[4]),
    ]
    for copy in outs:
        copy.start()

    def own_part(s):
        def one(h, _):
            spot, line = pl.ds(pl.multiple_of(h * HEAD_DIM, HEAD_DIM), HEAD_DIM), pl.ds(h, 1)
            for i in range(per_seq):
                span = column(i, block)
                low = low_ref[s, :, span] - far * rows
                top = i * block + lax.broadcasted_iota(jnp.int32, (1, block), 1)
                first = max(0, i * block - (DOC_MOST - 1)) // block * block
                many = (i + 1) * block - first
                place = first + lax.broadcasted_iota(jnp.int32, (many, 1), 0)
                scores = dot(ko_s[s, h, first : first + many, :], qt_s[s, h, :, span])
                scores = jnp.where((place >= low) & (place <= top), scores, MASKED)
                m = jnp.max(scores, axis=0, keepdims=True)
                p = jnp.exp(scores - m)
                m_s[s, line, span] = m
                l_s[s, line, span] = jnp.sum(p, axis=0, keepdims=True)
                out_t_ref[s, spot, span] = dot(vto_s[s, h, :, first : first + many], p.astype(bf))
            return 0

        lax.fori_loop(0, heads, one, 0)

    def far_part(s):
        for h in range(heads):
            kp_s[h] = prev_s[s, :, column(h)]
            vtp_s[h] = turn(prev_s[s, :, column(heads + h)])

        def one(h, _):
            spot, line = pl.ds(pl.multiple_of(h * HEAD_DIM, HEAD_DIM), HEAD_DIM), pl.ds(h, 1)
            for i in range(per_seq):
                span = column(i, block)
                first = max(0, far * rows + i * block - (DOC_MOST - 1)) // block * block
                if first >= far * rows:
                    continue
                many = far * rows - first
                place = first + lax.broadcasted_iota(jnp.int32, (many, 1), 0)
                scores = dot(kp_s[h, first : first + many, :], qt_s[s, h, :, span])
                scores = jnp.where(place >= low_ref[s, :, span], scores, MASKED)
                old = m_s[s, line, span]
                m = jnp.maximum(old, jnp.max(scores, axis=0, keepdims=True))
                p = jnp.exp(scores - m)
                alpha = jnp.exp(old - m)
                m_s[s, line, span] = m
                l_s[s, line, span] = alpha * l_s[s, line, span] + jnp.sum(p, axis=0, keepdims=True)
                out_t_ref[s, spot, span] = alpha * out_t_ref[s, spot, span] + dot(
                    vtp_s[h, :, first : first + many], p.astype(bf)
                )
            return 0

        lax.fori_loop(0, heads, one, 0)

    def finish_part(s):
        for h in range(heads):
            out_t_ref[s, column(h), :] = out_t_ref[s, column(h), :] / l_s[s, h : h + 1, :]
            log_ref[s, h : h + 1, :] = m_s[s, h : h + 1, :] + jnp.log(l_s[s, h : h + 1, :])
        for tt in range(T):
            att_s[tt, s] = out_t_ref[s, :, column(tt, own_rows)].astype(bf)

    every_p = range(2 * T - 1)
    for a in (2, 3):
        line_step(a, 1)

    def own_loop(s, _):
        own_part(s)
        return 0

    lax.fori_loop(0, 1, own_loop, 0)
    line_step(2, 2)
    line_step(4, 1)
    line_step(3, 2)
    lax.fori_loop(1, S, own_loop, 0)
    for k in range(3, T):
        line_step(2, k)
    every(relay, 2, every_p)

    def wait_far(s):
        for d in range(1, far + 1):
            @pl.when(c >= d)
            def _():
                kv_copy(s, d).wait_recv()

            @pl.when(c < d)
            def _():
                prev_s[s, (far - d) * rows : (far - d + 1) * rows, :] = jnp.zeros((rows, 2 * hw), bf)

    at = [[None] * S for _ in range(T)]
    for s in range(S):
        if far:
            wait_far(s)

            @pl.when(c > 0)
            def _():
                far_part(s)
        finish_part(s)
        for d in range(1, T):
            peer = lax.rem(t + d, T)
            at[d][s] = go(
                remote(att_s.at[peer, s], att_ref.at[t, s], at_sem.at[d, s], at_rec.at[d, s], tp=peer)
            )
        own_at = pltpu.make_async_copy(att_s.at[t, s], att_ref.at[t, s], at_loc.at[s])
        own_at.start()
        at[0][s] = own_at
        if s == 0:
            line_step(4, 2)
            for k in range(3, T):
                line_step(3, k)
            every(relay, 3, every_p)
    prev_out = pltpu.make_async_copy(prev_s, prev_ref, out_sem.at[3])
    if far:
        prev_out.start()
    for k in range(3, T):
        line_step(4, k)
    every(take_chip, 2, every_p)
    keeps[2].wait()
    for tt in range(T):
        for ff in range(F):
            ow_ref[column(tt, hw), column(ff, shard)] = wo_s[tt, ff]
    every(relay, 4, every_p)
    for a in (3, 4):
        every(take_chip, a, every_p)
        keeps[a].wait()
    for s in range(S):
        at[0][s].wait()
        for d in range(1, T):
            at[d][s].wait_recv()
    normed_out.wait()
    for copy in outs:
        copy.wait()
    if far:
        prev_out.wait()
    for copy in pending:
        copy.wait_send()
    for a in range(5):
        drain(a)
    for s in range(S):
        for d in range(1, far + 1):
            @pl.when(c + d < C)
            def _():
                kv_copy(s, d).wait_send()


def front(start, low, wq, wo, wf, wp, params, block, far, counts):
    F, C, T = counts
    S, rows, width = start.shape
    hw = wq.shape[2]
    shard = wq.shape[1]
    heads = hw // HEAD_DIM
    hidden = wf.shape[1]
    bf, f32 = jnp.bfloat16, jnp.float32
    vmem = pl.BlockSpec(memory_space=pltpu.VMEM)
    anywhere = pl.BlockSpec(memory_space=pl.ANY)
    dma = lambda *shape: pltpu.SemaphoreType.DMA(shape)
    past = max(far, 1) * rows
    shape = jax.ShapeDtypeStruct
    return pl.pallas_call(
        functools.partial(front_kernel, counts, block),
        in_specs=[anywhere, vmem, anywhere, anywhere, anywhere, anywhere, anywhere],
        out_specs=[
            anywhere, anywhere, anywhere, anywhere, vmem, vmem, anywhere, anywhere, vmem, anywhere, anywhere, vmem
        ],
        out_shape=[
            shape((T, S, hw, rows // T), bf),
            shape((S, rows, hw), bf),
            shape((S, rows, 2 * hw), bf),
            shape((S, past, 2 * hw), bf),
            shape((S, hw, rows), f32),
            shape((S, 8, rows), f32),
            shape((S, rows, width), bf),
            shape((3, F * shard, hw), bf),
            shape((T * hw, F * shard), bf),
            shape((F * shard, T * hidden), bf),
            shape((F * shard, T * hidden), bf),
            shape((8, F * shard), f32),
        ],
        scratch_shapes=[
            pltpu.VMEM((S, rows, width), bf),
            pltpu.VMEM((S, rows, width), bf),
            pltpu.VMEM((3, F * shard, hw), bf),
            pltpu.VMEM((T, F, hw, shard), bf),
            pltpu.VMEM((F, 8, shard), f32),
            pltpu.VMEM((S, rows, hw), bf),
            pltpu.VMEM((S, rows, 2 * hw), bf),
            pltpu.VMEM((S, past, 2 * hw), bf),
            pltpu.VMEM((S, heads, HEAD_DIM, rows), bf),
            pltpu.VMEM((S, heads, rows, HEAD_DIM), bf),
            pltpu.VMEM((S, heads, HEAD_DIM, rows), bf),
            pltpu.VMEM((heads, past, HEAD_DIM), bf),
            pltpu.VMEM((heads, HEAD_DIM, past), bf),
            pltpu.VMEM((S, 8, rows), f32),
            pltpu.VMEM((S, 8, rows), f32),
            pltpu.VMEM((T, S, hw, rows // T), bf),
            dma(1), dma(5), dma(5),
            dma(5, 2 * T, 2), dma(5, 2 * T), dma(5, 2 * T), dma(5, 2 * T), dma(5, 2 * T), dma(5, 2 * T), dma(5, 2 * T),
            dma(5, 2 * T),
            dma(far + 1, S), dma(far + 1, S), dma(T, S), dma(T, S), dma(S),
        ],
        compiler_params=pltpu.CompilerParams(
            vmem_limit_bytes=VMEM_LIMIT, collective_id=1, has_side_effects=True
        ),
        cost_estimate=pl.CostEstimate(flops=8 * 10**9, bytes_accessed=64 << 20, transcendentals=8 << 20),
    )(start, low, wq, wo, wf, wp, params)


def padded(size):
    return -(-size // 128) * 128


def add_rows(target, sources, rows_at_once=16):
    def one(i, _):
        here = pl.ds(pl.multiple_of(i * rows_at_once, rows_at_once), rows_at_once)
        total = target[here, :].astype(jnp.float32)
        for source in sources:
            total = total + source[here, :].astype(jnp.float32)
        target[here, :] = total.astype(target.dtype)
        return 0

    lax.fori_loop(0, target.shape[0] // rows_at_once, one, 0)


def gelu_parts(x):
    square = x * x
    th = jnp.tanh(0.7978845608028654 * (x + 0.044715 * (square * x)))
    half = 0.5 * (1.0 + th)
    slope = half + (0.5 * x) * (1.0 - th * th) * (0.7978845608028654 * (1.0 + (3 * 0.044715) * square))
    return x * half, slope


def back_kernel(
    sizes, block, far, step_cols,
    att_ref, start_ref, grad_ref, outw_ref, fc_ref, pj_ref, params_ref,
    q_ref, kv_ref, prev_ref, low_ref, out_t_ref, log_ref, normed_ref, wl_ref, pick_ref,
    output_ref, dstart_ref, gw_ref, gq_ref, small_ref,
    start_s, mid_s, grad_s, ob_s, gbuf, rcore, rx, rc, rz, g2, r2c, r2x,
    da_s, da_r, dp_s, rec_s, kv_s, dq_s, rs_r, gq_s, rgq, rgc, sm_s, rst, rsc, rsf,
    in_sem, w_sem, core_sem, core_rec, x_sem, x_rec, c2_sem, c2_rec, x2_sem, x2_rec,
    c_sem, c_rec, z_sem, z_rec, b_sem, b_rec, da_sem, da_rec, dp_sem, dp_rec,
    rs_sem, rs_rec, ag_sem, ag_rec, gq_sem, gq_rec, gc_sem, gc_rec,
    st_sem, st_rec, sc_sem, sc_rec, sf_sem, sf_rec, loc_sem, wl_sem, credit,
):
    F, C, T = sizes
    f, c, t = lax.axis_index("fsdp"), lax.axis_index("ctx"), lax.axis_index("tp")
    S, rows, hw = q_ref.shape
    heads = hw // HEAD_DIM
    width = start_s.shape[2]
    own_rows = rows // T
    tokens = S * own_rows
    shard = gbuf.shape[1]
    hidden = fc_ref.shape[1] // T
    wide = 2 * hidden
    per_seq = rows // block
    bf, f32 = jnp.bfloat16, jnp.float32
    sib, across = f ^ 1, f ^ 2

    def remote(src, dst, send, recv, **where):
        return pltpu.make_async_remote_copy(
            src_ref=src, dst_ref=dst, send_sem=send, recv_sem=recv, device_id=where, device_id_type=MESH
        )

    pending = []

    def go(copy, like):
        copy.start()
        pending.append(like)

    def landed(ref, sem):
        remote(ref, ref, b_rec, sem, fsdp=f).wait_recv()

    def sent(ref, sem):
        remote(ref, ref, sem, b_rec, fsdp=f).wait_send()

    def tp_peer(d):
        return lax.rem(t + d, T)

    def tp_source(d):
        return lax.rem(t + T - d, T)

    def rows_of(owner):
        return pl.ds(pl.multiple_of(owner * own_rows, own_rows), own_rows)

    ag_own, ag_whole = (ob_s, ob_s), (output_ref, dstart_ref)

    def ag_copy(a, s, owner, step, way):
        whole = ag_whole[a].at[s, rows_of(owner), :]
        src = ag_own[a].at[s] if step == 0 else whole
        return lambda to: remote(src, whole, ag_sem.at[a, s, step, way], ag_rec.at[a, s, step, way], tp=to)

    def ag_keep(a, s):
        return pltpu.make_async_copy(ag_own[a].at[s], ag_whole[a].at[s, rows_of(t), :], loc_sem.at[a, s])

    def ag_start(a, s):
        @pl.when(t < T - 1)
        def _():
            ag_copy(a, s, t, 0, 0)(t + 1).start()

        @pl.when(t > 0)
        def _():
            ag_copy(a, s, t, 0, 1)(t - 1).start()

        ag_keep(a, s).start()

    def ag_step(a, s, step):
        @pl.when(t >= step)
        def _():
            ag_copy(a, s, t - step, step - 1, 0)(t).wait_recv()

        @pl.when((t >= step) & (t < T - 1))
        def _():
            ag_copy(a, s, t - step, step, 0)(t + 1).start()

        @pl.when(t + step <= T - 1)
        def _():
            ag_copy(a, s, t + step, step - 1, 1)(t).wait_recv()

        @pl.when((t + step <= T - 1) & (t > 0))
        def _():
            ag_copy(a, s, t + step, step, 1)(t - 1).start()

    def ag_drain(a, s, first):
        if not first:
            ag_keep(a, s).wait()
        for step in range(first, T - 1 if first or a else 1):
            @pl.when((t >= step) & (t < T - 1))
            def _():
                ag_copy(a, s, t - step, step, 0)(t + 1).wait_send()

            @pl.when((t + step <= T - 1) & (t > 0))
            def _():
                ag_copy(a, s, t + step, step, 1)(t - 1).wait_send()

    across_at = lambda b: T + b
    main = pl.ds(0, wide)

    def core_send(b):
        slot = b % 2
        if b >= 2:
            pl.semaphore_wait(credit, 1)
        for k in range(2):
            remote(
                gbuf.at[2 * T + 2 * slot + k, :, main], rcore.at[slot, k],
                core_sem.at[b, k], core_rec.at[b, k], fsdp=sib,
            ).start()

    def core_add(b):
        slot = b % 2
        landed(rcore.at[slot, 1], core_rec.at[b, 1])
        add_rows(gbuf.at[across_at(b), :, main], [rcore.at[slot, 1]])
        out = gbuf.at[across_at(b), :, main]
        go(
            remote(out, rx.at[b, :, main], x_sem.at[b], x_rec.at[b], fsdp=across),
            lambda: (rx.at[b, :, main], x_sem.at[b]),
        )
        landed(rcore.at[slot, 0], core_rec.at[b, 0])
        add_rows(gbuf.at[b, :, main], [rcore.at[slot, 0]])
        if b < T - 2:
            pl.semaphore_signal(credit, inc=1, device_id={"fsdp": sib}, device_id_type=MESH)

    held = [b // C for b in range(T)]

    def ctx_copy(b, d, to):
        return remote(gbuf.at[b], rc.at[held[b], d - 1], c_sem.at[b], c_rec.at[b, d], ctx=to)

    def cross_add(b):
        landed(rx.at[b, :, main], x_rec.at[b])
        add_rows(gbuf.at[b, :, main], [rx.at[b, :, main]])

    def ctx_send(b):
        owner = b % C
        for d in range(1, C):
            @pl.when(lax.rem(c + d, C) == owner)
            def _():
                ctx_copy(b, d, owner).start()

    def ctx_wait(b):
        @pl.when(c == b % C)
        def _():
            for d in range(1, C):
                ctx_copy(b, d, c).wait_recv()
            if C > 1:
                add_rows(gbuf.at[b], [rc.at[held[b], d - 1] for d in range(1, C)])

    def z_round(b, step):
        def hop(to, way):
            return remote(gbuf.at[b], rz.at[held[b], way], z_sem.at[b], z_rec.at[b, way], tp=to)

        def visit(way, before, here):
            @pl.when((c == b % C) & here)
            def _():
                if step:
                    hop(t, way).wait_recv()
                    add_rows(gbuf.at[b], [rz.at[held[b], way]])

                @pl.when(before)
                def _():
                    hop(t - 1 if way == 0 else t + 1, way).start()

        if T - 1 - step >= b and b < T - 1:
            visit(0, t > b, t == T - 1 - step)
        if step <= b and b > 0:
            visit(1, t < b, t == step)

    def feed_phase(att_s, outw_s, w_s, x_s, nm_s, nmt_s, gt_s, acc_s):
        steps = hidden // step_cols
        ring = w_s.shape[0]
        total_steps = 2 * T * steps

        def stream(n):
            at = pl.ds(pl.multiple_of(lax.rem(n, T * steps) * step_cols, step_cols), step_cols)
            slot = lax.rem(n, ring)
            return [
                pltpu.make_async_copy(ref.at[:, at], w_s.at[slot, k], w_sem.at[slot, k])
                for k, ref in enumerate((fc_ref, pj_ref))
            ]

        def take(n):
            for copy in stream(n):
                copy.wait()

            @pl.when(n + ring - 1 < total_steps)
            def _():
                for copy in stream(n + ring - 1):
                    copy.start()

            return lax.rem(n, ring)

        loads = [
            pltpu.make_async_copy(att_ref, dq_s, in_sem.at[0]),
            pltpu.make_async_copy(outw_ref, outw_s, in_sem.at[1]),
            pltpu.make_async_copy(start_ref, start_s, in_sem.at[2]),
            pltpu.make_async_copy(grad_ref, grad_s, in_sem.at[3]),
        ]
        for copy in loads:
            copy.start()
        for n in range(ring - 1):
            for copy in stream(n):
                copy.start()

        barrier = pltpu.get_barrier_semaphore()
        peers = 0
        for d in range(1, F):
            pl.semaphore_signal(barrier, inc=1, device_id={"fsdp": f ^ d}, device_id_type=MESH)
            peers += 1
        for d in range(1, T):
            pl.semaphore_signal(barrier, inc=1, device_id={"tp": tp_peer(d)}, device_id_type=MESH)
            peers += 1
        for d in range(1, C):
            pl.semaphore_signal(barrier, inc=1, device_id={"ctx": lax.rem(c + d, C)}, device_id_type=MESH)
            peers += 1
        pl.semaphore_wait(barrier, peers)

        for copy in loads:
            copy.wait()
        mid = start_s[...].reshape(tokens, width).astype(f32)
        for g in range(T):
            for s in range(S):
                att_s[g, column(s, own_rows), :] = turn(dq_s[g, s])
            mid = mid + dot(att_s[g], outw_s[column(g, hw), :])
        mid_s[...] = mid
        hat, _ = hat_rows(mid)
        nm = hat * params_ref[1:2] + params_ref[3:4]
        nm_s[...] = nm.astype(bf)
        nmt_s[...] = turn_back(nm)
        gt_s[...] = turn(grad_s[...])
        acc_s[...] = jnp.zeros_like(acc_s)

        def forward(j, _):
            slot = take(j)
            x = dot(nm_s[...], w_s[slot, 0])
            x_s[j] = x
            act, _ = gelu_parts(x)
            acc_s[...] += dot(act.astype(bf), w_s[slot, 1], ((1,), (1,)))
            return 0

        lax.fori_loop(0, T * steps, forward, 0)
        ob_s[...] = (mid_s[...] + acc_s[...]).astype(bf).reshape(S, own_rows, width)
        for s in range(S):
            ag_start(0, s)
        acc_s[...] = jnp.zeros_like(acc_s)

        for n in range(T):
            if n >= 2:
                for k in range(2):
                    sent(rcore.at[0, 0], core_sem.at[n - 2, k])
            slot = n % 2

            def backward(j, _):
                here = pl.ds(pl.multiple_of(j * step_cols, step_cols), step_cols)
                there = pl.ds(pl.multiple_of(hidden + j * step_cols, step_cols), step_cols)
                at_w = take(T * steps + n * steps + j)
                fc, proj = w_s[at_w, 0], w_s[at_w, 1]
                act, slope = gelu_parts(x_s[n * steps + j])
                act = act.astype(bf)
                d_exp = (slope * dot(grad_s[...], proj)).astype(bf)
                acc_s[...] += dot(d_exp, fc, ((1,), (1,)))
                d_fc = dot(nmt_s[...], d_exp).astype(bf)
                d_proj = dot(gt_s[...], act).astype(bf)
                for ff in range(F):
                    r = f ^ ff
                    odd, half = lax.rem(r, 2), r // 2
                    at = (1 - odd) * (half * T + n) + odd * (2 * T + 2 * slot + half)
                    gbuf[at, :, here] = d_fc[column(ff, shard)]
                    gbuf[at, :, there] = d_proj[column(ff, shard)]
                return 0

            lax.fori_loop(0, steps, backward, 0)
            core_send(n)
            if n:
                core_add(n - 1)

        mid = mid_s[...]
        hat, inv = hat_rows(mid)
        d_nm = acc_s[...]
        d_mid = grad_s[...].astype(f32) + norm_back(hat, inv, params_ref[1:2], d_nm)
        d_mid_t = turn_back(d_mid)
        for g in range(T):
            d_att = dot(outw_s[column(g, hw), :], d_mid_t).astype(bf)
            for s in range(S):
                da_s[g, s] = d_att[:, column(s, own_rows)]
        for s in range(S):
            for d in range(1, T):
                go(
                    remote(da_s.at[tp_peer(d), s], da_r.at[t, s], da_sem.at[d, s], da_rec.at[d, s], tp=tp_peer(d)),
                    lambda d=d, s=s: (da_s.at[0, s], da_sem.at[d, s]),
                )
        sm_s[...] = jnp.zeros_like(sm_s)
        sm_s[1:2, :] = jnp.sum(d_nm * hat, axis=0, keepdims=True)
        sm_s[3:4, :] = jnp.sum(d_nm, axis=0, keepdims=True)
        mid_s[...] = d_mid
        if g2.shape[3] > hw:
            g2[:, :, :, hw:] = jnp.zeros(g2.shape[:3] + (g2.shape[3] - hw,), bf)
        for g in range(T):
            d_out = dot(d_mid_t, att_s[g]).astype(bf)
            for ff in range(F):
                g2[f ^ ff, g, :, :hw] = d_out[column(ff, shard)]
        core_add(T - 1)

    bf_mem = lambda *shape: pltpu.VMEM(shape, bf)
    f32_mem = lambda *shape: pltpu.VMEM(shape, f32)
    pl.run_scoped(
        feed_phase,
        bf_mem(T, tokens, hw), bf_mem(T * hw, width), bf_mem(3, 2, width, step_cols),
        f32_mem(T * hidden // step_cols, tokens, step_cols),
        bf_mem(tokens, width), bf_mem(width, tokens), bf_mem(width, tokens), f32_mem(tokens, width),
    )

    for k in range(2):
        out = g2.at[1 + 2 * k]
        go(
            remote(out, r2c.at[k], c2_sem.at[k], c2_rec.at[k], fsdp=sib),
            lambda k=k: (r2c.at[k], c2_sem.at[k]),
        )

    def dp_copy(d, s):
        return remote(
            dp_s.at[far - d, s], rec_s.at[d - 1, s], dp_sem.at[d, s], dp_rec.at[d, s], ctx=lax.rem(c + C - d, C)
        )

    def sums_along(snd, wl_s):
        def kv_sum(s):
            for d in range(1, far + 1):
                @pl.when(c + d < C)
                def _():
                    dp_copy(d, s).wait_recv()
                    for g in range(T):
                        kv_s[g, s] = (kv_s[g, s].astype(f32) + rec_s[d - 1, s, g].astype(f32)).astype(bf)

        def partials(s):
            if s == 0:
                pltpu.make_async_copy(wl_ref, wl_s, wl_sem).wait()

            def one(o, _):
                total = dot(wl_s[0], dq_s[o, s])
                for j in (1, 2):
                    total = total + dot(wl_s[j], kv_s[o, s, column(j - 1, hw), :])
                snd[s, o] = total.astype(bf)
                return 0

            lax.fori_loop(0, T, one, 0)

        def rs_copy(s, o, way, at):
            to = at - 1 if way == 0 else at + 1
            slot = T if (to == o and way == 1) else o
            return remote(
                snd.at[s, o], rs_r.at[s, slot], rs_sem.at[s, o], rs_rec.at[s, o, way], tp=t - 1 if way == 0 else t + 1
            )

        def rs_slot(s, k):
            for at in range(T):
                for way, o, begins in ((0, k - (T - 1 - at), at == T - 1), (1, T - 1 + at - k, at == 0)):
                    if not (0 <= o <= at if way == 0 else at <= o <= T - 1):
                        continue

                    @pl.when(t == at)
                    def _():
                        if not begins:
                            landed(rs_r.at[s, T if (o == at and way == 1) else o], rs_rec.at[s, o, way])
                        if o != at:
                            if not begins:
                                add_rows(snd.at[s, o], [rs_r.at[s, o]], 128)
                            before = o - 1 if way == 0 else o + 1
                            if 0 <= before < T:
                                sent(snd.at[s, before], rs_sem.at[s, before])
                            rs_copy(s, o, way, at).start()

        return kv_sum, partials, rs_slot

    def attention_phase(
        snd, wl_s, q_s, kvo_s, prv_s, ot_s, k_h, kt_h, v_h, q_h, qt_h, g_h, gt_h, dqt_s, dk_s, dv_s, del_s
    ):
        kv_sum, partials, rs_slot = sums_along(snd, wl_s)

        def loads(s):
            return [
                pltpu.make_async_copy(ref.at[s], mem, in_sem.at[k])
                for k, (ref, mem) in enumerate(((q_ref, q_s), (kv_ref, kvo_s), (out_t_ref, ot_s), (prev_ref, prv_s)))
            ]

        for copy in loads(0):
            copy.start()
        for k in (1, 0):
            landed(r2c.at[k], c2_rec.at[k])
            for b in range(T):
                add_rows(g2.at[2 * k, b], [r2c.at[k, b]])
            if k:
                go(remote(g2.at[2], r2x, x2_sem, x2_rec, fsdp=across), lambda: (r2x, x2_sem))

        def keys(s):
            for h in range(heads):
                q = q_s[:, column(h)].astype(f32) * 0.125
                q_h[h] = q.astype(bf)
                qt_h[h] = turn_back(q)
                if far:
                    k = prv_s[:, column(h)]
                    k_h[h, : far * rows] = k
                    kt_h[h, :, : far * rows] = turn(k)
                    v_h[h, : far * rows] = prv_s[:, column(heads + h)]
                k = kvo_s[:, column(h)]
                k_h[h, far * rows :] = k
                kt_h[h, :, far * rows :] = turn(k)
                v_h[h, far * rows :] = kvo_s[:, column(heads + h)]

        def grads(s):
            da_r[t, s] = da_s[t, s]
            for d in range(1, T):
                landed(da_r.at[tp_source(d), s], da_rec.at[d, s])
            for h in range(heads):
                for g in range(T):
                    gt_h[h, :, column(g, own_rows)] = da_r[g, s, column(h), :]
                g_t = gt_h[h].astype(f32)
                g_h[h] = turn_back(g_t)
                del_s[h : h + 1, :] = jnp.sum(g_t * ot_s[column(h), :], axis=0, keepdims=True)
            dqt_s[...] = jnp.zeros_like(dqt_s)

        def part(s, h, base, count, own):
            spot = pl.ds(pl.multiple_of(h * HEAD_DIM, HEAD_DIM), HEAD_DIM)
            dk_s[:count] = jnp.zeros((count, HEAD_DIM), f32)
            dv_s[:count] = jnp.zeros((count, HEAD_DIM), f32)
            for i in range(per_seq):
                span = column(i, block)
                reach = far * rows + i * block
                first = max(0, reach - (DOC_MOST - 1) - base) // block * block
                last = min(count, reach + block - base)
                if first >= last:
                    continue
                low = low_ref[s, :, span] - base
                place = first + lax.broadcasted_iota(jnp.int32, (last - first, 1), 0)
                allowed = place >= low
                if own:
                    allowed = allowed & (place <= i * block + lax.broadcasted_iota(jnp.int32, (1, block), 1))
                here = slice(base + first, base + last)
                scores = dot(k_h[h, here, :], qt_h[h, :, span])
                p = jnp.exp(jnp.where(allowed, scores - log_ref[s, pl.ds(h, 1), span], MASKED))
                ds = (p * (dot(v_h[h, here, :], gt_h[h, :, span]) - del_s[pl.ds(h, 1), span])).astype(bf)
                dv_s[first:last] += dot(p.astype(bf), g_h[h, span, :])
                dk_s[first:last] += dot(ds, q_h[h, span, :])
                dqt_s[spot, span] += dot(kt_h[h, :, here], ds)
            return spot, pl.ds(pl.multiple_of(hw + h * HEAD_DIM, HEAD_DIM), HEAD_DIM)

        def far_part(s):
            def one(h, _):
                k_at, v_at = part(s, h, 0, far * rows, False)
                for at, source in ((k_at, dk_s), (v_at, dv_s)):
                    turned = source[: far * rows].T.astype(bf)
                    for j in range(far):
                        for g in range(T):
                            dp_s[j, s, g, at, :] = turned[:, column(j * T + g, own_rows)]
                return 0

            lax.fori_loop(0, heads, one, 0)

        def own_part(s):
            def one(h, _):
                k_at, v_at = part(s, h, far * rows, rows, True)
                for at, source in ((k_at, dk_s), (v_at, dv_s)):
                    turned = source[:rows].T.astype(bf)
                    for g in range(T):
                        kv_s[g, s, at, :] = turned[:, column(g, own_rows)]
                return 0

            lax.fori_loop(0, heads, one, 0)

        for s in range(S):
            for copy in loads(s):
                copy.wait()
            keys(s)
            grads(s)
            if s + 1 < S:
                for copy in loads(s + 1):
                    copy.start()
            if s == 0:
                for other in range(S):
                    ag_step(0, other, 1)
            if far:
                @pl.when(c > 0)
                def _():
                    far_part(s)

                for d in range(1, far + 1):
                    @pl.when(c >= d)
                    def _():
                        dp_copy(d, s).start()
            if s:
                rs_slot(s - 1, 1)
            else:
                cross_add(0)
            own_part(s)
            for g in range(T):
                dq_s[g, s] = (0.125 * dqt_s[:, column(g, own_rows)]).astype(bf)
            if s:
                rs_slot(s - 1, 2)
            if s < T - 2:
                for other in range(S):
                    ag_step(0, other, s + 2)
            if s + 1 < T:
                cross_add(s + 1)
            kv_sum(s)
            partials(s)
            rs_slot(s, 0)

    def last_phase(snd, wl_s, normed_s, gq_acc, tot_s):
        kv_sum, partials, rs_slot = sums_along(snd, wl_s)
        normed_in = pltpu.make_async_copy(normed_ref, normed_s, in_sem.at[0])
        normed_in.start()

        gain = params_ref[0:1]

        def norm_stage(s):
            tot_s[...] = snd[s, t].astype(f32)

            @pl.when(t < T - 1)
            def _():
                tot_s[...] += rs_r[s, t].astype(f32)

            @pl.when(t > 0)
            def _():
                tot_s[...] += rs_r[s, T].astype(f32)

            d_normed = tot_s[...].T
            hat, inv = hat_rows(start_s[s].astype(f32))
            value = mid_s[column(s, own_rows), :] + norm_back(hat, inv, gain, d_normed)
            ag_drain(0, s, 0)
            ob_s[s] = value.astype(bf)
            ag_start(1, s)
            sm_s[0:1, :] += jnp.sum(d_normed * hat, axis=0, keepdims=True)
            sm_s[2:3, :] += jnp.sum(d_normed, axis=0, keepdims=True)

        for k in range(3, T):
            rs_slot(0, k)
        norm_stage(0)
        landed(r2x, x2_rec)
        side = pl.ds(wide, g2.shape[3])
        for b in range(T):
            gbuf[b, :, side] = (g2[0, b].astype(f32) + r2x[b].astype(f32)).astype(bf)
        for b in range(min(S + 1, T)):
            ctx_send(b)

        normed_in.wait()
        gq_acc[...] = jnp.zeros_like(gq_acc)
        for s in range(S):

            def one(o, _):
                near = normed_s[s, rows_of(o), :]
                gq_acc[:hw, :] += dot(dq_s[o, s], near)
                gq_acc[hw:, :] += dot(kv_s[o, s], near)
                return 0

            lax.fori_loop(0, T, one, 0)
        for k in range(F):
            gq_s[k] = gq_acc[:, column(k, shard)].astype(bf)
        for d in range(1, F):
            go(
                remote(gq_s.at[f ^ d], rgq.at[d - 1], gq_sem.at[d], gq_rec.at[d], fsdp=f ^ d),
                lambda d=d: (gq_s.at[0], gq_sem.at[d]),
            )
        for b in range(min(S + 1, T), T):
            cross_add(b)
            ctx_send(b)
        for s in range(1, S):
            for k in range(1, T):
                rs_slot(s, k)
                if k == T - 2:
                    ag_step(1, 0, 1)
            norm_stage(s)

        thoughts = jnp.zeros((pick_ref.shape[1], width), f32)
        for s in range(S):
            thoughts = thoughts + dot(pick_ref[s], ob_s[s])
        sm_s[8:, :] = thoughts
        for d in range(1, T):
            go(
                remote(sm_s, rst.at[d], st_sem.at[d], st_rec.at[d], tp=tp_peer(d)),
                lambda d=d: (sm_s, st_sem.at[d]),
            )
        for b in range(T):
            ctx_wait(b)
            z_round(b, 0)

        gq_sum = gq_s[f].astype(f32)
        for d in range(1, F):
            landed(rgq.at[d - 1], gq_rec.at[d])
            gq_sum = gq_sum + rgq[d - 1].astype(f32)
        rgc[c] = gq_sum.astype(bf)
        for d in range(1, C):
            go(
                remote(rgc.at[c], rgc.at[c], gc_sem.at[d], gc_rec.at[d], ctx=lax.rem(c + d, C)),
                lambda d=d: (rgc.at[0], gc_sem.at[d]),
            )

        for d in range(1, T):
            landed(rst.at[d], st_rec.at[d])
        rst[0] = sm_s[...]
        total = jnp.zeros(sm_s.shape, f32)
        for k in range(T):
            total = total + rst[lax.rem(t + T - k, T)]
        rsc[c] = total
        for d in range(1, C):
            go(
                remote(rsc.at[c], rsc.at[c], sc_sem.at[d], sc_rec.at[d], ctx=lax.rem(c + d, C)),
                lambda d=d: (rsc.at[0], sc_sem.at[d]),
            )
        for step in range(1, T):
            if step > 1:
                ag_step(1, 0, step)
            for s in range(1, S):
                ag_step(1, s, step)
            for b in range(T):
                z_round(b, step)
            if step == 1:
                for d in range(1, C):
                    landed(rsc.at[0], sc_rec.at[d])
                total = jnp.zeros(sm_s.shape, f32)
                for k in range(C):
                    total = total + rsc[k]
                small_ref[8:, :] = total[8:]
                rsf[f] = total
                for d in range(1, F):
                    go(
                        remote(rsf.at[f], rsf.at[f], sf_sem.at[d], sf_rec.at[d], fsdp=f ^ d),
                        lambda d=d: (rsf.at[0], sf_sem.at[d]),
                    )
        for d in range(1, F):
            landed(rsf.at[0], sf_rec.at[d])
        norms = jnp.zeros((8, sm_s.shape[1]), f32)
        for k in range(F):
            norms = norms + rsf[k, 0:8, :]
        small_ref[0:8, :] = norms

        for d in range(1, C):
            landed(rgc.at[0], gc_rec.at[d])
        total = jnp.zeros(gq_ref.shape, f32)
        for k in range(C):
            total = total + rgc[k].astype(f32)
        gq_ref[...] = total
        for o in range(T):
            @pl.when((t == o + 1) | (t == o - 1))
            def _():
                for s in range(S):
                    sent(snd.at[s, o], rs_sem.at[s, o])

    def after_feed(snd, wl_s):
        wl_in = pltpu.make_async_copy(wl_ref, wl_s, wl_sem)
        wl_in.start()
        pl.run_scoped(
            functools.partial(attention_phase, snd, wl_s),
            bf_mem(rows, hw), bf_mem(rows, 2 * hw), bf_mem(max(far, 1) * rows, 2 * hw), f32_mem(hw, rows),
            bf_mem(heads, (far + 1) * rows, HEAD_DIM), bf_mem(heads, HEAD_DIM, (far + 1) * rows),
            bf_mem(heads, (far + 1) * rows, HEAD_DIM),
            bf_mem(heads, rows, HEAD_DIM), bf_mem(heads, HEAD_DIM, rows),
            bf_mem(heads, rows, HEAD_DIM), bf_mem(heads, HEAD_DIM, rows),
            f32_mem(hw, rows), f32_mem(max(far, 1) * rows, HEAD_DIM), f32_mem(max(far, 1) * rows, HEAD_DIM),
            f32_mem(8, rows),
        )
        pl.run_scoped(
            functools.partial(last_phase, snd, wl_s),
            bf_mem(S, rows, width), f32_mem(3 * hw, width), f32_mem(width, own_rows),
        )

    pl.run_scoped(after_feed, bf_mem(S, T, width, own_rows), bf_mem(3, width, hw))

    for b in range(T):
        owner = b % C
        final = lambda d: remote(gbuf.at[b], rx.at[b], b_sem.at[d], b_rec, ctx=lax.rem(owner + d, C))

        @pl.when((t == b) & (c == owner))
        def _():
            for d in range(1, C):
                final(d).start()
            gw_ref[...] = gbuf[b]
            for d in range(1, C):
                final(d).wait_send()

        if C > 1:
            @pl.when((t == b) & (c != owner))
            def _():
                final(1).wait_recv()
                gw_ref[...] = rx[b]

    for like in pending:
        sent(*like())
    for n in range(max(T - 2, 0), T):
        for k in range(2):
            sent(rcore.at[0, 0], core_sem.at[n, k])
    for b in range(T):
        owner = b % C
        if C > 1:
            @pl.when(c != owner)
            def _():
                ctx_copy(b, 1, owner).wait_send()

        @pl.when((c == owner) & (t != b))
        def _():
            remote(gbuf.at[b], rz.at[held[b], 0], z_sem.at[b], z_rec.at[b, 0], tp=t).wait_send()
    for s in range(S):
        for d in range(1, far + 1):
            @pl.when(c >= d)
            def _():
                dp_copy(d, s).wait_send()
        ag_drain(0, s, 1)
        ag_drain(1, s, 0)


def back(att, start, grad, out_w, fc, proj_t, params, q, kv, prev, low, out_t, logs, normed, wl, pick, block, far, counts):
    F, C, T = counts
    S, rows, hw = q.shape
    width = normed.shape[2]
    own_rows = rows // T
    tokens = S * own_rows
    shard = width // F
    hidden = fc.shape[1] // T
    cols = padded(hw)
    wide = 2 * hidden + cols
    bf, f32 = jnp.bfloat16, jnp.float32
    extra = 8 + pick.shape[1]
    mine = -(-T // C)
    dists = max(far, 1)
    vmem = pl.BlockSpec(memory_space=pltpu.VMEM)
    anywhere = pl.BlockSpec(memory_space=pl.ANY)
    dma = lambda *shape: pltpu.SemaphoreType.DMA(shape)
    one = pltpu.SemaphoreType.DMA
    shape = jax.ShapeDtypeStruct
    b16 = lambda *size: pltpu.VMEM(size, bf)
    b32 = lambda *size: pltpu.VMEM(size, f32)
    return pl.pallas_call(
        functools.partial(back_kernel, counts, block, far, 256),
        in_specs=[anywhere] * 6 + [vmem] + [anywhere] * 3 + [vmem, anywhere, vmem, anywhere, anywhere, vmem],
        out_specs=[anywhere, anywhere, vmem, vmem, vmem],
        out_shape=[
            shape((S, rows, width), bf),
            shape((S, rows, width), bf),
            shape((shard, wide), bf),
            shape((3 * hw, shard), f32),
            shape((extra, width), f32),
        ],
        scratch_shapes=[
            b16(S, own_rows, width), b32(tokens, width), b16(tokens, width), b16(S, own_rows, width),
            b16(2 * T + 4, shard, wide), b16(2, 2, shard, 2 * hidden), b16(T, shard, wide),
            b16(mine, max(C - 1, 1), shard, wide), b16(mine, 2, shard, wide),
            b16(4, T, shard, cols), b16(2, T, shard, cols), b16(T, shard, cols),
            b16(T, S, hw, own_rows), b16(T, S, hw, own_rows),
            b16(dists, S, T, 2 * hw, own_rows), b16(dists, S, T, 2 * hw, own_rows),
            b16(T, S, 2 * hw, own_rows), b16(T, S, hw, own_rows),
            b16(S, T + 1, width, own_rows),
            b16(F, 3 * hw, shard), b16(F - 1, 3 * hw, shard), b16(C, 3 * hw, shard),
            b32(extra, width), b32(T, extra, width), b32(C, extra, width), b32(F, extra, width),
            dma(4), dma(3, 2), dma(T, 2), dma(T, 2), dma(T), dma(T), dma(2), dma(2), one, one,
            dma(T), dma(T, C), dma(T), dma(T, 2), dma(C), one, dma(T, S), dma(T, S), dma(far + 1, S), dma(far + 1, S),
            dma(S, T), dma(S, T, 2), dma(2, S, T, 2), dma(2, S, T, 2), dma(F), dma(F), dma(C), dma(C),
            dma(T), dma(T), dma(C), dma(C), dma(F), dma(F), dma(2, S), one, pltpu.SemaphoreType.REGULAR,
        ],
        compiler_params=pltpu.CompilerParams(
            vmem_limit_bytes=VMEM_LIMIT, collective_id=2, has_side_effects=True
        ),
        cost_estimate=pl.CostEstimate(flops=36 * 10**9, bytes_accessed=100 << 20, transcendentals=16 << 20),
    )(att, start, grad, out_w, fc, proj_t, params, q, kv, prev, low, out_t, logs, normed, wl, pick)


def local(
    inputs, thoughts, positions, lengths, w_qkv, w_out, w_fc, w_proj, norm_gains, norm_biases, out_grad,
):
    rows, seqs, width = inputs.shape
    ctx_count = lax.axis_size("ctx")
    tp_count = lax.axis_size("tp")
    fsdp_count = lax.axis_size("fsdp")
    ctx, tp, fsdp = lax.axis_index("ctx"), lax.axis_index("tp"), lax.axis_index("fsdp")
    first_row = ctx * rows
    own_rows = rows // tp_count
    own_tokens = own_rows * seqs
    far = min(ctx_count - 1, -(-(DOC_MOST - 1) // rows))
    block = min(256, rows)
    bf, f32 = jnp.bfloat16, jnp.float32

    counts = (fsdp_count, ctx_count, tp_count)
    local_width = w_qkv.shape[2]
    params = jnp.pad(jnp.concatenate([norm_gains, norm_biases]).astype(f32), ((0, 4), (0, 0)))
    places = first_row + jnp.arange(rows, dtype=jnp.int32)
    is_thought = places[None, None, :] == positions[:, :, None]
    keep = jnp.logical_not(jnp.any(is_thought, axis=0))
    start = jnp.transpose(inputs, (1, 0, 2))
    for t in range(thoughts.shape[0]):
        start = jnp.where(is_thought[t][:, :, None], thoughts[t][:, None, :], start)
    ends = jnp.cumsum(lengths, axis=1, dtype=jnp.int32)
    low = jnp.max(jnp.where(ends[:, :, None] <= places[None, None, :], ends[:, :, None], 0), axis=1)
    low = low - (first_row - far * rows)

    low3 = low[:, None, :]
    attended, q, kv, prev, out_t, logs, normed, w_local, out_full, fc_full, proj_full_t, params = front(
        start, low3, w_qkv, w_out, w_fc, w_proj.T, params, block, far, counts
    )
    start_own = lax.dynamic_slice_in_dim(start, tp * own_rows, own_rows, 1)
    grad_own = jnp.transpose(
        lax.dynamic_slice_in_dim(out_grad, tp * own_rows, own_rows, 0), (1, 0, 2)
    ).reshape(own_tokens, width)

    own_places = lax.dynamic_slice_in_dim(places, tp * own_rows, own_rows, 0)
    count = thoughts.shape[0]
    pick = (own_places[None, None, :] == positions[:, :, None]).astype(bf)
    picks = []
    for s in range(seqs):
        picks.append(jnp.concatenate(
            [jnp.where(k == s, pick[:, s], jnp.zeros_like(pick[:, s])) for k in range(seqs)], axis=0
        ))
    pick = jnp.stack(picks)
    pick = jnp.pad(pick, ((0, 0), (0, -(-pick.shape[1] // 16) * 16 - pick.shape[1]), (0, 0)))
    output, d_start, gw, gq, small = back(
        attended, start_own, grad_own, out_full, fc_full, proj_full_t, params, q, kv, prev, low3, out_t, logs, normed,
        w_local, pick, block, far, counts,
    )
    output = jnp.transpose(output, (1, 0, 2))
    d_start = lax.optimization_barrier(jnp.transpose(d_start, (1, 0, 2)))
    d_inputs = jnp.where(keep.T[:, :, None], d_start.astype(f32), 0.0)
    d_thoughts = jnp.transpose(small[8 : 8 + count * seqs].reshape(seqs, count, width), (1, 0, 2))
    hidden = w_fc.shape[1]
    gw = gw.astype(f32)
    norms = lax.dynamic_slice_in_dim(small[:4], fsdp * w_fc.shape[0], w_fc.shape[0], 1)
    return (
        output,
        d_inputs,
        d_thoughts,
        jnp.transpose(gq.reshape(3, local_width, -1), (0, 2, 1)),
        gw[:, 2 * hidden : 2 * hidden + local_width].T,
        gw[:, :hidden],
        gw[:, hidden : 2 * hidden].T,
        norms[:2],
        norms[2],
        norms[3],
    )


def solution(mesh):
    in_specs = (
        P("ctx", "fsdp", None),
        P(None, "fsdp", None),
        P(None, "fsdp"),
        P("fsdp", None),
        P(None, "fsdp", "tp"),
        P("tp", "fsdp"),
        P("fsdp", "tp"),
        P("tp", "fsdp"),
        P(None, "fsdp"),
        P(None, "fsdp"),
        P("ctx", "fsdp", None),
    )
    out_specs = (
        P("ctx", "fsdp", None),
        P("ctx", "fsdp", None),
        P(None, "fsdp", None),
        P(None, "fsdp", "tp"),
        P("tp", "fsdp"),
        P("fsdp", "tp"),
        P("tp", "fsdp"),
        P(None, "fsdp"),
        P("fsdp"),
        P("fsdp"),
    )
    return jax.shard_map(local, mesh=mesh, in_specs=in_specs, out_specs=out_specs, check_vma=False)
```

```python
import functools

import jax
import jax.numpy as jnp
from jax import lax
from jax.experimental import pallas as pl
from jax.experimental.pallas import tpu as pltpu
from jax.sharding import PartitionSpec as P

HEAD_DIM = 64
DOC_MOST = 1024
EPSILON = 1e-05
MASKED = -1e30


def dot(a, b, dims=((1,), (0,))):
    return lax.dot_general(a, b, (dims, ((), ())), preferred_element_type=jnp.float32)


def hat_rows(values):
    centre = jnp.mean(values, axis=-1, keepdims=True)
    shifted = values - centre
    spread = jnp.mean(shifted * shifted, axis=-1, keepdims=True)
    inv = lax.rsqrt(spread + EPSILON)
    return shifted * inv, inv


def norm_back(hat, inv, gain, grad):
    eg = grad * gain
    return inv * (
        eg
        - jnp.mean(eg, axis=-1, keepdims=True)
        - hat * jnp.mean(eg * hat, axis=-1, keepdims=True)
    )


MESH = pl.DeviceIdType.MESH
VMEM_LIMIT = 62 << 20


def column(index, size=HEAD_DIM):
    return slice(index * size, (index + 1) * size)


def turn(value):
    return value.astype(jnp.float32).T.astype(jnp.bfloat16)


def turn_back(value):
    return value.T.astype(jnp.bfloat16)


def front_kernel(
    sizes, block,
    start_ref, low_ref, wq_ref, wo_ref, wf_ref, wp_ref, par_ref,
    att_ref, q_ref, kv_ref, prev_ref, out_t_ref, log_ref, normed_ref, wl_ref, ow_ref, fc_ref, pj_ref, params_ref,
    start_s, normed_s, wl_s, wo_s, par_s, q_s, kv_s, prev_s, qt_s, ko_s, vto_s, kp_s, vtp_s, m_s, l_s, att_s,
    in_sem, out_sem, w_loc, z_sem, z_rec, s_sem, s_rec, x_sem, x_rec, r_sem, r_rec,
    kv_sem, kv_rec, at_sem, at_rec, at_loc,
):
    F, C, T = sizes
    f, c, t = lax.axis_index("fsdp"), lax.axis_index("ctx"), lax.axis_index("tp")
    S, rows, width = start_ref.shape
    hw = q_ref.shape[2]
    heads = hw // HEAD_DIM
    own_rows = rows // T
    far = prev_ref.shape[1] // rows if C > 1 else 0
    shard = wq_ref.shape[1]
    hidden = wf_ref.shape[1]
    bf, f32 = jnp.bfloat16, jnp.float32
    sib, across = f ^ 1, f ^ 2

    def remote(src, dst, send, recv, **where):
        return pltpu.make_async_remote_copy(
            src_ref=src, dst_ref=dst, send_sem=send, recv_sem=recv, device_id=where, device_id_type=MESH
        )

    start_in = pltpu.make_async_copy(start_ref, start_s, in_sem.at[0])
    start_in.start()

    barrier = pltpu.get_barrier_semaphore()
    peers = 0
    for d in range(1, F):
        pl.semaphore_signal(barrier, inc=1, device_id={"fsdp": f ^ d}, device_id_type=MESH)
        peers += 1
    for d in range(1, T):
        pl.semaphore_signal(barrier, inc=1, device_id={"tp": lax.rem(t + d, T)}, device_id_type=MESH)
        peers += 1
    for d in range(1, C):
        pl.semaphore_signal(barrier, inc=1, device_id={"ctx": lax.rem(c + d, C)}, device_id_type=MESH)
        peers += 1
    pl.semaphore_wait(barrier, peers)

    pending = []

    def go(copy):
        copy.start()
        pending.append(copy)
        return copy

    def at_shard(ff):
        return pl.ds(pl.multiple_of(ff * shard, shard), shard)

    def at_hidden(tt):
        return pl.ds(pl.multiple_of(tt * hidden, hidden), hidden)

    def block_at(a, tt, ff):
        if a == 0:
            return par_s.at[ff]
        if a == 1:
            return wl_s.at[:, at_shard(ff), :]
        if a == 2:
            return wo_s.at[tt, ff]
        return (fc_ref if a == 3 else pj_ref).at[at_shard(ff), at_hidden(tt)]

    sources = (par_ref, wq_ref, wo_ref, wf_ref, wp_ref)

    def origin(p):
        return t if p == 0 else (t - (p + 1) // 2 if p % 2 else t + p // 2)

    def has(p):
        return t >= (p + 1) // 2 if p % 2 else t + p // 2 <= T - 1

    def spread_chip(a, p):
        src = sources[a] if p == 0 else block_at(a, origin(p), f)
        dst = block_at(a, origin(p), f)
        remote(src, dst, x_sem.at[a, p], x_rec.at[a, p], fsdp=across).start()
        remote(src, dst, s_sem.at[a, p], s_rec.at[a, p], fsdp=sib).start()

    def along(a, p, way):
        src = sources[a] if p == 0 else block_at(a, origin(p), f)
        q = p + 2 if p else 1 + way
        return remote(
            src, block_at(a, origin(p), f), z_sem.at[a, p, way], z_rec.at[a, q], tp=t + 1 if way == 0 else t - 1
        )

    def line_start(a):
        @pl.when(t < T - 1)
        def _():
            along(a, 0, 0).start()

        @pl.when(t > 0)
        def _():
            along(a, 0, 1).start()

        spread_chip(a, 0)

    def line_step(a, k):
        for way, p in ((0, 2 * k - 1), (1, 2 * k)):
            on = t < T - 1 if way == 0 else t > 0

            @pl.when(has(p) & on)
            def _():
                here = block_at(a, origin(p), f)
                remote(here, here, z_sem.at[a, p, way], z_rec.at[a, p], tp=t).wait_recv()
                along(a, p, way).start()

            @pl.when(has(p) & jnp.logical_not(on))
            def _():
                here = block_at(a, origin(p), f)
                remote(here, here, z_sem.at[a, p, way], z_rec.at[a, p], tp=t).wait_recv()

            @pl.when(has(p))
            def _():
                spread_chip(a, p)

    def relay(a, p):
        here = block_at(a, origin(p), across)
        remote(here, here, x_sem.at[a, p], x_rec.at[a, p], fsdp=f).wait_recv()
        remote(here, here, r_sem.at[a, p], r_rec.at[a, p], fsdp=sib).start()

    def take_chip(a, p):
        for ff, rec in ((sib, s_rec), (sib ^ 2, r_rec)):
            here = block_at(a, origin(p), ff)
            remote(here, here, s_sem.at[a, p], rec.at[a, p], fsdp=f).wait_recv()

    def every(what, a, ps):
        for p in ps:
            if p == 0:
                what(a, 0)
            else:
                @pl.when(has(p))
                def _():
                    what(a, p)

    def drain(a):
        last = 1 if a < 2 else 2 * T - 1

        def chip(a, p):
            src = sources[a]
            for sem in (x_sem, s_sem, r_sem):
                remote(src, src, sem.at[a, p], x_rec.at[a, p], fsdp=f).wait_send()

        every(chip, a, range(last))
        if a >= 2:
            for p in range(2 * T - 1):
                for way in range(2):
                    if p and p % 2 != 1 - way:
                        continue
                    on = t < T - 1 if way == 0 else t > 0

                    @pl.when((on & has(p)) if p else on)
                    def _():
                        remote(sources[a], sources[a], z_sem.at[a, p, way], z_rec.at[a, p], tp=t).wait_send()

    keeps = []
    for a in range(5):
        keep = pltpu.make_async_copy(sources[a], block_at(a, t, f), w_loc.at[a])
        keep.start()
        keeps.append(keep)
    spread_chip(0, 0)
    spread_chip(1, 0)
    for a in (2, 3, 4):
        line_start(a)

    relay(0, 0)
    take_chip(0, 0)
    keeps[0].wait()
    params = jnp.concatenate([par_s[ff] for ff in range(F)], axis=1)
    params_ref[...] = params
    start_in.wait()
    per_seq = rows // block

    def norm_one(index, _):
        s = index // per_seq
        here = pl.ds(pl.multiple_of(lax.rem(index, per_seq) * block, block), block)
        hat, _ = hat_rows(start_s[s, here, :].astype(f32))
        normed_s[s, here, :] = (hat * params_ref[0:1, :] + params_ref[2:3, :]).astype(bf)
        return 0

    lax.fori_loop(0, S * per_seq, norm_one, 0)
    normed_out = pltpu.make_async_copy(normed_s, normed_ref, out_sem.at[0])
    normed_out.start()

    relay(1, 0)
    take_chip(1, 0)
    keeps[1].wait()

    def kv_one(s, _):
        def one(index, _):
            here = pl.ds(pl.multiple_of(index * block, block), block)
            rows_in = normed_s[s, here, :]
            k = dot(rows_in, wl_s[1]).astype(bf)
            v = dot(rows_in, wl_s[2]).astype(bf)
            kv_s[s, here, :] = jnp.concatenate([k, v], axis=1)
            v_t = turn(v)
            for h in range(heads):
                ko_s[s, h, here, :] = k[:, column(h)]
                vto_s[s, h, :, here] = v_t[column(h)]
            return 0

        lax.fori_loop(0, per_seq, one, 0)
        return 0

    def kv_copy(s, d):
        return remote(
            kv_s.at[s], prev_s.at[s, pl.ds((far - d) * rows, rows), :],
            kv_sem.at[d, s], kv_rec.at[d, s], ctx=lax.rem(c + d, C),
        )

    for s in range(S):
        kv_one(s, 0)
        for d in range(1, far + 1):
            @pl.when(c + d < C)
            def _():
                kv_copy(s, d).start()

    def q_one(index, _):
        s = index // per_seq
        here = pl.ds(pl.multiple_of(lax.rem(index, per_seq) * block, block), block)
        q = dot(normed_s[s, here, :], wl_s[0]).astype(bf)
        q_s[s, here, :] = q
        q_t = turn(q.astype(f32) * 0.125)
        for h in range(heads):
            qt_s[s, h, :, here] = q_t[column(h)]
        return 0

    lax.fori_loop(0, S * per_seq, q_one, 0)
    outs = [
        pltpu.make_async_copy(q_s, q_ref, out_sem.at[1]),
        pltpu.make_async_copy(kv_s, kv_ref, out_sem.at[2]),
        pltpu.make_async_copy(wl_s, wl_ref, out_sem.at[4]),
    ]
    for copy in outs:
        copy.start()

    def own_part(s):
        def one(h, _):
            spot, line = pl.ds(pl.multiple_of(h * HEAD_DIM, HEAD_DIM), HEAD_DIM), pl.ds(h, 1)
            for i in range(per_seq):
                span = column(i, block)
                low = low_ref[s, :, span] - far * rows
                top = i * block + lax.broadcasted_iota(jnp.int32, (1, block), 1)
                first = max(0, i * block - (DOC_MOST - 1)) // block * block
                many = (i + 1) * block - first
                place = first + lax.broadcasted_iota(jnp.int32, (many, 1), 0)
                scores = dot(ko_s[s, h, first : first + many, :], qt_s[s, h, :, span])
                scores = jnp.where((place >= low) & (place <= top), scores, MASKED)
                m = jnp.max(scores, axis=0, keepdims=True)
                p = jnp.exp(scores - m)
                m_s[s, line, span] = m
                l_s[s, line, span] = jnp.sum(p, axis=0, keepdims=True)
                out_t_ref[s, spot, span] = dot(vto_s[s, h, :, first : first + many], p.astype(bf))
            return 0

        lax.fori_loop(0, heads, one, 0)

    def far_part(s):
        for h in range(heads):
            kp_s[h] = prev_s[s, :, column(h)]
            vtp_s[h] = turn(prev_s[s, :, column(heads + h)])

        def one(h, _):
            spot, line = pl.ds(pl.multiple_of(h * HEAD_DIM, HEAD_DIM), HEAD_DIM), pl.ds(h, 1)
            for i in range(per_seq):
                span = column(i, block)
                first = max(0, far * rows + i * block - (DOC_MOST - 1)) // block * block
                if first >= far * rows:
                    continue
                many = far * rows - first
                place = first + lax.broadcasted_iota(jnp.int32, (many, 1), 0)
                scores = dot(kp_s[h, first : first + many, :], qt_s[s, h, :, span])
                scores = jnp.where(place >= low_ref[s, :, span], scores, MASKED)
                old = m_s[s, line, span]
                m = jnp.maximum(old, jnp.max(scores, axis=0, keepdims=True))
                p = jnp.exp(scores - m)
                alpha = jnp.exp(old - m)
                m_s[s, line, span] = m
                l_s[s, line, span] = alpha * l_s[s, line, span] + jnp.sum(p, axis=0, keepdims=True)
                out_t_ref[s, spot, span] = alpha * out_t_ref[s, spot, span] + dot(
                    vtp_s[h, :, first : first + many], p.astype(bf)
                )
            return 0

        lax.fori_loop(0, heads, one, 0)

    def finish_part(s):
        for h in range(heads):
            out_t_ref[s, column(h), :] = out_t_ref[s, column(h), :] / l_s[s, h : h + 1, :]
            log_ref[s, h : h + 1, :] = m_s[s, h : h + 1, :] + jnp.log(l_s[s, h : h + 1, :])
        for tt in range(T):
            att_s[tt, s] = out_t_ref[s, :, column(tt, own_rows)].astype(bf)

    every_p = range(2 * T - 1)
    for a in (2, 3):
        line_step(a, 1)

    def own_loop(s, _):
        own_part(s)
        return 0

    lax.fori_loop(0, S, own_loop, 0)
    line_step(2, 2)
    line_step(4, 1)
    line_step(3, 2)
    for k in range(3, T):
        line_step(2, k)
    every(relay, 2, every_p)

    def wait_far(s):
        for d in range(1, far + 1):
            @pl.when(c >= d)
            def _():
                kv_copy(s, d).wait_recv()

            @pl.when(c < d)
            def _():
                prev_s[s, (far - d) * rows : (far - d + 1) * rows, :] = jnp.zeros((rows, 2 * hw), bf)

    at = [[None] * S for _ in range(T)]
    for s in range(S):
        if far:
            wait_far(s)

            @pl.when(c > 0)
            def _():
                far_part(s)
        finish_part(s)
        for d in range(1, T):
            peer = lax.rem(t + d, T)
            at[d][s] = go(
                remote(att_s.at[peer, s], att_ref.at[t, s], at_sem.at[d, s], at_rec.at[d, s], tp=peer)
            )
        own_at = pltpu.make_async_copy(att_s.at[t, s], att_ref.at[t, s], at_loc.at[s])
        own_at.start()
        at[0][s] = own_at
        if s == 0:
            line_step(4, 2)
            for k in range(3, T):
                line_step(3, k)
            every(relay, 3, every_p)
    prev_out = pltpu.make_async_copy(prev_s, prev_ref, out_sem.at[3])
    if far:
        prev_out.start()
    for k in range(3, T):
        line_step(4, k)
    every(take_chip, 2, every_p)
    keeps[2].wait()
    for tt in range(T):
        for ff in range(F):
            ow_ref[column(tt, hw), column(ff, shard)] = wo_s[tt, ff]
    every(relay, 4, every_p)
    for a in (3, 4):
        every(take_chip, a, every_p)
        keeps[a].wait()
    for s in range(S):
        at[0][s].wait()
        for d in range(1, T):
            at[d][s].wait_recv()
    normed_out.wait()
    for copy in outs:
        copy.wait()
    if far:
        prev_out.wait()
    for copy in pending:
        copy.wait_send()
    for a in range(5):
        drain(a)
    for s in range(S):
        for d in range(1, far + 1):
            @pl.when(c + d < C)
            def _():
                kv_copy(s, d).wait_send()


def front(start, low, wq, wo, wf, wp, params, block, far, counts):
    F, C, T = counts
    S, rows, width = start.shape
    hw = wq.shape[2]
    shard = wq.shape[1]
    heads = hw // HEAD_DIM
    hidden = wf.shape[1]
    bf, f32 = jnp.bfloat16, jnp.float32
    vmem = pl.BlockSpec(memory_space=pltpu.VMEM)
    anywhere = pl.BlockSpec(memory_space=pl.ANY)
    dma = lambda *shape: pltpu.SemaphoreType.DMA(shape)
    past = max(far, 1) * rows
    shape = jax.ShapeDtypeStruct
    return pl.pallas_call(
        functools.partial(front_kernel, counts, block),
        in_specs=[anywhere, vmem, anywhere, anywhere, anywhere, anywhere, anywhere],
        out_specs=[
            anywhere, anywhere, anywhere, anywhere, vmem, vmem, anywhere, anywhere, vmem, anywhere, anywhere, vmem
        ],
        out_shape=[
            shape((T, S, hw, rows // T), bf),
            shape((S, rows, hw), bf),
            shape((S, rows, 2 * hw), bf),
            shape((S, past, 2 * hw), bf),
            shape((S, hw, rows), f32),
            shape((S, 8, rows), f32),
            shape((S, rows, width), bf),
            shape((3, F * shard, hw), bf),
            shape((T * hw, F * shard), bf),
            shape((F * shard, T * hidden), bf),
            shape((F * shard, T * hidden), bf),
            shape((8, F * shard), f32),
        ],
        scratch_shapes=[
            pltpu.VMEM((S, rows, width), bf),
            pltpu.VMEM((S, rows, width), bf),
            pltpu.VMEM((3, F * shard, hw), bf),
            pltpu.VMEM((T, F, hw, shard), bf),
            pltpu.VMEM((F, 8, shard), f32),
            pltpu.VMEM((S, rows, hw), bf),
            pltpu.VMEM((S, rows, 2 * hw), bf),
            pltpu.VMEM((S, past, 2 * hw), bf),
            pltpu.VMEM((S, heads, HEAD_DIM, rows), bf),
            pltpu.VMEM((S, heads, rows, HEAD_DIM), bf),
            pltpu.VMEM((S, heads, HEAD_DIM, rows), bf),
            pltpu.VMEM((heads, past, HEAD_DIM), bf),
            pltpu.VMEM((heads, HEAD_DIM, past), bf),
            pltpu.VMEM((S, 8, rows), f32),
            pltpu.VMEM((S, 8, rows), f32),
            pltpu.VMEM((T, S, hw, rows // T), bf),
            dma(1), dma(5), dma(5),
            dma(5, 2 * T, 2), dma(5, 2 * T), dma(5, 2 * T), dma(5, 2 * T), dma(5, 2 * T), dma(5, 2 * T), dma(5, 2 * T),
            dma(5, 2 * T),
            dma(far + 1, S), dma(far + 1, S), dma(T, S), dma(T, S), dma(S),
        ],
        compiler_params=pltpu.CompilerParams(
            vmem_limit_bytes=VMEM_LIMIT, collective_id=1, has_side_effects=True
        ),
        cost_estimate=pl.CostEstimate(flops=8 * 10**9, bytes_accessed=64 << 20, transcendentals=8 << 20),
    )(start, low, wq, wo, wf, wp, params)


def padded(size):
    return -(-size // 128) * 128


def add_rows(target, sources, rows_at_once=16):
    def one(i, _):
        here = pl.ds(pl.multiple_of(i * rows_at_once, rows_at_once), rows_at_once)
        total = target[here, :].astype(jnp.float32)
        for source in sources:
            total = total + source[here, :].astype(jnp.float32)
        target[here, :] = total.astype(target.dtype)
        return 0

    lax.fori_loop(0, target.shape[0] // rows_at_once, one, 0)


def gelu_parts(x):
    square = x * x
    th = jnp.tanh(0.7978845608028654 * (x + 0.044715 * (square * x)))
    half = 0.5 * (1.0 + th)
    slope = half + (0.5 * x) * (1.0 - th * th) * (0.7978845608028654 * (1.0 + (3 * 0.044715) * square))
    return x * half, slope


def back_kernel(
    sizes, block, far, step_cols,
    att_ref, start_ref, grad_ref, outw_ref, fc_ref, pj_ref, params_ref,
    q_ref, kv_ref, prev_ref, low_ref, out_t_ref, log_ref, normed_ref, wl_ref, pick_ref,
    output_ref, dstart_ref, gw_ref, gq_ref, small_ref,
    start_s, mid_s, grad_s, ob_s, gbuf, rcore, rx, rc, rz, g2, r2c, r2x,
    da_s, da_r, dp_s, rec_s, kv_s, dq_s, rs_r, gq_s, rgq, rgc, sm_s, rst, rsc, rsf,
    in_sem, w_sem, core_sem, core_rec, x_sem, x_rec, c2_sem, c2_rec, x2_sem, x2_rec,
    c_sem, c_rec, z_sem, z_rec, b_sem, b_rec, da_sem, da_rec, dp_sem, dp_rec,
    rs_sem, rs_rec, ag_sem, ag_rec, gq_sem, gq_rec, gc_sem, gc_rec,
    st_sem, st_rec, sc_sem, sc_rec, sf_sem, sf_rec, loc_sem, wl_sem, credit,
):
    F, C, T = sizes
    f, c, t = lax.axis_index("fsdp"), lax.axis_index("ctx"), lax.axis_index("tp")
    S, rows, hw = q_ref.shape
    heads = hw // HEAD_DIM
    width = start_s.shape[2]
    own_rows = rows // T
    tokens = S * own_rows
    shard = gbuf.shape[1]
    hidden = fc_ref.shape[1] // T
    wide = 2 * hidden
    per_seq = rows // block
    bf, f32 = jnp.bfloat16, jnp.float32
    sib, across = f ^ 1, f ^ 2

    def remote(src, dst, send, recv, **where):
        return pltpu.make_async_remote_copy(
            src_ref=src, dst_ref=dst, send_sem=send, recv_sem=recv, device_id=where, device_id_type=MESH
        )

    pending = []

    def go(copy, like):
        copy.start()
        pending.append(like)

    def landed(ref, sem):
        remote(ref, ref, b_rec, sem, fsdp=f).wait_recv()

    def sent(ref, sem):
        remote(ref, ref, sem, b_rec, fsdp=f).wait_send()

    def tp_peer(d):
        return lax.rem(t + d, T)

    def tp_source(d):
        return lax.rem(t + T - d, T)

    def rows_of(owner):
        return pl.ds(pl.multiple_of(owner * own_rows, own_rows), own_rows)

    ag_own, ag_whole = (ob_s, ob_s), (output_ref, dstart_ref)

    def ag_copy(a, s, owner, step, way):
        whole = ag_whole[a].at[s, rows_of(owner), :]
        src = ag_own[a].at[s] if step == 0 else whole
        return lambda to: remote(src, whole, ag_sem.at[a, s, step, way], ag_rec.at[a, s, step, way], tp=to)

    def ag_keep(a, s):
        return pltpu.make_async_copy(ag_own[a].at[s], ag_whole[a].at[s, rows_of(t), :], loc_sem.at[a, s])

    def ag_start(a, s):
        @pl.when(t < T - 1)
        def _():
            ag_copy(a, s, t, 0, 0)(t + 1).start()

        @pl.when(t > 0)
        def _():
            ag_copy(a, s, t, 0, 1)(t - 1).start()

        ag_keep(a, s).start()

    def ag_step(a, s, step):
        @pl.when(t >= step)
        def _():
            ag_copy(a, s, t - step, step - 1, 0)(t).wait_recv()

        @pl.when((t >= step) & (t < T - 1))
        def _():
            ag_copy(a, s, t - step, step, 0)(t + 1).start()

        @pl.when(t + step <= T - 1)
        def _():
            ag_copy(a, s, t + step, step - 1, 1)(t).wait_recv()

        @pl.when((t + step <= T - 1) & (t > 0))
        def _():
            ag_copy(a, s, t + step, step, 1)(t - 1).start()

    def ag_drain(a, s, first):
        if not first:
            ag_keep(a, s).wait()
        for step in range(first, T - 1 if first or a else 1):
            @pl.when((t >= step) & (t < T - 1))
            def _():
                ag_copy(a, s, t - step, step, 0)(t + 1).wait_send()

            @pl.when((t + step <= T - 1) & (t > 0))
            def _():
                ag_copy(a, s, t + step, step, 1)(t - 1).wait_send()

    across_at = lambda b: T + b
    main = pl.ds(0, wide)

    def core_send(b):
        slot = b % 2
        if b >= 2:
            pl.semaphore_wait(credit, 1)
        for k in range(2):
            remote(
                gbuf.at[2 * T + 2 * slot + k, :, main], rcore.at[slot, k],
                core_sem.at[b, k], core_rec.at[b, k], fsdp=sib,
            ).start()

    def core_add(b):
        slot = b % 2
        landed(rcore.at[slot, 1], core_rec.at[b, 1])
        add_rows(gbuf.at[across_at(b), :, main], [rcore.at[slot, 1]])
        out = gbuf.at[across_at(b), :, main]
        go(
            remote(out, rx.at[b, :, main], x_sem.at[b], x_rec.at[b], fsdp=across),
            lambda: (rx.at[b, :, main], x_sem.at[b]),
        )
        landed(rcore.at[slot, 0], core_rec.at[b, 0])
        add_rows(gbuf.at[b, :, main], [rcore.at[slot, 0]])
        if b < T - 2:
            pl.semaphore_signal(credit, inc=1, device_id={"fsdp": sib}, device_id_type=MESH)

    held = [b // C for b in range(T)]

    def ctx_copy(b, d, to):
        return remote(gbuf.at[b], rc.at[held[b], d - 1], c_sem.at[b], c_rec.at[b, d], ctx=to)

    def cross_add(b):
        landed(rx.at[b, :, main], x_rec.at[b])
        add_rows(gbuf.at[b, :, main], [rx.at[b, :, main]])

    def ctx_send(b):
        owner = b % C
        for d in range(1, C):
            @pl.when(lax.rem(c + d, C) == owner)
            def _():
                ctx_copy(b, d, owner).start()

    def ctx_wait(b):
        @pl.when(c == b % C)
        def _():
            for d in range(1, C):
                ctx_copy(b, d, c).wait_recv()
            if C > 1:
                add_rows(gbuf.at[b], [rc.at[held[b], d - 1] for d in range(1, C)])

    def z_round(b, step):
        def hop(to, way):
            return remote(gbuf.at[b], rz.at[held[b], way], z_sem.at[b], z_rec.at[b, way], tp=to)

        def visit(way, before, here):
            @pl.when((c == b % C) & here)
            def _():
                if step:
                    hop(t, way).wait_recv()
                    add_rows(gbuf.at[b], [rz.at[held[b], way]])

                @pl.when(before)
                def _():
                    hop(t - 1 if way == 0 else t + 1, way).start()

        if T - 1 - step >= b and b < T - 1:
            visit(0, t > b, t == T - 1 - step)
        if step <= b and b > 0:
            visit(1, t < b, t == step)

    def feed_phase(att_s, outw_s, w_s, x_s, nm_s, nmt_s, gt_s, acc_s):
        steps = hidden // step_cols
        ring = w_s.shape[0]
        total_steps = 2 * T * steps

        def stream(n):
            at = pl.ds(pl.multiple_of(lax.rem(n, T * steps) * step_cols, step_cols), step_cols)
            slot = lax.rem(n, ring)
            return [
                pltpu.make_async_copy(ref.at[:, at], w_s.at[slot, k], w_sem.at[slot, k])
                for k, ref in enumerate((fc_ref, pj_ref))
            ]

        def take(n):
            for copy in stream(n):
                copy.wait()

            @pl.when(n + ring - 1 < total_steps)
            def _():
                for copy in stream(n + ring - 1):
                    copy.start()

            return lax.rem(n, ring)

        loads = [
            pltpu.make_async_copy(att_ref, dq_s, in_sem.at[0]),
            pltpu.make_async_copy(outw_ref, outw_s, in_sem.at[1]),
            pltpu.make_async_copy(start_ref, start_s, in_sem.at[2]),
            pltpu.make_async_copy(grad_ref, grad_s, in_sem.at[3]),
        ]
        for copy in loads:
            copy.start()
        for n in range(ring - 1):
            for copy in stream(n):
                copy.start()

        barrier = pltpu.get_barrier_semaphore()
        peers = 0
        for d in range(1, F):
            pl.semaphore_signal(barrier, inc=1, device_id={"fsdp": f ^ d}, device_id_type=MESH)
            peers += 1
        for d in range(1, T):
            pl.semaphore_signal(barrier, inc=1, device_id={"tp": tp_peer(d)}, device_id_type=MESH)
            peers += 1
        for d in range(1, C):
            pl.semaphore_signal(barrier, inc=1, device_id={"ctx": lax.rem(c + d, C)}, device_id_type=MESH)
            peers += 1
        pl.semaphore_wait(barrier, peers)

        for copy in loads:
            copy.wait()
        mid = start_s[...].reshape(tokens, width).astype(f32)
        for g in range(T):
            for s in range(S):
                att_s[g, column(s, own_rows), :] = turn(dq_s[g, s])
            mid = mid + dot(att_s[g], outw_s[column(g, hw), :])
        mid_s[...] = mid
        hat, _ = hat_rows(mid)
        nm = hat * params_ref[1:2] + params_ref[3:4]
        nm_s[...] = nm.astype(bf)
        nmt_s[...] = turn_back(nm)
        gt_s[...] = turn(grad_s[...])
        acc_s[...] = jnp.zeros_like(acc_s)

        def forward(j, _):
            slot = take(j)
            x = dot(nm_s[...], w_s[slot, 0])
            x_s[j] = x
            act, _ = gelu_parts(x)
            acc_s[...] += dot(act.astype(bf), w_s[slot, 1], ((1,), (1,)))
            return 0

        lax.fori_loop(0, T * steps, forward, 0)
        ob_s[...] = (mid_s[...] + acc_s[...]).astype(bf).reshape(S, own_rows, width)
        for s in range(S):
            ag_start(0, s)
        acc_s[...] = jnp.zeros_like(acc_s)

        for n in range(T):
            if n >= 2:
                for k in range(2):
                    sent(rcore.at[0, 0], core_sem.at[n - 2, k])
            slot = n % 2

            def backward(j, _):
                here = pl.ds(pl.multiple_of(j * step_cols, step_cols), step_cols)
                there = pl.ds(pl.multiple_of(hidden + j * step_cols, step_cols), step_cols)
                at_w = take(T * steps + n * steps + j)
                fc, proj = w_s[at_w, 0], w_s[at_w, 1]
                act, slope = gelu_parts(x_s[n * steps + j])
                act = act.astype(bf)
                d_exp = (slope * dot(grad_s[...], proj)).astype(bf)
                acc_s[...] += dot(d_exp, fc, ((1,), (1,)))
                d_fc = dot(nmt_s[...], d_exp).astype(bf)
                d_proj = dot(gt_s[...], act).astype(bf)
                for ff in range(F):
                    r = f ^ ff
                    odd, half = lax.rem(r, 2), r // 2
                    at = (1 - odd) * (half * T + n) + odd * (2 * T + 2 * slot + half)
                    gbuf[at, :, here] = d_fc[column(ff, shard)]
                    gbuf[at, :, there] = d_proj[column(ff, shard)]
                return 0

            lax.fori_loop(0, steps, backward, 0)
            core_send(n)
            if n:
                core_add(n - 1)

        mid = mid_s[...]
        hat, inv = hat_rows(mid)
        d_nm = acc_s[...]
        d_mid = grad_s[...].astype(f32) + norm_back(hat, inv, params_ref[1:2], d_nm)
        d_mid_t = turn_back(d_mid)
        for g in range(T):
            d_att = dot(outw_s[column(g, hw), :], d_mid_t).astype(bf)
            for s in range(S):
                da_s[g, s] = d_att[:, column(s, own_rows)]
        for s in range(S):
            for d in range(1, T):
                go(
                    remote(da_s.at[tp_peer(d), s], da_r.at[t, s], da_sem.at[d, s], da_rec.at[d, s], tp=tp_peer(d)),
                    lambda d=d, s=s: (da_s.at[0, s], da_sem.at[d, s]),
                )
        sm_s[...] = jnp.zeros_like(sm_s)
        sm_s[1:2, :] = jnp.sum(d_nm * hat, axis=0, keepdims=True)
        sm_s[3:4, :] = jnp.sum(d_nm, axis=0, keepdims=True)
        mid_s[...] = d_mid
        if g2.shape[3] > hw:
            g2[:, :, :, hw:] = jnp.zeros(g2.shape[:3] + (g2.shape[3] - hw,), bf)
        for g in range(T):
            d_out = dot(d_mid_t, att_s[g]).astype(bf)
            for ff in range(F):
                g2[f ^ ff, g, :, :hw] = d_out[column(ff, shard)]
        core_add(T - 1)

    bf_mem = lambda *shape: pltpu.VMEM(shape, bf)
    f32_mem = lambda *shape: pltpu.VMEM(shape, f32)
    pl.run_scoped(
        feed_phase,
        bf_mem(T, tokens, hw), bf_mem(T * hw, width), bf_mem(3, 2, width, step_cols),
        f32_mem(T * hidden // step_cols, tokens, step_cols),
        bf_mem(tokens, width), bf_mem(width, tokens), bf_mem(width, tokens), f32_mem(tokens, width),
    )

    for k in range(2):
        out = g2.at[1 + 2 * k]
        go(
            remote(out, r2c.at[k], c2_sem.at[k], c2_rec.at[k], fsdp=sib),
            lambda k=k: (r2c.at[k], c2_sem.at[k]),
        )

    def dp_copy(d, s):
        return remote(
            dp_s.at[far - d, s], rec_s.at[d - 1, s], dp_sem.at[d, s], dp_rec.at[d, s], ctx=lax.rem(c + C - d, C)
        )

    def sums_along(snd, wl_s):
        def kv_sum(s):
            for d in range(1, far + 1):
                @pl.when(c + d < C)
                def _():
                    dp_copy(d, s).wait_recv()
                    for g in range(T):
                        kv_s[g, s] = (kv_s[g, s].astype(f32) + rec_s[d - 1, s, g].astype(f32)).astype(bf)

        def partials(s):
            if s == 0:
                pltpu.make_async_copy(wl_ref, wl_s, wl_sem).wait()

            def one(o, _):
                total = dot(wl_s[0], dq_s[o, s])
                for j in (1, 2):
                    total = total + dot(wl_s[j], kv_s[o, s, column(j - 1, hw), :])
                snd[s, o] = total.astype(bf)
                return 0

            lax.fori_loop(0, T, one, 0)

        def rs_copy(s, o, way, at):
            to = at - 1 if way == 0 else at + 1
            slot = T if (to == o and way == 1) else o
            return remote(
                snd.at[s, o], rs_r.at[s, slot], rs_sem.at[s, o], rs_rec.at[s, o, way], tp=t - 1 if way == 0 else t + 1
            )

        def rs_slot(s, k):
            for at in range(T):
                for way, o, begins in ((0, k - (T - 1 - at), at == T - 1), (1, T - 1 + at - k, at == 0)):
                    if not (0 <= o <= at if way == 0 else at <= o <= T - 1):
                        continue

                    @pl.when(t == at)
                    def _():
                        if not begins:
                            landed(rs_r.at[s, T if (o == at and way == 1) else o], rs_rec.at[s, o, way])
                        if o != at:
                            if not begins:
                                add_rows(snd.at[s, o], [rs_r.at[s, o]], 128)
                            before = o - 1 if way == 0 else o + 1
                            if 0 <= before < T:
                                sent(snd.at[s, before], rs_sem.at[s, before])
                            rs_copy(s, o, way, at).start()

        return kv_sum, partials, rs_slot

    def attention_phase(
        snd, wl_s, q_s, kvo_s, prv_s, ot_s, k_h, kt_h, v_h, q_h, qt_h, g_h, gt_h, dqt_s, dk_s, dv_s, del_s
    ):
        kv_sum, partials, rs_slot = sums_along(snd, wl_s)

        def loads(s):
            return [
                pltpu.make_async_copy(ref.at[s], mem, in_sem.at[k])
                for k, (ref, mem) in enumerate(((q_ref, q_s), (kv_ref, kvo_s), (out_t_ref, ot_s), (prev_ref, prv_s)))
            ]

        for copy in loads(0):
            copy.start()
        for k in (1, 0):
            landed(r2c.at[k], c2_rec.at[k])
            for b in range(T):
                add_rows(g2.at[2 * k, b], [r2c.at[k, b]])
            if k:
                go(remote(g2.at[2], r2x, x2_sem, x2_rec, fsdp=across), lambda: (r2x, x2_sem))

        def keys(s):
            for h in range(heads):
                q = q_s[:, column(h)].astype(f32) * 0.125
                q_h[h] = q.astype(bf)
                qt_h[h] = turn_back(q)
                if far:
                    k = prv_s[:, column(h)]
                    k_h[h, : far * rows] = k
                    kt_h[h, :, : far * rows] = turn(k)
                    v_h[h, : far * rows] = prv_s[:, column(heads + h)]
                k = kvo_s[:, column(h)]
                k_h[h, far * rows :] = k
                kt_h[h, :, far * rows :] = turn(k)
                v_h[h, far * rows :] = kvo_s[:, column(heads + h)]

        def grads(s):
            da_r[t, s] = da_s[t, s]
            for d in range(1, T):
                landed(da_r.at[tp_source(d), s], da_rec.at[d, s])
            for h in range(heads):
                for g in range(T):
                    gt_h[h, :, column(g, own_rows)] = da_r[g, s, column(h), :]
                g_t = gt_h[h].astype(f32)
                g_h[h] = turn_back(g_t)
                del_s[h : h + 1, :] = jnp.sum(g_t * ot_s[column(h), :], axis=0, keepdims=True)
            dqt_s[...] = jnp.zeros_like(dqt_s)

        def part(s, h, base, count, own):
            spot = pl.ds(pl.multiple_of(h * HEAD_DIM, HEAD_DIM), HEAD_DIM)
            dk_s[:count] = jnp.zeros((count, HEAD_DIM), f32)
            dv_s[:count] = jnp.zeros((count, HEAD_DIM), f32)
            for i in range(per_seq):
                span = column(i, block)
                reach = far * rows + i * block
                first = max(0, reach - (DOC_MOST - 1) - base) // block * block
                last = min(count, reach + block - base)
                if first >= last:
                    continue
                low = low_ref[s, :, span] - base
                place = first + lax.broadcasted_iota(jnp.int32, (last - first, 1), 0)
                allowed = place >= low
                if own:
                    allowed = allowed & (place <= i * block + lax.broadcasted_iota(jnp.int32, (1, block), 1))
                here = slice(base + first, base + last)
                scores = dot(k_h[h, here, :], qt_h[h, :, span])
                p = jnp.exp(jnp.where(allowed, scores - log_ref[s, pl.ds(h, 1), span], MASKED))
                ds = (p * (dot(v_h[h, here, :], gt_h[h, :, span]) - del_s[pl.ds(h, 1), span])).astype(bf)
                dv_s[first:last] += dot(p.astype(bf), g_h[h, span, :])
                dk_s[first:last] += dot(ds, q_h[h, span, :])
                dqt_s[spot, span] += dot(kt_h[h, :, here], ds)
            return spot, pl.ds(pl.multiple_of(hw + h * HEAD_DIM, HEAD_DIM), HEAD_DIM)

        def far_part(s):
            def one(h, _):
                k_at, v_at = part(s, h, 0, far * rows, False)
                for at, source in ((k_at, dk_s), (v_at, dv_s)):
                    turned = source[: far * rows].T.astype(bf)
                    for j in range(far):
                        for g in range(T):
                            dp_s[j, s, g, at, :] = turned[:, column(j * T + g, own_rows)]
                return 0

            lax.fori_loop(0, heads, one, 0)

        def own_part(s):
            def one(h, _):
                k_at, v_at = part(s, h, far * rows, rows, True)
                for at, source in ((k_at, dk_s), (v_at, dv_s)):
                    turned = source[:rows].T.astype(bf)
                    for g in range(T):
                        kv_s[g, s, at, :] = turned[:, column(g, own_rows)]
                return 0

            lax.fori_loop(0, heads, one, 0)

        for s in range(S):
            for copy in loads(s):
                copy.wait()
            keys(s)
            grads(s)
            if s + 1 < S:
                for copy in loads(s + 1):
                    copy.start()
            if s == 0:
                for other in range(S):
                    ag_step(0, other, 1)
            if far:
                @pl.when(c > 0)
                def _():
                    far_part(s)

                for d in range(1, far + 1):
                    @pl.when(c >= d)
                    def _():
                        dp_copy(d, s).start()
            if s:
                rs_slot(s - 1, 1)
            else:
                cross_add(0)
            own_part(s)
            for g in range(T):
                dq_s[g, s] = (0.125 * dqt_s[:, column(g, own_rows)]).astype(bf)
            if s:
                rs_slot(s - 1, 2)
            if s < T - 2:
                for other in range(S):
                    ag_step(0, other, s + 2)
            if s + 1 < T:
                cross_add(s + 1)
            kv_sum(s)
            partials(s)
            rs_slot(s, 0)

    def last_phase(snd, wl_s, normed_s, gq_acc, tot_s):
        kv_sum, partials, rs_slot = sums_along(snd, wl_s)
        normed_in = pltpu.make_async_copy(normed_ref, normed_s, in_sem.at[0])
        normed_in.start()

        gain = params_ref[0:1]

        def norm_stage(s):
            tot_s[...] = snd[s, t].astype(f32)

            @pl.when(t < T - 1)
            def _():
                tot_s[...] += rs_r[s, t].astype(f32)

            @pl.when(t > 0)
            def _():
                tot_s[...] += rs_r[s, T].astype(f32)

            d_normed = tot_s[...].T
            hat, inv = hat_rows(start_s[s].astype(f32))
            value = mid_s[column(s, own_rows), :] + norm_back(hat, inv, gain, d_normed)
            ag_drain(0, s, 0)
            ob_s[s] = value.astype(bf)
            ag_start(1, s)
            sm_s[0:1, :] += jnp.sum(d_normed * hat, axis=0, keepdims=True)
            sm_s[2:3, :] += jnp.sum(d_normed, axis=0, keepdims=True)

        for k in range(3, T):
            rs_slot(0, k)
        norm_stage(0)
        landed(r2x, x2_rec)
        side = pl.ds(wide, g2.shape[3])
        for b in range(T):
            gbuf[b, :, side] = (g2[0, b].astype(f32) + r2x[b].astype(f32)).astype(bf)
        for b in range(min(S + 1, T)):
            ctx_send(b)

        normed_in.wait()
        gq_acc[...] = jnp.zeros_like(gq_acc)
        for s in range(S):

            def one(o, _):
                near = normed_s[s, rows_of(o), :]
                gq_acc[:hw, :] += dot(dq_s[o, s], near)
                gq_acc[hw:, :] += dot(kv_s[o, s], near)
                return 0

            lax.fori_loop(0, T, one, 0)
        for k in range(F):
            gq_s[k] = gq_acc[:, column(k, shard)].astype(bf)
        for d in range(1, F):
            go(
                remote(gq_s.at[f ^ d], rgq.at[d - 1], gq_sem.at[d], gq_rec.at[d], fsdp=f ^ d),
                lambda d=d: (gq_s.at[0], gq_sem.at[d]),
            )
        for b in range(min(S + 1, T), T):
            cross_add(b)
            ctx_send(b)
        for s in range(1, S):
            for k in range(1, T):
                rs_slot(s, k)
                if k == T - 2:
                    ag_step(1, 0, 1)
            norm_stage(s)

        thoughts = jnp.zeros((pick_ref.shape[1], width), f32)
        for s in range(S):
            thoughts = thoughts + dot(pick_ref[s], ob_s[s])
        sm_s[8:, :] = thoughts
        for d in range(1, T):
            go(
                remote(sm_s, rst.at[d], st_sem.at[d], st_rec.at[d], tp=tp_peer(d)),
                lambda d=d: (sm_s, st_sem.at[d]),
            )
        for b in range(T):
            ctx_wait(b)
            z_round(b, 0)

        gq_sum = gq_s[f].astype(f32)
        for d in range(1, F):
            landed(rgq.at[d - 1], gq_rec.at[d])
            gq_sum = gq_sum + rgq[d - 1].astype(f32)
        rgc[c] = gq_sum.astype(bf)
        for d in range(1, C):
            go(
                remote(rgc.at[c], rgc.at[c], gc_sem.at[d], gc_rec.at[d], ctx=lax.rem(c + d, C)),
                lambda d=d: (rgc.at[0], gc_sem.at[d]),
            )

        for d in range(1, T):
            landed(rst.at[d], st_rec.at[d])
        rst[0] = sm_s[...]
        total = jnp.zeros(sm_s.shape, f32)
        for k in range(T):
            total = total + rst[lax.rem(t + T - k, T)]
        rsc[c] = total
        for d in range(1, C):
            go(
                remote(rsc.at[c], rsc.at[c], sc_sem.at[d], sc_rec.at[d], ctx=lax.rem(c + d, C)),
                lambda d=d: (rsc.at[0], sc_sem.at[d]),
            )
        for step in range(1, T):
            if step > 1:
                ag_step(1, 0, step)
            for s in range(1, S):
                ag_step(1, s, step)
            for b in range(T):
                z_round(b, step)
            if step == 1:
                for d in range(1, C):
                    landed(rsc.at[0], sc_rec.at[d])
                total = jnp.zeros(sm_s.shape, f32)
                for k in range(C):
                    total = total + rsc[k]
                small_ref[8:, :] = total[8:]
                rsf[f] = total
                for d in range(1, F):
                    go(
                        remote(rsf.at[f], rsf.at[f], sf_sem.at[d], sf_rec.at[d], fsdp=f ^ d),
                        lambda d=d: (rsf.at[0], sf_sem.at[d]),
                    )
        for d in range(1, F):
            landed(rsf.at[0], sf_rec.at[d])
        norms = jnp.zeros((8, sm_s.shape[1]), f32)
        for k in range(F):
            norms = norms + rsf[k, 0:8, :]
        small_ref[0:8, :] = norms

        for d in range(1, C):
            landed(rgc.at[0], gc_rec.at[d])
        total = jnp.zeros(gq_ref.shape, f32)
        for k in range(C):
            total = total + rgc[k].astype(f32)
        gq_ref[...] = total
        for o in range(T):
            @pl.when((t == o + 1) | (t == o - 1))
            def _():
                for s in range(S):
                    sent(snd.at[s, o], rs_sem.at[s, o])

    def after_feed(snd, wl_s):
        wl_in = pltpu.make_async_copy(wl_ref, wl_s, wl_sem)
        wl_in.start()
        pl.run_scoped(
            functools.partial(attention_phase, snd, wl_s),
            bf_mem(rows, hw), bf_mem(rows, 2 * hw), bf_mem(max(far, 1) * rows, 2 * hw), f32_mem(hw, rows),
            bf_mem(heads, (far + 1) * rows, HEAD_DIM), bf_mem(heads, HEAD_DIM, (far + 1) * rows),
            bf_mem(heads, (far + 1) * rows, HEAD_DIM),
            bf_mem(heads, rows, HEAD_DIM), bf_mem(heads, HEAD_DIM, rows),
            bf_mem(heads, rows, HEAD_DIM), bf_mem(heads, HEAD_DIM, rows),
            f32_mem(hw, rows), f32_mem(max(far, 1) * rows, HEAD_DIM), f32_mem(max(far, 1) * rows, HEAD_DIM),
            f32_mem(8, rows),
        )
        pl.run_scoped(
            functools.partial(last_phase, snd, wl_s),
            bf_mem(S, rows, width), f32_mem(3 * hw, width), f32_mem(width, own_rows),
        )

    pl.run_scoped(after_feed, bf_mem(S, T, width, own_rows), bf_mem(3, width, hw))

    for b in range(T):
        owner = b % C
        final = lambda d: remote(gbuf.at[b], rx.at[b], b_sem.at[d], b_rec, ctx=lax.rem(owner + d, C))

        @pl.when((t == b) & (c == owner))
        def _():
            for d in range(1, C):
                final(d).start()
            gw_ref[...] = gbuf[b]
            for d in range(1, C):
                final(d).wait_send()

        if C > 1:
            @pl.when((t == b) & (c != owner))
            def _():
                final(1).wait_recv()
                gw_ref[...] = rx[b]

    for like in pending:
        sent(*like())
    for n in range(max(T - 2, 0), T):
        for k in range(2):
            sent(rcore.at[0, 0], core_sem.at[n, k])
    for b in range(T):
        owner = b % C
        if C > 1:
            @pl.when(c != owner)
            def _():
                ctx_copy(b, 1, owner).wait_send()

        @pl.when((c == owner) & (t != b))
        def _():
            remote(gbuf.at[b], rz.at[held[b], 0], z_sem.at[b], z_rec.at[b, 0], tp=t).wait_send()
    for s in range(S):
        for d in range(1, far + 1):
            @pl.when(c >= d)
            def _():
                dp_copy(d, s).wait_send()
        ag_drain(0, s, 1)
        ag_drain(1, s, 0)


def back(att, start, grad, out_w, fc, proj_t, params, q, kv, prev, low, out_t, logs, normed, wl, pick, block, far, counts):
    F, C, T = counts
    S, rows, hw = q.shape
    width = normed.shape[2]
    own_rows = rows // T
    tokens = S * own_rows
    shard = width // F
    hidden = fc.shape[1] // T
    cols = padded(hw)
    wide = 2 * hidden + cols
    bf, f32 = jnp.bfloat16, jnp.float32
    extra = 8 + pick.shape[1]
    mine = -(-T // C)
    dists = max(far, 1)
    vmem = pl.BlockSpec(memory_space=pltpu.VMEM)
    anywhere = pl.BlockSpec(memory_space=pl.ANY)
    dma = lambda *shape: pltpu.SemaphoreType.DMA(shape)
    one = pltpu.SemaphoreType.DMA
    shape = jax.ShapeDtypeStruct
    b16 = lambda *size: pltpu.VMEM(size, bf)
    b32 = lambda *size: pltpu.VMEM(size, f32)
    return pl.pallas_call(
        functools.partial(back_kernel, counts, block, far, 256),
        in_specs=[anywhere] * 6 + [vmem] + [anywhere] * 3 + [vmem, anywhere, vmem, anywhere, anywhere, vmem],
        out_specs=[anywhere, anywhere, vmem, vmem, vmem],
        out_shape=[
            shape((S, rows, width), bf),
            shape((S, rows, width), bf),
            shape((shard, wide), bf),
            shape((3 * hw, shard), f32),
            shape((extra, width), f32),
        ],
        scratch_shapes=[
            b16(S, own_rows, width), b32(tokens, width), b16(tokens, width), b16(S, own_rows, width),
            b16(2 * T + 4, shard, wide), b16(2, 2, shard, 2 * hidden), b16(T, shard, wide),
            b16(mine, max(C - 1, 1), shard, wide), b16(mine, 2, shard, wide),
            b16(4, T, shard, cols), b16(2, T, shard, cols), b16(T, shard, cols),
            b16(T, S, hw, own_rows), b16(T, S, hw, own_rows),
            b16(dists, S, T, 2 * hw, own_rows), b16(dists, S, T, 2 * hw, own_rows),
            b16(T, S, 2 * hw, own_rows), b16(T, S, hw, own_rows),
            b16(S, T + 1, width, own_rows),
            b16(F, 3 * hw, shard), b16(F - 1, 3 * hw, shard), b16(C, 3 * hw, shard),
            b32(extra, width), b32(T, extra, width), b32(C, extra, width), b32(F, extra, width),
            dma(4), dma(3, 2), dma(T, 2), dma(T, 2), dma(T), dma(T), dma(2), dma(2), one, one,
            dma(T), dma(T, C), dma(T), dma(T, 2), dma(C), one, dma(T, S), dma(T, S), dma(far + 1, S), dma(far + 1, S),
            dma(S, T), dma(S, T, 2), dma(2, S, T, 2), dma(2, S, T, 2), dma(F), dma(F), dma(C), dma(C),
            dma(T), dma(T), dma(C), dma(C), dma(F), dma(F), dma(2, S), one, pltpu.SemaphoreType.REGULAR,
        ],
        compiler_params=pltpu.CompilerParams(
            vmem_limit_bytes=VMEM_LIMIT, collective_id=2, has_side_effects=True
        ),
        cost_estimate=pl.CostEstimate(flops=36 * 10**9, bytes_accessed=100 << 20, transcendentals=16 << 20),
    )(att, start, grad, out_w, fc, proj_t, params, q, kv, prev, low, out_t, logs, normed, wl, pick)


def local(
    inputs, thoughts, positions, lengths, w_qkv, w_out, w_fc, w_proj, norm_gains, norm_biases, out_grad,
):
    rows, seqs, width = inputs.shape
    ctx_count = lax.axis_size("ctx")
    tp_count = lax.axis_size("tp")
    fsdp_count = lax.axis_size("fsdp")
    ctx, tp, fsdp = lax.axis_index("ctx"), lax.axis_index("tp"), lax.axis_index("fsdp")
    first_row = ctx * rows
    own_rows = rows // tp_count
    own_tokens = own_rows * seqs
    far = min(ctx_count - 1, -(-(DOC_MOST - 1) // rows))
    block = min(256, rows)
    bf, f32 = jnp.bfloat16, jnp.float32

    counts = (fsdp_count, ctx_count, tp_count)
    local_width = w_qkv.shape[2]
    params = jnp.pad(jnp.concatenate([norm_gains, norm_biases]).astype(f32), ((0, 4), (0, 0)))
    places = first_row + jnp.arange(rows, dtype=jnp.int32)
    is_thought = places[None, None, :] == positions[:, :, None]
    keep = jnp.logical_not(jnp.any(is_thought, axis=0))
    start = jnp.transpose(inputs, (1, 0, 2))
    for t in range(thoughts.shape[0]):
        start = jnp.where(is_thought[t][:, :, None], thoughts[t][:, None, :], start)
    ends = jnp.cumsum(lengths, axis=1, dtype=jnp.int32)
    low = jnp.max(jnp.where(ends[:, :, None] <= places[None, None, :], ends[:, :, None], 0), axis=1)
    low = low - (first_row - far * rows)

    low3 = low[:, None, :]
    attended, q, kv, prev, out_t, logs, normed, w_local, out_full, fc_full, proj_full_t, params = front(
        start, low3, w_qkv, w_out, w_fc, w_proj.T, params, block, far, counts
    )
    start_own = lax.dynamic_slice_in_dim(start, tp * own_rows, own_rows, 1)
    grad_own = jnp.transpose(
        lax.dynamic_slice_in_dim(out_grad, tp * own_rows, own_rows, 0), (1, 0, 2)
    ).reshape(own_tokens, width)

    own_places = lax.dynamic_slice_in_dim(places, tp * own_rows, own_rows, 0)
    count = thoughts.shape[0]
    pick = (own_places[None, None, :] == positions[:, :, None]).astype(bf)
    picks = []
    for s in range(seqs):
        picks.append(jnp.concatenate(
            [jnp.where(k == s, pick[:, s], jnp.zeros_like(pick[:, s])) for k in range(seqs)], axis=0
        ))
    pick = jnp.stack(picks)
    pick = jnp.pad(pick, ((0, 0), (0, -(-pick.shape[1] // 16) * 16 - pick.shape[1]), (0, 0)))
    output, d_start, gw, gq, small = back(
        attended, start_own, grad_own, out_full, fc_full, proj_full_t, params, q, kv, prev, low3, out_t, logs, normed,
        w_local, pick, block, far, counts,
    )
    output = jnp.transpose(output, (1, 0, 2))
    d_start = lax.optimization_barrier(jnp.transpose(d_start, (1, 0, 2)))
    d_inputs = jnp.where(keep.T[:, :, None], d_start.astype(f32), 0.0)
    d_thoughts = jnp.transpose(small[8 : 8 + count * seqs].reshape(seqs, count, width), (1, 0, 2))
    hidden = w_fc.shape[1]
    gw = gw.astype(f32)
    norms = lax.dynamic_slice_in_dim(small[:4], fsdp * w_fc.shape[0], w_fc.shape[0], 1)
    return (
        output,
        d_inputs,
        d_thoughts,
        jnp.transpose(gq.reshape(3, local_width, -1), (0, 2, 1)),
        gw[:, 2 * hidden : 2 * hidden + local_width].T,
        gw[:, :hidden],
        gw[:, hidden : 2 * hidden].T,
        norms[:2],
        norms[2],
        norms[3],
    )


def solution(mesh):
    in_specs = (
        P("ctx", "fsdp", None),
        P(None, "fsdp", None),
        P(None, "fsdp"),
        P("fsdp", None),
        P(None, "fsdp", "tp"),
        P("tp", "fsdp"),
        P("fsdp", "tp"),
        P("tp", "fsdp"),
        P(None, "fsdp"),
        P(None, "fsdp"),
        P("ctx", "fsdp", None),
    )
    out_specs = (
        P("ctx", "fsdp", None),
        P("ctx", "fsdp", None),
        P(None, "fsdp", None),
        P(None, "fsdp", "tp"),
        P("tp", "fsdp"),
        P("fsdp", "tp"),
        P("tp", "fsdp"),
        P(None, "fsdp"),
        P("fsdp"),
        P("fsdp"),
    )
    return jax.shard_map(local, mesh=mesh, in_specs=in_specs, out_specs=out_specs, check_vma=False)
```
